32 devices in a mesh: expert: 16 (over z, y, x), dp: 2 (over core).
Axes of the slice: x: 2, y: 2, z: 4, core: 2. Of those that a mesh axis runs over, the one named last changes fastest.
Arguments:
- tokens: bfloat16 [8192, 2048], P(('expert', 'dp')), may hold values from -6 to 6
- cotangent: bfloat16 [8192, 2048], P(('expert', 'dp')), may hold values from -6 to 6
- lengths: int32 [32], P(('expert', 'dp')), may hold values from 1 to 256, 5120 in all
- routes: int32 [8192, 8], P(('expert', 'dp')), may hold values from 0 to 15, all different within a row
- attention_gain: bfloat16 [2048], P('dp'), may hold values from 0.25 to 1.75
- query_gain: bfloat16 [2048], P('dp'), may hold values from 0.25 to 1.75
- key_gain: bfloat16 [2048], P('dp'), may hold values from 0.25 to 1.75
- feedforward_gain: bfloat16 [2048], P('dp'), may hold values from 0.25 to 1.75
- query_weight: bfloat16 [2048, 2048], P('dp'), may hold values from -0.125 to 0.125
- key_weight: bfloat16 [2048, 2048], P('dp'), may hold values from -0.125 to 0.125
- value_weight: bfloat16 [2048, 2048], P('dp'), may hold values from -0.125 to 0.125
- output_weight: bfloat16 [2048, 2048], P('dp'), may hold values from -1 to 1
- router_weight: bfloat16 [2048, 16], P('dp'), may hold values from -0.0625 to 0.0625
- expert_gate_up: bfloat16 [16, 2, 2048, 1024], P('expert', None, None, 'dp'), may hold values from -0.125 to 0.125
- expert_down: bfloat16 [16, 2048, 1024], P('expert', None, 'dp'), may hold values from -6 to 6
Outputs:
- result: bfloat16 [8192, 2048], P(('expert', 'dp'))
- grad_tokens: float32 [8192, 2048], P(('expert', 'dp'))
- grad_attention_gain: float32 [2048], P(('expert', 'dp'))
- grad_query_gain: float32 [2048], P(('expert', 'dp'))
- grad_key_gain: float32 [2048], P(('expert', 'dp'))
- grad_feedforward_gain: float32 [2048], P(('expert', 'dp'))
- grad_query_weight: float32 [2048, 2048], P(('expert', 'dp'))
- grad_key_weight: float32 [2048, 2048], P(('expert', 'dp'))
- grad_value_weight: float32 [2048, 2048], P(('expert', 'dp'))
- grad_output_weight: float32 [2048, 2048], P(('expert', 'dp'))
- grad_router_weight: float32 [2048, 16], P(('expert', 'dp'))
- grad_expert_gate_up: float32 [16, 2, 2048, 1024], P('expert', None, None, 'dp')
- grad_expert_down: float32 [16, 2048, 1024], P('expert', None, 'dp')
The draws below stay inside these ranges and needn't reach their ends.
Inputs may be any that keep to these rules, and one draw needn't show every extreme that they name: `routes`: each token names 8 different experts.
All inputs are finite; a program needn't handle non-finite values. No bound on the sum of `lengths` on one device may be relied on, other than what follows from the above.
Results may differ from the reference program's by a relative error of at most 0.019.
Values may be sent and summed in bfloat16 or wider, within the bound.
A program may use at most 384 MiB of HBM per device.

```python
import math
import jax
import jax.numpy as jnp
import numpy as np
from jax import lax

D = 2048
NH = 16
HD = 128
FF = 1024
TOP = 8
TOK_DEV = 256
EXPERTS = 16
CAP = 128
SEQS = 32
TOKENS = 8192


def raised(entries, own_key, source, target, shards_of, factor):
    def block_of(position):
        return (jnp.arange(entries.shape[position]) // (entries.shape[position] // shards_of)).reshape((-1,) + (1,) * (entries.ndim - 1 - position))

    first = jax.random.permutation(own_key, shards_of)[block_of(target)]
    other_side = (block_of(target) + shards_of // 2) % shards_of
    return jnp.where((block_of(source) == first) | (block_of(source) == other_side), factor * entries, entries)


def level_of(key, extent, cuts, least, largest):
    def one(position, blocks):
        heights = jax.random.uniform(jax.random.fold_in(jax.random.fold_in(key, 6), position), (blocks,), jnp.float32, least / len(cuts), largest / len(cuts))
        return jnp.repeat(jnp.exp(heights), extent[position] // blocks).reshape((-1,) + (1,) * (len(extent) - position - 1))

    loudness = one(*cuts[0])
    for cut in cuts[1:]:
        loudness = loudness * one(*cut)
    return loudness


def choose_distinct(own_key, rows, number_of, top, lift):
    sequence = jax.random.permutation(jax.random.fold_in(own_key, 1), number_of)
    favour = sequence
    for power in range(3):
        favour = favour * favour // number_of
    favour = favour * lift // number_of
    lots = jax.random.randint(jax.random.fold_in(own_key, 2), (rows, number_of), 0, 4096) + favour
    fixed_rows = jax.random.permutation(jax.random.fold_in(own_key, 3), rows)[jnp.arange(number_of) % rows]
    lots = jnp.where(jnp.arange(rows)[:, None] == fixed_rows[None, :], 1 << 14, lots)
    score = lots * number_of + jnp.arange(number_of)
    return lax.top_k(score.astype(jnp.int32), top)[1].astype(jnp.int32)


def split_up(amount, total, reach, slope):
    weights = [(1 << 20) // math.isqrt(rank ** slope) + 1 for rank in range(2, amount + 1)]
    spare, given = total - reach - (amount - 1), [1] * (amount - 1)
    while spare > 0:
        movable = [i for i in range(amount - 1) if given[i] < reach]
        mass, budget = sum([weights[i] for i in movable]), spare
        for i in movable:
            more = min(reach - given[i], max(1, budget * weights[i] // mass), spare)
            given[i] = given[i] + more
            spare = spare - more
    return np.array([reach] + given)


def uneven_parts(rng, count, total, bound, lean):
    if count == 2:
        one = jax.random.randint(rng, (), max(1, total - bound), min(bound, total - 1) + 1)
        return jnp.stack([one, total - one])
    sizes = jnp.asarray(split_up(count, total, bound, lean), jnp.int32)
    couples = (count - 1) // 2
    donor, taker = sizes[1:1 + 2 * couples:2], sizes[2:2 + 2 * couples:2]
    room = jnp.minimum(donor - 1, bound - taker)
    moved = jax.random.randint(jax.random.fold_in(rng, 1), (couples,), 0, 1 << 20) % (room + 1)
    sizes = sizes.at[1:1 + 2 * couples:2].set(donor - moved).at[2:2 + 2 * couples:2].set(taker + moved)
    return sizes[jax.random.permutation(jax.random.fold_in(rng, 2), count)]


def gaussian(own_key, shape, scale, reach, shards=(), held_as=jnp.bfloat16):
    values = scale * jax.random.normal(own_key, shape, jnp.float32)
    if shards:
        values = values * level_of(own_key, shape, shards, -0.22, 0.18)
    return jnp.clip(values, -reach, reach).astype(held_as)


def bell_draw_with(key, shape, deviation, bound, cuts, heavy, kind=jnp.bfloat16):
    result = deviation * jax.random.normal(key, shape, jnp.float32)
    if cuts:
        result = result * level_of(key, shape, cuts, -0.22, 0.18)
    return jnp.clip(raised(result, jax.random.fold_in(key, 3), *heavy), -bound, bound).astype(kind)


def setup_inputs(seed: int = 0) -> dict:
    arg_keys = jax.random.split(jax.random.key(seed), 16)
    tokens = bell_draw_with(arg_keys[0], (TOKENS, D), 1.0, 6.0, ((0, 32),), (0, 1, 32, 2.75))
    cotangent = gaussian(arg_keys[1], (TOKENS, D), 1.0, 6.0, ((0, 32),))
    lengths = uneven_parts(arg_keys[2], SEQS, SEQS * TOK_DEV * 5 // 8, TOK_DEV, 1).astype(jnp.int32)
    routes = choose_distinct(arg_keys[3], TOKENS, EXPERTS, TOP, 4096)
    attention_gain = jnp.clip(1.0 + 0.15 * jax.random.normal(arg_keys[4], (D,), jnp.float32), 0.25, 1.75).astype(jnp.bfloat16)
    query_gain = jnp.clip(1.0 + 0.15 * jax.random.normal(arg_keys[5], (D,), jnp.float32), 0.25, 1.75).astype(jnp.bfloat16)
    key_gain = jnp.clip(1.0 + 0.15 * jax.random.normal(arg_keys[6], (D,), jnp.float32), 0.25, 1.75).astype(jnp.bfloat16)
    feedforward_gain = jnp.clip(1.0 + 0.15 * jax.random.normal(arg_keys[7], (D,), jnp.float32), 0.25, 1.75).astype(jnp.bfloat16)
    query_weight = gaussian(arg_keys[8], (D, D), D ** -0.5, 0.125, ((0, 2),))
    key_weight = gaussian(arg_keys[9], (D, D), D ** -0.5, 0.125, ((0, 2),))
    value_weight = gaussian(arg_keys[10], (D, D), D ** -0.5, 0.125, ((0, 2),))
    output_weight = gaussian(arg_keys[11], (D, D), (D // 64) ** -0.5, 1.0, ((0, 2),))
    router_weight = gaussian(arg_keys[12], (D, EXPERTS), (4 * D) ** -0.5, 0.0625, ((0, 2),))
    expert_gate_up = gaussian(arg_keys[13], (EXPERTS, 2, D, FF), D ** -0.5, 0.125, ((0, 16), (3, 2)))
    expert_down = gaussian(arg_keys[14], (EXPERTS, D, FF), (max(FF // 1024, 1)) ** -0.5, 6.0, ((0, 16), (2, 2)))
    return {"tokens": tokens, "cotangent": cotangent, "lengths": lengths, "routes": routes, "attention_gain": attention_gain, "query_gain": query_gain, "key_gain": key_gain, "feedforward_gain": feedforward_gain, "query_weight": query_weight, "key_weight": key_weight, "value_weight": value_weight, "output_weight": output_weight, "router_weight": router_weight, "expert_gate_up": expert_gate_up, "expert_down": expert_down}


EPSILON = 1e-05
ROPE_BASE = 10000.0

@jax.custom_vjp
def low(v):
    return lax.optimization_barrier(v.astype(jnp.bfloat16)).astype(jnp.float32)

@jax.custom_vjp
def low_back(v):
    return v

def low_keep(v):
    return (low(v), None)

def low_pass(kept, grad):
    return (grad,)

def back_keep(v):
    return (v, None)

def back_low(kept, grad):
    return (low(grad),)
low.defvjp(low_keep, low_pass)
low_back.defvjp(back_keep, back_low)

def highest_dot(left, right):
    return jnp.dot(left, right, precision=lax.Precision.HIGHEST)

def rms_scale(values):
    return lax.rsqrt(lax.optimization_barrier(jnp.mean(values * values, axis=-1, keepdims=True)) + EPSILON)

def rotary_tables(positions):
    frequencies = 1.0 / ROPE_BASE ** (jnp.arange(0, HD, 2).astype(jnp.float32) / HD)
    angles = positions[:, None] * frequencies[None, :]
    angles = jnp.concatenate([angles, angles], axis=-1)
    return (jnp.cos(angles), jnp.sin(angles))

def rotary_norm(projected, gain_vector, cosine_table, sine_table):
    normed = projected * rms_scale(projected) * gain_vector
    shaped = normed.reshape(normed.shape[0], NH, HD)
    half_width = HD // 2
    turned = jnp.concatenate([-shaped[..., half_width:], shaped[..., :half_width]], axis=-1)
    rotated = shaped * cosine_table[:, None, :] + turned * sine_table[:, None, :]
    return rotated.reshape(normed.shape[0], NH * HD)

def routing_plan(routes, lengths):
    seq_count = lengths.shape[0]
    flat_routes = routes.reshape(seq_count, TOK_DEV * TOP).astype(jnp.int32)
    place_in_seq = (jnp.arange(TOK_DEV * TOP, dtype=jnp.int32) // TOP).astype(jnp.int32)
    live_pick = place_in_seq[None, :] < lengths[:, None]
    expert_ids = jnp.arange(EXPERTS, dtype=jnp.int32)
    route_hits = ((flat_routes[..., None] == expert_ids[None, None, :]) & live_pick[..., None]).astype(jnp.int32)
    before = jnp.cumsum(route_hits, axis=1) - route_hits
    slot_of = lax.optimization_barrier(jnp.sum(before * route_hits, axis=-1)).astype(jnp.int32)
    kept_pick = live_pick & (slot_of < CAP)
    seq_id = jnp.arange(seq_count, dtype=jnp.int32)[:, None]
    outside = EXPERTS * seq_count * CAP
    target = jnp.where(kept_pick, (flat_routes * seq_count + seq_id) * CAP + slot_of, outside).astype(jnp.int32)
    token_of = (seq_id * TOK_DEV + place_in_seq[None, :]).astype(jnp.int32)
    slot_token = jnp.zeros((outside + 1,), jnp.int32).at[target.reshape(-1)].set(token_of.reshape(-1))[:outside]
    filled = jnp.zeros((outside + 1,), jnp.float32).at[target.reshape(-1)].set(1.0)[:outside]
    return (slot_token.reshape(EXPERTS, seq_count * CAP), filled.reshape(EXPERTS, seq_count * CAP))

def attention_group(blocks):
    query_block, key_block, value_block, group_lengths = blocks
    seq_span = query_block.shape[1]
    scores = jnp.einsum('gthd,gshd->ghts', query_block, key_block, precision=lax.Precision.HIGHEST) * HD ** (-0.5)
    scores = low_back(scores)
    index_rows = jnp.arange(seq_span, dtype=jnp.int32)
    key_limit = jnp.minimum(index_rows[None, :], group_lengths[:, None] - 1)
    allowed = index_rows[None, None, :] <= key_limit[:, :, None]
    scores = jnp.where(allowed[:, None], scores, -1e+30)
    weights = low(jax.nn.softmax(scores, axis=-1))
    return jnp.einsum('ghts,gshd->gthd', weights, value_block, precision=lax.Precision.HIGHEST)

def reference(tokens, cotangent, lengths, routes, attention_gain, query_gain, key_gain, feedforward_gain, query_weight, key_weight, value_weight, output_weight, router_weight, expert_gate_up, expert_down):
    positions = (jnp.arange(TOKENS, dtype=jnp.int32) % TOK_DEV).astype(jnp.float32)
    cosine_table, sine_table = rotary_tables(positions)
    slot_token, filled = routing_plan(routes, lengths)
    group_size = math.gcd(SEQS, max(1, 4096 // TOK_DEV))

    def grouped(array):
        return array.reshape(SEQS // group_size, group_size, TOK_DEV, NH, HD)

    def forward(inputs, gain_in, gain_query, gain_key, gain_mid, query_full, key_full, value_full, output_full, router_full, gate_up_all, down_all):
        normed_in = low(inputs * rms_scale(inputs) * gain_in)
        query_pre = low_back(highest_dot(normed_in, query_full))
        key_pre = low_back(highest_dot(normed_in, key_full))
        value_all = low_back(low(highest_dot(normed_in, value_full)))
        query_rot = low(rotary_norm(query_pre, gain_query, cosine_table, sine_table))
        key_rot = low(rotary_norm(key_pre, gain_key, cosine_table, sine_table))
        attention_out = lax.map(jax.checkpoint(attention_group), (grouped(query_rot), grouped(key_rot), grouped(value_all), lengths.reshape(SEQS // group_size, group_size)))
        attended = low_back(low(attention_out.reshape(TOKENS, D)))
        middle = inputs + low_back(highest_dot(attended, output_full))
        normed_mid = low(middle * rms_scale(middle) * gain_mid)
        logits = low_back(highest_dot(normed_mid, router_full))
        gates = jax.nn.softmax(logits, axis=-1)

        def expert_step(running, expert_item):
            gate_up, down, index_rows, fill_rows, number = expert_item
            slot_rows = low_back(normed_mid[index_rows])
            gate_pre = low_back(highest_dot(slot_rows, gate_up[0]))
            up_pre = low_back(highest_dot(slot_rows, gate_up[1]))
            hidden = low(jax.nn.silu(gate_pre) * up_pre)
            outcome = low_back(low(highest_dot(hidden, down.T)))
            slot_share = gates[index_rows, number] * fill_rows
            return (running.at[index_rows].add(slot_share[:, None] * outcome), None)
        mixture = lax.scan(jax.checkpoint(expert_step), jnp.zeros((TOKENS, D), jnp.float32), (gate_up_all, down_all, slot_token, filled, jnp.arange(EXPERTS, dtype=jnp.int32)))[0]
        return middle + mixture
    floats = [tokens, attention_gain, query_gain, key_gain, feedforward_gain, query_weight, key_weight, value_weight, output_weight, router_weight, expert_gate_up, expert_down]
    floats = [array.astype(jnp.float32) for array in floats]
    output, pullback = jax.vjp(forward, *floats)
    gradients = pullback(cotangent.astype(jnp.float32))
    return (output.astype(jnp.bfloat16), gradients[0], gradients[1], gradients[2], gradients[3], gradients[4], gradients[5], gradients[6], gradients[7], gradients[8], gradients[9], gradients[10], gradients[11])
```

```python
import functools
import math

import jax
import jax.numpy as jnp
from jax import lax
from jax.experimental import pallas as pl
from jax.experimental.pallas import tpu as pltpu
from jax.sharding import PartitionSpec as P

NH = 16
HD = 128
TOP = 8
OUTER = 4

EPSILON = 1e-05
ROPE_BASE = 10000.0
MESH = pl.DeviceIdType.MESH
F32 = jnp.float32
BF16 = jnp.bfloat16


def rms_scale(values):
    return lax.rsqrt(jnp.mean(values * values, axis=-1, keepdims=True) + EPSILON)


def norm_apply(values, gain_vector):
    return values * rms_scale(values) * gain_vector


def rotary_tables(positions):
    frequencies = 1.0 / ROPE_BASE ** (jnp.arange(0, HD, 2).astype(F32) / HD)
    angles = positions[:, None] * frequencies[None, :]
    angles = jnp.concatenate([angles, angles], axis=-1)
    return (jnp.cos(angles), jnp.sin(angles))


def rotary_norm(projected, gain_vector, cosine_table, sine_table):
    normed = projected * rms_scale(projected) * gain_vector
    shaped = normed.reshape(normed.shape[0], NH, HD)
    half_width = HD // 2
    turned = jnp.concatenate([-shaped[..., half_width:], shaped[..., :half_width]], axis=-1)
    rotated = shaped * cosine_table[:, None, :] + turned * sine_table[:, None, :]
    return rotated.reshape(normed.shape[0], NH * HD)


def flip(r, n):
    out, bit = r, 1
    while bit <= n:
        if n & bit:
            out = out + bit - 2 * bit * ((r // bit) % 2)
        bit *= 2
    return out


def pick(table, z):
    code = sum(v * 4**k for k, v in enumerate(table))
    return (code // ((1 + 3 * (z % 2)) * (1 + 15 * (z // 2)))) % 4


NEAR = ((1, 0, 1, 2), (2, 2, 3, 1), (3, 3, 0, 0))
FAR = ((3, 3, 0, 0), (2, 0, 3, 1), (1, 2, 1, 2))


def group_barrier(z, r, c, per):
    bar = pltpu.get_barrier_semaphore()
    for d in range(1, OUTER):
        pl.semaphore_signal(
            bar, inc=1, device_id=((z + d) % OUTER * per + r, c), device_id_type=MESH
        )
    for n in range(1, per):
        pl.semaphore_signal(bar, inc=1, device_id=(z * per + flip(r, n), c), device_id_type=MESH)
    pl.semaphore_wait(bar, OUTER - 1 + per - 1)


def one_hot(pos_ref, z, r, j, per, cap):
    span = pos_ref.shape[-1]
    rows = []
    slot = lax.broadcasted_iota(jnp.int32, (cap, span), 0).astype(F32)
    for n in range(per):
        line = pos_ref[j * per + r, pl.ds(z * per + flip(r, n), 1), :]
        rows.append(jnp.where(line == slot, 1.0, 0.0).astype(BF16))
    return jnp.concatenate(rows, axis=0)


def dispatch_body(per, cap, x_ref, pos_ref, out_ref, zbuf, sbuf, zs, zr, ps, pr, ls):
    e, c = lax.axis_index("expert"), lax.axis_index("dp")
    z, r = e // per, e % per
    group_barrier(z, r, c, per)
    width = x_ref.shape[1]
    step = min(512, width)

    def up(src, j):
        return pltpu.make_async_remote_copy(
            src_ref=src, dst_ref=zbuf.at[j], send_sem=zs.at[0, j], recv_sem=zr.at[j],
            device_id=((z + 1) * per + r, c), device_id_type=MESH,
        )

    def down(src, j):
        return pltpu.make_async_remote_copy(
            src_ref=src, dst_ref=zbuf.at[j], send_sem=zs.at[1, j], recv_sem=zr.at[j],
            device_id=((z - 1) * per + r, c), device_id_type=MESH,
        )

    def plane(i, j, n):
        return pltpu.make_async_remote_copy(
            src_ref=sbuf.at[i, n], dst_ref=out_ref.at[j, n], send_sem=ps.at[i, n],
            recv_sem=pr.at[i, n], device_id=(z * per + flip(r, n), c), device_id_type=MESH,
        )

    def local(i, j):
        return pltpu.make_async_copy(sbuf.at[i, 0], out_ref.at[j, 0], ls.at[i])

    @pl.when(z < OUTER - 1)
    def _():
        up(x_ref, z).start()

    @pl.when(z > 0)
    def _():
        down(x_ref, z).start()

    order = [z] + [pick(t, z) for t in NEAR]
    for i, j in enumerate(order):
        if i == 0:
            block = x_ref
        else:
            block = zbuf.at[j]
            up(x_ref, j).wait_recv()

            @pl.when(jnp.logical_and(j < z, z < OUTER - 1))
            def _():
                up(zbuf.at[j], j).start()

            @pl.when(jnp.logical_and(j > z, z > 0))
            def _():
                down(zbuf.at[j], j).start()

        marks = one_hot(pos_ref, z, r, j, per, cap)

        @pl.loop(0, width // step)
        def _(k):
            columns = pl.ds(pl.multiple_of(k * step, step), step)
            got = jnp.dot(marks, block[:, columns], preferred_element_type=F32).astype(BF16)
            for n in range(per):
                sbuf[i, n, :, columns] = got[n * cap : (n + 1) * cap]

        for n in range(1, per):
            plane(i, j, n).start()
        local(i, j).start()
    for i, j in enumerate(order):
        local(i, j).wait()
        for n in range(1, per):
            plane(i, j, n).wait()

    @pl.when(z < OUTER - 1)
    def _():
        up(x_ref, z).wait_send()

    @pl.when(z > 0)
    def _():
        down(x_ref, z).wait_send()

    for j in order[1:]:
        @pl.when(jnp.logical_and(j < z, z < OUTER - 1))
        def _():
            up(zbuf.at[j], j).wait_send()

        @pl.when(jnp.logical_and(j > z, z > 0))
        def _():
            down(zbuf.at[j], j).wait_send()


def dispatch(x, pos_all, cap, number):
    experts = pos_all.shape[0]
    per = experts // OUTER
    span, width = x.shape
    return pl.pallas_call(
        functools.partial(dispatch_body, per, cap),
        out_shape=jax.ShapeDtypeStruct((OUTER, per, cap, width), BF16),
        in_specs=[pl.BlockSpec(memory_space=pltpu.VMEM)] * 2,
        out_specs=pl.BlockSpec(memory_space=pltpu.HBM),
        scratch_shapes=[
            pltpu.VMEM((OUTER, span, width), BF16),
            pltpu.VMEM((OUTER, per, cap, width), BF16),
            pltpu.SemaphoreType.DMA((2, OUTER)),
            pltpu.SemaphoreType.DMA((OUTER,)),
            pltpu.SemaphoreType.DMA((OUTER, per)),
            pltpu.SemaphoreType.DMA((OUTER, per)),
            pltpu.SemaphoreType.DMA((OUTER,)),
        ],
        compiler_params=pltpu.CompilerParams(
            collective_id=number, has_side_effects=True, vmem_limit_bytes=56 << 20
        ),
        name="dispatch",
    )(x, pos_all)


def combine_body(per, cap, y_ref, pos_ref, out_ref, ybuf, ubuf, rbuf, zs, zr, ps, pr, ls):
    e, c = lax.axis_index("expert"), lax.axis_index("dp")
    z, r = e // per, e % per
    group_barrier(z, r, c, per)
    span, width = out_ref.shape
    step = min(512, width)

    def plane(i, j, n):
        return pltpu.make_async_remote_copy(
            src_ref=y_ref.at[j, n], dst_ref=ybuf.at[i, n], send_sem=ps.at[i, n],
            recv_sem=pr.at[i, n], device_id=(z * per + flip(r, n), c), device_id_type=MESH,
        )

    def local(i, j):
        return pltpu.make_async_copy(y_ref.at[j, 0], ybuf.at[i, 0], ls.at[i])

    def up(i, j):
        return pltpu.make_async_remote_copy(
            src_ref=ubuf.at[i], dst_ref=rbuf.at[0, j], send_sem=zs.at[i], recv_sem=zr.at[0, j],
            device_id=((z + 1) * per + r, c), device_id_type=MESH,
        )

    def down(i, j):
        return pltpu.make_async_remote_copy(
            src_ref=ubuf.at[i], dst_ref=rbuf.at[1, j], send_sem=zs.at[i], recv_sem=zr.at[1, j],
            device_id=((z - 1) * per + r, c), device_id_type=MESH,
        )

    order = [pick(t, z) for t in FAR] + [z]
    for i, j in enumerate(order):
        for n in range(1, per):
            plane(i, j, n).start()
        local(i, j).start()
    for i, j in enumerate(order):
        marks = one_hot(pos_ref, z, r, j, per, cap)
        local(i, j).wait()
        for n in range(1, per):
            plane(i, j, n).wait_recv()

        @pl.loop(0, width // step)
        def _(k):
            columns = pl.ds(pl.multiple_of(k * step, step), step)
            rows = jnp.concatenate([ybuf[i, n, :, columns] for n in range(per)], axis=0)
            out_ref[:, columns] = lax.dot_general(
                marks, rows, (((0,), (0,)), ((), ())), preferred_element_type=F32
            )

        if i < OUTER - 1:

            @pl.when(jnp.logical_and(j > z, z > 0))
            def _():
                up(0, j).wait_recv()
                out_ref[...] += rbuf[0, j].astype(F32)

            @pl.when(jnp.logical_and(j < z, z < OUTER - 1))
            def _():
                down(0, j).wait_recv()
                out_ref[...] += rbuf[1, j].astype(F32)

            ubuf[i] = out_ref[...].astype(BF16)

            @pl.when(j > z)
            def _():
                up(i, j).start()

            @pl.when(j < z)
            def _():
                down(i, j).start()
        else:

            @pl.when(z > 0)
            def _():
                up(0, z).wait_recv()
                out_ref[...] += rbuf[0, z].astype(F32)

            @pl.when(z < OUTER - 1)
            def _():
                down(0, z).wait_recv()
                out_ref[...] += rbuf[1, z].astype(F32)

    for i, j in enumerate(order):
        for n in range(1, per):
            plane(i, j, n).wait_send()
        if i < OUTER - 1:
            up(i, j).wait_send()


def combine(y, pos_all, span, number):
    outer, per, cap, width = y.shape
    return pl.pallas_call(
        functools.partial(combine_body, per, cap),
        out_shape=jax.ShapeDtypeStruct((span, width), F32),
        in_specs=[
            pl.BlockSpec(memory_space=pltpu.HBM),
            pl.BlockSpec(memory_space=pltpu.VMEM),
        ],
        out_specs=pl.BlockSpec(memory_space=pltpu.VMEM),
        scratch_shapes=[
            pltpu.VMEM((OUTER, per, cap, width), BF16),
            pltpu.VMEM((OUTER - 1, span, width), BF16),
            pltpu.VMEM((2, OUTER, span, width), BF16),
            pltpu.SemaphoreType.DMA((OUTER - 1,)),
            pltpu.SemaphoreType.DMA((2, OUTER)),
            pltpu.SemaphoreType.DMA((OUTER, per)),
            pltpu.SemaphoreType.DMA((OUTER, per)),
            pltpu.SemaphoreType.DMA((OUTER,)),
        ],
        compiler_params=pltpu.CompilerParams(
            collective_id=number, has_side_effects=True, vmem_limit_bytes=56 << 20
        ),
        name="combine",
    )(y, pos_all)


def body(
    tokens,
    cotangent,
    lengths,
    routes,
    attention_gain,
    query_gain,
    key_gain,
    feedforward_gain,
    query_weight,
    key_weight,
    value_weight,
    output_weight,
    router_weight,
    expert_gate_up,
    expert_down,
):
    span, width = tokens.shape
    gains = lax.all_gather(
        jnp.stack([attention_gain, query_gain, key_gain, feedforward_gain]),
        "dp", axis=1, tiled=True,
    ).astype(F32)
    gain_in, gain_query, gain_key, gain_mid = gains[0], gains[1], gains[2], gains[3]

    def full(part, axis=0):
        return lax.all_gather(part, "dp", axis=axis, tiled=True)

    query_full, key_full, value_full, output_full, router_full = [
        full(part)
        for part in (query_weight, key_weight, value_weight, output_weight, router_weight)
    ]
    gate_full = full(expert_gate_up[0, 0], 1)
    up_full = full(expert_gate_up[0, 1], 1)
    down_full = full(expert_down[0], 1)
    experts = router_full.shape[1]
    cap = span * TOP // experts
    per = experts // OUTER
    me = lax.axis_index("expert")
    core = lax.axis_index("dp")

    seq_length = lengths[0]
    index_rows = jnp.arange(span, dtype=jnp.int32)
    expert_ids = jnp.arange(experts, dtype=jnp.int32)
    hits = jnp.any(routes[None, :, :] == expert_ids[:, None, None], axis=-1)
    hits = hits & (index_rows < seq_length)[None, :]
    earlier = (index_rows[:, None] < index_rows[None, :]).astype(BF16)
    before = jnp.dot(hits.astype(BF16), earlier, preferred_element_type=F32)
    kept = hits & (before < cap)
    pos = jnp.where(kept, before, -1.0)
    pos_all = lax.all_gather(pos, "expert", axis=0)

    cot_slots = dispatch(cotangent, pos_all, cap, 1).reshape(experts * cap, width)

    inputs = tokens.astype(F32)
    normed_f, norm_in_back = jax.vjp(norm_apply, inputs, gain_in)
    normed_in = normed_f.astype(BF16)
    query_pre = jnp.dot(normed_in, query_full, preferred_element_type=F32)
    key_pre = jnp.dot(normed_in, key_full, preferred_element_type=F32)
    value_all = jnp.dot(normed_in, value_full, preferred_element_type=F32).astype(BF16)
    cosine_table, sine_table = rotary_tables(jnp.arange(span).astype(F32))
    query_f, query_back = jax.vjp(
        lambda projected, gain: rotary_norm(projected, gain, cosine_table, sine_table),
        query_pre, gain_query,
    )
    key_f, key_back = jax.vjp(
        lambda projected, gain: rotary_norm(projected, gain, cosine_table, sine_table),
        key_pre, gain_key,
    )
    query_rot = query_f.astype(BF16).reshape(span, NH, HD)
    key_rot = key_f.astype(BF16).reshape(span, NH, HD)
    value_heads = value_all.reshape(span, NH, HD)
    key_limit = jnp.minimum(index_rows, seq_length - 1)
    allowed = index_rows[None, :] <= key_limit[:, None]
    score_scale = HD ** (-0.5)

    def scores_of():
        raw = jnp.einsum("thd,shd->hts", query_rot, key_rot, preferred_element_type=F32)
        return jnp.where(allowed[None], raw * score_scale, -1e30)

    scores = scores_of()
    row_peak = jnp.max(scores, axis=-1, keepdims=True)
    log_total = row_peak + jnp.log(jnp.sum(jnp.exp(scores - row_peak), axis=-1, keepdims=True))
    weights_low = jnp.exp(scores - log_total).astype(BF16)
    attended = jnp.einsum("hts,shd->thd", weights_low, value_heads, preferred_element_type=F32)
    attended = attended.reshape(span, width).astype(BF16)
    middle = inputs + jnp.dot(attended, output_full, preferred_element_type=F32)
    normed_mid_f, norm_mid_back = jax.vjp(norm_apply, middle, gain_mid)
    normed_mid = normed_mid_f.astype(BF16)
    logits = jnp.dot(normed_mid, router_full, preferred_element_type=F32)
    gates = jax.nn.softmax(logits, axis=-1)
    gates_all = lax.all_gather(gates.T, "expert", axis=0)

    slots = dispatch(normed_mid, pos_all, cap, 2).reshape(experts * cap, width)

    rank = me % per
    ring = jnp.arange(per, dtype=jnp.int32) ^ rank
    seqs = (jnp.arange(OUTER, dtype=jnp.int32)[:, None] * per + ring[None, :]).reshape(-1)
    pos_here = lax.dynamic_index_in_dim(pos_all, me, axis=1, keepdims=False)[seqs]
    gates_here = lax.dynamic_index_in_dim(gates_all, me, axis=1, keepdims=False)[seqs]
    marks = pos_here[:, None, :] == jnp.arange(cap, dtype=jnp.int32).astype(F32)[None, :, None]
    slot_gate = jnp.sum(jnp.where(marks, gates_here[:, None, :], 0.0), axis=-1)
    slot_gate = slot_gate.reshape(experts * cap, 1)

    def mul(left, right, spec):
        return jnp.einsum(spec, left, right, preferred_element_type=F32)

    gate_pre = mul(slots, gate_full, "sd,df->sf")
    up_pre = mul(slots, up_full, "sd,df->sf")
    sigmoid_gate = jax.nn.sigmoid(gate_pre)
    silu_gate = gate_pre * sigmoid_gate
    hidden = (silu_gate * up_pre).astype(BF16)
    pulled = mul(cot_slots, down_full, "sd,df->sf")
    gate_grad = jnp.sum(hidden.astype(F32) * pulled, axis=-1)
    hidden_grad = pulled * slot_gate
    gate_grad_low = (
        hidden_grad * up_pre * sigmoid_gate * (1.0 + gate_pre * (1.0 - sigmoid_gate))
    ).astype(BF16)
    up_grad_low = (hidden_grad * silu_gate).astype(BF16)
    row_grad = mul(gate_grad_low, gate_full, "sf,df->sd") + mul(up_grad_low, up_full, "sf,df->sd")
    back_rows = combine(row_grad.astype(BF16).reshape(OUTER, per, cap, width), pos_all, span, 3)

    gate_grad = gate_grad.reshape(experts, cap, 1)
    token_grad = jnp.sum(jnp.where(marks, gate_grad, 0.0), axis=1)
    token_grad = token_grad.reshape(OUTER, per, span)[:, ring].reshape(experts, span)
    prob_grad = lax.all_to_all(token_grad, "expert", split_axis=0, concat_axis=0, tiled=True).T

    expert_out = mul(hidden, down_full, "sf,df->sd") * slot_gate
    mixture = combine(expert_out.astype(BF16).reshape(OUTER, per, cap, width), pos_all, span, 4)
    output = (middle + mixture).astype(BF16)

    hidden_gated = (hidden.astype(F32) * slot_gate).astype(BF16)
    local_gate = mul(slots, gate_grad_low, "sd,sf->df")
    local_up = mul(slots, up_grad_low, "sd,sf->df")
    local_down = mul(cot_slots, hidden_gated, "sd,sf->df")
    grad_gate_up = lax.psum_scatter(
        jnp.stack([local_gate, local_up]), "dp", scatter_dimension=2, tiled=True
    )[None]
    grad_down = lax.psum_scatter(local_down, "dp", scatter_dimension=1, tiled=True)[None]

    upstream = cotangent.astype(F32)
    logit_grad = (
        gates * (prob_grad - jnp.sum(gates * prob_grad, axis=-1, keepdims=True))
    ).astype(BF16)
    grad_router = mul(normed_mid, logit_grad, "td,te->de")
    mid_normed_grad = mul(logit_grad, router_full, "te,de->td") + back_rows
    mid_input_grad, grad_mid_gain = norm_mid_back(mid_normed_grad)
    middle_grad = upstream + mid_input_grad
    branch_grad = middle_grad.astype(BF16)
    grad_output = mul(attended, branch_grad, "ti,to->io")
    attended_grad = mul(branch_grad, output_full, "to,io->ti").astype(BF16)
    attended_grad = attended_grad.reshape(span, NH, HD)
    weights_full = jnp.exp(scores_of() - log_total)
    weights_grad = mul(attended_grad, value_heads, "thd,shd->hts")
    value_grad = mul(weights_full.astype(BF16), attended_grad, "hts,thd->shd")
    value_grad = value_grad.reshape(span, width).astype(BF16)
    centre = jnp.sum(weights_full * weights_grad, axis=-1, keepdims=True)
    score_grad = (weights_full * (weights_grad - centre)).astype(BF16)
    query_rot_grad = mul(score_grad, key_rot, "hts,shd->thd").reshape(span, width) * score_scale
    key_rot_grad = mul(score_grad, query_rot, "hts,thd->shd").reshape(span, width) * score_scale
    query_pre_grad, grad_query_gain = query_back(query_rot_grad)
    key_pre_grad, grad_key_gain = key_back(key_rot_grad)
    query_low = query_pre_grad.astype(BF16)
    key_low = key_pre_grad.astype(BF16)
    grad_query = mul(normed_in, query_low, "ti,to->io")
    grad_key = mul(normed_in, key_low, "ti,to->io")
    grad_value = mul(normed_in, value_grad, "ti,to->io")
    normed_in_grad = mul(query_low, query_full, "to,io->ti")
    normed_in_grad = normed_in_grad + mul(key_low, key_full, "to,io->ti")
    normed_in_grad = normed_in_grad + mul(value_grad, value_full, "to,io->ti")
    input_grad, grad_in_gain = norm_in_back(normed_in_grad)
    grad_tokens = middle_grad + input_grad

    def spread(grad):
        rows, columns = grad.shape
        grid = grad.astype(BF16).reshape(experts, 2, rows // experts // 2, columns)
        half = lax.psum_scatter(grid.swapaxes(0, 1), "dp", scatter_dimension=0, tiled=False)
        return lax.psum_scatter(half, "expert", scatter_dimension=0, tiled=False).astype(F32)

    small = jnp.concatenate(
        [
            jnp.stack([grad_in_gain, grad_query_gain, grad_key_gain, grad_mid_gain]).T,
            grad_router,
        ],
        axis=1,
    )
    small = lax.psum_scatter(small, ("expert", "dp"), scatter_dimension=0, tiled=True)
    return (
        output,
        grad_tokens,
        small[:, 0],
        small[:, 1],
        small[:, 2],
        small[:, 3],
        spread(grad_query),
        spread(grad_key),
        spread(grad_value),
        spread(grad_output),
        small[:, 4:],
        grad_gate_up,
        grad_down,
    )


def solution(mesh):
    both = P(("expert", "dp"))
    rows = P(("expert", "dp"), None)
    in_specs = (rows, rows, both, rows) + (P("dp"),) * 4 + (P("dp", None),) * 5 + (
        P("expert", None, None, "dp"),
        P("expert", None, "dp"),
    )
    out_specs = (rows, rows) + (both,) * 4 + (rows,) * 5 + (
        P("expert", None, None, "dp"),
        P("expert", None, "dp"),
    )
    return jax.shard_map(body, mesh=mesh, in_specs=in_specs, out_specs=out_specs, check_vma=False)
```

```python
import functools
import math

import jax
import jax.numpy as jnp
from jax import lax
from jax.experimental import pallas as pl
from jax.experimental.layout import Layout, with_layout_constraint
from jax.experimental.pallas import tpu as pltpu
from jax.sharding import PartitionSpec as P

NH = 16
HD = 128
TOP = 8
OUTER = 4

EPSILON = 1e-05
ROPE_BASE = 10000.0
MESH = pl.DeviceIdType.MESH
F32 = jnp.float32
BF16 = jnp.bfloat16


def rms_scale(values):
    return lax.rsqrt(jnp.mean(values * values, axis=-1, keepdims=True) + EPSILON)


def norm_apply(values, gain_vector):
    return values * rms_scale(values) * gain_vector


def rotary_tables(positions):
    frequencies = 1.0 / ROPE_BASE ** (jnp.arange(0, HD, 2).astype(F32) / HD)
    angles = positions[:, None] * frequencies[None, :]
    angles = jnp.concatenate([angles, angles], axis=-1)
    return (jnp.cos(angles), jnp.sin(angles))


def rotary_norm(projected, gain_vector, cosine_table, sine_table):
    normed = projected * rms_scale(projected) * gain_vector
    shaped = normed.reshape(normed.shape[0], NH, HD)
    half_width = HD // 2
    turned = jnp.concatenate([-shaped[..., half_width:], shaped[..., :half_width]], axis=-1)
    rotated = shaped * cosine_table[:, None, :] + turned * sine_table[:, None, :]
    return rotated.reshape(normed.shape[0], NH * HD)


def flip(r, n):
    out, bit = r, 1
    while bit <= n:
        if n & bit:
            out = out + bit - 2 * bit * ((r // bit) % 2)
        bit *= 2
    return out


def pick(table, z):
    code = sum(v * 4**k for k, v in enumerate(table))
    return (code // ((1 + 3 * (z % 2)) * (1 + 15 * (z // 2)))) % 4


NEAR = ((1, 0, 1, 2), (2, 2, 3, 1), (3, 3, 0, 0))
FAR = ((3, 3, 0, 0), (2, 0, 3, 1), (1, 2, 1, 2))


def group_barrier(z, r, c, per):
    bar = pltpu.get_barrier_semaphore()
    for d in range(1, OUTER):
        pl.semaphore_signal(
            bar, inc=1, device_id=((z + d) % OUTER * per + r, c), device_id_type=MESH
        )
    for n in range(1, per):
        pl.semaphore_signal(bar, inc=1, device_id=(z * per + flip(r, n), c), device_id_type=MESH)
    pl.semaphore_wait(bar, OUTER - 1 + per - 1)


def one_hot(pos_ref, r, j, per, cap):
    span = pos_ref.shape[-1]
    rows = []
    slot = lax.broadcasted_iota(jnp.int32, (cap, span), 0).astype(F32)
    for n in range(per):
        line = pos_ref[j, flip(r, n)]
        rows.append(jnp.where(line == slot, 1.0, 0.0).astype(BF16))
    return jnp.concatenate(rows, axis=0)


def dispatch_body(per, cap, first, *refs):
    if first:
        x_ref, meta_ref, out_ref, here_ref, pos_ref, zbuf, sbuf = refs[:7]
        zs, zr, ps, pr, ls, ms, mr, ts, tr = refs[7:]
    else:
        x_ref, meta_ref, pos_ref, out_ref, here_ref, zbuf, sbuf = refs[:7]
        zs, zr, ps, pr, ls, ms, mr = refs[7:]
    e, c = lax.axis_index("expert"), lax.axis_index("dp")
    z, r = e // per, e % per
    experts = OUTER * per
    bar = pltpu.get_barrier_semaphore()
    for d in range(1, experts):
        pl.semaphore_signal(bar, inc=1, device_id=((e + d) % experts, c), device_id_type=MESH)
    pl.semaphore_wait(bar, experts - 1)
    width = x_ref.shape[1]
    step = min(512, width)

    def share(d):
        to = (e + d) % experts
        return pltpu.make_async_remote_copy(
            src_ref=meta_ref.at[to], dst_ref=here_ref.at[e], send_sem=ms.at[d - 1],
            recv_sem=mr.at[d - 1], device_id=(to, c), device_id_type=MESH,
        )

    def table(d):
        to = (z + d) % OUTER
        return pltpu.make_async_remote_copy(
            src_ref=meta_ref.at[pl.ds(to * per, per)], dst_ref=pos_ref.at[z],
            send_sem=ts.at[d - 1], recv_sem=tr.at[z],
            device_id=(to * per + r, c), device_id_type=MESH,
        )

    def tabled(j):
        return pltpu.make_async_remote_copy(
            src_ref=meta_ref.at[pl.ds(0, per)], dst_ref=pos_ref.at[j], send_sem=ts.at[0],
            recv_sem=tr.at[j], device_id=(j * per + r, c), device_id_type=MESH,
        )

    def up(src, j):
        return pltpu.make_async_remote_copy(
            src_ref=src, dst_ref=zbuf.at[j], send_sem=zs.at[0, j], recv_sem=zr.at[j],
            device_id=((z + 1) * per + r, c), device_id_type=MESH,
        )

    def down(src, j):
        return pltpu.make_async_remote_copy(
            src_ref=src, dst_ref=zbuf.at[j], send_sem=zs.at[1, j], recv_sem=zr.at[j],
            device_id=((z - 1) * per + r, c), device_id_type=MESH,
        )

    def plane(i, j, n):
        return pltpu.make_async_remote_copy(
            src_ref=sbuf.at[i, n], dst_ref=out_ref.at[j, n], send_sem=ps.at[i, n],
            recv_sem=pr.at[i, n], device_id=(z * per + flip(r, n), c), device_id_type=MESH,
        )

    def local(i, j):
        return pltpu.make_async_copy(sbuf.at[i, 0], out_ref.at[j, 0], ls.at[i])

    if first:
        for d in range(1, OUTER):
            table(d).start()

    @pl.when(z < OUTER - 1)
    def _():
        up(x_ref, z).start()

    @pl.when(z > 0)
    def _():
        down(x_ref, z).start()

    if first:
        pos_ref[z] = meta_ref[pl.ds(z * per, per)]
    here_ref[e] = meta_ref[e]
    order = [z] + [pick(t, z) for t in NEAR]
    for i, j in enumerate(order):
        if i == 0:
            block = x_ref
        else:
            block = zbuf.at[j]
            up(x_ref, j).wait_recv()

            @pl.when(jnp.logical_and(j < z, z < OUTER - 1))
            def _():
                up(zbuf.at[j], j).start()

            @pl.when(jnp.logical_and(j > z, z > 0))
            def _():
                down(zbuf.at[j], j).start()

            if first:
                tabled(j).wait_recv()

        marks = one_hot(pos_ref, r, j, per, cap)

        @pl.loop(0, width // step)
        def _(k):
            columns = pl.ds(pl.multiple_of(k * step, step), step)
            got = jnp.dot(marks, block[:, columns], preferred_element_type=F32).astype(BF16)
            for n in range(per):
                sbuf[i, n, :, columns] = got[n * cap : (n + 1) * cap]

        for n in range(1, per):
            plane(i, j, n).start()
        local(i, j).start()
        if i == 0:
            for d in range(1, experts):
                share(d).start()
    for i, j in enumerate(order):
        local(i, j).wait()
        for n in range(1, per):
            plane(i, j, n).wait()

    @pl.when(z < OUTER - 1)
    def _():
        up(x_ref, z).wait_send()

    @pl.when(z > 0)
    def _():
        down(x_ref, z).wait_send()

    for i, j in enumerate(order):
        if i > 0:

            @pl.when(jnp.logical_and(j < z, z < OUTER - 1))
            def _():
                up(zbuf.at[j], j).wait_send()

            @pl.when(jnp.logical_and(j > z, z > 0))
            def _():
                down(zbuf.at[j], j).wait_send()

    for d in range(1, experts):
        share(d).wait()
    if first:
        for d in range(1, OUTER):
            table(d).wait_send()


def dispatch(x, meta, pos, cap, number):
    experts, _, span = meta.shape
    per = experts // OUTER
    width = x.shape[1]
    first = pos is None
    vmem = pl.BlockSpec(memory_space=pltpu.VMEM)
    dma = pltpu.SemaphoreType.DMA
    return pl.pallas_call(
        functools.partial(dispatch_body, per, cap, first),
        out_shape=(
            jax.ShapeDtypeStruct((OUTER, per, cap, width), BF16),
            jax.ShapeDtypeStruct((experts, 1, span), F32),
        )
        + ((jax.ShapeDtypeStruct((OUTER, per, 1, span), F32),) if first else ()),
        in_specs=[vmem] * (2 if first else 3),
        out_specs=(pl.BlockSpec(memory_space=pltpu.HBM), vmem) + ((vmem,) if first else ()),
        scratch_shapes=[
            pltpu.VMEM((OUTER, span, width), BF16),
            pltpu.VMEM((OUTER, per, cap, width), BF16),
            dma((2, OUTER)),
            dma((OUTER,)),
            dma((OUTER, per)),
            dma((OUTER, per)),
            dma((OUTER,)),
            dma((experts,)),
            dma((experts,)),
        ]
        + ([dma((OUTER,)), dma((OUTER,))] if first else []),
        compiler_params=pltpu.CompilerParams(
            collective_id=number, has_side_effects=True, vmem_limit_bytes=56 << 20
        ),
        name="dispatch",
    )(x, meta, *(() if first else (pos,)))


def combine_body(per, cap, y_ref, pos_ref, out_ref, ybuf, ubuf, rbuf, zs, zr, ps, pr, ls):
    e, c = lax.axis_index("expert"), lax.axis_index("dp")
    z, r = e // per, e % per
    group_barrier(z, r, c, per)
    span, width = out_ref.shape
    step = min(512, width)

    def plane(i, j, n):
        return pltpu.make_async_remote_copy(
            src_ref=y_ref.at[j, n], dst_ref=ybuf.at[i, n], send_sem=ps.at[i, n],
            recv_sem=pr.at[i, n], device_id=(z * per + flip(r, n), c), device_id_type=MESH,
        )

    def local(i, j):
        return pltpu.make_async_copy(y_ref.at[j, 0], ybuf.at[i, 0], ls.at[i])

    def up(i, j):
        return pltpu.make_async_remote_copy(
            src_ref=ubuf.at[i], dst_ref=rbuf.at[0, j], send_sem=zs.at[i], recv_sem=zr.at[0, j],
            device_id=((z + 1) * per + r, c), device_id_type=MESH,
        )

    def down(i, j):
        return pltpu.make_async_remote_copy(
            src_ref=ubuf.at[i], dst_ref=rbuf.at[1, j], send_sem=zs.at[i], recv_sem=zr.at[1, j],
            device_id=((z - 1) * per + r, c), device_id_type=MESH,
        )

    order = [pick(t, z) for t in FAR] + [z]
    for i, j in enumerate(order):
        for n in range(1, per):
            plane(i, j, n).start()
        local(i, j).start()
    for i, j in enumerate(order):
        marks = one_hot(pos_ref, r, j, per, cap)
        local(i, j).wait()
        for n in range(1, per):
            plane(i, j, n).wait_recv()

        @pl.loop(0, width // step)
        def _(k):
            columns = pl.ds(pl.multiple_of(k * step, step), step)
            rows = jnp.concatenate([ybuf[i, n, :, columns] for n in range(per)], axis=0)
            out_ref[:, columns] = lax.dot_general(
                marks, rows, (((0,), (0,)), ((), ())), preferred_element_type=F32
            )

        if i < OUTER - 1:

            @pl.when(jnp.logical_and(j > z, z > 0))
            def _():
                up(0, j).wait_recv()
                out_ref[...] += rbuf[0, j].astype(F32)

            @pl.when(jnp.logical_and(j < z, z < OUTER - 1))
            def _():
                down(0, j).wait_recv()
                out_ref[...] += rbuf[1, j].astype(F32)

            ubuf[i] = out_ref[...].astype(BF16)

            @pl.when(j > z)
            def _():
                up(i, j).start()

            @pl.when(j < z)
            def _():
                down(i, j).start()
        else:

            @pl.when(z > 0)
            def _():
                up(0, z).wait_recv()
                out_ref[...] += rbuf[0, z].astype(F32)

            @pl.when(z < OUTER - 1)
            def _():
                down(0, z).wait_recv()
                out_ref[...] += rbuf[1, z].astype(F32)

    for i, j in enumerate(order):
        for n in range(1, per):
            plane(i, j, n).wait_send()
        if i < OUTER - 1:
            up(i, j).wait_send()


def combine(y, pos_all, span, number):
    outer, per, cap, width = y.shape
    return pl.pallas_call(
        functools.partial(combine_body, per, cap),
        out_shape=jax.ShapeDtypeStruct((span, width), F32),
        in_specs=[
            pl.BlockSpec(memory_space=pltpu.HBM),
            pl.BlockSpec(memory_space=pltpu.VMEM),
        ],
        out_specs=pl.BlockSpec(memory_space=pltpu.VMEM),
        scratch_shapes=[
            pltpu.VMEM((OUTER, per, cap, width), BF16),
            pltpu.VMEM((OUTER - 1, span, width), BF16),
            pltpu.VMEM((2, OUTER, span, width), BF16),
            pltpu.SemaphoreType.DMA((OUTER - 1,)),
            pltpu.SemaphoreType.DMA((2, OUTER)),
            pltpu.SemaphoreType.DMA((OUTER, per)),
            pltpu.SemaphoreType.DMA((OUTER, per)),
            pltpu.SemaphoreType.DMA((OUTER,)),
        ],
        compiler_params=pltpu.CompilerParams(
            collective_id=number, has_side_effects=True, vmem_limit_bytes=56 << 20
        ),
        name="combine",
    )(y, pos_all)


def weights_body(per, rows, *refs):
    mats = len(SOURCE)
    x_refs, refs = refs[: 2 * per], refs[2 * per :]
    y_refs, refs = refs[:mats], refs[mats:]
    out_ref, xbuf, ybuf, gbuf, ubuf, rbuf, hbuf, obuf = refs[:8]
    xs, ys, yr, zs, zr, fs, fr = refs[8:]
    e, c = lax.axis_index("expert"), lax.axis_index("dp")
    z, r = e // per, e % per
    width = y_refs[0].shape[1]
    part = width // (2 * per)
    lines = width // OUTER
    peers = [(n, f) for n in range(per) for f in range(2)]

    def device(n, f):
        return flip(r, n), (c + f) % 2

    bar = pltpu.get_barrier_semaphore()
    for d in range(1, OUTER):
        pl.semaphore_signal(
            bar, inc=1, device_id=((z + d) % OUTER * per + r, c), device_id_type=MESH
        )
    for n, f in peers[1:]:
        q, k = device(n, f)
        pl.semaphore_signal(bar, inc=1, device_id=(z * per + q, k), device_id_type=MESH)
    pl.semaphore_wait(bar, OUTER - 1 + 2 * per - 1)

    def columns(q, k):
        return pl.ds(pl.multiple_of((q * 2 + k) * part, part), part)

    def spread(m, i):
        q, k = device(*peers[i])
        return pltpu.make_async_remote_copy(
            src_ref=y_refs[m].at[:, columns(q, k)], dst_ref=ybuf.at[m, i],
            send_sem=ys.at[m, i], recv_sem=yr.at[m, i],
            device_id=(z * per + q, k), device_id_type=MESH,
        )

    def hop(m, i, j, way):
        return pltpu.make_async_remote_copy(
            src_ref=ubuf.at[m, i], dst_ref=rbuf.at[m, way, j],
            send_sem=zs.at[m, i], recv_sem=zr.at[m, way, j],
            device_id=((z + 1 - 2 * way) * per + r, c), device_id_type=MESH,
        )

    def final(m, i):
        q, k = device(*peers[i])
        return pltpu.make_async_remote_copy(
            src_ref=hbuf.at[m, pl.ds(pl.multiple_of((q * 2 + k) * rows, rows), rows)],
            dst_ref=obuf.at[m, i], send_sem=fs.at[m, i], recv_sem=fr.at[m, i],
            device_id=(z * per + q, k), device_id_type=MESH,
        )

    for m in range(mats):
        for i in range(1, 2 * per):
            spread(m, i).start()
    for i in range(2 * per):
        pltpu.make_async_copy(x_refs[i], xbuf.at[i], xs.at[i]).start()
    for m in range(mats):
        ybuf[m, 0] = y_refs[m][:, columns(r, c)]
    for i in range(2 * per):
        pltpu.make_async_copy(x_refs[i], xbuf.at[i], xs.at[i]).wait()

    order = [pick(t, z) for t in FAR]
    for m in range(mats):
        for i in range(1, 2 * per):
            spread(m, i).wait_recv()
        for i, j in enumerate(order + [z]):
            at = pl.ds(pl.multiple_of(j * lines, lines), lines)
            total = jnp.zeros((lines, part), F32)
            for s in range(2 * per):
                total += jnp.dot(
                    xbuf[s, SOURCE[m], at, :], ybuf[m, s], preferred_element_type=F32
                )
            gbuf[m, i] = total
            if i < OUTER - 1:

                @pl.when(jnp.logical_and(j > z, z == 0))
                def _():
                    ubuf[m, i] = total.astype(BF16)
                    hop(m, i, j, 0).start()

                @pl.when(jnp.logical_and(j < z, z == OUTER - 1))
                def _():
                    ubuf[m, i] = total.astype(BF16)
                    hop(m, i, j, 1).start()

    for m in range(mats):
        for i, j in enumerate(order):

            @pl.when(jnp.logical_and(j > z, z > 0))
            def _():
                hop(m, 0, j, 0).wait_recv()
                ubuf[m, i] = (gbuf[m, i] + rbuf[m, 0, j].astype(F32)).astype(BF16)
                hop(m, i, j, 0).start()

            @pl.when(jnp.logical_and(j < z, z < OUTER - 1))
            def _():
                hop(m, 0, j, 1).wait_recv()
                ubuf[m, i] = (gbuf[m, i] + rbuf[m, 1, j].astype(F32)).astype(BF16)
                hop(m, i, j, 1).start()

        @pl.when(z > 0)
        def _():
            hop(m, 0, z, 0).wait_recv()
            gbuf[m, OUTER - 1] += rbuf[m, 0, z].astype(F32)

        @pl.when(z < OUTER - 1)
        def _():
            hop(m, 0, z, 1).wait_recv()
            gbuf[m, OUTER - 1] += rbuf[m, 1, z].astype(F32)

        hbuf[m] = gbuf[m, OUTER - 1].astype(BF16)
        for i in range(1, 2 * per):
            final(m, i).start()
    for m in range(mats):
        mine = pl.ds(pl.multiple_of((r * 2 + c) * rows, rows), rows)
        out_ref[m, :, columns(r, c)] = gbuf[m, OUTER - 1, mine, :]
        for i in range(1, 2 * per):
            final(m, i).wait_recv()
            out_ref[m, :, columns(*device(*peers[i]))] = obuf[m, i].astype(F32)
    for m in range(mats):
        for i in range(1, 2 * per):
            spread(m, i).wait_send()
            final(m, i).wait_send()
        for i, j in enumerate(order):
            hop(m, i, j, 0).wait_send()


SOURCE = (1, 0, 0, 0)


def weight_grads(lefts, rights, experts, number):
    per = experts // OUTER
    span, width = rights[0].shape
    rows = width // (2 * experts)
    part = width // (2 * per)
    mats = len(rights)
    vmem = pl.BlockSpec(memory_space=pltpu.VMEM)
    dma = pltpu.SemaphoreType.DMA
    return pl.pallas_call(
        functools.partial(weights_body, per, rows),
        out_shape=jax.ShapeDtypeStruct((mats, rows, width), F32),
        in_specs=[pl.BlockSpec(memory_space=pltpu.HBM)] * (2 * per) + [vmem] * mats,
        out_specs=vmem,
        scratch_shapes=[
            pltpu.VMEM((2 * per, 2, width, span), BF16),
            pltpu.VMEM((mats, 2 * per, span, part), BF16),
            pltpu.VMEM((mats, OUTER, width // OUTER, part), F32),
            pltpu.VMEM((mats, OUTER - 1, width // OUTER, part), BF16),
            pltpu.VMEM((mats, 2, OUTER, width // OUTER, part), BF16),
            pltpu.VMEM((mats, width // OUTER, part), BF16),
            pltpu.VMEM((mats, 2 * per, rows, part), BF16),
            dma((2 * per,)),
            dma((mats, 2 * per)),
            dma((mats, 2 * per)),
            dma((mats, OUTER - 1)),
            dma((mats, 2, OUTER)),
            dma((mats, 2 * per)),
            dma((mats, 2 * per)),
        ],
        compiler_params=pltpu.CompilerParams(
            collective_id=number, has_side_effects=True, vmem_limit_bytes=58 << 20
        ),
        name="weight_grads",
    )(*lefts, *rights)


def body(
    tokens,
    cotangent,
    lengths,
    routes,
    attention_gain,
    query_gain,
    key_gain,
    feedforward_gain,
    query_weight,
    key_weight,
    value_weight,
    output_weight,
    router_weight,
    expert_gate_up,
    expert_down,
):
    span, width = tokens.shape
    core = lax.axis_index("dp")
    both = ("expert", "dp")
    devices = lax.axis_size("expert") * 2
    gains = jnp.stack([attention_gain, query_gain, key_gain, feedforward_gain]).astype(F32)
    other = lax.ppermute(gains, both, [(d, d ^ 1) for d in range(devices)])
    gains = jnp.where(
        core == 0,
        jnp.concatenate([gains, other], axis=1),
        jnp.concatenate([other, gains], axis=1),
    )
    gain_in, gain_query, gain_key, gain_mid = gains[0], gains[1], gains[2], gains[3]

    def full(part, axis=0):
        return lax.all_gather(part, "dp", axis=axis, tiled=True)

    query_full, key_full, value_full, output_full, router_full = [
        full(part)
        for part in (query_weight, key_weight, value_weight, output_weight, router_weight)
    ]
    gate_full = full(expert_gate_up[0, 0], 1)
    up_full = full(expert_gate_up[0, 1], 1)
    down_full = full(expert_down[0], 1)
    experts = router_full.shape[1]
    cap = span * TOP // experts
    per = experts // OUTER
    me = lax.axis_index("expert")

    seq_length = lengths[0]
    index_rows = jnp.arange(span, dtype=jnp.int32)
    expert_ids = jnp.arange(experts, dtype=jnp.int32)
    hits = jnp.any(routes[None, :, :] == expert_ids[:, None, None], axis=-1)
    hits = hits & (index_rows < seq_length)[None, :]
    earlier = (index_rows[:, None] < index_rows[None, :]).astype(BF16)
    before = jnp.dot(hits.astype(BF16), earlier, preferred_element_type=F32)
    kept = hits & (before < cap)
    pos = jnp.where(kept, before, -1.0)
    cot_slots, pos_here, pos_all = dispatch(cotangent, pos[:, None, :], None, cap, 1)
    cot_slots = cot_slots.reshape(experts * cap, width)

    inputs = tokens.astype(F32)
    normed_f, norm_in_back = jax.vjp(norm_apply, inputs, gain_in)
    normed_in = normed_f.astype(BF16)
    query_pre = jnp.dot(normed_in, query_full, preferred_element_type=F32)
    key_pre = jnp.dot(normed_in, key_full, preferred_element_type=F32)
    value_all = jnp.dot(normed_in, value_full, preferred_element_type=F32).astype(BF16)
    cosine_table, sine_table = rotary_tables(jnp.arange(span).astype(F32))
    query_f, query_back = jax.vjp(
        lambda projected, gain: rotary_norm(projected, gain, cosine_table, sine_table),
        query_pre, gain_query,
    )
    key_f, key_back = jax.vjp(
        lambda projected, gain: rotary_norm(projected, gain, cosine_table, sine_table),
        key_pre, gain_key,
    )
    query_rot = query_f.astype(BF16).reshape(span, NH, HD)
    key_rot = key_f.astype(BF16).reshape(span, NH, HD)
    value_heads = value_all.reshape(span, NH, HD)
    key_limit = jnp.minimum(index_rows, seq_length - 1)
    allowed = index_rows[None, :] <= key_limit[:, None]
    score_scale = HD ** (-0.5)

    def scores_of():
        raw = jnp.einsum("thd,shd->hts", query_rot, key_rot, preferred_element_type=F32)
        return jnp.where(allowed[None], raw * score_scale, -1e30)

    scores = scores_of()
    row_peak = jnp.max(scores, axis=-1, keepdims=True)
    log_total = row_peak + jnp.log(jnp.sum(jnp.exp(scores - row_peak), axis=-1, keepdims=True))
    weights_low = jnp.exp(scores - log_total).astype(BF16)
    attended = jnp.einsum("hts,shd->thd", weights_low, value_heads, preferred_element_type=F32)
    attended = attended.reshape(span, width).astype(BF16)
    middle = inputs + jnp.dot(attended, output_full, preferred_element_type=F32)
    normed_mid_f, norm_mid_back = jax.vjp(norm_apply, middle, gain_mid)
    normed_mid = normed_mid_f.astype(BF16)
    logits = jnp.dot(normed_mid, router_full, preferred_element_type=F32)
    gates = jax.nn.softmax(logits, axis=-1)
    slots, gates_here = dispatch(normed_mid, gates.T[:, None, :], pos_all, cap, 2)
    slots, normed_in, attended = lax.optimization_barrier((slots, normed_in, attended))
    slots = slots.reshape(experts * cap, width)

    turned = with_layout_constraint(jnp.stack([normed_in.T, attended.T]), Layout((0, 1, 2)))
    wide = (width // (2 * per)) % 128 == 0
    if wide:
        lefts = []
        for n in range(per):
            near = turned
            if n:
                near = lax.ppermute(turned, both, [(d, d ^ (2 * n)) for d in range(devices)])
            lefts += [near, lax.ppermute(near, both, [(d, d ^ 1) for d in range(devices)])]

    rank = me % per
    ring = jnp.arange(per, dtype=jnp.int32) ^ rank
    seqs = (jnp.arange(OUTER, dtype=jnp.int32)[:, None] * per + ring[None, :]).reshape(-1)
    marks = pos_here[seqs] == jnp.arange(cap, dtype=jnp.int32).astype(F32)[None, :, None]
    slot_gate = jnp.sum(jnp.where(marks, gates_here[seqs], 0.0), axis=-1)
    slot_gate = slot_gate.reshape(experts * cap, 1)

    def mul(left, right, spec):
        return jnp.einsum(spec, left, right, preferred_element_type=F32)

    gate_pre = mul(slots, gate_full, "sd,df->sf")
    up_pre = mul(slots, up_full, "sd,df->sf")
    sigmoid_gate = jax.nn.sigmoid(gate_pre)
    silu_gate = gate_pre * sigmoid_gate
    hidden = (silu_gate * up_pre).astype(BF16)
    pulled = mul(cot_slots, down_full, "sd,df->sf")
    gate_grad = jnp.sum(hidden.astype(F32) * pulled, axis=-1)
    hidden_grad = pulled * slot_gate
    gate_grad_low = (
        hidden_grad * up_pre * sigmoid_gate * (1.0 + gate_pre * (1.0 - sigmoid_gate))
    ).astype(BF16)
    up_grad_low = (hidden_grad * silu_gate).astype(BF16)
    row_grad = mul(gate_grad_low, gate_full, "sf,df->sd") + mul(up_grad_low, up_full, "sf,df->sd")
    row_grad = row_grad.astype(BF16)
    if wide:
        row_grad, lefts = lax.optimization_barrier((row_grad, lefts))
    back_rows = combine(row_grad.reshape(OUTER, per, cap, width), pos_all, span, 3)

    gate_grad = gate_grad.reshape(experts, cap, 1)
    token_grad = jnp.sum(jnp.where(marks, gate_grad, 0.0), axis=1)
    token_grad = token_grad.reshape(OUTER, per, span)[:, ring].reshape(experts, span)
    prob_grad = lax.all_to_all(token_grad, "expert", split_axis=0, concat_axis=0, tiled=True).T

    expert_out = mul(hidden, down_full, "sf,df->sd") * slot_gate
    mixture = combine(expert_out.astype(BF16).reshape(OUTER, per, cap, width), pos_all, span, 4)
    output = (middle + mixture).astype(BF16)

    hidden_gated = (hidden.astype(F32) * slot_gate).astype(BF16)
    local_gate = mul(slots, gate_grad_low, "sd,sf->df")
    local_up = mul(slots, up_grad_low, "sd,sf->df")
    local_down = mul(cot_slots, hidden_gated, "sd,sf->df")
    grad_gate_up = lax.psum_scatter(
        jnp.stack([local_gate, local_up]), "dp", scatter_dimension=2, tiled=True
    )[None]
    grad_down = lax.psum_scatter(local_down, "dp", scatter_dimension=1, tiled=True)[None]

    upstream = cotangent.astype(F32)
    logit_grad = (
        gates * (prob_grad - jnp.sum(gates * prob_grad, axis=-1, keepdims=True))
    ).astype(BF16)
    grad_router = mul(normed_mid, logit_grad, "td,te->de")
    mid_normed_grad = mul(logit_grad, router_full, "te,de->td") + back_rows
    mid_input_grad, grad_mid_gain = norm_mid_back(mid_normed_grad)
    middle_grad = upstream + mid_input_grad
    branch_grad = middle_grad.astype(BF16)
    attended_grad = mul(branch_grad, output_full, "to,io->ti").astype(BF16)
    attended_grad = attended_grad.reshape(span, NH, HD)
    weights_full = jnp.exp(scores_of() - log_total)
    weights_grad = mul(attended_grad, value_heads, "thd,shd->hts")
    value_grad = mul(weights_full.astype(BF16), attended_grad, "hts,thd->shd")
    value_grad = value_grad.reshape(span, width).astype(BF16)
    centre = jnp.sum(weights_full * weights_grad, axis=-1, keepdims=True)
    score_grad = (weights_full * (weights_grad - centre)).astype(BF16)
    query_rot_grad = mul(score_grad, key_rot, "hts,shd->thd").reshape(span, width) * score_scale
    key_rot_grad = mul(score_grad, query_rot, "hts,thd->shd").reshape(span, width) * score_scale
    query_pre_grad, grad_query_gain = query_back(query_rot_grad)
    key_pre_grad, grad_key_gain = key_back(key_rot_grad)
    query_low = query_pre_grad.astype(BF16)
    key_low = key_pre_grad.astype(BF16)
    normed_in_grad = mul(query_low, query_full, "to,io->ti")
    normed_in_grad = normed_in_grad + mul(key_low, key_full, "to,io->ti")
    normed_in_grad = normed_in_grad + mul(value_grad, value_full, "to,io->ti")
    input_grad, grad_in_gain = norm_in_back(normed_in_grad)
    grad_tokens = middle_grad + input_grad

    small = jnp.concatenate(
        [
            jnp.stack([grad_in_gain, grad_query_gain, grad_key_gain, grad_mid_gain]).T,
            grad_router,
        ],
        axis=1,
    )
    small = lax.psum_scatter(small, both, scatter_dimension=0, tiled=True)
    rights = (branch_grad, value_grad, key_low, query_low)
    if wide:
        grads = weight_grads(lefts, rights, experts, 5)
    else:
        grads = []
        for source, right in zip(SOURCE, rights):
            grad = jnp.dot(turned[source], right, preferred_element_type=F32).astype(BF16)
            grid = grad.reshape(experts, 2, width // experts // 2, width).swapaxes(0, 1)
            half = lax.psum_scatter(grid, "dp", scatter_dimension=0, tiled=False)
            half = lax.psum_scatter(half, "expert", scatter_dimension=0, tiled=False)
            grads.append(half.astype(F32))
    return (
        output,
        grad_tokens,
        small[:, 0],
        small[:, 1],
        small[:, 2],
        small[:, 3],
        grads[3],
        grads[2],
        grads[1],
        grads[0],
        small[:, 4:],
        grad_gate_up,
        grad_down,
    )


def solution(mesh):
    both = P(("expert", "dp"))
    rows = P(("expert", "dp"), None)
    in_specs = (rows, rows, both, rows) + (P("dp"),) * 4 + (P("dp", None),) * 5 + (
        P("expert", None, None, "dp"),
        P("expert", None, "dp"),
    )
    out_specs = (rows, rows) + (both,) * 4 + (rows,) * 5 + (
        P("expert", None, None, "dp"),
        P("expert", None, "dp"),
    )
    return jax.shard_map(body, mesh=mesh, in_specs=in_specs, out_specs=out_specs, check_vma=False)
```

```python
import functools
import math

import jax
import jax.numpy as jnp
from jax import lax
from jax.experimental import pallas as pl
from jax.experimental.layout import Layout, with_layout_constraint
from jax.experimental.pallas import tpu as pltpu
from jax.sharding import PartitionSpec as P

NH = 16
HD = 128
TOP = 8
OUTER = 4

EPSILON = 1e-05
ROPE_BASE = 10000.0
MESH = pl.DeviceIdType.MESH
F32 = jnp.float32
BF16 = jnp.bfloat16


def rms_scale(values):
    return lax.rsqrt(jnp.mean(values * values, axis=-1, keepdims=True) + EPSILON)


def norm_apply(values, gain_vector):
    return values * rms_scale(values) * gain_vector


def rotary_tables(positions):
    frequencies = 1.0 / ROPE_BASE ** (jnp.arange(0, HD, 2).astype(F32) / HD)
    angles = positions[:, None] * frequencies[None, :]
    angles = jnp.concatenate([angles, angles], axis=-1)
    return (jnp.cos(angles), jnp.sin(angles))


def rotary_norm(projected, gain_vector, cosine_table, sine_table):
    normed = projected * rms_scale(projected) * gain_vector
    shaped = normed.reshape(normed.shape[0], NH, HD)
    half_width = HD // 2
    turned = jnp.concatenate([-shaped[..., half_width:], shaped[..., :half_width]], axis=-1)
    rotated = shaped * cosine_table[:, None, :] + turned * sine_table[:, None, :]
    return rotated.reshape(normed.shape[0], NH * HD)


def flip(r, n):
    out, bit = r, 1
    while bit <= n:
        if n & bit:
            out = out + bit - 2 * bit * ((r // bit) % 2)
        bit *= 2
    return out


def pick(table, z):
    code = sum(v * 4**k for k, v in enumerate(table))
    return (code // ((1 + 3 * (z % 2)) * (1 + 15 * (z // 2)))) % 4


NEAR = ((1, 0, 1, 2), (2, 2, 3, 1), (3, 3, 0, 0))
FAR = ((3, 3, 0, 0), (2, 0, 3, 1), (1, 2, 1, 2))


def one_hot(pos_ref, r, j, per, cap):
    span = pos_ref.shape[-1]
    rows = []
    slot = lax.broadcasted_iota(jnp.int32, (cap, span), 0).astype(F32)
    for n in range(per):
        line = pos_ref[j, flip(r, n)]
        rows.append(jnp.where(line == slot, 1.0, 0.0).astype(BF16))
    return jnp.concatenate(rows, axis=0)


def dispatch_body(per, cap, first, *refs):
    if first:
        x_ref, meta_ref, out_ref, here_ref, pos_ref, zbuf, sbuf = refs[:7]
        zs, zr, ps, pr, ls, ms, mr, ts, tr = refs[7:]
    else:
        x_ref, meta_ref, pos_ref, out_ref, here_ref, zbuf, sbuf = refs[:7]
        zs, zr, ps, pr, ls, ms, mr = refs[7:]
    e, c = lax.axis_index("expert"), lax.axis_index("dp")
    z, r = e // per, e % per
    experts = OUTER * per
    bar = pltpu.get_barrier_semaphore()
    for d in range(1, experts):
        pl.semaphore_signal(bar, inc=1, device_id=((e + d) % experts, c), device_id_type=MESH)
    pl.semaphore_wait(bar, experts - 1)
    width = x_ref.shape[1]
    step = min(512, width)

    def share(d):
        to = (e + d) % experts
        return pltpu.make_async_remote_copy(
            src_ref=meta_ref.at[to], dst_ref=here_ref.at[e], send_sem=ms.at[d - 1],
            recv_sem=mr.at[d - 1], device_id=(to, c), device_id_type=MESH,
        )

    def table(d):
        to = (z + d) % OUTER
        return pltpu.make_async_remote_copy(
            src_ref=meta_ref.at[pl.ds(to * per, per)], dst_ref=pos_ref.at[z],
            send_sem=ts.at[d - 1], recv_sem=tr.at[z],
            device_id=(to * per + r, c), device_id_type=MESH,
        )

    def tabled(j):
        return pltpu.make_async_remote_copy(
            src_ref=meta_ref.at[pl.ds(0, per)], dst_ref=pos_ref.at[j], send_sem=ts.at[0],
            recv_sem=tr.at[j], device_id=(j * per + r, c), device_id_type=MESH,
        )

    def up(src, j):
        return pltpu.make_async_remote_copy(
            src_ref=src, dst_ref=zbuf.at[j], send_sem=zs.at[0, j], recv_sem=zr.at[j],
            device_id=((z + 1) * per + r, c), device_id_type=MESH,
        )

    def down(src, j):
        return pltpu.make_async_remote_copy(
            src_ref=src, dst_ref=zbuf.at[j], send_sem=zs.at[1, j], recv_sem=zr.at[j],
            device_id=((z - 1) * per + r, c), device_id_type=MESH,
        )

    def plane(i, j, n):
        return pltpu.make_async_remote_copy(
            src_ref=sbuf.at[i, n], dst_ref=out_ref.at[j, n], send_sem=ps.at[i, n],
            recv_sem=pr.at[i, n], device_id=(z * per + flip(r, n), c), device_id_type=MESH,
        )

    def local(i, j):
        return pltpu.make_async_copy(sbuf.at[i, 0], out_ref.at[j, 0], ls.at[i])

    if first:
        for d in range(1, OUTER):
            table(d).start()

    @pl.when(z < OUTER - 1)
    def _():
        up(x_ref, z).start()

    @pl.when(z > 0)
    def _():
        down(x_ref, z).start()

    if first:
        pos_ref[z] = meta_ref[pl.ds(z * per, per)]
    here_ref[e] = meta_ref[e]
    order = [z] + [pick(t, z) for t in NEAR]
    for i, j in enumerate(order):
        if i == 0:
            block = x_ref
        else:
            block = zbuf.at[j]
            up(x_ref, j).wait_recv()

            @pl.when(jnp.logical_and(j < z, z < OUTER - 1))
            def _():
                up(zbuf.at[j], j).start()

            @pl.when(jnp.logical_and(j > z, z > 0))
            def _():
                down(zbuf.at[j], j).start()

            if first:
                tabled(j).wait_recv()

        marks = one_hot(pos_ref, r, j, per, cap)

        @pl.loop(0, width // step)
        def _(k):
            columns = pl.ds(pl.multiple_of(k * step, step), step)
            got = jnp.dot(marks, block[:, columns], preferred_element_type=F32).astype(BF16)
            for n in range(per):
                sbuf[i, n, :, columns] = got[n * cap : (n + 1) * cap]

        for n in range(1, per):
            plane(i, j, n).start()
        local(i, j).start()
        if i == 0:
            for d in range(1, experts):
                share(d).start()
    for i, j in enumerate(order):
        local(i, j).wait()
        for n in range(1, per):
            plane(i, j, n).wait()

    @pl.when(z < OUTER - 1)
    def _():
        up(x_ref, z).wait_send()

    @pl.when(z > 0)
    def _():
        down(x_ref, z).wait_send()

    for i, j in enumerate(order):
        if i > 0:

            @pl.when(jnp.logical_and(j < z, z < OUTER - 1))
            def _():
                up(zbuf.at[j], j).wait_send()

            @pl.when(jnp.logical_and(j > z, z > 0))
            def _():
                down(zbuf.at[j], j).wait_send()

    for d in range(1, experts):
        share(d).wait()
    if first:
        for d in range(1, OUTER):
            table(d).wait_send()


def dispatch(x, meta, pos, cap, number):
    experts, _, span = meta.shape
    per = experts // OUTER
    width = x.shape[1]
    first = pos is None
    vmem = pl.BlockSpec(memory_space=pltpu.VMEM)
    dma = pltpu.SemaphoreType.DMA
    return pl.pallas_call(
        functools.partial(dispatch_body, per, cap, first),
        out_shape=(
            jax.ShapeDtypeStruct((OUTER, per, cap, width), BF16),
            jax.ShapeDtypeStruct((experts, 1, span), F32),
        )
        + ((jax.ShapeDtypeStruct((OUTER, per, 1, span), F32),) if first else ()),
        in_specs=[vmem] * (2 if first else 3),
        out_specs=(pl.BlockSpec(memory_space=pltpu.HBM), vmem) + ((vmem,) if first else ()),
        scratch_shapes=[
            pltpu.VMEM((OUTER, span, width), BF16),
            pltpu.VMEM((OUTER, per, cap, width), BF16),
            dma((2, OUTER)),
            dma((OUTER,)),
            dma((OUTER, per)),
            dma((OUTER, per)),
            dma((OUTER,)),
            dma((experts,)),
            dma((experts,)),
        ]
        + ([dma((OUTER,)), dma((OUTER,))] if first else []),
        compiler_params=pltpu.CompilerParams(
            collective_id=number, has_side_effects=True, vmem_limit_bytes=56 << 20
        ),
        name="dispatch",
    )(x, meta, *(() if first else (pos,)))


def experts_body(per, cap, *refs):
    x_ref, gates_ref, pos_ref, posh_ref, cot_ref, wg_ref, wu_ref, wd_ref = refs[:8]
    back_ref, pg_ref, out_ref, gl_ref, ul_ref, hg_ref, eo_ref = refs[8:15]
    zbuf, sbuf, wg, wu, wd, slb, ctb, glb, ulb, hlb, hgb, eob, ybuf, ubuf, rbuf = refs[15:30]
    here, ggv, tgv = refs[30:33]
    zs, zr, ps, pr, ls, ms, mr, ws, cs, os, es, bs, br, us, ur, gs, gr = refs[33:]
    e, c = lax.axis_index("expert"), lax.axis_index("dp")
    z, r = e // per, e % per
    experts = OUTER * per
    bar = pltpu.get_barrier_semaphore()
    for d in range(1, experts):
        pl.semaphore_signal(bar, inc=1, device_id=((e + d) % experts, c), device_id_type=MESH)
    pl.semaphore_wait(bar, experts - 1)
    span, width = x_ref.shape
    hidden = wg.shape[1]
    step = min(512, width)
    thin = min(256, hidden)
    halves = 2
    half = width // halves

    def share(d):
        to = (e + d) % experts
        return pltpu.make_async_remote_copy(
            src_ref=gates_ref.at[to], dst_ref=here.at[e], send_sem=ms.at[d - 1],
            recv_sem=mr.at[d - 1], device_id=(to, c), device_id_type=MESH,
        )

    def up(src, j):
        return pltpu.make_async_remote_copy(
            src_ref=src, dst_ref=zbuf.at[j], send_sem=zs.at[0, j], recv_sem=zr.at[j],
            device_id=((z + 1) * per + r, c), device_id_type=MESH,
        )

    def down(src, j):
        return pltpu.make_async_remote_copy(
            src_ref=src, dst_ref=zbuf.at[j], send_sem=zs.at[1, j], recv_sem=zr.at[j],
            device_id=((z - 1) * per + r, c), device_id_type=MESH,
        )

    def plane(i, j, n):
        return pltpu.make_async_remote_copy(
            src_ref=sbuf.at[i, n], dst_ref=out_ref.at[j, n], send_sem=ps.at[i, n],
            recv_sem=pr.at[i, n], device_id=(z * per + flip(r, n), c), device_id_type=MESH,
        )

    def local(i, j):
        return pltpu.make_async_copy(sbuf.at[i, 0], out_ref.at[j, 0], ls.at[i])

    def returned(i, n):
        return pltpu.make_async_remote_copy(
            src_ref=sbuf.at[i, n], dst_ref=ybuf.at[i, n], send_sem=bs.at[i, n],
            recv_sem=br.at[i, n], device_id=(z * per + flip(r, n), c), device_id_type=MESH,
        )

    def part(h):
        return pl.ds(h * half, half)

    def rise(i, j, h, slot):
        return pltpu.make_async_remote_copy(
            src_ref=ubuf.at[i, h], dst_ref=rbuf.at[slot, h], send_sem=us.at[i, h],
            recv_sem=ur.at[slot, h], device_id=((z + 1) * per + r, c), device_id_type=MESH,
        )

    def fall(i, j, h, slot):
        return pltpu.make_async_remote_copy(
            src_ref=ubuf.at[i, h], dst_ref=rbuf.at[slot, h], send_sem=us.at[i, h],
            recv_sem=ur.at[slot, h], device_id=((z - 1) * per + r, c), device_id_type=MESH,
        )

    def graded(i, n, seq):
        return pltpu.make_async_remote_copy(
            src_ref=tgv.at[i, n], dst_ref=pg_ref.at[e], send_sem=gs.at[i, n],
            recv_sem=gr.at[e], device_id=(seq, c), device_id_type=MESH,
        )

    def grade(s):
        return pltpu.make_async_remote_copy(
            src_ref=tgv.at[0, 0], dst_ref=pg_ref.at[s], send_sem=gs.at[0, 0],
            recv_sem=gr.at[s], device_id=(s, c), device_id_type=MESH,
        )

    weights = [
        pltpu.make_async_copy(src, dst, ws.at[k])
        for k, (src, dst) in enumerate(((wg_ref, wg), (wu_ref, wu), (wd_ref, wd)))
    ]

    def pull(j):
        return pltpu.make_async_copy(cot_ref.at[j], ctb, cs)

    for d in range(1, experts):
        share(d).start()

    @pl.when(z < OUTER - 1)
    def _():
        up(x_ref, z).start()

    @pl.when(z > 0)
    def _():
        down(x_ref, z).start()

    here[e] = gates_ref[e]
    order = [z] + [pick(t, z) for t in NEAR]

    def choose(i, j):
        if i == 0:
            block = x_ref
        else:
            block = zbuf.at[j]
            up(x_ref, j).wait_recv()

            @pl.when(jnp.logical_and(j < z, z < OUTER - 1))
            def _():
                up(zbuf.at[j], j).start()

            @pl.when(jnp.logical_and(j > z, z > 0))
            def _():
                down(zbuf.at[j], j).start()

        marks = one_hot(pos_ref, r, j, per, cap)

        @pl.loop(0, width // step)
        def _(k):
            columns = pl.ds(pl.multiple_of(k * step, step), step)
            got = jnp.dot(marks, block[:, columns], preferred_element_type=F32).astype(BF16)
            for n in range(per):
                sbuf[i, n, :, columns] = got[n * cap : (n + 1) * cap]

        for n in range(1, per):
            plane(i, j, n).start()
        local(i, j).start()

    def outs(j):
        return [
            pltpu.make_async_copy(src, dst.at[j], os.at[k])
            for k, (src, dst) in enumerate(((glb, gl_ref), (ulb, ul_ref), (hgb, hg_ref)))
        ]

    def away(j):
        return pltpu.make_async_copy(eob, eo_ref.at[j], es)

    def marked(j, n):
        slot = lax.broadcasted_iota(jnp.int32, (cap, span), 0).astype(F32)
        return posh_ref[j * per + flip(r, n)] == slot

    def expert(i, j):
        for n in range(1, per):
            plane(i, j, n).wait()
        local(i, j).wait()
        fetch = pltpu.make_async_copy(out_ref.at[j], slb, ls.at[OUTER])
        fetch.start()
        slot_gate = jnp.concatenate(
            [
                jnp.sum(
                    jnp.where(marked(j, n), here[j * per + flip(r, n)], 0.0), axis=1, keepdims=True
                )
                for n in range(per)
            ],
            axis=0,
        )
        ggv[...] = jnp.zeros_like(ggv)
        pull(j).wait()
        fetch.wait()
        if i > 0:
            for copy in outs(order[i - 1]):
                copy.wait()

        @pl.loop(0, hidden // thin)
        def _(k):
            columns = pl.ds(pl.multiple_of(k * thin, thin), thin)
            rows = slb[...].reshape(per * cap, width)
            gate_pre = jnp.dot(rows, wg[:, columns], preferred_element_type=F32)
            up_pre = jnp.dot(rows, wu[:, columns], preferred_element_type=F32)
            pulled = jnp.dot(
                ctb[...].reshape(per * cap, width), wd[:, columns], preferred_element_type=F32
            )
            sigmoid_gate = jax.nn.sigmoid(gate_pre)
            silu_gate = gate_pre * sigmoid_gate
            low = (silu_gate * up_pre).astype(BF16)
            wide = low.astype(F32)
            ggv[...] += jnp.sum(wide * pulled, axis=1, keepdims=True)
            hidden_grad = pulled * slot_gate
            glb[:, columns] = (
                hidden_grad * up_pre * sigmoid_gate * (1.0 + gate_pre * (1.0 - sigmoid_gate))
            ).astype(BF16)
            ulb[:, columns] = (hidden_grad * silu_gate).astype(BF16)
            hlb[:, columns] = low
            hgb[:, columns] = (wide * slot_gate).astype(BF16)

        if i < OUTER - 1:
            pull(order[i + 1]).start()
        for copy in outs(j):
            copy.start()

        @pl.loop(0, width // step)
        def _(k):
            columns = pl.ds(pl.multiple_of(k * step, step), step)
            got = lax.dot_general(
                glb[...], wg[columns, :], (((1,), (1,)), ((), ())), preferred_element_type=F32
            ) + lax.dot_general(
                ulb[...], wu[columns, :], (((1,), (1,)), ((), ())), preferred_element_type=F32
            )
            got = got.astype(BF16)
            for n in range(per):
                sbuf[i, n, :, columns] = got[n * cap : (n + 1) * cap]

        return slot_gate

    def send_back(i):
        for n in range(1, per):
            returned(i, n).start()

    def finish(i, j, slot_gate):
        for n in range(per):
            seq = j * per + flip(r, n)
            row = jnp.sum(
                jnp.where(marked(j, n), ggv[n * cap : (n + 1) * cap], 0.0), axis=0, keepdims=True
            )
            tgv[i, n] = row
            if i == 0 and n == 0:
                pg_ref[e] = row
            else:
                graded(i, n, seq).start()
        if i > 0:
            away(order[i - 1]).wait()

        @pl.loop(0, width // step)
        def _(k):
            columns = pl.ds(pl.multiple_of(k * step, step), step)
            got = lax.dot_general(
                hlb[...], wd[columns, :], (((1,), (1,)), ((), ())), preferred_element_type=F32
            )
            got = (got * slot_gate).astype(BF16)
            for n in range(per):
                eob[n, :, columns] = got[n * cap : (n + 1) * cap]

        away(j).start()

    choose(0, z)
    for copy in weights:
        copy.start()
    pull(z).start()
    choose(1, order[1])
    for copy in weights:
        copy.wait()
    for d in range(1, experts):
        share(d).wait()
    last = OUTER - 1
    for i in range(last):
        slot_gate = expert(i, order[i])
        finish(i, order[i], slot_gate)
        if i + 2 <= last:
            choose(i + 2, order[i + 2])
    send_back(0)
    slot_gate = expert(last, order[last])
    for i in range(last, 0, -1):
        send_back(i)
    finish(last, order[last], slot_gate)

    def fold(i, j, h):
        marks = one_hot(pos_ref, r, j, per, cap)

        @pl.loop(0, half // step)
        def _(k):
            columns = pl.ds(pl.multiple_of(h * half + k * step, step), step)
            rows = jnp.concatenate(
                [(ybuf if n else sbuf)[i, n, :, columns] for n in range(per)], axis=0
            )
            back_ref[:, columns] = lax.dot_general(
                marks, rows, (((0,), (0,)), ((), ())), preferred_element_type=F32
            )

    for i in range(last, 0, -1):
        j = order[i]
        for n in range(1, per):
            returned(i, n).wait_recv()
        for h in range(halves):
            fold(i, j, h)

            @pl.when(jnp.logical_and(j > z, z > 0))
            def _():
                rise(0, j, h, j).wait_recv()
                back_ref[:, part(h)] += rbuf[j, h].astype(F32)

            @pl.when(jnp.logical_and(j < z, z < OUTER - 1))
            def _():
                fall(0, j, h, j).wait_recv()
                back_ref[:, part(h)] += rbuf[j, h].astype(F32)

            ubuf[i - 1, h] = back_ref[:, part(h)].astype(BF16)

            @pl.when(jnp.logical_and(j > z, j - z > 1))
            def _():
                rise(i - 1, j, h, j).start()

            @pl.when(j - z == 1)
            def _():
                rise(i - 1, j, h, j).start()

            @pl.when(jnp.logical_and(j < z, z - j > 1))
            def _():
                fall(i - 1, j, h, j).start()

            @pl.when(z - j == 1)
            def _():
                fall(i - 1, j, h, OUTER).start()

    for n in range(1, per):
        returned(0, n).wait_recv()
    for h in range(halves):
        fold(0, z, h)

        @pl.when(z > 0)
        def _():
            rise(0, z, h, z).wait_recv()
            back_ref[:, part(h)] += rbuf[z, h].astype(F32)

        @pl.when(z < OUTER - 1)
        def _():
            fall(0, z, h, OUTER).wait_recv()
            back_ref[:, part(h)] += rbuf[OUTER, h].astype(F32)

    @pl.when(z < OUTER - 1)
    def _():
        up(x_ref, z).wait_send()

    @pl.when(z > 0)
    def _():
        down(x_ref, z).wait_send()

    for i, j in enumerate(order):
        for n in range(1, per):
            returned(i, n).wait_send()
        if i > 0:

            @pl.when(jnp.logical_and(j < z, z < OUTER - 1))
            def _():
                up(zbuf.at[j], j).wait_send()

            @pl.when(jnp.logical_and(j > z, z > 0))
            def _():
                down(zbuf.at[j], j).wait_send()

            for h in range(halves):
                rise(i - 1, j, h, j).wait_send()
        for n in range(per):
            if i or n:
                graded(i, n, j * per + flip(r, n)).wait_send()
    for d in range(1, experts):
        grade((e + d) % experts).wait_recv()
    for copy in outs(order[last]):
        copy.wait()
    away(order[last]).wait()


def run_experts(x, gates, pos, pos_here, cot_slots, gate_full, up_full, down_full, number):
    experts, _, span = gates.shape
    outer, per, cap, width = cot_slots.shape
    hidden = gate_full.shape[1]
    block = per * cap
    vmem = pl.BlockSpec(memory_space=pltpu.VMEM)
    hbm = pl.BlockSpec(memory_space=pltpu.HBM)
    dma = pltpu.SemaphoreType.DMA
    rows = jax.ShapeDtypeStruct((OUTER, per, cap, width), BF16)
    thin = jax.ShapeDtypeStruct((OUTER, block, hidden), BF16)
    return pl.pallas_call(
        functools.partial(experts_body, per, cap),
        out_shape=(
            jax.ShapeDtypeStruct((span, width), F32),
            jax.ShapeDtypeStruct((experts, 1, span), F32),
            rows, thin, thin, thin, rows,
        ),
        in_specs=[vmem] * 4 + [hbm] * 4,
        out_specs=(vmem, vmem) + (hbm,) * 5,
        scratch_shapes=[
            pltpu.VMEM((OUTER, span, width), BF16),
            pltpu.VMEM((OUTER, per, cap, width), BF16),
            pltpu.VMEM((width, hidden), BF16),
            pltpu.VMEM((width, hidden), BF16),
            pltpu.VMEM((width, hidden), BF16),
            pltpu.VMEM((per, cap, width), BF16),
            pltpu.VMEM((per, cap, width), BF16),
            pltpu.VMEM((block, hidden), BF16),
            pltpu.VMEM((block, hidden), BF16),
            pltpu.VMEM((block, hidden), BF16),
            pltpu.VMEM((block, hidden), BF16),
            pltpu.VMEM((per, cap, width), BF16),
            pltpu.VMEM((OUTER, per, cap, width), BF16),
            pltpu.VMEM((OUTER - 1, 2, span, width // 2), BF16),
            pltpu.VMEM((OUTER + 1, 2, span, width // 2), BF16),
            pltpu.VMEM((experts, 1, span), F32),
            pltpu.VMEM((block, 1), F32),
            pltpu.VMEM((OUTER, per, 1, span), F32),
            dma((2, OUTER)),
            dma((OUTER,)),
            dma((OUTER, per)),
            dma((OUTER, per)),
            dma((OUTER + 1,)),
            dma((experts,)),
            dma((experts,)),
            dma((3,)),
            dma,
            dma((3,)),
            dma,
            dma((OUTER, per)),
            dma((OUTER, per)),
            dma((OUTER - 1, 2)),
            dma((OUTER + 1, 2)),
            dma((OUTER, per)),
            dma((experts,)),
        ],
        compiler_params=pltpu.CompilerParams(
            collective_id=number, has_side_effects=True, vmem_limit_bytes=62 << 20
        ),
        name="experts",
    )(x, gates, pos, pos_here, cot_slots, gate_full, up_full, down_full)


def combine_body(per, cap, *refs):
    y_ref, pos_ref, slots_ref, cot_ref, gl_ref, ul_ref, hg_ref = refs[:7]
    out_ref, gu_ref, dn_ref, ybuf, ubuf, rbuf = refs[7:13]
    theirs, ours, lbuf, lturn, tbuf, rx, stage = refs[13:20]
    zs, zr, ps, pr, ls, rs, ws, ds, dr, gs = refs[20:]
    e, c = lax.axis_index("expert"), lax.axis_index("dp")
    z, r = e // per, e % per
    bar = pltpu.get_barrier_semaphore()
    for d in range(1, OUTER):
        pl.semaphore_signal(
            bar, inc=1, device_id=((z + d) % OUTER * per + r, c), device_id_type=MESH
        )
    for n in range(1, per):
        pl.semaphore_signal(bar, inc=1, device_id=(z * per + flip(r, n), c), device_id_type=MESH)
    pl.semaphore_signal(bar, inc=1, device_id=(e, 1 - c), device_id_type=MESH)
    pl.semaphore_wait(bar, OUTER - 1 + per - 1 + 1)
    span, width = out_ref.shape
    step = min(512, width)
    share = dn_ref.shape[1]
    thin = min(256, share)
    total = OUTER * per * cap

    def plane(i, j, n):
        return pltpu.make_async_remote_copy(
            src_ref=y_ref.at[j, n], dst_ref=ybuf.at[i, n], send_sem=ps.at[i, n],
            recv_sem=pr.at[i, n], device_id=(z * per + flip(r, n), c), device_id_type=MESH,
        )

    def local(i, j):
        return pltpu.make_async_copy(y_ref.at[j, 0], ybuf.at[i, 0], ls.at[i])

    def up(i, j):
        return pltpu.make_async_remote_copy(
            src_ref=ubuf.at[i], dst_ref=rbuf.at[0, j], send_sem=zs.at[i], recv_sem=zr.at[0, j],
            device_id=((z + 1) * per + r, c), device_id_type=MESH,
        )

    def down(i, j):
        return pltpu.make_async_remote_copy(
            src_ref=ubuf.at[i], dst_ref=rbuf.at[1, j], send_sem=zs.at[i], recv_sem=zr.at[1, j],
            device_id=((z - 1) * per + r, c), device_id_type=MESH,
        )

    def rights(k, src, other):
        owner = 1 - c if other else c
        return pltpu.make_async_copy(
            src.at[:, :, pl.ds(pl.multiple_of(owner * share, share), share)],
            (theirs if other else ours).at[:, :, pl.ds(k * share, share)],
            rs.at[k, int(other)],
        )

    def across(k):
        return pltpu.make_async_remote_copy(
            src_ref=tbuf.at[k % 2], dst_ref=rx.at[k], send_sem=ds.at[k], recv_sem=dr.at[k],
            device_id=(e, 1 - c), device_id_type=MESH,
        )

    def stores(k):
        lines = pl.ds(k * step, step)
        return [
            pltpu.make_async_copy(
                stage.at[:, pl.ds(m * share, share)],
                dn_ref.at[lines] if m == 2 else gu_ref.at[m, lines],
                gs.at[m],
            )
            for m in range(3)
        ]

    sources = (gl_ref, ul_ref, hg_ref)
    loads = [rights(k, src, other) for k, src in enumerate(sources) for other in (True, False)]

    def tile(k):
        if k == 0:
            for copy in loads:
                copy.wait()
        if k >= 2:
            across(k - 2).wait_send()
        if k >= 1:
            for copy in stores(k - 1):
                copy.wait()
        for src, first, count in ((slots_ref, 0, 2), (cot_ref, 2, 1)):
            fetch = pltpu.make_async_copy(
                src.at[:, :, :, pl.ds(k * step, step)], lbuf, ws
            )
            fetch.start()
            fetch.wait()
            lturn[...] = lbuf[...].reshape(total, step).T

            @pl.loop(0, count * share // thin)
            def _(q):
                at = pl.ds(pl.multiple_of(first * share + q * thin, thin), thin)
                tbuf[k % 2, :, at] = jnp.dot(
                    lturn[...], theirs[:, :, at].reshape(total, thin), preferred_element_type=F32
                ).astype(BF16)
                stage[:, at] = jnp.dot(
                    lturn[...], ours[:, :, at].reshape(total, thin), preferred_element_type=F32
                )

        across(k).start()
        across(k).wait_recv()
        stage[...] += rx[k].astype(F32)
        for copy in stores(k):
            copy.start()

    order = [pick(t, z) for t in FAR] + [z]
    for i, j in enumerate(order):
        for n in range(1, per):
            plane(i, j, n).start()
        local(i, j).start()
    for copy in loads:
        copy.start()
    tiles = width // step
    done = 0
    for i, j in enumerate(order):
        while done < tiles and (done < 2 or done < i + 2):
            tile(done)
            done += 1
        marks = one_hot(pos_ref, r, j, per, cap)
        local(i, j).wait()
        for n in range(1, per):
            plane(i, j, n).wait_recv()

        @pl.loop(0, width // step)
        def _(k):
            columns = pl.ds(pl.multiple_of(k * step, step), step)
            rows = jnp.concatenate([ybuf[i, n, :, columns] for n in range(per)], axis=0)
            out_ref[:, columns] = lax.dot_general(
                marks, rows, (((0,), (0,)), ((), ())), preferred_element_type=F32
            )

        if i < OUTER - 1:

            @pl.when(jnp.logical_and(j > z, z > 0))
            def _():
                up(0, j).wait_recv()
                out_ref[...] += rbuf[0, j].astype(F32)

            @pl.when(jnp.logical_and(j < z, z < OUTER - 1))
            def _():
                down(0, j).wait_recv()
                out_ref[...] += rbuf[1, j].astype(F32)

            ubuf[i] = out_ref[...].astype(BF16)

            @pl.when(j > z)
            def _():
                up(i, j).start()

            @pl.when(j < z)
            def _():
                down(i, j).start()
        else:

            @pl.when(z > 0)
            def _():
                up(0, z).wait_recv()
                out_ref[...] += rbuf[0, z].astype(F32)

            @pl.when(z < OUTER - 1)
            def _():
                down(0, z).wait_recv()
                out_ref[...] += rbuf[1, z].astype(F32)

    for i, j in enumerate(order):
        for n in range(1, per):
            plane(i, j, n).wait_send()
        if i < OUTER - 1:
            up(i, j).wait_send()
    for k in range(max(0, tiles - 2), tiles):
        across(k).wait_send()
    for copy in stores(tiles - 1):
        copy.wait()


def combine(y, pos_all, slots, cot_slots, gate_low, up_low, hidden_gated, number):
    outer, per, cap, width = y.shape
    span = pos_all.shape[-1]
    block, hidden = gate_low.shape[1:]
    share = hidden // 2
    step = min(512, width)
    tiles = width // step
    vmem = pl.BlockSpec(memory_space=pltpu.VMEM)
    hbm = pl.BlockSpec(memory_space=pltpu.HBM)
    dma = pltpu.SemaphoreType.DMA
    return pl.pallas_call(
        functools.partial(combine_body, per, cap),
        out_shape=(
            jax.ShapeDtypeStruct((span, width), F32),
            jax.ShapeDtypeStruct((2, width, share), F32),
            jax.ShapeDtypeStruct((width, share), F32),
        ),
        in_specs=[hbm, vmem] + [hbm] * 5,
        out_specs=(vmem, hbm, hbm),
        scratch_shapes=[
            pltpu.VMEM((OUTER, per, cap, width), BF16),
            pltpu.VMEM((OUTER - 1, span, width), BF16),
            pltpu.VMEM((2, OUTER, span, width), BF16),
            pltpu.VMEM((OUTER, block, 3 * share), BF16),
            pltpu.VMEM((OUTER, block, 3 * share), BF16),
            pltpu.VMEM((OUTER, per, cap, step), BF16),
            pltpu.VMEM((step, OUTER * block), BF16),
            pltpu.VMEM((2, step, 3 * share), BF16),
            pltpu.VMEM((tiles, step, 3 * share), BF16),
            pltpu.VMEM((step, 3 * share), F32),
            dma((OUTER - 1,)),
            dma((2, OUTER)),
            dma((OUTER, per)),
            dma((OUTER, per)),
            dma((OUTER,)),
            dma((3, 2)),
            dma,
            dma((tiles,)),
            dma((tiles,)),
            dma((3,)),
        ],
        compiler_params=pltpu.CompilerParams(
            collective_id=number, has_side_effects=True, vmem_limit_bytes=62 << 20
        ),
        name="combine",
    )(y, pos_all, slots, cot_slots, gate_low, up_low, hidden_gated)


def weights_body(rows, *refs):
    mats, per = len(SOURCE), 4
    x_refs, y_refs, small_ref = refs[:4], refs[4 : 4 + mats], refs[4 + mats]
    out_ref, total_ref, xbuf, ybuf, keep, sbuf, srecv, ubuf, rbuf, hbuf, obuf = refs[5 + mats : 16 + mats]
    lbuf, lsum, lz = refs[16 + mats : 19 + mats]
    xs, ys, yr, ss, sr, zs, zr, fs, fr, ls, lr, ts, tr = refs[19 + mats :]
    e, c = lax.axis_index("expert"), lax.axis_index("dp")
    z, r = e // per, e % per
    x, y = r % 2, r // 2
    width = y_refs[0].shape[1]
    part = width // 4
    lines = width // OUTER
    peers = [(n, f) for n in range(per) for f in range(2)]
    trade = (y + c * (1 - 2 * y)) * 2 + x + (1 - c) * (1 - 2 * x)
    other = (y + (1 - c) * (1 - 2 * y)) * 2 + x + c * (1 - 2 * x)
    a_bit = (1 - c) * x + c * y
    b_bit = (1 - c) * y + c * x
    quarter = 2 * c + a_bit

    def device(n, f):
        return flip(r, n), (c + f) % 2

    bar = pltpu.get_barrier_semaphore()
    for d in range(1, OUTER):
        pl.semaphore_signal(
            bar, inc=1, device_id=((z + d) % OUTER * per + r, c), device_id_type=MESH
        )
    for n, f in peers[1:]:
        q, k = device(n, f)
        pl.semaphore_signal(bar, inc=1, device_id=(z * per + q, k), device_id_type=MESH)
    pl.semaphore_wait(bar, OUTER - 1 + 2 * per - 1)

    def block(q):
        return pl.ds(pl.multiple_of(q * part, part), part)

    targets = (
        (r, 1 - c, 2 * (1 - c) + (1 - c) * y + c * x),
        (trade, c, 2 * c + 1 - a_bit),
        (other, 1 - c, 2 * (1 - c) + 1 - b_bit),
    )

    def spread(m, i):
        q, k, at = targets[i]
        return pltpu.make_async_remote_copy(
            src_ref=y_refs[m].at[:, block(at)], dst_ref=ybuf.at[m, i + 1],
            send_sem=ys.at[m, i], recv_sem=yr.at[m, i],
            device_id=(z * per + q, k), device_id_type=MESH,
        )

    def swap(m, i):
        return pltpu.make_async_remote_copy(
            src_ref=sbuf.at[m, i], dst_ref=srecv.at[m, i], send_sem=ss.at[m, i],
            recv_sem=sr.at[m, i], device_id=(z * per + other, c), device_id_type=MESH,
        )

    def hop(m, i, j, way):
        return pltpu.make_async_remote_copy(
            src_ref=ubuf.at[m, i], dst_ref=rbuf.at[m, way, j],
            send_sem=zs.at[m, i], recv_sem=zr.at[m, way, j],
            device_id=((z + 1 - 2 * way) * per + r, c), device_id_type=MESH,
        )

    def final(m, t, f):
        there = a_bit + t * (1 - 2 * a_bit)
        core = (c + f) % 2
        q = ((1 - c) * y + c * there) * 2 + (1 - c) * there + c * x
        return pltpu.make_async_remote_copy(
            src_ref=hbuf.at[m, pl.ds(pl.multiple_of((there * 2 + core) * rows, rows), rows)],
            dst_ref=obuf.at[m, quarter], send_sem=fs.at[m, 2 * t + f],
            recv_sem=fr.at[m, quarter], device_id=(z * per + q, core), device_id_type=MESH,
        )

    def landed(m, q):
        return pltpu.make_async_remote_copy(
            src_ref=hbuf.at[m, pl.ds(0, rows)], dst_ref=obuf.at[m, q], send_sem=fs.at[m, 0],
            recv_sem=fr.at[m, q], device_id=(z * per + r, 1 - c), device_id_type=MESH,
        )

    def little(i):
        q, k = device(*peers[i])
        return pltpu.make_async_remote_copy(
            src_ref=small_ref.at[q * 2 + k], dst_ref=lbuf.at[i], send_sem=ls.at[i],
            recv_sem=lr.at[i], device_id=(z * per + q, k), device_id_type=MESH,
        )

    def tall(d):
        to = (z + d) % OUTER
        return pltpu.make_async_remote_copy(
            src_ref=lsum.at[to], dst_ref=lz.at[d], send_sem=ts.at[d], recv_sem=tr.at[d],
            device_id=(to * per + r, c), device_id_type=MESH,
        )

    loads = [pltpu.make_async_copy(x_refs[i], xbuf.at[i], xs.at[i]) for i in range(4)]
    for m in range(mats):
        for i in range(3):
            spread(m, i).start()
    for copy in loads:
        copy.start()
    for i in range(1, 2 * per):
        little(i).start()
    lbuf[0] = small_ref[r * 2 + c]
    for m in range(mats):
        ybuf[m, 0] = y_refs[m][:, block(quarter)]
    for copy in loads:
        copy.wait()
    order = [pick(t, z) for t in FAR]

    def pieces(j, bit):
        for t in range(2):
            at = j * lines + (1 - c) * (bit * 2 + t) * 2 * rows + c * (t * 2 + bit) * 2 * rows
            yield pl.ds(pl.multiple_of(at, 2 * rows), 2 * rows)

    def product(m, j, bit):
        total = None
        for i in range(4):
            left = jnp.concatenate([xbuf[i, SOURCE[m], at, :] for at in pieces(j, bit)], axis=0)
            term = jnp.dot(left, ybuf[m, i], preferred_element_type=F32)
            total = term if total is None else total + term
        return total

    for m in range(mats):
        for i in range(3):
            spread(m, i).wait_recv()
        for i, j in enumerate(order + [z]):
            sbuf[m, i] = product(m, j, 1 - b_bit).astype(BF16)
            swap(m, i).start()
        for i, j in enumerate(order + [z]):
            keep[m, i] = product(m, j, b_bit)

    for i in range(1, 2 * per):
        little(i).wait_recv()
    lsum[...] = sum(lbuf[i] for i in range(2 * per))
    for d in range(1, OUTER):
        tall(d).start()

    edge = jnp.logical_or(z == 0, z == OUTER - 1)

    @pl.when(edge)
    def _():
        for m in range(mats):
            for i, j in enumerate(order):
                swap(m, i).wait_recv()
                ubuf[m, i] = (keep[m, i] + srecv[m, i].astype(F32)).astype(BF16)

                @pl.when(z == 0)
                def _():
                    hop(m, i, j, 0).start()

                @pl.when(z > 0)
                def _():
                    hop(m, i, j, 1).start()

    @pl.when(jnp.logical_not(edge))
    def _():
        for m in range(mats):
            for i, j in enumerate(order):
                swap(m, i).wait_recv()

                @pl.when(j > z)
                def _():
                    hop(m, 0, j, 0).wait_recv()
                    ubuf[m, i] = (
                        keep[m, i] + srecv[m, i].astype(F32) + rbuf[m, 0, j].astype(F32)
                    ).astype(BF16)
                    hop(m, i, j, 0).start()

                @pl.when(j < z)
                def _():
                    hop(m, 0, j, 1).wait_recv()
                    ubuf[m, i] = (
                        keep[m, i] + srecv[m, i].astype(F32) + rbuf[m, 1, j].astype(F32)
                    ).astype(BF16)
                    hop(m, i, j, 1).start()

    last = OUTER - 1
    for m in range(mats):
        swap(m, last).wait_recv()
        keep[m, last] += srecv[m, last].astype(F32)

        @pl.when(z > 0)
        def _():
            hop(m, 0, z, 0).wait_recv()
            keep[m, last] += rbuf[m, 0, z].astype(F32)

        @pl.when(z < OUTER - 1)
        def _():
            hop(m, 0, z, 1).wait_recv()
            keep[m, last] += rbuf[m, 1, z].astype(F32)

        hbuf[m] = keep[m, last].astype(BF16)
        for t, f in ((1, 0), (1, 1), (0, 1)):
            final(m, t, f).start()

    for d in range(1, OUTER):
        tall(d).wait()
    total_ref[...] = lsum[z] + sum(lz[d] for d in range(1, OUTER))
    for m in range(mats):
        mine = pl.ds(pl.multiple_of((a_bit * 2 + c) * rows, rows), rows)
        out_ref[m, :, block(quarter)] = keep[m, last, mine, :]
        for d in range(1, 4):
            q = (quarter + d) % 4
            landed(m, q).wait_recv()
            out_ref[m, :, block(q)] = obuf[m, q].astype(F32)
    for m in range(mats):
        for i in range(3):
            spread(m, i).wait_send()
        for i in range(OUTER):
            swap(m, i).wait_send()
        for t, f in ((1, 0), (1, 1), (0, 1)):
            final(m, t, f).wait_send()
        for i, j in enumerate(order):
            hop(m, i, j, 0).wait_send()
    for i in range(1, 2 * per):
        little(i).wait_send()


SOURCE = (1, 0, 0, 0)


def weight_grads(lefts, rights, small, experts, number):
    span, width = rights[0].shape
    rows = width // (2 * experts)
    part = width // 4
    half = width // OUTER // 2
    mats = len(rights)
    count = small.shape[-1]
    vmem = pl.BlockSpec(memory_space=pltpu.VMEM)
    dma = pltpu.SemaphoreType.DMA
    return pl.pallas_call(
        functools.partial(weights_body, rows),
        out_shape=(
            jax.ShapeDtypeStruct((mats, rows, width), F32),
            jax.ShapeDtypeStruct((1, count), F32),
        ),
        in_specs=[pl.BlockSpec(memory_space=pltpu.HBM)] * 4 + [vmem] * (mats + 1),
        out_specs=(vmem, vmem),
        scratch_shapes=[
            pltpu.VMEM((4, 2, width, span), BF16),
            pltpu.VMEM((mats, 4, span, part), BF16),
            pltpu.VMEM((mats, OUTER, half, part), F32),
            pltpu.VMEM((mats, OUTER, half, part), BF16),
            pltpu.VMEM((mats, OUTER, half, part), BF16),
            pltpu.VMEM((mats, OUTER - 1, half, part), BF16),
            pltpu.VMEM((mats, 2, OUTER, half, part), BF16),
            pltpu.VMEM((mats, half, part), BF16),
            pltpu.VMEM((mats, 4, rows, part), BF16),
            pltpu.VMEM(small.shape, F32),
            pltpu.VMEM(small.shape[1:], F32),
            pltpu.VMEM(small.shape[1:], F32),
            dma((4,)),
            dma((mats, 3)),
            dma((mats, 3)),
            dma((mats, OUTER)),
            dma((mats, OUTER)),
            dma((mats, OUTER - 1)),
            dma((mats, 2, OUTER)),
            dma((mats, 4)),
            dma((mats, 4)),
            dma((8,)),
            dma((8,)),
            dma((OUTER,)),
            dma((OUTER,)),
        ],
        compiler_params=pltpu.CompilerParams(
            collective_id=number, has_side_effects=True, vmem_limit_bytes=58 << 20
        ),
        name="weight_grads",
    )(*lefts, *rights, small)


def body(
    tokens,
    cotangent,
    lengths,
    routes,
    attention_gain,
    query_gain,
    key_gain,
    feedforward_gain,
    query_weight,
    key_weight,
    value_weight,
    output_weight,
    router_weight,
    expert_gate_up,
    expert_down,
):
    span, width = tokens.shape
    core = lax.axis_index("dp")
    both = ("expert", "dp")
    devices = lax.axis_size("expert") * 2
    gains = jnp.stack([attention_gain, query_gain, key_gain, feedforward_gain]).astype(F32)
    other = lax.ppermute(gains, both, [(d, d ^ 1) for d in range(devices)])
    gains = jnp.where(
        core == 0,
        jnp.concatenate([gains, other], axis=1),
        jnp.concatenate([other, gains], axis=1),
    )
    gain_in, gain_query, gain_key, gain_mid = gains[0], gains[1], gains[2], gains[3]

    def full(part, axis=0):
        return lax.all_gather(part, "dp", axis=axis, tiled=True)

    query_full, key_full, value_full, output_full, router_full = [
        full(part)
        for part in (query_weight, key_weight, value_weight, output_weight, router_weight)
    ]
    gate_full = full(expert_gate_up[0, 0], 1)
    up_full = full(expert_gate_up[0, 1], 1)
    down_full = full(expert_down[0], 1)
    experts = router_full.shape[1]
    cap = span * TOP // experts
    per = experts // OUTER

    seq_length = lengths[0]
    index_rows = jnp.arange(span, dtype=jnp.int32)
    expert_ids = jnp.arange(experts, dtype=jnp.int32)
    hits = jnp.any(routes[None, :, :] == expert_ids[:, None, None], axis=-1)
    hits = hits & (index_rows < seq_length)[None, :]
    earlier = (index_rows[:, None] < index_rows[None, :]).astype(BF16)
    before = jnp.dot(hits.astype(BF16), earlier, preferred_element_type=F32)
    kept = hits & (before < cap)
    pos = jnp.where(kept, before, -1.0)
    cot_slots, pos_here, pos_all = dispatch(cotangent, pos[:, None, :], None, cap, 1)

    inputs = tokens.astype(F32)
    normed_f, norm_in_back = jax.vjp(norm_apply, inputs, gain_in)
    normed_in = normed_f.astype(BF16)
    query_pre = jnp.dot(normed_in, query_full, preferred_element_type=F32)
    key_pre = jnp.dot(normed_in, key_full, preferred_element_type=F32)
    value_all = jnp.dot(normed_in, value_full, preferred_element_type=F32).astype(BF16)
    cosine_table, sine_table = rotary_tables(jnp.arange(span).astype(F32))
    query_f, query_back = jax.vjp(
        lambda projected, gain: rotary_norm(projected, gain, cosine_table, sine_table),
        query_pre, gain_query,
    )
    key_f, key_back = jax.vjp(
        lambda projected, gain: rotary_norm(projected, gain, cosine_table, sine_table),
        key_pre, gain_key,
    )
    query_rot = query_f.astype(BF16).reshape(span, NH, HD)
    key_rot = key_f.astype(BF16).reshape(span, NH, HD)
    value_heads = value_all.reshape(span, NH, HD)
    key_limit = jnp.minimum(index_rows, seq_length - 1)
    allowed = index_rows[None, :] <= key_limit[:, None]
    score_scale = HD ** (-0.5)

    def scores_of():
        raw = jnp.einsum("thd,shd->hts", query_rot, key_rot, preferred_element_type=F32)
        return jnp.where(allowed[None], raw * score_scale, -1e30)

    scores = scores_of()
    row_peak = jnp.max(scores, axis=-1, keepdims=True)
    log_total = row_peak + jnp.log(jnp.sum(jnp.exp(scores - row_peak), axis=-1, keepdims=True))
    weights_low = jnp.exp(scores - log_total).astype(BF16)
    attended = jnp.einsum("hts,shd->thd", weights_low, value_heads, preferred_element_type=F32)
    attended = attended.reshape(span, width).astype(BF16)
    middle = inputs + jnp.dot(attended, output_full, preferred_element_type=F32)
    normed_mid_f, norm_mid_back = jax.vjp(norm_apply, middle, gain_mid)
    normed_mid = normed_mid_f.astype(BF16)
    logits = jnp.dot(normed_mid, router_full, preferred_element_type=F32)
    gates = jax.nn.softmax(logits, axis=-1)
    def mul(left, right, spec):
        return jnp.einsum(spec, left, right, preferred_element_type=F32)

    back_rows, prob_grad, slots, gate_grad_low, up_grad_low, hidden_gated, expert_out = run_experts(
        normed_mid, gates.T[:, None, :], pos_all, pos_here, cot_slots,
        gate_full, up_full, down_full, 2,
    )
    prob_grad = prob_grad[:, 0].T
    back_rows, normed_in, attended = lax.optimization_barrier((back_rows, normed_in, attended))
    turned = with_layout_constraint(jnp.stack([normed_in.T, attended.T]), Layout((0, 1, 2)))
    wide = per == 4 and width % 512 == 0
    if wide:

        def moved(d, cross):
            to = d % 2 ^ cross
            return (d // 2 ^ 1 + to) * 2 + to

        lefts = [turned, lax.ppermute(turned, both, [(d, d ^ 1) for d in range(devices)])] + [
            lax.ppermute(turned, both, [(d, moved(d, cross)) for d in range(devices)])
            for cross in range(2)
        ]

    upstream = cotangent.astype(F32)
    logit_grad = (
        gates * (prob_grad - jnp.sum(gates * prob_grad, axis=-1, keepdims=True))
    ).astype(BF16)
    grad_router = mul(normed_mid, logit_grad, "td,te->de")
    mid_normed_grad = mul(logit_grad, router_full, "te,de->td") + back_rows
    mid_input_grad, grad_mid_gain = norm_mid_back(mid_normed_grad)
    middle_grad = upstream + mid_input_grad
    branch_grad = middle_grad.astype(BF16)
    attended_grad = mul(branch_grad, output_full, "to,io->ti").astype(BF16)
    attended_grad = attended_grad.reshape(span, NH, HD)
    weights_full = jnp.exp(scores_of() - log_total)
    weights_grad = mul(attended_grad, value_heads, "thd,shd->hts")
    value_grad = mul(weights_full.astype(BF16), attended_grad, "hts,thd->shd")
    value_grad = value_grad.reshape(span, width).astype(BF16)
    centre = jnp.sum(weights_full * weights_grad, axis=-1, keepdims=True)
    score_grad = (weights_full * (weights_grad - centre)).astype(BF16)
    query_rot_grad = mul(score_grad, key_rot, "hts,shd->thd").reshape(span, width) * score_scale
    key_rot_grad = mul(score_grad, query_rot, "hts,thd->shd").reshape(span, width) * score_scale
    query_pre_grad, grad_query_gain = query_back(query_rot_grad)
    key_pre_grad, grad_key_gain = key_back(key_rot_grad)
    query_low = query_pre_grad.astype(BF16)
    key_low = key_pre_grad.astype(BF16)
    normed_in_grad = mul(query_low, query_full, "to,io->ti")
    normed_in_grad = normed_in_grad + mul(key_low, key_full, "to,io->ti")
    normed_in_grad = normed_in_grad + mul(value_grad, value_full, "to,io->ti")
    input_grad, grad_in_gain = norm_in_back(normed_in_grad)
    grad_tokens = middle_grad + input_grad

    small = jnp.concatenate(
        [
            jnp.stack([grad_in_gain, grad_query_gain, grad_key_gain, grad_mid_gain]).T,
            grad_router,
        ],
        axis=1,
    )
    rights = (branch_grad, value_grad, key_low, query_low)
    if wide:
        expert_out, lefts, rights = lax.optimization_barrier((expert_out, lefts, rights))
    mixture, grad_gate_up, grad_down = combine(
        expert_out, pos_all, slots, cot_slots, gate_grad_low, up_grad_low, hidden_gated, 4
    )
    output = (middle + mixture).astype(BF16)
    if wide:
        kinds = small.shape[1]
        split = small.reshape(OUTER, 2 * per, -1, kinds).transpose(1, 0, 3, 2)
        split = split.reshape(2 * per, OUTER, 1, -1)
        grads, small = weight_grads(lefts, rights, split, experts, 5)
        small = small.reshape(kinds, -1).T
    else:
        small = lax.psum_scatter(small, both, scatter_dimension=0, tiled=True)
        grads = []
        for source, right in zip(SOURCE, rights):
            grad = jnp.dot(turned[source], right, preferred_element_type=F32).astype(BF16)
            grid = grad.reshape(experts, 2, width // experts // 2, width).swapaxes(0, 1)
            half = lax.psum_scatter(grid, "dp", scatter_dimension=0, tiled=False)
            half = lax.psum_scatter(half, "expert", scatter_dimension=0, tiled=False)
            grads.append(half.astype(F32))
    return (
        output,
        grad_tokens,
        small[:, 0],
        small[:, 1],
        small[:, 2],
        small[:, 3],
        grads[3],
        grads[2],
        grads[1],
        grads[0],
        small[:, 4:],
        grad_gate_up[None],
        grad_down[None],
    )


def solution(mesh):
    both = P(("expert", "dp"))
    rows = P(("expert", "dp"), None)
    in_specs = (rows, rows, both, rows) + (P("dp"),) * 4 + (P("dp", None),) * 5 + (
        P("expert", None, None, "dp"),
        P("expert", None, "dp"),
    )
    out_specs = (rows, rows) + (both,) * 4 + (rows,) * 5 + (
        P("expert", None, None, "dp"),
        P("expert", None, "dp"),
    )
    return jax.shard_map(body, mesh=mesh, in_specs=in_specs, out_specs=out_specs, check_vma=False)
```

```python
import functools
import math

import jax
import jax.numpy as jnp
from jax import lax
from jax.experimental import pallas as pl
from jax.experimental.pallas import tpu as pltpu
from jax.sharding import PartitionSpec as P

NH = 16
HD = 128
TOP = 8
OUTER = 4

EPSILON = 1e-05
ROPE_BASE = 10000.0
MESH = pl.DeviceIdType.MESH
F32 = jnp.float32
BF16 = jnp.bfloat16


def rms_scale(values):
    return lax.rsqrt(jnp.mean(values * values, axis=-1, keepdims=True) + EPSILON)


def norm_apply(values, gain_vector):
    return values * rms_scale(values) * gain_vector


def rotary_tables(positions):
    frequencies = 1.0 / ROPE_BASE ** (jnp.arange(0, HD, 2).astype(F32) / HD)
    angles = positions[:, None] * frequencies[None, :]
    angles = jnp.concatenate([angles, angles], axis=-1)
    return (jnp.cos(angles), jnp.sin(angles))


def rotary_norm(projected, gain_vector, cosine_table, sine_table):
    normed = projected * rms_scale(projected) * gain_vector
    shaped = normed.reshape(normed.shape[0], NH, HD)
    half_width = HD // 2
    turned = jnp.concatenate([-shaped[..., half_width:], shaped[..., :half_width]], axis=-1)
    rotated = shaped * cosine_table[:, None, :] + turned * sine_table[:, None, :]
    return rotated.reshape(normed.shape[0], NH * HD)


def flip(r, n):
    out, bit = r, 1
    while bit <= n:
        if n & bit:
            out = out + bit - 2 * bit * ((r // bit) % 2)
        bit *= 2
    return out


def pick(table, z):
    code = sum(v * 4**k for k, v in enumerate(table))
    return (code // ((1 + 3 * (z % 2)) * (1 + 15 * (z // 2)))) % 4


NEAR = ((1, 0, 1, 2), (2, 2, 3, 1), (3, 3, 0, 0))
PLACE = ((1, 3, 3, 1), (3, 1, 2, 3), (2, 2, 1, 2))
BLOCK = ((1, 3, 0, 2), (3, 0, 3, 0), (2, 2, 1, 1))
FAR = ((3, 3, 0, 0), (2, 0, 3, 1), (1, 2, 1, 2))


def one_hot(pos_ref, r, j, per, cap):
    span = pos_ref.shape[-1]
    rows = []
    slot = lax.broadcasted_iota(jnp.int32, (cap, span), 0).astype(F32)
    for n in range(per):
        line = pos_ref[j, flip(r, n)]
        rows.append(jnp.where(line == slot, 1.0, 0.0).astype(BF16))
    return jnp.concatenate(rows, axis=0)


def attend_body(per, cap, *refs):
    tok_ref, x_ref, meta_ref, gains_ref, cos_ref, sin_ref, limit_ref, router_ref = refs[:8]
    parts, refs = refs[8:12], refs[12:]
    out_ref, here_ref, pos_ref = refs[:3]
    fulls, refs = refs[3:7], refs[7:]
    turned_ref, nin_ref, qpre, kpre, qrot, krot, val_ref, lse_ref, att_ref, mid_ref = refs[:10]
    nmid_ref, gates_ref, zbuf, sbuf, wbuf, vacc = refs[10:16]
    zs, zr, ps, pr, ls, ms, mr, ts, tr, ds, dr, ks, fs = refs[16:]
    e, c = lax.axis_index("expert"), lax.axis_index("dp")
    z, r = e // per, e % per
    experts = OUTER * per
    bar = pltpu.get_barrier_semaphore()
    for d in range(1, experts):
        pl.semaphore_signal(bar, inc=1, device_id=((e + d) % experts, c), device_id_type=MESH)
    pl.semaphore_signal(bar, inc=1, device_id=(e, 1 - c), device_id_type=MESH)
    pl.semaphore_wait(bar, experts)
    span, width = x_ref.shape
    step = min(512, width)
    half = width // 2

    def share(d):
        to = (e + d) % experts
        return pltpu.make_async_remote_copy(
            src_ref=meta_ref.at[to], dst_ref=here_ref.at[e], send_sem=ms.at[d - 1],
            recv_sem=mr.at[d - 1], device_id=(to, c), device_id_type=MESH,
        )

    def table(d):
        to = (z + d) % OUTER
        return pltpu.make_async_remote_copy(
            src_ref=meta_ref.at[pl.ds(to * per, per)], dst_ref=pos_ref.at[z],
            send_sem=ts.at[d - 1], recv_sem=tr.at[z],
            device_id=(to * per + r, c), device_id_type=MESH,
        )

    def tabled(j):
        return pltpu.make_async_remote_copy(
            src_ref=meta_ref.at[pl.ds(0, per)], dst_ref=pos_ref.at[j], send_sem=ts.at[0],
            recv_sem=tr.at[j], device_id=(j * per + r, c), device_id_type=MESH,
        )

    def up(src, j):
        return pltpu.make_async_remote_copy(
            src_ref=src, dst_ref=zbuf.at[j], send_sem=zs.at[0, j], recv_sem=zr.at[j],
            device_id=((z + 1) * per + r, c), device_id_type=MESH,
        )

    def down(src, j):
        return pltpu.make_async_remote_copy(
            src_ref=src, dst_ref=zbuf.at[j], send_sem=zs.at[1, j], recv_sem=zr.at[j],
            device_id=((z - 1) * per + r, c), device_id_type=MESH,
        )

    def plane(i, j, n):
        return pltpu.make_async_remote_copy(
            src_ref=sbuf.at[i, n], dst_ref=out_ref.at[j, n], send_sem=ps.at[i, n],
            recv_sem=pr.at[i, n], device_id=(z * per + flip(r, n), c), device_id_type=MESH,
        )

    def local(i, j):
        return pltpu.make_async_copy(sbuf.at[i, 0], out_ref.at[j, 0], ls.at[i])

    def lines(owner):
        return pl.ds(pl.multiple_of(owner * half, half), half)

    def give(k):
        return pltpu.make_async_remote_copy(
            src_ref=parts[k], dst_ref=fulls[k].at[lines(c)], send_sem=ds.at[k],
            recv_sem=dr.at[k], device_id=(e, 1 - c), device_id_type=MESH,
        )

    def hold(t):
        return pltpu.make_async_copy(wbuf.at[t % 2], fulls[jobs[t][0]].at[lines(c)], ks.at[t % 2])

    jobs = [(0, 0), (1, 0), (2, 0), (0, 1), (1, 1), (2, 1), (3, 0), (3, 1)]

    def fetch(t):
        k, far = jobs[t]
        src = fulls[k].at[lines(1 - c)] if far else parts[k]
        return pltpu.make_async_copy(src, wbuf.at[t % 2], fs.at[t % 2])

    def project(t):
        k, far = jobs[t]
        left = att_ref if k == 3 else nin_ref
        into = (qpre, kpre, vacc, mid_ref)[k]
        fetch(t).wait()
        if not far:
            hold(t).start()
        mine = lines(1 - c if far else c)

        @pl.loop(0, width // step)
        def _(q):
            columns = pl.ds(pl.multiple_of(q * step, step), step)
            got = jnp.dot(left[:, mine], wbuf[t % 2, :, columns], preferred_element_type=F32)
            if k == 3 and not far:
                into[:, columns] = tok_ref[:, columns].astype(F32) + got
            elif far:
                into[:, columns] += got
            else:
                into[:, columns] = got

        if not far:
            hold(t).wait()
        if t + 2 < len(jobs):
            if jobs[t + 2][1]:
                give(jobs[t + 2][0]).wait_recv()
            fetch(t + 2).start()

    order = [z] + [pick(t, z) for t in NEAR]

    def choose(i, j):
        if i == 0:
            block = x_ref
        else:
            block = zbuf.at[j]
            up(x_ref, j).wait_recv()

            @pl.when(jnp.logical_and(j < z, z < OUTER - 1))
            def _():
                up(zbuf.at[j], j).start()

            @pl.when(jnp.logical_and(j > z, z > 0))
            def _():
                down(zbuf.at[j], j).start()

            tabled(j).wait_recv()

        marks = one_hot(pos_ref, r, j, per, cap)

        @pl.loop(0, width // step)
        def _(k):
            columns = pl.ds(pl.multiple_of(k * step, step), step)
            got = jnp.dot(marks, block[:, columns], preferred_element_type=F32).astype(BF16)
            for n in range(per):
                sbuf[i, n, :, columns] = got[n * cap : (n + 1) * cap]

        for n in range(1, per):
            plane(i, j, n).start()
        local(i, j).start()

    for d in range(1, OUTER):
        table(d).start()

    @pl.when(z < OUTER - 1)
    def _():
        up(x_ref, z).start()

    @pl.when(z > 0)
    def _():
        down(x_ref, z).start()

    fetch(0).start()
    fetch(1).start()
    pos_ref[z] = meta_ref[pl.ds(z * per, per)]
    here_ref[e] = meta_ref[e]
    choose(0, z)
    for k in range(4):
        give(k).start()
    for d in range(1, experts):
        share(d).start()

    inputs = tok_ref[...].astype(F32)
    nin_ref[...] = norm_apply(inputs, gains_ref[0:1]).astype(BF16)
    for t in range(6):
        project(t)
    val_ref[...] = vacc[...].astype(BF16)
    query_scale = rms_scale(qpre[...])
    key_scale = rms_scale(kpre[...])
    choose(1, order[1])
    turned_ref[0] = nin_ref[...].T
    score_scale = HD ** (-0.5)
    column = lax.broadcasted_iota(jnp.int32, (span, span), 1).astype(F32)

    def heads(first, last):
        @pl.loop(first, last)
        def _(h):
            columns = pl.ds(pl.multiple_of(h * HD, HD), HD)

            def turn(pre, scale, row):
                normed = pre[:, columns] * scale * gains_ref[row : row + 1, columns]
                return (
                    normed * cos_ref[...] + pltpu.roll(normed, HD // 2, 1) * sin_ref[...]
                ).astype(BF16)

            query = turn(qpre, query_scale, 1)
            key = turn(kpre, key_scale, 2)
            qrot[:, columns] = query
            krot[:, columns] = key
            scores = lax.dot_general(
                query, key, (((1,), (1,)), ((), ())), preferred_element_type=F32
            )
            scores = jnp.where(column <= limit_ref[...], scores * score_scale, -1e30)
            peak = jnp.max(scores, axis=-1, keepdims=True)
            total = peak + jnp.log(jnp.sum(jnp.exp(scores - peak), axis=-1, keepdims=True))
            lse_ref[h] = total
            weights = jnp.exp(scores - total).astype(BF16)
            att_ref[:, columns] = jnp.dot(
                weights, val_ref[:, columns], preferred_element_type=F32
            ).astype(BF16)

    heads(0, NH // 2)
    choose(2, order[2])
    heads(NH // 2, NH)
    project(6)
    choose(3, order[3])
    project(7)
    turned_ref[1] = att_ref[...].T
    middle = mid_ref[...]
    nmid_ref[...] = norm_apply(middle, gains_ref[3:4]).astype(BF16)
    logits = jnp.dot(nmid_ref[...], router_ref[...], preferred_element_type=F32)
    raised = jnp.exp(logits - jnp.max(logits, axis=-1, keepdims=True))
    gates_ref[...] = raised / jnp.sum(raised, axis=-1, keepdims=True)

    for i, j in enumerate(order):
        local(i, j).wait()
        for n in range(1, per):
            plane(i, j, n).wait()

    @pl.when(z < OUTER - 1)
    def _():
        up(x_ref, z).wait_send()

    @pl.when(z > 0)
    def _():
        down(x_ref, z).wait_send()

    for j in order[1:]:

        @pl.when(jnp.logical_and(j < z, z < OUTER - 1))
        def _():
            up(zbuf.at[j], j).wait_send()

        @pl.when(jnp.logical_and(j > z, z > 0))
        def _():
            down(zbuf.at[j], j).wait_send()

    for d in range(1, experts):
        share(d).wait()
    for d in range(1, OUTER):
        table(d).wait_send()
    for k in range(4):
        give(k).wait_send()


def attend(tokens, cotangent, meta, gains, tables, limit, router, parts, cap, number):
    experts, _, span = meta.shape
    per = experts // OUTER
    width = tokens.shape[1]
    half = parts[0].shape[0]
    vmem = pl.BlockSpec(memory_space=pltpu.VMEM)
    hbm = pl.BlockSpec(memory_space=pltpu.HBM)
    dma = pltpu.SemaphoreType.DMA
    low = jax.ShapeDtypeStruct((span, width), BF16)
    high = jax.ShapeDtypeStruct((span, width), F32)
    return pl.pallas_call(
        functools.partial(attend_body, per, cap),
        out_shape=(
            jax.ShapeDtypeStruct((OUTER, per, cap, width), BF16),
            jax.ShapeDtypeStruct((experts, 1, span), F32),
            jax.ShapeDtypeStruct((OUTER, per, 1, span), F32),
        )
        + (jax.ShapeDtypeStruct((2 * half, width), BF16),) * 4
        + (jax.ShapeDtypeStruct((2, width, span), BF16), low, high, high, low, low, low)
        + (jax.ShapeDtypeStruct((NH, span, 1), F32), low, high, low)
        + (jax.ShapeDtypeStruct((span, experts), F32),),
        in_specs=[vmem] * 8 + [hbm] * 4,
        out_specs=(hbm, vmem, vmem) + (hbm,) * 4 + (vmem,) * 12,
        scratch_shapes=[
            pltpu.VMEM((OUTER, span, width), BF16),
            pltpu.VMEM((OUTER, per, cap, width), BF16),
            pltpu.VMEM((2, half, width), BF16),
            pltpu.VMEM((span, width), F32),
            dma((2, OUTER)),
            dma((OUTER,)),
            dma((OUTER, per)),
            dma((OUTER, per)),
            dma((OUTER,)),
            dma((experts,)),
            dma((experts,)),
            dma((OUTER,)),
            dma((OUTER,)),
            dma((4,)),
            dma((4,)),
            dma((2,)),
            dma((2,)),
        ],
        compiler_params=pltpu.CompilerParams(
            collective_id=number, has_side_effects=True, vmem_limit_bytes=60 << 20
        ),
        name="attend",
    )(tokens, cotangent, meta, gains, *tables, limit, router, *parts)


def experts_body(per, cap, *refs):
    x_ref, gates_ref, pos_ref, posh_ref, cot_ref, wg_ref, wu_ref, wd_ref = refs[:8]
    back_ref, pg_ref, out_ref, gl_ref, ul_ref, hg_ref, eo_ref = refs[8:15]
    zbuf, sbuf, wg, wu, wd, slb, ctb, glb, ulb, hlb, hgb, eob, ybuf, ubuf, rbuf = refs[15:30]
    here, ggv, sgv, tgv = refs[30:34]
    zs, zr, ps, pr, ls, ms, mr, ws, cs, os, es, bs, br, us, ur, gs, gr = refs[34:]
    e, c = lax.axis_index("expert"), lax.axis_index("dp")
    z, r = e // per, e % per
    experts = OUTER * per
    bar = pltpu.get_barrier_semaphore()
    for d in range(1, experts):
        pl.semaphore_signal(bar, inc=1, device_id=((e + d) % experts, c), device_id_type=MESH)
    pl.semaphore_wait(bar, experts - 1)
    span, width = x_ref.shape
    hidden = wg.shape[1]
    step = min(512, width)
    thin = min(256, hidden)
    halves = 2
    half = width // halves

    def share(d):
        to = (e + d) % experts
        return pltpu.make_async_remote_copy(
            src_ref=gates_ref.at[to], dst_ref=here.at[e], send_sem=ms.at[d - 1],
            recv_sem=mr.at[d - 1], device_id=(to, c), device_id_type=MESH,
        )

    def up(src, j):
        return pltpu.make_async_remote_copy(
            src_ref=src, dst_ref=zbuf.at[j], send_sem=zs.at[0, j], recv_sem=zr.at[j],
            device_id=((z + 1) * per + r, c), device_id_type=MESH,
        )

    def down(src, j):
        return pltpu.make_async_remote_copy(
            src_ref=src, dst_ref=zbuf.at[j], send_sem=zs.at[1, j], recv_sem=zr.at[j],
            device_id=((z - 1) * per + r, c), device_id_type=MESH,
        )

    def plane(i, j, n):
        return pltpu.make_async_remote_copy(
            src_ref=sbuf.at[i, n], dst_ref=out_ref.at[j, n], send_sem=ps.at[i, n],
            recv_sem=pr.at[i, n], device_id=(z * per + flip(r, n), c), device_id_type=MESH,
        )

    def local(i, j):
        return pltpu.make_async_copy(sbuf.at[i, 0], out_ref.at[j, 0], ls.at[i])

    def returned(i, n):
        return pltpu.make_async_remote_copy(
            src_ref=sbuf.at[i, n], dst_ref=ybuf.at[i, n - 1], send_sem=bs.at[i, n],
            recv_sem=br.at[i, n], device_id=(z * per + flip(r, n), c), device_id_type=MESH,
        )

    def part(h):
        return pl.ds(h * half, half)

    def rise(i, j, h, slot):
        return pltpu.make_async_remote_copy(
            src_ref=ubuf.at[i, h], dst_ref=rbuf.at[slot, h], send_sem=us.at[i, h],
            recv_sem=ur.at[slot, h], device_id=((z + 1) * per + r, c), device_id_type=MESH,
        )

    def fall(i, j, h, slot):
        return pltpu.make_async_remote_copy(
            src_ref=ubuf.at[i, h], dst_ref=rbuf.at[slot, h], send_sem=us.at[i, h],
            recv_sem=ur.at[slot, h], device_id=((z - 1) * per + r, c), device_id_type=MESH,
        )

    def graded(i, n, seq):
        return pltpu.make_async_remote_copy(
            src_ref=tgv.at[i, n], dst_ref=pg_ref.at[e], send_sem=gs.at[i, n],
            recv_sem=gr.at[e], device_id=(seq, c), device_id_type=MESH,
        )

    def grade(s):
        return pltpu.make_async_remote_copy(
            src_ref=tgv.at[0, 0], dst_ref=pg_ref.at[s], send_sem=gs.at[0, 0],
            recv_sem=gr.at[s], device_id=(s, c), device_id_type=MESH,
        )

    weights = [
        pltpu.make_async_copy(src, dst, ws.at[k])
        for k, (src, dst) in enumerate(((wg_ref, wg), (wu_ref, wu), (wd_ref, wd)))
    ]

    def pull(j):
        return pltpu.make_async_copy(cot_ref.at[j], ctb, cs)

    for d in range(1, experts):
        share(d).start()

    @pl.when(z < OUTER - 1)
    def _():
        up(x_ref, z).start()

    @pl.when(z > 0)
    def _():
        down(x_ref, z).start()

    here[e] = gates_ref[e]
    order = [z] + [pick(t, z) for t in NEAR]

    def choose(i, j):
        if i == 0:
            block = x_ref
        else:
            block = zbuf.at[j]
            up(x_ref, j).wait_recv()

            @pl.when(jnp.logical_and(j < z, z < OUTER - 1))
            def _():
                up(zbuf.at[j], j).start()

            @pl.when(jnp.logical_and(j > z, z > 0))
            def _():
                down(zbuf.at[j], j).start()

        marks = one_hot(pos_ref, r, j, per, cap)

        @pl.loop(0, width // step)
        def _(k):
            columns = pl.ds(pl.multiple_of(k * step, step), step)
            got = jnp.dot(marks, block[:, columns], preferred_element_type=F32).astype(BF16)
            for n in range(per):
                sbuf[i, n, :, columns] = got[n * cap : (n + 1) * cap]

        for n in range(1, per):
            plane(i, j, n).start()
        local(i, j).start()

    def outs(j):
        return [
            pltpu.make_async_copy(src, dst.at[j], os.at[k])
            for k, (src, dst) in enumerate(((glb, gl_ref), (ulb, ul_ref), (hgb, hg_ref)))
        ]

    def away(j):
        return pltpu.make_async_copy(eob, eo_ref.at[j], es)

    def marked(j, n):
        slot = lax.broadcasted_iota(jnp.int32, (cap, span), 0).astype(F32)
        return posh_ref[j * per + flip(r, n)] == slot

    def expert(i, j):
        for n in range(1, per):
            plane(i, j, n).wait()
        local(i, j).wait()
        if i == OUTER - 1:
            send_back(1)
        fetch = pltpu.make_async_copy(out_ref.at[j], slb, ls.at[OUTER])
        fetch.start()
        slot_gate = jnp.concatenate(
            [
                jnp.sum(
                    jnp.where(marked(j, n), here[j * per + flip(r, n)], 0.0), axis=1, keepdims=True
                )
                for n in range(per)
            ],
            axis=0,
        )
        sgv[i % 2] = slot_gate
        ggv[i % 2] = jnp.zeros(ggv.shape[1:], F32)
        pull(j).wait()
        fetch.wait()
        if i > 0:
            for copy in outs(order[i - 1]):
                copy.wait()

        @pl.loop(0, hidden // thin)
        def _(k):
            columns = pl.ds(pl.multiple_of(k * thin, thin), thin)
            rows = slb[...].reshape(per * cap, width)
            gate_pre = jnp.dot(rows, wg[:, columns], preferred_element_type=F32)
            up_pre = jnp.dot(rows, wu[:, columns], preferred_element_type=F32)
            pulled = jnp.dot(
                ctb[...].reshape(per * cap, width), wd[:, columns], preferred_element_type=F32
            )
            sigmoid_gate = jax.nn.sigmoid(gate_pre)
            silu_gate = gate_pre * sigmoid_gate
            low = (silu_gate * up_pre).astype(BF16)
            wide = low.astype(F32)
            ggv[i % 2] += jnp.sum(wide * pulled, axis=1, keepdims=True)
            hidden_grad = pulled * slot_gate
            glb[:, columns] = (
                hidden_grad * up_pre * sigmoid_gate * (1.0 + gate_pre * (1.0 - sigmoid_gate))
            ).astype(BF16)
            ulb[:, columns] = (hidden_grad * silu_gate).astype(BF16)
            hlb[i % 2, :, columns] = low
            hgb[:, columns] = (wide * slot_gate).astype(BF16)

        if i < OUTER - 1:
            pull(order[i + 1]).start()
        for copy in outs(j):
            copy.start()

        @pl.loop(0, width // step)
        def _(k):
            columns = pl.ds(pl.multiple_of(k * step, step), step)
            got = lax.dot_general(
                glb[...], wg[columns, :], (((1,), (1,)), ((), ())), preferred_element_type=F32
            ) + lax.dot_general(
                ulb[...], wu[columns, :], (((1,), (1,)), ((), ())), preferred_element_type=F32
            )
            got = got.astype(BF16)
            for n in range(per):
                sbuf[i, n, :, columns] = got[n * cap : (n + 1) * cap]

    def send_back(i):
        for n in range(1, per):
            returned(i, n).start()

    def finish(i, j):
        for n in range(per):
            seq = j * per + flip(r, n)
            row = jnp.sum(
                jnp.where(marked(j, n), ggv[i % 2, n * cap : (n + 1) * cap], 0.0),
                axis=0,
                keepdims=True,
            )
            tgv[i, n] = row
            if i == 0 and n == 0:
                pg_ref[e] = row
            else:
                graded(i, n, seq).start()
        if i > 0:
            away(order[i - 1]).wait()

        @pl.loop(0, width // step)
        def _(k):
            columns = pl.ds(pl.multiple_of(k * step, step), step)
            got = lax.dot_general(
                hlb[i % 2], wd[columns, :], (((1,), (1,)), ((), ())), preferred_element_type=F32
            )
            got = (got * sgv[i % 2]).astype(BF16)
            for n in range(per):
                eob[n, :, columns] = got[n * cap : (n + 1) * cap]

        away(j).start()

    choose(0, z)
    for copy in weights:
        copy.start()
    pull(z).start()
    choose(1, order[1])
    for copy in weights:
        copy.wait()
    for d in range(1, experts):
        share(d).wait()
    last = OUTER - 1
    for i in range(last):
        expert(i, order[i])
        if i + 2 <= last:
            choose(i + 2, order[i + 2])
            finish(i, order[i])
    expert(last, order[last])
    for i in (last, last - 1, 0):
        send_back(i)
    finish(last - 1, order[last - 1])

    def fold(i, j, h):
        marks = one_hot(pos_ref, r, j, per, cap)

        @pl.loop(0, half // step)
        def _(k):
            columns = pl.ds(pl.multiple_of(h * half + k * step, step), step)
            rows = jnp.concatenate(
                [ybuf[i, n - 1, :, columns] if n else sbuf[i, 0, :, columns] for n in range(per)],
                axis=0,
            )
            back_ref[:, columns] = lax.dot_general(
                marks, rows, (((0,), (0,)), ((), ())), preferred_element_type=F32
            )

    for p in range(last):
        i, j = pick(PLACE[p], z), pick(BLOCK[p], z)
        for n in range(1, per):
            returned(i, n).wait_recv()
        for h in range(halves):
            fold(i, j, h)

            @pl.when(jnp.logical_and(j > z, z > 0))
            def _():
                rise(0, j, h, j).wait_recv()
                back_ref[:, part(h)] += rbuf[j, h].astype(F32)

            @pl.when(jnp.logical_and(j < z, z < OUTER - 1))
            def _():
                fall(0, j, h, j).wait_recv()
                back_ref[:, part(h)] += rbuf[j, h].astype(F32)

            ubuf[p, h] = back_ref[:, part(h)].astype(BF16)

            @pl.when(j > z)
            def _():
                rise(p, j, h, j).start()

            @pl.when(jnp.logical_and(j < z, z - j > 1))
            def _():
                fall(p, j, h, j).start()

            @pl.when(z - j == 1)
            def _():
                fall(p, j, h, OUTER).start()

        if p == 0:
            finish(last, order[last])

    for n in range(1, per):
        returned(0, n).wait_recv()
    for h in range(halves):
        fold(0, z, h)

        @pl.when(z > 0)
        def _():
            rise(0, z, h, z).wait_recv()
            back_ref[:, part(h)] += rbuf[z, h].astype(F32)

        @pl.when(z < OUTER - 1)
        def _():
            fall(0, z, h, OUTER).wait_recv()
            back_ref[:, part(h)] += rbuf[OUTER, h].astype(F32)

    @pl.when(z < OUTER - 1)
    def _():
        up(x_ref, z).wait_send()

    @pl.when(z > 0)
    def _():
        down(x_ref, z).wait_send()

    for i, j in enumerate(order):
        for n in range(1, per):
            returned(i, n).wait_send()
        if i > 0:

            @pl.when(jnp.logical_and(j < z, z < OUTER - 1))
            def _():
                up(zbuf.at[j], j).wait_send()

            @pl.when(jnp.logical_and(j > z, z > 0))
            def _():
                down(zbuf.at[j], j).wait_send()

            for h in range(halves):
                rise(i - 1, j, h, j).wait_send()
        for n in range(per):
            if i or n:
                graded(i, n, j * per + flip(r, n)).wait_send()
    for d in range(1, experts):
        grade((e + d) % experts).wait_recv()
    for copy in outs(order[last]):
        copy.wait()
    away(order[last]).wait()


def run_experts(x, gates, pos, pos_here, cot_slots, gate_full, up_full, down_full, number):
    experts, _, span = gates.shape
    outer, per, cap, width = cot_slots.shape
    hidden = gate_full.shape[1]
    block = per * cap
    vmem = pl.BlockSpec(memory_space=pltpu.VMEM)
    hbm = pl.BlockSpec(memory_space=pltpu.HBM)
    dma = pltpu.SemaphoreType.DMA
    rows = jax.ShapeDtypeStruct((OUTER, per, cap, width), BF16)
    thin = jax.ShapeDtypeStruct((OUTER, block, hidden), BF16)
    return pl.pallas_call(
        functools.partial(experts_body, per, cap),
        out_shape=(
            jax.ShapeDtypeStruct((span, width), F32),
            jax.ShapeDtypeStruct((experts, 1, span), F32),
            rows, thin, thin, thin, rows,
        ),
        in_specs=[vmem] * 4 + [hbm] * 4,
        out_specs=(vmem, vmem) + (hbm,) * 5,
        scratch_shapes=[
            pltpu.VMEM((OUTER, span, width), BF16),
            pltpu.VMEM((OUTER, per, cap, width), BF16),
            pltpu.VMEM((width, hidden), BF16),
            pltpu.VMEM((width, hidden), BF16),
            pltpu.VMEM((width, hidden), BF16),
            pltpu.VMEM((per, cap, width), BF16),
            pltpu.VMEM((per, cap, width), BF16),
            pltpu.VMEM((block, hidden), BF16),
            pltpu.VMEM((block, hidden), BF16),
            pltpu.VMEM((2, block, hidden), BF16),
            pltpu.VMEM((block, hidden), BF16),
            pltpu.VMEM((per, cap, width), BF16),
            pltpu.VMEM((OUTER, per - 1, cap, width), BF16),
            pltpu.VMEM((OUTER - 1, 2, span, width // 2), BF16),
            pltpu.VMEM((OUTER + 1, 2, span, width // 2), BF16),
            pltpu.VMEM((experts, 1, span), F32),
            pltpu.VMEM((2, block, 1), F32),
            pltpu.VMEM((2, block, 1), F32),
            pltpu.VMEM((OUTER, per, 1, span), F32),
            dma((2, OUTER)),
            dma((OUTER,)),
            dma((OUTER, per)),
            dma((OUTER, per)),
            dma((OUTER + 1,)),
            dma((experts,)),
            dma((experts,)),
            dma((3,)),
            dma,
            dma((3,)),
            dma,
            dma((OUTER, per)),
            dma((OUTER, per)),
            dma((OUTER - 1, 2)),
            dma((OUTER + 1, 2)),
            dma((OUTER, per)),
            dma((experts,)),
        ],
        compiler_params=pltpu.CompilerParams(
            collective_id=number, has_side_effects=True, vmem_limit_bytes=62 << 20
        ),
        name="experts",
    )(x, gates, pos, pos_here, cot_slots, gate_full, up_full, down_full)


def combine_body(per, cap, *refs):
    y_ref, pos_ref, mid_ref, slots_ref, cot_ref, gl_ref, ul_ref, hg_ref = refs[:8]
    res_ref, gu_ref, dn_ref, out_ref, ybuf, ubuf, rbuf = refs[8:15]
    theirs, ours, lbuf, lturn, tbuf, rx, stage = refs[15:22]
    zs, zr, ps, pr, ls, rs, ws, ds, dr, gs = refs[22:]
    e, c = lax.axis_index("expert"), lax.axis_index("dp")
    z, r = e // per, e % per
    bar = pltpu.get_barrier_semaphore()
    for d in range(1, OUTER):
        pl.semaphore_signal(
            bar, inc=1, device_id=((z + d) % OUTER * per + r, c), device_id_type=MESH
        )
    for n in range(1, per):
        pl.semaphore_signal(bar, inc=1, device_id=(z * per + flip(r, n), c), device_id_type=MESH)
    pl.semaphore_signal(bar, inc=1, device_id=(e, 1 - c), device_id_type=MESH)
    pl.semaphore_wait(bar, OUTER - 1 + per - 1 + 1)
    span, width = out_ref.shape
    step = min(512, width)
    share = dn_ref.shape[1]
    thin = min(256, share)
    total = OUTER * per * cap

    def plane(i, j, n):
        return pltpu.make_async_remote_copy(
            src_ref=y_ref.at[j, n], dst_ref=ybuf.at[i, n], send_sem=ps.at[i, n],
            recv_sem=pr.at[i, n], device_id=(z * per + flip(r, n), c), device_id_type=MESH,
        )

    def local(i, j):
        return pltpu.make_async_copy(y_ref.at[j, 0], ybuf.at[i, 0], ls.at[i])

    halves = 2
    half = width // halves

    def part(h):
        return pl.ds(h * half, half)

    def rise(i, h, slot):
        return pltpu.make_async_remote_copy(
            src_ref=ubuf.at[i, h], dst_ref=rbuf.at[slot, h], send_sem=zs.at[i, h],
            recv_sem=zr.at[slot, h], device_id=((z + 1) * per + r, c), device_id_type=MESH,
        )

    def fall(i, h, slot):
        return pltpu.make_async_remote_copy(
            src_ref=ubuf.at[i, h], dst_ref=rbuf.at[slot, h], send_sem=zs.at[i, h],
            recv_sem=zr.at[slot, h], device_id=((z - 1) * per + r, c), device_id_type=MESH,
        )

    def rights(k, src, other):
        owner = 1 - c if other else c
        return pltpu.make_async_copy(
            src.at[:, :, pl.ds(pl.multiple_of(owner * share, share), share)],
            (theirs if other else ours).at[:, :, pl.ds(k * share, share)],
            rs.at[k, int(other)],
        )

    def across(k):
        return pltpu.make_async_remote_copy(
            src_ref=tbuf.at[k % 2], dst_ref=rx.at[k], send_sem=ds.at[k], recv_sem=dr.at[k],
            device_id=(e, 1 - c), device_id_type=MESH,
        )

    def stores(k):
        lines = pl.ds(k * step, step)
        return [
            pltpu.make_async_copy(
                stage.at[:, pl.ds(m * share, share)],
                dn_ref.at[lines] if m == 2 else gu_ref.at[m, lines],
                gs.at[m],
            )
            for m in range(3)
        ]

    sources = (gl_ref, ul_ref, hg_ref)
    loads = [rights(k, src, other) for k, src in enumerate(sources) for other in (True, False)]

    def tile(k):
        if k == 0:
            for copy in loads:
                copy.wait()
        if k >= 2:
            across(k - 2).wait_send()
        if k >= 1:
            for copy in stores(k - 1):
                copy.wait()
        for src, first, count in ((slots_ref, 0, 2), (cot_ref, 2, 1)):
            fetch = pltpu.make_async_copy(
                src.at[:, :, :, pl.ds(k * step, step)], lbuf, ws
            )
            fetch.start()
            fetch.wait()
            lturn[...] = lbuf[...].reshape(total, step).T

            @pl.loop(0, count * share // thin)
            def _(q):
                at = pl.ds(pl.multiple_of(first * share + q * thin, thin), thin)
                tbuf[k % 2, :, at] = jnp.dot(
                    lturn[...], theirs[:, :, at].reshape(total, thin), preferred_element_type=F32
                ).astype(BF16)
                stage[:, at] = jnp.dot(
                    lturn[...], ours[:, :, at].reshape(total, thin), preferred_element_type=F32
                )

        across(k).start()
        across(k).wait_recv()
        stage[...] += rx[k].astype(F32)
        for copy in stores(k):
            copy.start()

    order = [pick(t, z) for t in FAR] + [z]
    for i, j in enumerate(order):
        for n in range(1, per):
            plane(i, j, n).start()
        local(i, j).start()
    for copy in loads:
        copy.start()
    tiles = width // step
    done = 0
    for i, j in enumerate(order):
        while done < tiles * (2, 3, 3, 4)[i] // 4:
            tile(done)
            done += 1
        marks = one_hot(pos_ref, r, j, per, cap)
        local(i, j).wait()
        for n in range(1, per):
            plane(i, j, n).wait_recv()
        for h in range(halves):

            @pl.loop(0, half // step)
            def _(k):
                columns = pl.ds(pl.multiple_of(h * half + k * step, step), step)
                rows = jnp.concatenate([ybuf[i, n, :, columns] for n in range(per)], axis=0)
                out_ref[:, columns] = lax.dot_general(
                    marks, rows, (((0,), (0,)), ((), ())), preferred_element_type=F32
                )

            if i < OUTER - 1:

                @pl.when(jnp.logical_and(j > z, z > 0))
                def _():
                    rise(0, h, j).wait_recv()
                    out_ref[:, part(h)] += rbuf[j, h].astype(F32)

                @pl.when(jnp.logical_and(j < z, z < OUTER - 1))
                def _():
                    fall(0, h, j).wait_recv()
                    out_ref[:, part(h)] += rbuf[j, h].astype(F32)

                ubuf[i, h] = out_ref[:, part(h)].astype(BF16)

                @pl.when(j > z)
                def _():
                    rise(i, h, j).start()

                @pl.when(jnp.logical_and(j < z, z - j > 1))
                def _():
                    fall(i, h, j).start()

                @pl.when(z - j == 1)
                def _():
                    fall(i, h, OUTER).start()
            else:

                @pl.when(z > 0)
                def _():
                    rise(0, h, z).wait_recv()
                    out_ref[:, part(h)] += rbuf[z, h].astype(F32)

                @pl.when(z < OUTER - 1)
                def _():
                    fall(0, h, OUTER).wait_recv()
                    out_ref[:, part(h)] += rbuf[OUTER, h].astype(F32)

                res_ref[:, part(h)] = (mid_ref[:, part(h)] + out_ref[:, part(h)]).astype(BF16)

    for i, j in enumerate(order):
        for n in range(1, per):
            plane(i, j, n).wait_send()
        if i < OUTER - 1:
            for h in range(halves):
                rise(i, h, j).wait_send()
    for k in range(max(0, tiles - 2), tiles):
        across(k).wait_send()
    for copy in stores(tiles - 1):
        copy.wait()


def combine(y, pos_all, middle, slots, cot_slots, gate_low, up_low, hidden_gated, number):
    outer, per, cap, width = y.shape
    span = pos_all.shape[-1]
    block, hidden = gate_low.shape[1:]
    share = hidden // 2
    step = min(512, width)
    tiles = width // step
    vmem = pl.BlockSpec(memory_space=pltpu.VMEM)
    hbm = pl.BlockSpec(memory_space=pltpu.HBM)
    dma = pltpu.SemaphoreType.DMA
    return pl.pallas_call(
        functools.partial(combine_body, per, cap),
        out_shape=(
            jax.ShapeDtypeStruct((span, width), BF16),
            jax.ShapeDtypeStruct((2, width, share), F32),
            jax.ShapeDtypeStruct((width, share), F32),
        ),
        in_specs=[hbm, vmem, vmem] + [hbm] * 5,
        out_specs=(vmem, hbm, hbm),
        scratch_shapes=[
            pltpu.VMEM((span, width), F32),
            pltpu.VMEM((OUTER, per, cap, width), BF16),
            pltpu.VMEM((OUTER - 1, 2, span, width // 2), BF16),
            pltpu.VMEM((OUTER + 1, 2, span, width // 2), BF16),
            pltpu.VMEM((OUTER, block, 3 * share), BF16),
            pltpu.VMEM((OUTER, block, 3 * share), BF16),
            pltpu.VMEM((OUTER, per, cap, step), BF16),
            pltpu.VMEM((step, OUTER * block), BF16),
            pltpu.VMEM((2, step, 3 * share), BF16),
            pltpu.VMEM((tiles, step, 3 * share), BF16),
            pltpu.VMEM((step, 3 * share), F32),
            dma((OUTER - 1, 2)),
            dma((OUTER + 1, 2)),
            dma((OUTER, per)),
            dma((OUTER, per)),
            dma((OUTER,)),
            dma((3, 2)),
            dma,
            dma((tiles,)),
            dma((tiles,)),
            dma((3,)),
        ],
        compiler_params=pltpu.CompilerParams(
            collective_id=number, has_side_effects=True, vmem_limit_bytes=62 << 20
        ),
        name="combine",
    )(y, pos_all, middle, slots, cot_slots, gate_low, up_low, hidden_gated)


def weights_body(rows, *refs):
    mats, per = len(SOURCE), 4
    x_refs, y_refs, small_ref = refs[:4], refs[4 : 4 + mats], refs[4 + mats]
    out_ref, total_ref, xbuf, ybuf, keep, sbuf, srecv, ubuf, rbuf, hbuf, obuf = refs[5 + mats : 16 + mats]
    lbuf, lsum, lz = refs[16 + mats : 19 + mats]
    xs, ys, yr, ss, sr, zs, zr, fs, fr, ls, lr, ts, tr = refs[19 + mats :]
    e, c = lax.axis_index("expert"), lax.axis_index("dp")
    z, r = e // per, e % per
    x, y = r % 2, r // 2
    width = y_refs[0].shape[1]
    part = width // 4
    lines = width // OUTER
    peers = [(n, f) for n in range(per) for f in range(2)]
    trade = (y + c * (1 - 2 * y)) * 2 + x + (1 - c) * (1 - 2 * x)
    other = (y + (1 - c) * (1 - 2 * y)) * 2 + x + c * (1 - 2 * x)
    a_bit = (1 - c) * x + c * y
    b_bit = (1 - c) * y + c * x
    quarter = 2 * c + a_bit

    def device(n, f):
        return flip(r, n), (c + f) % 2

    bar = pltpu.get_barrier_semaphore()
    for d in range(1, OUTER):
        pl.semaphore_signal(
            bar, inc=1, device_id=((z + d) % OUTER * per + r, c), device_id_type=MESH
        )
    for n, f in peers[1:]:
        q, k = device(n, f)
        pl.semaphore_signal(bar, inc=1, device_id=(z * per + q, k), device_id_type=MESH)
    pl.semaphore_wait(bar, OUTER - 1 + 2 * per - 1)

    def block(q):
        return pl.ds(pl.multiple_of(q * part, part), part)

    targets = (
        (r, 1 - c, 2 * (1 - c) + (1 - c) * y + c * x),
        (trade, c, 2 * c + 1 - a_bit),
        (other, 1 - c, 2 * (1 - c) + 1 - b_bit),
    )

    def spread(m, i):
        q, k, at = targets[i]
        return pltpu.make_async_remote_copy(
            src_ref=y_refs[m].at[:, block(at)], dst_ref=ybuf.at[m, i + 1],
            send_sem=ys.at[m, i], recv_sem=yr.at[m, i],
            device_id=(z * per + q, k), device_id_type=MESH,
        )

    def swap(m, i):
        return pltpu.make_async_remote_copy(
            src_ref=sbuf.at[m, i], dst_ref=srecv.at[m, i], send_sem=ss.at[m, i],
            recv_sem=sr.at[m, i], device_id=(z * per + other, c), device_id_type=MESH,
        )

    def hop(m, i, j, way):
        return pltpu.make_async_remote_copy(
            src_ref=ubuf.at[m, i], dst_ref=rbuf.at[m, way, j],
            send_sem=zs.at[m, i], recv_sem=zr.at[m, way, j],
            device_id=((z + 1 - 2 * way) * per + r, c), device_id_type=MESH,
        )

    def final(m, t, f):
        there = a_bit + t * (1 - 2 * a_bit)
        core = (c + f) % 2
        q = ((1 - c) * y + c * there) * 2 + (1 - c) * there + c * x
        return pltpu.make_async_remote_copy(
            src_ref=hbuf.at[m, pl.ds(pl.multiple_of((there * 2 + core) * rows, rows), rows)],
            dst_ref=obuf.at[m, quarter], send_sem=fs.at[m, 2 * t + f],
            recv_sem=fr.at[m, quarter], device_id=(z * per + q, core), device_id_type=MESH,
        )

    def landed(m, q):
        return pltpu.make_async_remote_copy(
            src_ref=hbuf.at[m, pl.ds(0, rows)], dst_ref=obuf.at[m, q], send_sem=fs.at[m, 0],
            recv_sem=fr.at[m, q], device_id=(z * per + r, 1 - c), device_id_type=MESH,
        )

    def little(i):
        q, k = device(*peers[i])
        return pltpu.make_async_remote_copy(
            src_ref=small_ref.at[q * 2 + k], dst_ref=lbuf.at[i], send_sem=ls.at[i],
            recv_sem=lr.at[i], device_id=(z * per + q, k), device_id_type=MESH,
        )

    def tall(d):
        to = (z + d) % OUTER
        return pltpu.make_async_remote_copy(
            src_ref=lsum.at[to], dst_ref=lz.at[d], send_sem=ts.at[d], recv_sem=tr.at[d],
            device_id=(to * per + r, c), device_id_type=MESH,
        )

    loads = [pltpu.make_async_copy(x_refs[i], xbuf.at[i], xs.at[i]) for i in range(4)]
    def begin(m):
        for i in range(3):
            spread(m, i).start()

    begin(0)
    begin(1)
    for copy in loads:
        copy.start()
    for i in range(1, 2 * per):
        little(i).start()
    lbuf[0] = small_ref[r * 2 + c]
    for m in range(mats):
        ybuf[m, 0] = y_refs[m][:, block(quarter)]
    for copy in loads:
        copy.wait()
    order = [pick(t, z) for t in FAR]

    def pieces(j, bit):
        for t in range(2):
            at = j * lines + (1 - c) * (bit * 2 + t) * 2 * rows + c * (t * 2 + bit) * 2 * rows
            yield pl.ds(pl.multiple_of(at, 2 * rows), 2 * rows)

    def product(m, j, bit):
        total = None
        for i in range(4):
            left = jnp.concatenate([xbuf[i, SOURCE[m], at, :] for at in pieces(j, bit)], axis=0)
            term = jnp.dot(left, ybuf[m, i], preferred_element_type=F32)
            total = term if total is None else total + term
        return total

    edge = jnp.logical_or(z == 0, z == OUTER - 1)

    def outer(m):
        for i, j in enumerate(order):
            swap(m, i).wait_recv()
            ubuf[m, i] = (keep[m, i] + srecv[m, i].astype(F32)).astype(BF16)

            @pl.when(z == 0)
            def _():
                hop(m, i, j, 0).start()

            @pl.when(z > 0)
            def _():
                hop(m, i, j, 1).start()

    def inner(m):
        for i, j in enumerate(order):
            swap(m, i).wait_recv()

            @pl.when(j > z)
            def _():
                hop(m, 0, j, 0).wait_recv()
                ubuf[m, i] = (
                    keep[m, i] + srecv[m, i].astype(F32) + rbuf[m, 0, j].astype(F32)
                ).astype(BF16)
                hop(m, i, j, 0).start()

            @pl.when(j < z)
            def _():
                hop(m, 0, j, 1).wait_recv()
                ubuf[m, i] = (
                    keep[m, i] + srecv[m, i].astype(F32) + rbuf[m, 1, j].astype(F32)
                ).astype(BF16)
                hop(m, i, j, 1).start()

    for m in range(mats + 2):
        if m < mats:
            for i in range(3):
                spread(m, i).wait_recv()
            for i, j in enumerate(order + [z]):
                sbuf[m, i] = product(m, j, 1 - b_bit).astype(BF16)
                swap(m, i).start()
            if m + 2 < mats:
                begin(m + 2)
            for i, j in enumerate(order + [z]):
                keep[m, i] = product(m, j, b_bit)
        if 1 <= m <= mats:
            pl.when(edge)(functools.partial(outer, m - 1))
        if m >= 2:
            pl.when(jnp.logical_not(edge))(functools.partial(inner, m - 2))
        if m == mats - 1:
            for i in range(1, 2 * per):
                little(i).wait_recv()
            lsum[...] = sum(lbuf[i] for i in range(2 * per))
            for d in range(1, OUTER):
                tall(d).start()

    last = OUTER - 1
    for m in range(mats):
        swap(m, last).wait_recv()
        keep[m, last] += srecv[m, last].astype(F32)

        @pl.when(z > 0)
        def _():
            hop(m, 0, z, 0).wait_recv()
            keep[m, last] += rbuf[m, 0, z].astype(F32)

        @pl.when(z < OUTER - 1)
        def _():
            hop(m, 0, z, 1).wait_recv()
            keep[m, last] += rbuf[m, 1, z].astype(F32)

        hbuf[m] = keep[m, last].astype(BF16)
        for t, f in ((1, 0), (1, 1), (0, 1)):
            final(m, t, f).start()

    for d in range(1, OUTER):
        tall(d).wait()
    total_ref[...] = lsum[z] + sum(lz[d] for d in range(1, OUTER))
    for m in range(mats):
        mine = pl.ds(pl.multiple_of((a_bit * 2 + c) * rows, rows), rows)
        out_ref[m, :, block(quarter)] = keep[m, last, mine, :]
        for d in range(1, 4):
            q = (quarter + d) % 4
            landed(m, q).wait_recv()
            out_ref[m, :, block(q)] = obuf[m, q].astype(F32)
    for m in range(mats):
        for i in range(3):
            spread(m, i).wait_send()
        for i in range(OUTER):
            swap(m, i).wait_send()
        for t, f in ((1, 0), (1, 1), (0, 1)):
            final(m, t, f).wait_send()
        for i, j in enumerate(order):
            hop(m, i, j, 0).wait_send()
    for i in range(1, 2 * per):
        little(i).wait_send()


SOURCE = (1, 0, 0, 0)


def weight_grads(lefts, rights, small, experts, number):
    span, width = rights[0].shape
    rows = width // (2 * experts)
    part = width // 4
    half = width // OUTER // 2
    mats = len(rights)
    count = small.shape[-1]
    vmem = pl.BlockSpec(memory_space=pltpu.VMEM)
    dma = pltpu.SemaphoreType.DMA
    return pl.pallas_call(
        functools.partial(weights_body, rows),
        out_shape=(
            jax.ShapeDtypeStruct((mats, rows, width), F32),
            jax.ShapeDtypeStruct((1, count), F32),
        ),
        in_specs=[pl.BlockSpec(memory_space=pltpu.HBM)] * 4 + [vmem] * (mats + 1),
        out_specs=(vmem, vmem),
        scratch_shapes=[
            pltpu.VMEM((4, 2, width, span), BF16),
            pltpu.VMEM((mats, 4, span, part), BF16),
            pltpu.VMEM((mats, OUTER, half, part), F32),
            pltpu.VMEM((mats, OUTER, half, part), BF16),
            pltpu.VMEM((mats, OUTER, half, part), BF16),
            pltpu.VMEM((mats, OUTER - 1, half, part), BF16),
            pltpu.VMEM((mats, 2, OUTER, half, part), BF16),
            pltpu.VMEM((mats, half, part), BF16),
            pltpu.VMEM((mats, 4, rows, part), BF16),
            pltpu.VMEM(small.shape, F32),
            pltpu.VMEM(small.shape[1:], F32),
            pltpu.VMEM(small.shape[1:], F32),
            dma((4,)),
            dma((mats, 3)),
            dma((mats, 3)),
            dma((mats, OUTER)),
            dma((mats, OUTER)),
            dma((mats, OUTER - 1)),
            dma((mats, 2, OUTER)),
            dma((mats, 4)),
            dma((mats, 4)),
            dma((8,)),
            dma((8,)),
            dma((OUTER,)),
            dma((OUTER,)),
        ],
        compiler_params=pltpu.CompilerParams(
            collective_id=number, has_side_effects=True, vmem_limit_bytes=58 << 20
        ),
        name="weight_grads",
    )(*lefts, *rights, small)


def body(
    tokens,
    cotangent,
    lengths,
    routes,
    attention_gain,
    query_gain,
    key_gain,
    feedforward_gain,
    query_weight,
    key_weight,
    value_weight,
    output_weight,
    router_weight,
    expert_gate_up,
    expert_down,
):
    span, width = tokens.shape
    core = lax.axis_index("dp")
    both = ("expert", "dp")
    devices = lax.axis_size("expert") * 2
    gains = jnp.stack([attention_gain, query_gain, key_gain, feedforward_gain]).astype(F32)
    other = lax.ppermute(gains, both, [(d, d ^ 1) for d in range(devices)])
    gains = jnp.where(
        core == 0,
        jnp.concatenate([gains, other], axis=1),
        jnp.concatenate([other, gains], axis=1),
    )
    gain_in, gain_query, gain_key, gain_mid = gains[0], gains[1], gains[2], gains[3]

    def full(part, axis=0):
        return lax.all_gather(part, "dp", axis=axis, tiled=True)

    router_other = lax.ppermute(router_weight, both, [(d, d ^ 1) for d in range(devices)])
    router_full = jnp.where(
        core == 0,
        jnp.concatenate([router_weight, router_other], axis=0),
        jnp.concatenate([router_other, router_weight], axis=0),
    )
    gate_full = full(expert_gate_up[0, 0], 1)
    up_full = full(expert_gate_up[0, 1], 1)
    down_full = full(expert_down[0], 1)
    experts = router_full.shape[1]
    cap = span * TOP // experts
    per = experts // OUTER

    seq_length = lengths[0]
    index_rows = jnp.arange(span, dtype=jnp.int32)
    expert_ids = jnp.arange(experts, dtype=jnp.int32)
    hits = jnp.any(routes[None, :, :] == expert_ids[:, None, None], axis=-1)
    hits = hits & (index_rows < seq_length)[None, :]
    earlier = (index_rows[:, None] < index_rows[None, :]).astype(BF16)
    before = jnp.dot(hits.astype(BF16), earlier, preferred_element_type=F32)
    kept = hits & (before < cap)
    pos = jnp.where(kept, before, -1.0)
    inputs = tokens.astype(F32)
    cosine_table, sine_table = rotary_tables(index_rows.astype(F32))
    signs = jnp.where(jnp.arange(HD) < HD // 2, -1.0, 1.0)
    key_limit = jnp.minimum(index_rows, seq_length - 1)
    (
        cot_slots, pos_here, pos_all, query_full, key_full, value_full, output_full, turned,
        normed_in, query_pre, key_pre, query_rot, key_rot, value_all, log_total, attended,
        middle, normed_mid, gates,
    ) = attend(
        tokens, cotangent, pos[:, None, :], gains, (cosine_table, sine_table * signs),
        key_limit.astype(F32)[:, None], router_full,
        (query_weight, key_weight, value_weight, output_weight), cap, 1,
    )
    norm_in_back = jax.vjp(norm_apply, inputs, gain_in)[1]
    norm_mid_back = jax.vjp(norm_apply, middle, gain_mid)[1]
    query_back, key_back = [
        jax.vjp(
            lambda projected, gain: rotary_norm(projected, gain, cosine_table, sine_table),
            pre, gain,
        )[1]
        for pre, gain in ((query_pre, gain_query), (key_pre, gain_key))
    ]
    query_rot, key_rot, value_heads = [
        value.reshape(span, NH, HD) for value in (query_rot, key_rot, value_all)
    ]
    allowed = index_rows[None, :] <= key_limit[:, None]
    score_scale = HD ** (-0.5)

    def scores_of():
        raw = jnp.einsum("thd,shd->hts", query_rot, key_rot, preferred_element_type=F32)
        return jnp.where(allowed[None], raw * score_scale, -1e30)

    def mul(left, right, spec):
        return jnp.einsum(spec, left, right, preferred_element_type=F32)

    back_rows, prob_grad, slots, gate_grad_low, up_grad_low, hidden_gated, expert_out = run_experts(
        normed_mid, gates.T[:, None, :], pos_all, pos_here, cot_slots,
        gate_full, up_full, down_full, 2,
    )
    prob_grad = prob_grad[:, 0].T
    back_rows, turned = lax.optimization_barrier((back_rows, turned))
    wide = per == 4 and width % 512 == 0
    if wide:

        def moved(d, cross):
            to = d % 2 ^ cross
            return (d // 2 ^ 1 + to) * 2 + to

        lefts = [turned, lax.ppermute(turned, both, [(d, d ^ 1) for d in range(devices)])] + [
            lax.ppermute(turned, both, [(d, moved(d, cross)) for d in range(devices)])
            for cross in range(2)
        ]

    upstream = cotangent.astype(F32)
    logit_grad = (
        gates * (prob_grad - jnp.sum(gates * prob_grad, axis=-1, keepdims=True))
    ).astype(BF16)
    grad_router = mul(normed_mid, logit_grad, "td,te->de")
    mid_normed_grad = mul(logit_grad, router_full, "te,de->td") + back_rows
    mid_input_grad, grad_mid_gain = norm_mid_back(mid_normed_grad)
    middle_grad = upstream + mid_input_grad
    branch_grad = middle_grad.astype(BF16)
    attended_grad = mul(branch_grad, output_full, "to,io->ti").astype(BF16)
    attended_grad = attended_grad.reshape(span, NH, HD)
    weights_full = jnp.exp(scores_of() - log_total)
    weights_grad = mul(attended_grad, value_heads, "thd,shd->hts")
    value_grad = mul(weights_full.astype(BF16), attended_grad, "hts,thd->shd")
    value_grad = value_grad.reshape(span, width).astype(BF16)
    centre = jnp.sum(weights_full * weights_grad, axis=-1, keepdims=True)
    score_grad = (weights_full * (weights_grad - centre)).astype(BF16)
    query_rot_grad = mul(score_grad, key_rot, "hts,shd->thd").reshape(span, width) * score_scale
    key_rot_grad = mul(score_grad, query_rot, "hts,thd->shd").reshape(span, width) * score_scale
    query_pre_grad, grad_query_gain = query_back(query_rot_grad)
    key_pre_grad, grad_key_gain = key_back(key_rot_grad)
    query_low = query_pre_grad.astype(BF16)
    key_low = key_pre_grad.astype(BF16)
    normed_in_grad = mul(query_low, query_full, "to,io->ti")
    normed_in_grad = normed_in_grad + mul(key_low, key_full, "to,io->ti")
    normed_in_grad = normed_in_grad + mul(value_grad, value_full, "to,io->ti")
    input_grad, grad_in_gain = norm_in_back(normed_in_grad)
    grad_tokens = middle_grad + input_grad

    small = jnp.concatenate(
        [
            jnp.stack([grad_in_gain, grad_query_gain, grad_key_gain, grad_mid_gain]).T,
            grad_router,
        ],
        axis=1,
    )
    rights = (branch_grad, value_grad, key_low, query_low)
    if wide:
        expert_out, lefts, rights = lax.optimization_barrier((expert_out, lefts, rights))
    output, grad_gate_up, grad_down = combine(
        expert_out, pos_all, middle, slots, cot_slots, gate_grad_low, up_grad_low, hidden_gated, 4
    )
    if wide:
        kinds = small.shape[1]
        split = small.reshape(OUTER, 2 * per, -1, kinds).transpose(1, 0, 3, 2)
        split = split.reshape(2 * per, OUTER, 1, -1)
        grads, small = weight_grads(lefts, rights, split, experts, 5)
        small = small.reshape(kinds, -1).T
    else:
        small = lax.psum_scatter(small, both, scatter_dimension=0, tiled=True)
        grads = []
        for source, right in zip(SOURCE, rights):
            grad = jnp.dot(turned[source], right, preferred_element_type=F32).astype(BF16)
            grid = grad.reshape(experts, 2, width // experts // 2, width).swapaxes(0, 1)
            half = lax.psum_scatter(grid, "dp", scatter_dimension=0, tiled=False)
            half = lax.psum_scatter(half, "expert", scatter_dimension=0, tiled=False)
            grads.append(half.astype(F32))
    return (
        output,
        grad_tokens,
        small[:, 0],
        small[:, 1],
        small[:, 2],
        small[:, 3],
        grads[3],
        grads[2],
        grads[1],
        grads[0],
        small[:, 4:],
        grad_gate_up[None],
        grad_down[None],
    )


def solution(mesh):
    both = P(("expert", "dp"))
    rows = P(("expert", "dp"), None)
    in_specs = (rows, rows, both, rows) + (P("dp"),) * 4 + (P("dp", None),) * 5 + (
        P("expert", None, None, "dp"),
        P("expert", None, "dp"),
    )
    out_specs = (rows, rows) + (both,) * 4 + (rows,) * 5 + (
        P("expert", None, None, "dp"),
        P("expert", None, "dp"),
    )
    return jax.shard_map(body, mesh=mesh, in_specs=in_specs, out_specs=out_specs, check_vma=False)
```

```python
import functools
import math

import jax
import jax.numpy as jnp
from jax import lax
from jax.experimental import pallas as pl
from jax.experimental.pallas import tpu as pltpu
from jax.sharding import PartitionSpec as P

NH = 16
HD = 128
TOP = 8
OUTER = 4

EPSILON = 1e-05
ROPE_BASE = 10000.0
MESH = pl.DeviceIdType.MESH
F32 = jnp.float32
BF16 = jnp.bfloat16


def rms_scale(values):
    return lax.rsqrt(jnp.mean(values * values, axis=-1, keepdims=True) + EPSILON)


def norm_apply(values, gain_vector):
    return values * rms_scale(values) * gain_vector


def rotary_tables(positions):
    frequencies = 1.0 / ROPE_BASE ** (jnp.arange(0, HD, 2).astype(F32) / HD)
    angles = positions[:, None] * frequencies[None, :]
    angles = jnp.concatenate([angles, angles], axis=-1)
    return (jnp.cos(angles), jnp.sin(angles))


def rotary_norm(projected, gain_vector, cosine_table, sine_table):
    normed = projected * rms_scale(projected) * gain_vector
    shaped = normed.reshape(normed.shape[0], NH, HD)
    half_width = HD // 2
    turned = jnp.concatenate([-shaped[..., half_width:], shaped[..., :half_width]], axis=-1)
    rotated = shaped * cosine_table[:, None, :] + turned * sine_table[:, None, :]
    return rotated.reshape(normed.shape[0], NH * HD)


def flip(r, n):
    out, bit = r, 1
    while bit <= n:
        if n & bit:
            out = out + bit - 2 * bit * ((r // bit) % 2)
        bit *= 2
    return out


def pick(table, z):
    code = sum(v * 4**k for k, v in enumerate(table))
    return (code // ((1 + 3 * (z % 2)) * (1 + 15 * (z // 2)))) % 4


NEAR = ((1, 0, 1, 2), (2, 2, 3, 1), (3, 3, 0, 0))
PLACE = ((1, 3, 3, 1), (3, 1, 2, 3), (2, 2, 1, 2))
BLOCK = ((1, 3, 0, 2), (3, 0, 3, 0), (2, 2, 1, 1))
FAR = ((3, 3, 0, 0), (2, 0, 3, 1), (1, 2, 1, 2))


def one_hot(pos_ref, r, j, per, cap):
    span = pos_ref.shape[-1]
    rows = []
    slot = lax.broadcasted_iota(jnp.int32, (cap, span), 0).astype(F32)
    for n in range(per):
        line = pos_ref[j, flip(r, n)]
        rows.append(jnp.where(line == slot, 1.0, 0.0).astype(BF16))
    return jnp.concatenate(rows, axis=0)


def attend_body(per, cap, *refs):
    tok_ref, x_ref, meta_ref, gains_ref, cos_ref, sin_ref, limit_ref, router_ref = refs[:8]
    parts, refs = refs[8:14], refs[14:]
    out_ref, here_ref, pos_ref = refs[:3]
    fulls, refs = refs[3:9], refs[9:]
    turned_ref, nin_ref, qpre, kpre, qrot, krot, val_ref, lse_ref, att_ref, mid_ref = refs[:10]
    nmid_ref, gates_ref, zbuf, sbuf, wbuf, vacc = refs[10:16]
    zs, zr, ps, pr, ls, ms, mr, ts, tr, ds, dr, ks, fs = refs[16:]
    e, c = lax.axis_index("expert"), lax.axis_index("dp")
    z, r = e // per, e % per
    experts = OUTER * per
    bar = pltpu.get_barrier_semaphore()
    for d in range(1, experts):
        pl.semaphore_signal(bar, inc=1, device_id=((e + d) % experts, c), device_id_type=MESH)
    pl.semaphore_signal(bar, inc=1, device_id=(e, 1 - c), device_id_type=MESH)
    pl.semaphore_wait(bar, experts)
    span, width = x_ref.shape
    step = min(512, width)
    half = width // 2

    def share(d):
        to = (e + d) % experts
        return pltpu.make_async_remote_copy(
            src_ref=meta_ref.at[to], dst_ref=here_ref.at[e], send_sem=ms.at[d - 1],
            recv_sem=mr.at[d - 1], device_id=(to, c), device_id_type=MESH,
        )

    def table(d):
        to = (z + d) % OUTER
        return pltpu.make_async_remote_copy(
            src_ref=meta_ref.at[pl.ds(to * per, per)], dst_ref=pos_ref.at[z],
            send_sem=ts.at[d - 1], recv_sem=tr.at[z],
            device_id=(to * per + r, c), device_id_type=MESH,
        )

    def tabled(j):
        return pltpu.make_async_remote_copy(
            src_ref=meta_ref.at[pl.ds(0, per)], dst_ref=pos_ref.at[j], send_sem=ts.at[0],
            recv_sem=tr.at[j], device_id=(j * per + r, c), device_id_type=MESH,
        )

    def up(src, j):
        return pltpu.make_async_remote_copy(
            src_ref=src, dst_ref=zbuf.at[j], send_sem=zs.at[0, j], recv_sem=zr.at[j],
            device_id=((z + 1) * per + r, c), device_id_type=MESH,
        )

    def down(src, j):
        return pltpu.make_async_remote_copy(
            src_ref=src, dst_ref=zbuf.at[j], send_sem=zs.at[1, j], recv_sem=zr.at[j],
            device_id=((z - 1) * per + r, c), device_id_type=MESH,
        )

    def plane(i, j, n):
        return pltpu.make_async_remote_copy(
            src_ref=sbuf.at[i, n], dst_ref=out_ref.at[j, n], send_sem=ps.at[i, n],
            recv_sem=pr.at[i, n], device_id=(z * per + flip(r, n), c), device_id_type=MESH,
        )

    def local(i, j):
        return pltpu.make_async_copy(sbuf.at[i, 0], out_ref.at[j, 0], ls.at[i])

    def lines(owner):
        return pl.ds(pl.multiple_of(owner * half, half), half)

    def give(k):
        return pltpu.make_async_remote_copy(
            src_ref=parts[k], dst_ref=fulls[k].at[lines(c)] if k < 4 else fulls[k], send_sem=ds.at[k],
            recv_sem=dr.at[k], device_id=(e, 1 - c), device_id_type=MESH,
        )

    def hold(t):
        return pltpu.make_async_copy(wbuf.at[t % 2], fulls[jobs[t][0]].at[lines(c)], ks.at[t % 2])

    jobs = [(0, 0), (1, 0), (2, 0), (0, 1), (1, 1), (2, 1), (3, 0), (3, 1)]

    def fetch(t):
        k, far = jobs[t]
        src = fulls[k].at[lines(1 - c)] if far else parts[k]
        return pltpu.make_async_copy(src, wbuf.at[t % 2], fs.at[t % 2])

    def project(t):
        k, far = jobs[t]
        left = att_ref if k == 3 else nin_ref
        into = (qpre, kpre, vacc, mid_ref)[k]
        fetch(t).wait()
        if not far:
            hold(t).start()
        mine = lines(1 - c if far else c)

        @pl.loop(0, width // step)
        def _(q):
            columns = pl.ds(pl.multiple_of(q * step, step), step)
            got = jnp.dot(left[:, mine], wbuf[t % 2, :, columns], preferred_element_type=F32)
            if k == 3 and not far:
                into[:, columns] = tok_ref[:, columns].astype(F32) + got
            elif far:
                into[:, columns] += got
            else:
                into[:, columns] = got

        if not far:
            hold(t).wait()
        if t + 2 < len(jobs):
            if jobs[t + 2][1]:
                give(jobs[t + 2][0]).wait_recv()
            fetch(t + 2).start()

    order = [z] + [pick(t, z) for t in NEAR]

    edge = jnp.logical_or(z == 0, z == OUTER - 1)

    def relay(places):
        @pl.when(jnp.logical_not(edge))
        def _():
            for i in places:
                j = order[i]
                up(x_ref, j).wait_recv()

                @pl.when(j < z)
                def _():
                    up(zbuf.at[j], j).start()

                @pl.when(j > z)
                def _():
                    down(zbuf.at[j], j).start()

    def choose(i, j):
        block = x_ref if i == 0 else zbuf.at[j]
        if i > 0:

            @pl.when(edge)
            def _():
                up(x_ref, j).wait_recv()

            tabled(j).wait_recv()

        marks = one_hot(pos_ref, r, j, per, cap)

        @pl.loop(0, width // step)
        def _(k):
            columns = pl.ds(pl.multiple_of(k * step, step), step)
            got = jnp.dot(marks, block[:, columns], preferred_element_type=F32).astype(BF16)
            for n in range(per):
                sbuf[i, n, :, columns] = got[n * cap : (n + 1) * cap]

        for n in range(1, per):
            plane(i, j, n).start()
        local(i, j).start()

    for d in range(1, OUTER):
        table(d).start()

    @pl.when(z < OUTER - 1)
    def _():
        up(x_ref, z).start()

    @pl.when(z > 0)
    def _():
        down(x_ref, z).start()

    fetch(0).start()
    fetch(1).start()
    pos_ref[z] = meta_ref[pl.ds(z * per, per)]
    here_ref[e] = meta_ref[e]
    choose(0, z)
    for k in range(6):
        give(k).start()
    for d in range(1, experts):
        share(d).start()

    inputs = tok_ref[...].astype(F32)
    nin_ref[...] = norm_apply(inputs, gains_ref[0:1]).astype(BF16)
    for t in range(6):
        project(t)
    val_ref[...] = vacc[...].astype(BF16)
    query_scale = rms_scale(qpre[...])
    key_scale = rms_scale(kpre[...])
    relay((1, 2))
    choose(1, order[1])
    turned_ref[0] = nin_ref[...].T
    score_scale = HD ** (-0.5)
    column = lax.broadcasted_iota(jnp.int32, (span, span), 1).astype(F32)

    def heads(first, last):
        @pl.loop(first, last)
        def _(h):
            columns = pl.ds(pl.multiple_of(h * HD, HD), HD)

            def turn(pre, scale, row):
                normed = pre[:, columns] * scale * gains_ref[row : row + 1, columns]
                return (
                    normed * cos_ref[...] + pltpu.roll(normed, HD // 2, 1) * sin_ref[...]
                ).astype(BF16)

            query = turn(qpre, query_scale, 1)
            key = turn(kpre, key_scale, 2)
            qrot[:, columns] = query
            krot[:, columns] = key
            scores = lax.dot_general(
                query, key, (((1,), (1,)), ((), ())), preferred_element_type=F32
            )
            scores = jnp.where(column <= limit_ref[...], scores * score_scale, -1e30)
            peak = jnp.max(scores, axis=-1, keepdims=True)
            total = peak + jnp.log(jnp.sum(jnp.exp(scores - peak), axis=-1, keepdims=True))
            lse_ref[h] = total
            weights = jnp.exp(scores - total).astype(BF16)
            att_ref[:, columns] = jnp.dot(
                weights, val_ref[:, columns], preferred_element_type=F32
            ).astype(BF16)

    heads(0, NH // 2)
    choose(2, order[2])
    relay((3,))
    heads(NH // 2, NH)
    project(6)
    choose(3, order[3])
    project(7)
    turned_ref[1] = att_ref[...].T
    middle = mid_ref[...]
    nmid_ref[...] = norm_apply(middle, gains_ref[3:4]).astype(BF16)
    logits = jnp.dot(nmid_ref[...], router_ref[...], preferred_element_type=F32)
    raised = jnp.exp(logits - jnp.max(logits, axis=-1, keepdims=True))
    gates_ref[...] = raised / jnp.sum(raised, axis=-1, keepdims=True)

    for i, j in enumerate(order):
        local(i, j).wait()
        for n in range(1, per):
            plane(i, j, n).wait()

    @pl.when(z < OUTER - 1)
    def _():
        up(x_ref, z).wait_send()

    @pl.when(z > 0)
    def _():
        down(x_ref, z).wait_send()

    for j in order[1:]:

        @pl.when(jnp.logical_and(j < z, z < OUTER - 1))
        def _():
            up(zbuf.at[j], j).wait_send()

        @pl.when(jnp.logical_and(j > z, z > 0))
        def _():
            down(zbuf.at[j], j).wait_send()

    for d in range(1, experts):
        share(d).wait()
    for d in range(1, OUTER):
        table(d).wait_send()
    for k in range(6):
        give(k).wait_send()
    for k in range(4, 6):
        give(k).wait_recv()


def attend(tokens, cotangent, meta, gains, tables, limit, router, parts, cap, number):
    experts, _, span = meta.shape
    per = experts // OUTER
    width = tokens.shape[1]
    half = parts[0].shape[0]
    vmem = pl.BlockSpec(memory_space=pltpu.VMEM)
    hbm = pl.BlockSpec(memory_space=pltpu.HBM)
    dma = pltpu.SemaphoreType.DMA
    low = jax.ShapeDtypeStruct((span, width), BF16)
    high = jax.ShapeDtypeStruct((span, width), F32)
    return pl.pallas_call(
        functools.partial(attend_body, per, cap),
        out_shape=(
            jax.ShapeDtypeStruct((OUTER, per, cap, width), BF16),
            jax.ShapeDtypeStruct((experts, 1, span), F32),
            jax.ShapeDtypeStruct((OUTER, per, 1, span), F32),
        )
        + (jax.ShapeDtypeStruct((2 * half, width), BF16),) * 4
        + tuple(jax.ShapeDtypeStruct(part.shape, BF16) for part in parts[4:])
        + (jax.ShapeDtypeStruct((2, width, span), BF16), low, high, high, low, low, low)
        + (jax.ShapeDtypeStruct((NH, span, 1), F32), low, high, low)
        + (jax.ShapeDtypeStruct((span, experts), F32),),
        in_specs=[vmem] * 8 + [hbm] * 6,
        out_specs=(hbm, vmem, vmem) + (hbm,) * 6 + (vmem,) * 12,
        scratch_shapes=[
            pltpu.VMEM((OUTER, span, width), BF16),
            pltpu.VMEM((OUTER, per, cap, width), BF16),
            pltpu.VMEM((2, half, width), BF16),
            pltpu.VMEM((span, width), F32),
            dma((2, OUTER)),
            dma((OUTER,)),
            dma((OUTER, per)),
            dma((OUTER, per)),
            dma((OUTER,)),
            dma((experts,)),
            dma((experts,)),
            dma((OUTER,)),
            dma((OUTER,)),
            dma((6,)),
            dma((6,)),
            dma((2,)),
            dma((2,)),
        ],
        compiler_params=pltpu.CompilerParams(
            collective_id=number, has_side_effects=True, vmem_limit_bytes=60 << 20
        ),
        name="attend",
    )(tokens, cotangent, meta, gains, *tables, limit, router, *parts)


def experts_body(per, cap, *refs):
    x_ref, gates_ref, pos_ref, posh_ref, cot_ref, gu_mine, dn_mine, gu_other, dn_other = refs[:9]
    refs = refs[1:]
    back_ref, pg_ref, out_ref, gl_ref, ul_ref, hg_ref, eo_ref = refs[8:15]
    zbuf, sbuf, wg, wu, wd, slb, ctb, glb, ulb, hlb, hgb, eob, ybuf, ubuf, rbuf = refs[15:30]
    here, ggv, sgv, tgv = refs[30:34]
    zs, zr, ps, pr, ls, ms, mr, ws, cs, os, es, bs, br, us, ur, gs, gr = refs[34:]
    e, c = lax.axis_index("expert"), lax.axis_index("dp")
    z, r = e // per, e % per
    experts = OUTER * per
    bar = pltpu.get_barrier_semaphore()
    for d in range(1, experts):
        pl.semaphore_signal(bar, inc=1, device_id=((e + d) % experts, c), device_id_type=MESH)
    pl.semaphore_wait(bar, experts - 1)
    span, width = x_ref.shape
    hidden = wg.shape[1]
    step = min(512, width)
    thin = min(256, hidden)
    halves = 2
    half = width // halves

    def share(d):
        to = (e + d) % experts
        return pltpu.make_async_remote_copy(
            src_ref=gates_ref.at[to], dst_ref=here.at[e], send_sem=ms.at[d - 1],
            recv_sem=mr.at[d - 1], device_id=(to, c), device_id_type=MESH,
        )

    def up(src, j):
        return pltpu.make_async_remote_copy(
            src_ref=src, dst_ref=zbuf.at[j], send_sem=zs.at[0, j], recv_sem=zr.at[j],
            device_id=((z + 1) * per + r, c), device_id_type=MESH,
        )

    def down(src, j):
        return pltpu.make_async_remote_copy(
            src_ref=src, dst_ref=zbuf.at[j], send_sem=zs.at[1, j], recv_sem=zr.at[j],
            device_id=((z - 1) * per + r, c), device_id_type=MESH,
        )

    def plane(i, j, n):
        return pltpu.make_async_remote_copy(
            src_ref=sbuf.at[i, n], dst_ref=out_ref.at[j, n], send_sem=ps.at[i, n],
            recv_sem=pr.at[i, n], device_id=(z * per + flip(r, n), c), device_id_type=MESH,
        )

    def local(i, j):
        return pltpu.make_async_copy(sbuf.at[i, 0], out_ref.at[j, 0], ls.at[i])

    def returned(i, n):
        return pltpu.make_async_remote_copy(
            src_ref=sbuf.at[i, n], dst_ref=ybuf.at[i, n - 1], send_sem=bs.at[i, n],
            recv_sem=br.at[i, n], device_id=(z * per + flip(r, n), c), device_id_type=MESH,
        )

    def part(h):
        return pl.ds(h * half, half)

    def rise(i, j, h, slot):
        return pltpu.make_async_remote_copy(
            src_ref=ubuf.at[i, h], dst_ref=rbuf.at[slot, h], send_sem=us.at[i, h],
            recv_sem=ur.at[slot, h], device_id=((z + 1) * per + r, c), device_id_type=MESH,
        )

    def fall(i, j, h, slot):
        return pltpu.make_async_remote_copy(
            src_ref=ubuf.at[i, h], dst_ref=rbuf.at[slot, h], send_sem=us.at[i, h],
            recv_sem=ur.at[slot, h], device_id=((z - 1) * per + r, c), device_id_type=MESH,
        )

    def graded(i, n, seq):
        return pltpu.make_async_remote_copy(
            src_ref=tgv.at[i, n], dst_ref=pg_ref.at[e], send_sem=gs.at[i, n],
            recv_sem=gr.at[e], device_id=(seq, c), device_id_type=MESH,
        )

    def grade(s):
        return pltpu.make_async_remote_copy(
            src_ref=tgv.at[0, 0], dst_ref=pg_ref.at[s], send_sem=gs.at[0, 0],
            recv_sem=gr.at[s], device_id=(s, c), device_id_type=MESH,
        )

    def columns_of(owner):
        return pl.ds(pl.multiple_of(owner * (hidden // 2), hidden // 2), hidden // 2)

    weights = [
        pltpu.make_async_copy(src, dst.at[:, columns_of(owner)], ws.at[k, f])
        for f, (owner, both, down_part) in enumerate(
            ((c, gu_mine, dn_mine), (1 - c, gu_other, dn_other))
        )
        for k, (src, dst) in enumerate(
            ((both.at[0, 0], wg), (both.at[0, 1], wu), (down_part.at[0], wd))
        )
    ]

    def pull(j):
        return pltpu.make_async_copy(cot_ref.at[j], ctb, cs)

    for d in range(1, experts):
        share(d).start()

    @pl.when(z < OUTER - 1)
    def _():
        up(x_ref, z).start()

    @pl.when(z > 0)
    def _():
        down(x_ref, z).start()

    here[e] = gates_ref[e]
    order = [z] + [pick(t, z) for t in NEAR]

    edge = jnp.logical_or(z == 0, z == OUTER - 1)

    def relay(places):
        @pl.when(jnp.logical_not(edge))
        def _():
            for i in places:
                j = order[i]
                up(x_ref, j).wait_recv()

                @pl.when(j < z)
                def _():
                    up(zbuf.at[j], j).start()

                @pl.when(j > z)
                def _():
                    down(zbuf.at[j], j).start()

    def choose(i, j):
        block = x_ref if i == 0 else zbuf.at[j]
        if i > 0:

            @pl.when(edge)
            def _():
                up(x_ref, j).wait_recv()

        marks = one_hot(pos_ref, r, j, per, cap)

        @pl.loop(0, width // step)
        def _(k):
            columns = pl.ds(pl.multiple_of(k * step, step), step)
            got = jnp.dot(marks, block[:, columns], preferred_element_type=F32).astype(BF16)
            for n in range(per):
                sbuf[i, n, :, columns] = got[n * cap : (n + 1) * cap]

        for n in range(1, per):
            plane(i, j, n).start()
        local(i, j).start()

    def outs(j):
        return [
            pltpu.make_async_copy(src, dst.at[j], os.at[k])
            for k, (src, dst) in enumerate(((glb, gl_ref), (ulb, ul_ref), (hgb, hg_ref)))
        ]

    def away(j):
        return pltpu.make_async_copy(eob, eo_ref.at[j], es)

    def marked(j, n):
        slot = lax.broadcasted_iota(jnp.int32, (cap, span), 0).astype(F32)
        return posh_ref[j * per + flip(r, n)] == slot

    def expert(i, j):
        for n in range(1, per):
            plane(i, j, n).wait()
        local(i, j).wait()
        if i == OUTER - 1:
            send_back(1)
        fetch = pltpu.make_async_copy(out_ref.at[j], slb, ls.at[OUTER])
        fetch.start()
        slot_gate = jnp.concatenate(
            [
                jnp.sum(
                    jnp.where(marked(j, n), here[j * per + flip(r, n)], 0.0), axis=1, keepdims=True
                )
                for n in range(per)
            ],
            axis=0,
        )
        sgv[i % 2] = slot_gate
        ggv[i % 2] = jnp.zeros(ggv.shape[1:], F32)
        pull(j).wait()
        fetch.wait()
        if i > 0:
            for copy in outs(order[i - 1]):
                copy.wait()

        @pl.loop(0, hidden // thin)
        def _(k):
            columns = pl.ds(pl.multiple_of(k * thin, thin), thin)
            rows = slb[...].reshape(per * cap, width)
            gate_pre = jnp.dot(rows, wg[:, columns], preferred_element_type=F32)
            up_pre = jnp.dot(rows, wu[:, columns], preferred_element_type=F32)
            pulled = jnp.dot(
                ctb[...].reshape(per * cap, width), wd[:, columns], preferred_element_type=F32
            )
            sigmoid_gate = jax.nn.sigmoid(gate_pre)
            silu_gate = gate_pre * sigmoid_gate
            low = (silu_gate * up_pre).astype(BF16)
            wide = low.astype(F32)
            ggv[i % 2] += jnp.sum(wide * pulled, axis=1, keepdims=True)
            hidden_grad = pulled * slot_gate
            glb[:, columns] = (
                hidden_grad * up_pre * sigmoid_gate * (1.0 + gate_pre * (1.0 - sigmoid_gate))
            ).astype(BF16)
            ulb[:, columns] = (hidden_grad * silu_gate).astype(BF16)
            hlb[i % 2, :, columns] = low
            hgb[:, columns] = (wide * slot_gate).astype(BF16)

        if i < OUTER - 1:
            pull(order[i + 1]).start()
        for copy in outs(j):
            copy.start()

        @pl.loop(0, width // step)
        def _(k):
            columns = pl.ds(pl.multiple_of(k * step, step), step)
            got = lax.dot_general(
                glb[...], wg[columns, :], (((1,), (1,)), ((), ())), preferred_element_type=F32
            ) + lax.dot_general(
                ulb[...], wu[columns, :], (((1,), (1,)), ((), ())), preferred_element_type=F32
            )
            got = got.astype(BF16)
            for n in range(per):
                sbuf[i, n, :, columns] = got[n * cap : (n + 1) * cap]

    def send_back(i):
        for n in range(1, per):
            returned(i, n).start()

    def finish(i, j):
        for n in range(per):
            seq = j * per + flip(r, n)
            row = jnp.sum(
                jnp.where(marked(j, n), ggv[i % 2, n * cap : (n + 1) * cap], 0.0),
                axis=0,
                keepdims=True,
            )
            tgv[i, n] = row
            if i == 0 and n == 0:
                pg_ref[e] = row
            else:
                graded(i, n, seq).start()
        if i > 0:
            away(order[i - 1]).wait()

        @pl.loop(0, width // step)
        def _(k):
            columns = pl.ds(pl.multiple_of(k * step, step), step)
            got = lax.dot_general(
                hlb[i % 2], wd[columns, :], (((1,), (1,)), ((), ())), preferred_element_type=F32
            )
            got = (got * sgv[i % 2]).astype(BF16)
            for n in range(per):
                eob[n, :, columns] = got[n * cap : (n + 1) * cap]

        away(j).start()

    choose(0, z)
    for copy in weights:
        copy.start()
    pull(z).start()
    relay((1, 2))
    choose(1, order[1])
    for copy in weights:
        copy.wait()
    for d in range(1, experts):
        share(d).wait()
    last = OUTER - 1
    for i in range(last):
        expert(i, order[i])
        if i + 2 <= last:
            choose(i + 2, order[i + 2])
            if i == 0:
                relay((3,))
            finish(i, order[i])
    expert(last, order[last])
    for i in (last, last - 1, 0):
        send_back(i)
    finish(last - 1, order[last - 1])

    def fold(i, j, h):
        marks = one_hot(pos_ref, r, j, per, cap)

        @pl.loop(0, half // step)
        def _(k):
            columns = pl.ds(pl.multiple_of(h * half + k * step, step), step)
            rows = jnp.concatenate(
                [ybuf[i, n - 1, :, columns] if n else sbuf[i, 0, :, columns] for n in range(per)],
                axis=0,
            )
            back_ref[:, columns] = lax.dot_general(
                marks, rows, (((0,), (0,)), ((), ())), preferred_element_type=F32
            )

    for p in range(last):
        i, j = pick(PLACE[p], z), pick(BLOCK[p], z)
        for n in range(1, per):
            returned(i, n).wait_recv()
        for h in range(halves):
            fold(i, j, h)

            @pl.when(jnp.logical_and(j > z, z > 0))
            def _():
                rise(0, j, h, j).wait_recv()
                back_ref[:, part(h)] += rbuf[j, h].astype(F32)

            @pl.when(jnp.logical_and(j < z, z < OUTER - 1))
            def _():
                fall(0, j, h, j).wait_recv()
                back_ref[:, part(h)] += rbuf[j, h].astype(F32)

            ubuf[p, h] = back_ref[:, part(h)].astype(BF16)

            @pl.when(j > z)
            def _():
                rise(p, j, h, j).start()

            @pl.when(jnp.logical_and(j < z, z - j > 1))
            def _():
                fall(p, j, h, j).start()

            @pl.when(z - j == 1)
            def _():
                fall(p, j, h, OUTER).start()

        if p == 0:
            finish(last, order[last])

    for n in range(1, per):
        returned(0, n).wait_recv()
    for h in range(halves):
        fold(0, z, h)

        @pl.when(z > 0)
        def _():
            rise(0, z, h, z).wait_recv()
            back_ref[:, part(h)] += rbuf[z, h].astype(F32)

        @pl.when(z < OUTER - 1)
        def _():
            fall(0, z, h, OUTER).wait_recv()
            back_ref[:, part(h)] += rbuf[OUTER, h].astype(F32)

    @pl.when(z < OUTER - 1)
    def _():
        up(x_ref, z).wait_send()

    @pl.when(z > 0)
    def _():
        down(x_ref, z).wait_send()

    for i, j in enumerate(order):
        for n in range(1, per):
            returned(i, n).wait_send()
        if i > 0:

            @pl.when(jnp.logical_and(j < z, z < OUTER - 1))
            def _():
                up(zbuf.at[j], j).wait_send()

            @pl.when(jnp.logical_and(j > z, z > 0))
            def _():
                down(zbuf.at[j], j).wait_send()

            for h in range(halves):
                rise(i - 1, j, h, j).wait_send()
        for n in range(per):
            if i or n:
                graded(i, n, j * per + flip(r, n)).wait_send()
    for d in range(1, experts):
        grade((e + d) % experts).wait_recv()
    for copy in outs(order[last]):
        copy.wait()
    away(order[last]).wait()


def run_experts(x, gates, pos, pos_here, cot_slots, weights, number):
    experts, _, span = gates.shape
    outer, per, cap, width = cot_slots.shape
    hidden = 2 * weights[0].shape[-1]
    block = per * cap
    vmem = pl.BlockSpec(memory_space=pltpu.VMEM)
    hbm = pl.BlockSpec(memory_space=pltpu.HBM)
    dma = pltpu.SemaphoreType.DMA
    rows = jax.ShapeDtypeStruct((OUTER, per, cap, width), BF16)
    thin = jax.ShapeDtypeStruct((OUTER, block, hidden), BF16)
    return pl.pallas_call(
        functools.partial(experts_body, per, cap),
        out_shape=(
            jax.ShapeDtypeStruct((span, width), F32),
            jax.ShapeDtypeStruct((experts, 1, span), F32),
            rows, thin, thin, thin, rows,
        ),
        in_specs=[vmem] * 4 + [hbm] * 5,
        out_specs=(vmem, vmem) + (hbm,) * 5,
        scratch_shapes=[
            pltpu.VMEM((OUTER, span, width), BF16),
            pltpu.VMEM((OUTER, per, cap, width), BF16),
            pltpu.VMEM((width, hidden), BF16),
            pltpu.VMEM((width, hidden), BF16),
            pltpu.VMEM((width, hidden), BF16),
            pltpu.VMEM((per, cap, width), BF16),
            pltpu.VMEM((per, cap, width), BF16),
            pltpu.VMEM((block, hidden), BF16),
            pltpu.VMEM((block, hidden), BF16),
            pltpu.VMEM((2, block, hidden), BF16),
            pltpu.VMEM((block, hidden), BF16),
            pltpu.VMEM((per, cap, width), BF16),
            pltpu.VMEM((OUTER, per - 1, cap, width), BF16),
            pltpu.VMEM((OUTER - 1, 2, span, width // 2), BF16),
            pltpu.VMEM((OUTER + 1, 2, span, width // 2), BF16),
            pltpu.VMEM((experts, 1, span), F32),
            pltpu.VMEM((2, block, 1), F32),
            pltpu.VMEM((2, block, 1), F32),
            pltpu.VMEM((OUTER, per, 1, span), F32),
            dma((2, OUTER)),
            dma((OUTER,)),
            dma((OUTER, per)),
            dma((OUTER, per)),
            dma((OUTER + 1,)),
            dma((experts,)),
            dma((experts,)),
            dma((3, 2)),
            dma,
            dma((3,)),
            dma,
            dma((OUTER, per)),
            dma((OUTER, per)),
            dma((OUTER - 1, 2)),
            dma((OUTER + 1, 2)),
            dma((OUTER, per)),
            dma((experts,)),
        ],
        compiler_params=pltpu.CompilerParams(
            collective_id=number, has_side_effects=True, vmem_limit_bytes=62 << 20
        ),
        name="experts",
    )(x, gates, pos, pos_here, cot_slots, *weights)


def combine_body(per, cap, *refs):
    y_ref, pos_ref, mid_ref, small_ref, slots_ref, cot_ref, gl_ref, ul_ref, hg_ref = refs[:9]
    res_ref, total_ref, gu_ref, dn_ref, out_ref, ybuf, ubuf, rbuf = refs[9:17]
    theirs, ours, lbuf, lturn, tbuf, rx, stage, lall, lsum, lz = refs[17:27]
    zs, zr, ps, pr, ls, rs, ws, ds, dr, gs, las, lar, tas, tar = refs[27:]
    e, c = lax.axis_index("expert"), lax.axis_index("dp")
    z, r = e // per, e % per
    bar = pltpu.get_barrier_semaphore()
    for d in range(1, OUTER):
        pl.semaphore_signal(
            bar, inc=1, device_id=((z + d) % OUTER * per + r, c), device_id_type=MESH
        )
    peers = [(n, f) for n in range(per) for f in range(2)]

    def device(n, f):
        return flip(r, n), (c + f) % 2

    for n, f in peers[1:]:
        q, k = device(n, f)
        pl.semaphore_signal(bar, inc=1, device_id=(z * per + q, k), device_id_type=MESH)
    pl.semaphore_wait(bar, OUTER - 1 + 2 * per - 1)
    span, width = out_ref.shape
    step = min(512, width)
    share = dn_ref.shape[1]
    thin = min(256, share)
    total = OUTER * per * cap

    def plane(i, j, n):
        return pltpu.make_async_remote_copy(
            src_ref=y_ref.at[j, n], dst_ref=ybuf.at[i, n], send_sem=ps.at[i, n],
            recv_sem=pr.at[i, n], device_id=(z * per + flip(r, n), c), device_id_type=MESH,
        )

    def local(i, j):
        return pltpu.make_async_copy(y_ref.at[j, 0], ybuf.at[i, 0], ls.at[i])

    halves = 2
    half = width // halves

    def part(h):
        return pl.ds(h * half, half)

    def rise(i, h, slot):
        return pltpu.make_async_remote_copy(
            src_ref=ubuf.at[i, h], dst_ref=rbuf.at[slot, h], send_sem=zs.at[i, h],
            recv_sem=zr.at[slot, h], device_id=((z + 1) * per + r, c), device_id_type=MESH,
        )

    def fall(i, h, slot):
        return pltpu.make_async_remote_copy(
            src_ref=ubuf.at[i, h], dst_ref=rbuf.at[slot, h], send_sem=zs.at[i, h],
            recv_sem=zr.at[slot, h], device_id=((z - 1) * per + r, c), device_id_type=MESH,
        )

    def rights(k, src, other):
        owner = 1 - c if other else c
        return pltpu.make_async_copy(
            src.at[:, :, pl.ds(pl.multiple_of(owner * share, share), share)],
            (theirs if other else ours).at[:, :, pl.ds(k * share, share)],
            rs.at[k, int(other)],
        )

    def across(k):
        return pltpu.make_async_remote_copy(
            src_ref=tbuf.at[k % 2], dst_ref=rx.at[k], send_sem=ds.at[k], recv_sem=dr.at[k],
            device_id=(e, 1 - c), device_id_type=MESH,
        )

    def stores(k):
        lines = pl.ds(k * step, step)
        return [
            pltpu.make_async_copy(
                stage.at[:, pl.ds(m * share, share)],
                dn_ref.at[lines] if m == 2 else gu_ref.at[m, lines],
                gs.at[m],
            )
            for m in range(3)
        ]

    def little(i):
        q, k = device(*peers[i])
        return pltpu.make_async_remote_copy(
            src_ref=small_ref.at[q * 2 + k], dst_ref=lall.at[i], send_sem=las.at[i],
            recv_sem=lar.at[i], device_id=(z * per + q, k), device_id_type=MESH,
        )

    def tall(d):
        to = (z + d) % OUTER
        return pltpu.make_async_remote_copy(
            src_ref=lsum.at[to], dst_ref=lz.at[d], send_sem=tas.at[d], recv_sem=tar.at[d],
            device_id=(to * per + r, c), device_id_type=MESH,
        )

    sources = (gl_ref, ul_ref, hg_ref)
    loads = [rights(k, src, other) for k, src in enumerate(sources) for other in (True, False)]

    def tile(k):
        if k == 0:
            for copy in loads:
                copy.wait()
        if k >= 2:
            across(k - 2).wait_send()
        if k >= 1:
            for copy in stores(k - 1):
                copy.wait()
        for src, first, count in ((slots_ref, 0, 2), (cot_ref, 2, 1)):
            fetch = pltpu.make_async_copy(
                src.at[:, :, :, pl.ds(k * step, step)], lbuf, ws
            )
            fetch.start()
            fetch.wait()
            lturn[...] = lbuf[...].reshape(total, step).T

            @pl.loop(0, count * share // thin)
            def _(q):
                at = pl.ds(pl.multiple_of(first * share + q * thin, thin), thin)
                tbuf[k % 2, :, at] = jnp.dot(
                    lturn[...], theirs[:, :, at].reshape(total, thin), preferred_element_type=F32
                ).astype(BF16)
                stage[:, at] = jnp.dot(
                    lturn[...], ours[:, :, at].reshape(total, thin), preferred_element_type=F32
                )

        across(k).start()
        across(k).wait_recv()
        stage[...] += rx[k].astype(F32)
        for copy in stores(k):
            copy.start()

    order = [pick(t, z) for t in FAR] + [z]
    for i, j in enumerate(order):
        for n in range(1, per):
            plane(i, j, n).start()
        local(i, j).start()
    for copy in loads:
        copy.start()
    for i in range(1, 2 * per):
        little(i).start()
    lall[0] = small_ref[r * 2 + c]
    tiles = width // step
    done = 0
    for i, j in enumerate(order):
        while done < tiles * (2, 3, 3, 4)[i] // 4:
            tile(done)
            done += 1
        if i == OUTER - 1:
            for k in range(1, 2 * per):
                little(k).wait_recv()
            lsum[...] = sum(lall[k] for k in range(2 * per))
            for d in range(1, OUTER):
                tall(d).start()
        marks = one_hot(pos_ref, r, j, per, cap)
        local(i, j).wait()
        for n in range(1, per):
            plane(i, j, n).wait_recv()
        for h in range(halves):

            @pl.loop(0, half // step)
            def _(k):
                columns = pl.ds(pl.multiple_of(h * half + k * step, step), step)
                rows = jnp.concatenate([ybuf[i, n, :, columns] for n in range(per)], axis=0)
                out_ref[:, columns] = lax.dot_general(
                    marks, rows, (((0,), (0,)), ((), ())), preferred_element_type=F32
                )

            if i < OUTER - 1:

                @pl.when(jnp.logical_and(j > z, z > 0))
                def _():
                    rise(0, h, j).wait_recv()
                    out_ref[:, part(h)] += rbuf[j, h].astype(F32)

                @pl.when(jnp.logical_and(j < z, z < OUTER - 1))
                def _():
                    fall(0, h, j).wait_recv()
                    out_ref[:, part(h)] += rbuf[j, h].astype(F32)

                ubuf[i, h] = out_ref[:, part(h)].astype(BF16)

                @pl.when(j > z)
                def _():
                    rise(i, h, j).start()

                @pl.when(jnp.logical_and(j < z, z - j > 1))
                def _():
                    fall(i, h, j).start()

                @pl.when(z - j == 1)
                def _():
                    fall(i, h, OUTER).start()
            else:

                @pl.when(z > 0)
                def _():
                    rise(0, h, z).wait_recv()
                    out_ref[:, part(h)] += rbuf[z, h].astype(F32)

                @pl.when(z < OUTER - 1)
                def _():
                    fall(0, h, OUTER).wait_recv()
                    out_ref[:, part(h)] += rbuf[OUTER, h].astype(F32)

                res_ref[:, part(h)] = (mid_ref[:, part(h)] + out_ref[:, part(h)]).astype(BF16)

    for i, j in enumerate(order):
        for n in range(1, per):
            plane(i, j, n).wait_send()
        if i < OUTER - 1:
            for h in range(halves):
                rise(i, h, j).wait_send()
    for d in range(1, OUTER):
        tall(d).wait()
    total_ref[...] = lsum[z] + sum(lz[d] for d in range(1, OUTER))
    for i in range(1, 2 * per):
        little(i).wait_send()
    for k in range(max(0, tiles - 2), tiles):
        across(k).wait_send()
    for copy in stores(tiles - 1):
        copy.wait()


def combine(y, pos_all, middle, small, slots, cot_slots, gate_low, up_low, hidden_gated, number):
    outer, per, cap, width = y.shape
    span = pos_all.shape[-1]
    block, hidden = gate_low.shape[1:]
    share = hidden // 2
    step = min(512, width)
    tiles = width // step
    vmem = pl.BlockSpec(memory_space=pltpu.VMEM)
    hbm = pl.BlockSpec(memory_space=pltpu.HBM)
    dma = pltpu.SemaphoreType.DMA
    return pl.pallas_call(
        functools.partial(combine_body, per, cap),
        out_shape=(
            jax.ShapeDtypeStruct((span, width), BF16),
            jax.ShapeDtypeStruct((1, small.shape[-1]), F32),
            jax.ShapeDtypeStruct((2, width, share), F32),
            jax.ShapeDtypeStruct((width, share), F32),
        ),
        in_specs=[hbm, vmem, vmem, vmem] + [hbm] * 5,
        out_specs=(vmem, vmem, hbm, hbm),
        scratch_shapes=[
            pltpu.VMEM((span, width), F32),
            pltpu.VMEM((OUTER, per, cap, width), BF16),
            pltpu.VMEM((OUTER - 1, 2, span, width // 2), BF16),
            pltpu.VMEM((OUTER + 1, 2, span, width // 2), BF16),
            pltpu.VMEM((OUTER, block, 3 * share), BF16),
            pltpu.VMEM((OUTER, block, 3 * share), BF16),
            pltpu.VMEM((OUTER, per, cap, step), BF16),
            pltpu.VMEM((step, OUTER * block), BF16),
            pltpu.VMEM((2, step, 3 * share), BF16),
            pltpu.VMEM((tiles, step, 3 * share), BF16),
            pltpu.VMEM((step, 3 * share), F32),
            pltpu.VMEM(small.shape, F32),
            pltpu.VMEM(small.shape[1:], F32),
            pltpu.VMEM(small.shape[1:], F32),
            dma((OUTER - 1, 2)),
            dma((OUTER + 1, 2)),
            dma((OUTER, per)),
            dma((OUTER, per)),
            dma((OUTER,)),
            dma((3, 2)),
            dma,
            dma((tiles,)),
            dma((tiles,)),
            dma((3,)),
            dma((2 * per,)),
            dma((2 * per,)),
            dma((OUTER,)),
            dma((OUTER,)),
        ],
        compiler_params=pltpu.CompilerParams(
            collective_id=number, has_side_effects=True, vmem_limit_bytes=62 << 20
        ),
        name="combine",
    )(y, pos_all, middle, small, slots, cot_slots, gate_low, up_low, hidden_gated)


def weights_body(rows, *refs):
    mats, per = len(SOURCE), 4
    x_refs, y_refs, refs = refs[:4], refs[4 : 4 + mats], refs[4 + mats :]
    w_refs, tok_ref, gain_ref, mg_ref, refs = refs[:3], refs[3], refs[4], refs[5], refs[6:]
    out_ref, tg_ref, gg_ref, xbuf, ybuf, keep, sbuf, srecv, ubuf, rbuf, hbuf, obuf, wbuf = refs[:13]
    xs, ys, yr, ss, sr, zs, zr, fs, fr, ws = refs[13:]
    e, c = lax.axis_index("expert"), lax.axis_index("dp")
    z, r = e // per, e % per
    x, y = r % 2, r // 2
    width = y_refs[0].shape[1]
    part = width // 4
    lines = width // OUTER
    peers = [(n, f) for n in range(per) for f in range(2)]
    trade = (y + c * (1 - 2 * y)) * 2 + x + (1 - c) * (1 - 2 * x)
    other = (y + (1 - c) * (1 - 2 * y)) * 2 + x + c * (1 - 2 * x)
    a_bit = (1 - c) * x + c * y
    b_bit = (1 - c) * y + c * x
    quarter = 2 * c + a_bit

    def device(n, f):
        return flip(r, n), (c + f) % 2

    bar = pltpu.get_barrier_semaphore()
    for d in range(1, OUTER):
        pl.semaphore_signal(
            bar, inc=1, device_id=((z + d) % OUTER * per + r, c), device_id_type=MESH
        )
    for n, f in peers[1:]:
        q, k = device(n, f)
        pl.semaphore_signal(bar, inc=1, device_id=(z * per + q, k), device_id_type=MESH)
    pl.semaphore_wait(bar, OUTER - 1 + 2 * per - 1)

    def block(q):
        return pl.ds(pl.multiple_of(q * part, part), part)

    targets = (
        (r, 1 - c, 2 * (1 - c) + (1 - c) * y + c * x),
        (trade, c, 2 * c + 1 - a_bit),
        (other, 1 - c, 2 * (1 - c) + 1 - b_bit),
    )

    def spread(m, i):
        q, k, at = targets[i]
        return pltpu.make_async_remote_copy(
            src_ref=y_refs[m].at[:, block(at)], dst_ref=ybuf.at[m, i + 1],
            send_sem=ys.at[m, i], recv_sem=yr.at[m, i],
            device_id=(z * per + q, k), device_id_type=MESH,
        )

    def swap(m, i):
        return pltpu.make_async_remote_copy(
            src_ref=sbuf.at[m, i], dst_ref=srecv.at[m, i], send_sem=ss.at[m, i],
            recv_sem=sr.at[m, i], device_id=(z * per + other, c), device_id_type=MESH,
        )

    def hop(m, i, j, way):
        return pltpu.make_async_remote_copy(
            src_ref=ubuf.at[m, i], dst_ref=rbuf.at[m, way, j],
            send_sem=zs.at[m, i], recv_sem=zr.at[m, way, j],
            device_id=((z + 1 - 2 * way) * per + r, c), device_id_type=MESH,
        )

    def final(m, t, f):
        there = a_bit + t * (1 - 2 * a_bit)
        core = (c + f) % 2
        q = ((1 - c) * y + c * there) * 2 + (1 - c) * there + c * x
        return pltpu.make_async_remote_copy(
            src_ref=hbuf.at[m, pl.ds(pl.multiple_of((there * 2 + core) * rows, rows), rows)],
            dst_ref=obuf.at[m, quarter], send_sem=fs.at[m, 2 * t + f],
            recv_sem=fr.at[m, quarter], device_id=(z * per + q, core), device_id_type=MESH,
        )

    def landed(m, q):
        return pltpu.make_async_remote_copy(
            src_ref=hbuf.at[m, pl.ds(0, rows)], dst_ref=obuf.at[m, q], send_sem=fs.at[m, 0],
            recv_sem=fr.at[m, q], device_id=(z * per + r, 1 - c), device_id_type=MESH,
        )

    strip = wbuf.shape[1]
    strips = width // strip
    jobs = [(k, q) for k in range(3) for q in range(strips)]

    def fetch(t):
        k, q = jobs[t]
        return pltpu.make_async_copy(
            w_refs[k].at[pl.ds(q * strip, strip)], wbuf.at[t % 2], ws.at[t % 2]
        )

    def pull_back(t):
        k, q = jobs[t]
        if t == 0:
            fetch(0).start()
        if t + 1 < len(jobs):
            fetch(t + 1).start()
        fetch(t).wait()
        got = lax.dot_general(
            y_refs[3 - k][...], wbuf[t % 2], (((1,), (1,)), ((), ())), preferred_element_type=F32
        )
        if k == 0:
            tg_ref[:, q * strip : (q + 1) * strip] = got
        else:
            tg_ref[:, q * strip : (q + 1) * strip] += got

    def norm_back():
        grad = tg_ref[...]
        values = tok_ref[...].astype(F32)
        scale = rms_scale(values)
        normed = values * scale
        gg_ref[...] = jnp.sum(grad * normed, axis=0, keepdims=True)
        grad = grad * gain_ref[...]
        centre = jnp.mean(grad * normed, axis=-1, keepdims=True)
        tg_ref[...] = mg_ref[...] + scale * (grad - normed * centre)

    loads = [pltpu.make_async_copy(x_refs[i], xbuf.at[i], xs.at[i]) for i in range(4)]
    def begin(m):
        for i in range(3):
            spread(m, i).start()

    begin(0)
    begin(1)
    for copy in loads:
        copy.start()
    for m in range(mats):
        ybuf[m, 0] = y_refs[m][:, block(quarter)]
    for copy in loads:
        copy.wait()
    order = [pick(t, z) for t in FAR]

    def pieces(j, bit):
        for t in range(2):
            at = j * lines + (1 - c) * (bit * 2 + t) * 2 * rows + c * (t * 2 + bit) * 2 * rows
            yield pl.ds(pl.multiple_of(at, 2 * rows), 2 * rows)

    def product(m, j, bit):
        total = None
        for i in range(4):
            left = jnp.concatenate([xbuf[i, SOURCE[m], at, :] for at in pieces(j, bit)], axis=0)
            term = jnp.dot(left, ybuf[m, i], preferred_element_type=F32)
            total = term if total is None else total + term
        return total

    edge = jnp.logical_or(z == 0, z == OUTER - 1)

    def outer(m):
        for i, j in enumerate(order):
            swap(m, i).wait_recv()
            ubuf[m, i] = (keep[m, i] + srecv[m, i].astype(F32)).astype(BF16)

            @pl.when(z == 0)
            def _():
                hop(m, i, j, 0).start()

            @pl.when(z > 0)
            def _():
                hop(m, i, j, 1).start()

    def inner(m):
        for i, j in enumerate(order):
            swap(m, i).wait_recv()

            @pl.when(j > z)
            def _():
                hop(m, 0, j, 0).wait_recv()
                ubuf[m, i] = (
                    keep[m, i] + srecv[m, i].astype(F32) + rbuf[m, 0, j].astype(F32)
                ).astype(BF16)
                hop(m, i, j, 0).start()

            @pl.when(j < z)
            def _():
                hop(m, 0, j, 1).wait_recv()
                ubuf[m, i] = (
                    keep[m, i] + srecv[m, i].astype(F32) + rbuf[m, 1, j].astype(F32)
                ).astype(BF16)
                hop(m, i, j, 1).start()

    for m in range(mats + 2):
        if m < mats:
            for i in range(3):
                spread(m, i).wait_recv()
            for i, j in enumerate(order + [z]):
                sbuf[m, i] = product(m, j, 1 - b_bit).astype(BF16)
                swap(m, i).start()
            if m + 2 < mats:
                begin(m + 2)
            for i, j in enumerate(order + [z]):
                keep[m, i] = product(m, j, b_bit)
        if 1 <= m <= mats:
            pl.when(edge)(functools.partial(outer, m - 1))
        if m >= 2:
            pl.when(jnp.logical_not(edge))(functools.partial(inner, m - 2))
        if m < 3:
            for t in range(m * strips, (m + 1) * strips):
                pull_back(t)
        elif m == 3:
            norm_back()

    last = OUTER - 1
    for m in range(mats):
        swap(m, last).wait_recv()
        keep[m, last] += srecv[m, last].astype(F32)

        @pl.when(z > 0)
        def _():
            hop(m, 0, z, 0).wait_recv()
            keep[m, last] += rbuf[m, 0, z].astype(F32)

        @pl.when(z < OUTER - 1)
        def _():
            hop(m, 0, z, 1).wait_recv()
            keep[m, last] += rbuf[m, 1, z].astype(F32)

        hbuf[m] = keep[m, last].astype(BF16)
        for t, f in ((1, 0), (1, 1), (0, 1)):
            final(m, t, f).start()

    for m in range(mats):
        mine = pl.ds(pl.multiple_of((a_bit * 2 + c) * rows, rows), rows)
        out_ref[m, :, block(quarter)] = keep[m, last, mine, :]
        for d in range(1, 4):
            q = (quarter + d) % 4
            landed(m, q).wait_recv()
            out_ref[m, :, block(q)] = obuf[m, q].astype(F32)
    for m in range(mats):
        for i in range(3):
            spread(m, i).wait_send()
        for i in range(OUTER):
            swap(m, i).wait_send()
        for t, f in ((1, 0), (1, 1), (0, 1)):
            final(m, t, f).wait_send()
        for i, j in enumerate(order):
            hop(m, i, j, 0).wait_send()


SOURCE = (1, 0, 0, 0)


def weight_grads(lefts, rights, weights, tokens, gain, middle_grad, experts, number):
    span, width = rights[0].shape
    rows = width // (2 * experts)
    part = width // 4
    half = width // OUTER // 2
    mats = len(rights)
    vmem = pl.BlockSpec(memory_space=pltpu.VMEM)
    hbm = pl.BlockSpec(memory_space=pltpu.HBM)
    dma = pltpu.SemaphoreType.DMA
    return pl.pallas_call(
        functools.partial(weights_body, rows),
        out_shape=(
            jax.ShapeDtypeStruct((mats, rows, width), F32),
            jax.ShapeDtypeStruct((span, width), F32),
            jax.ShapeDtypeStruct((1, width), F32),
        ),
        in_specs=[hbm] * 4 + [vmem] * mats + [hbm] * 3 + [vmem] * 3,
        out_specs=(vmem,) * 3,
        scratch_shapes=[
            pltpu.VMEM((4, 2, width, span), BF16),
            pltpu.VMEM((mats, 4, span, part), BF16),
            pltpu.VMEM((mats, OUTER, half, part), F32),
            pltpu.VMEM((mats, OUTER, half, part), BF16),
            pltpu.VMEM((mats, OUTER, half, part), BF16),
            pltpu.VMEM((mats, OUTER - 1, half, part), BF16),
            pltpu.VMEM((mats, 2, OUTER, half, part), BF16),
            pltpu.VMEM((mats, half, part), BF16),
            pltpu.VMEM((mats, 4, rows, part), BF16),
            pltpu.VMEM((2, width // OUTER // 2, width), BF16),
            dma((4,)),
            dma((mats, 3)),
            dma((mats, 3)),
            dma((mats, OUTER)),
            dma((mats, OUTER)),
            dma((mats, OUTER - 1)),
            dma((mats, 2, OUTER)),
            dma((mats, 4)),
            dma((mats, 4)),
            dma((2,)),
        ],
        compiler_params=pltpu.CompilerParams(
            collective_id=number, has_side_effects=True, vmem_limit_bytes=62 << 20
        ),
        name="weight_grads",
    )(*lefts, *rights, *weights, tokens, gain, middle_grad)


def body(
    tokens,
    cotangent,
    lengths,
    routes,
    attention_gain,
    query_gain,
    key_gain,
    feedforward_gain,
    query_weight,
    key_weight,
    value_weight,
    output_weight,
    router_weight,
    expert_gate_up,
    expert_down,
):
    span, width = tokens.shape
    core = lax.axis_index("dp")
    both = ("expert", "dp")
    devices = lax.axis_size("expert") * 2
    gains = jnp.stack([attention_gain, query_gain, key_gain, feedforward_gain]).astype(F32)
    other = lax.ppermute(gains, both, [(d, d ^ 1) for d in range(devices)])
    gains = jnp.where(
        core == 0,
        jnp.concatenate([gains, other], axis=1),
        jnp.concatenate([other, gains], axis=1),
    )
    gain_in, gain_query, gain_key, gain_mid = gains[0], gains[1], gains[2], gains[3]

    router_other = lax.ppermute(router_weight, both, [(d, d ^ 1) for d in range(devices)])
    router_full = jnp.where(
        core == 0,
        jnp.concatenate([router_weight, router_other], axis=0),
        jnp.concatenate([router_other, router_weight], axis=0),
    )
    experts = router_full.shape[1]
    cap = span * TOP // experts
    per = experts // OUTER

    seq_length = lengths[0]
    index_rows = jnp.arange(span, dtype=jnp.int32)
    expert_ids = jnp.arange(experts, dtype=jnp.int32)
    hits = jnp.any(routes[None, :, :] == expert_ids[:, None, None], axis=-1)
    hits = hits & (index_rows < seq_length)[None, :]
    earlier = (index_rows[:, None] < index_rows[None, :]).astype(BF16)
    before = jnp.dot(hits.astype(BF16), earlier, preferred_element_type=F32)
    kept = hits & (before < cap)
    pos = jnp.where(kept, before, -1.0)
    inputs = tokens.astype(F32)
    cosine_table, sine_table = rotary_tables(index_rows.astype(F32))
    signs = jnp.where(jnp.arange(HD) < HD // 2, -1.0, 1.0)
    key_limit = jnp.minimum(index_rows, seq_length - 1)
    (
        cot_slots, pos_here, pos_all, query_full, key_full, value_full, output_full,
        other_gate_up, other_down, turned,
        normed_in, query_pre, key_pre, query_rot, key_rot, value_all, log_total, attended,
        middle, normed_mid, gates,
    ) = attend(
        tokens, cotangent, pos[:, None, :], gains, (cosine_table, sine_table * signs),
        key_limit.astype(F32)[:, None], router_full,
        (query_weight, key_weight, value_weight, output_weight, expert_gate_up, expert_down),
        cap, 1,
    )
    norm_mid_back = jax.vjp(norm_apply, middle, gain_mid)[1]
    query_back, key_back = [
        jax.vjp(
            lambda projected, gain: rotary_norm(projected, gain, cosine_table, sine_table),
            pre, gain,
        )[1]
        for pre, gain in ((query_pre, gain_query), (key_pre, gain_key))
    ]
    query_rot, key_rot, value_heads = [
        value.reshape(span, NH, HD) for value in (query_rot, key_rot, value_all)
    ]
    allowed = index_rows[None, :] <= key_limit[:, None]
    score_scale = HD ** (-0.5)

    def scores_of():
        raw = jnp.einsum("thd,shd->hts", query_rot, key_rot, preferred_element_type=F32)
        return jnp.where(allowed[None], raw * score_scale, -1e30)

    def mul(left, right, spec):
        return jnp.einsum(spec, left, right, preferred_element_type=F32)

    back_rows, prob_grad, slots, gate_grad_low, up_grad_low, hidden_gated, expert_out = run_experts(
        normed_mid, gates.T[:, None, :], pos_all, pos_here, cot_slots,
        (expert_gate_up, expert_down, other_gate_up, other_down), 2,
    )
    prob_grad = prob_grad[:, 0].T
    back_rows, turned = lax.optimization_barrier((back_rows, turned))
    wide = per == 4 and width % 512 == 0
    if wide:

        def moved(d, cross):
            to = d % 2 ^ cross
            return (d // 2 ^ 1 + to) * 2 + to

        lefts = [turned, lax.ppermute(turned, both, [(d, d ^ 1) for d in range(devices)])] + [
            lax.ppermute(turned, both, [(d, moved(d, cross)) for d in range(devices)])
            for cross in range(2)
        ]

    upstream = cotangent.astype(F32)
    logit_grad = (
        gates * (prob_grad - jnp.sum(gates * prob_grad, axis=-1, keepdims=True))
    ).astype(BF16)
    grad_router = mul(normed_mid, logit_grad, "td,te->de")
    mid_normed_grad = mul(logit_grad, router_full, "te,de->td") + back_rows
    mid_input_grad, grad_mid_gain = norm_mid_back(mid_normed_grad)
    middle_grad = upstream + mid_input_grad
    branch_grad = middle_grad.astype(BF16)
    attended_grad = mul(branch_grad, output_full, "to,io->ti").astype(BF16)
    attended_grad = attended_grad.reshape(span, NH, HD)
    weights_full = jnp.exp(scores_of() - log_total)
    weights_grad = mul(attended_grad, value_heads, "thd,shd->hts")
    value_grad = mul(weights_full.astype(BF16), attended_grad, "hts,thd->shd")
    value_grad = value_grad.reshape(span, width).astype(BF16)
    centre = jnp.sum(weights_full * weights_grad, axis=-1, keepdims=True)
    score_grad = (weights_full * (weights_grad - centre)).astype(BF16)
    query_rot_grad = mul(score_grad, key_rot, "hts,shd->thd").reshape(span, width) * score_scale
    key_rot_grad = mul(score_grad, query_rot, "hts,thd->shd").reshape(span, width) * score_scale
    query_pre_grad, grad_query_gain = query_back(query_rot_grad)
    key_pre_grad, grad_key_gain = key_back(key_rot_grad)
    query_low = query_pre_grad.astype(BF16)
    key_low = key_pre_grad.astype(BF16)
    rights = (branch_grad, value_grad, key_low, query_low)
    if wide:
        expert_out, lefts, rights = lax.optimization_barrier((expert_out, lefts, rights))
        grads, grad_tokens, grad_in_gain = weight_grads(
            lefts, rights, (query_full, key_full, value_full), tokens, gain_in[None],
            middle_grad, experts, 5,
        )
        grad_in_gain = grad_in_gain[0]
    else:
        grads = []
        for source, right in zip(SOURCE, rights):
            grad = jnp.dot(turned[source], right, preferred_element_type=F32).astype(BF16)
            grid = grad.reshape(experts, 2, width // experts // 2, width).swapaxes(0, 1)
            half = lax.psum_scatter(grid, "dp", scatter_dimension=0, tiled=False)
            half = lax.psum_scatter(half, "expert", scatter_dimension=0, tiled=False)
            grads.append(half.astype(F32))
        normed_in_grad = mul(query_low, query_full, "to,io->ti")
        normed_in_grad = normed_in_grad + mul(key_low, key_full, "to,io->ti")
        normed_in_grad = normed_in_grad + mul(value_grad, value_full, "to,io->ti")
        input_grad, grad_in_gain = jax.vjp(norm_apply, inputs, gain_in)[1](normed_in_grad)
        grad_tokens = middle_grad + input_grad

    small = jnp.concatenate(
        [
            jnp.stack([grad_in_gain, grad_query_gain, grad_key_gain, grad_mid_gain]).T,
            grad_router,
        ],
        axis=1,
    )
    kinds = small.shape[1]
    small = small.reshape(OUTER, 2 * per, -1, kinds).transpose(1, 0, 3, 2)
    output, small, grad_gate_up, grad_down = combine(
        expert_out, pos_all, middle, small.reshape(2 * per, OUTER, 1, -1), slots, cot_slots,
        gate_grad_low, up_grad_low, hidden_gated, 4,
    )
    small = small.reshape(kinds, -1).T
    return (
        output,
        grad_tokens,
        small[:, 0],
        small[:, 1],
        small[:, 2],
        small[:, 3],
        grads[3],
        grads[2],
        grads[1],
        grads[0],
        small[:, 4:],
        grad_gate_up[None],
        grad_down[None],
    )


def solution(mesh):
    both = P(("expert", "dp"))
    rows = P(("expert", "dp"), None)
    in_specs = (rows, rows, both, rows) + (P("dp"),) * 4 + (P("dp", None),) * 5 + (
        P("expert", None, None, "dp"),
        P("expert", None, "dp"),
    )
    out_specs = (rows, rows) + (both,) * 4 + (rows,) * 5 + (
        P("expert", None, None, "dp"),
        P("expert", None, "dp"),
    )
    return jax.shard_map(body, mesh=mesh, in_specs=in_specs, out_specs=out_specs, check_vma=False)
```

```python
import functools
import math

import jax
import jax.numpy as jnp
from jax import lax
from jax.experimental import pallas as pl
from jax.experimental.pallas import tpu as pltpu
from jax.sharding import PartitionSpec as P

NH = 16
HD = 128
TOP = 8
OUTER = 4

EPSILON = 1e-05
ROPE_BASE = 10000.0
MESH = pl.DeviceIdType.MESH
F32 = jnp.float32
BF16 = jnp.bfloat16


def rms_scale(values):
    return lax.rsqrt(jnp.mean(values * values, axis=-1, keepdims=True) + EPSILON)


def norm_apply(values, gain_vector):
    return values * rms_scale(values) * gain_vector


def rotary_tables(positions):
    frequencies = 1.0 / ROPE_BASE ** (jnp.arange(0, HD, 2).astype(F32) / HD)
    angles = positions[:, None] * frequencies[None, :]
    angles = jnp.concatenate([angles, angles], axis=-1)
    return (jnp.cos(angles), jnp.sin(angles))


def rotary_norm(projected, gain_vector, cosine_table, sine_table):
    normed = projected * rms_scale(projected) * gain_vector
    shaped = normed.reshape(normed.shape[0], NH, HD)
    half_width = HD // 2
    turned = jnp.concatenate([-shaped[..., half_width:], shaped[..., :half_width]], axis=-1)
    rotated = shaped * cosine_table[:, None, :] + turned * sine_table[:, None, :]
    return rotated.reshape(normed.shape[0], NH * HD)


def flip(r, n):
    out, bit = r, 1
    while bit <= n:
        if n & bit:
            out = out + bit - 2 * bit * ((r // bit) % 2)
        bit *= 2
    return out


def pick(table, z):
    code = sum(v * 4**k for k, v in enumerate(table))
    return (code // ((1 + 3 * (z % 2)) * (1 + 15 * (z // 2)))) % 4


NEAR = ((1, 0, 1, 2), (2, 2, 3, 1), (3, 3, 0, 0))
PLACE = ((1, 3, 3, 1), (3, 1, 2, 3), (2, 2, 1, 2))
BLOCK = ((1, 3, 0, 2), (3, 0, 3, 0), (2, 2, 1, 1))
FAR = ((3, 3, 0, 0), (2, 0, 3, 1), (1, 2, 1, 2))


def one_hot(pos_ref, r, j, per, cap):
    span = pos_ref.shape[-1]
    rows = []
    slot = lax.broadcasted_iota(jnp.int32, (cap, span), 0).astype(F32)
    for n in range(per):
        line = pos_ref[j, flip(r, n)]
        rows.append(jnp.where(line == slot, 1.0, 0.0).astype(BF16))
    return jnp.concatenate(rows, axis=0)


def attend_body(per, cap, *refs):
    tok_ref, x_ref, meta_ref, gains_ref, cos_ref, sin_ref, limit_ref, router_ref = refs[:8]
    parts, refs = refs[8:14], refs[14:]
    out_ref, here_ref, pos_ref = refs[:3]
    fulls, refs = refs[3:9], refs[9:]
    turned_ref, nin_ref, qpre, kpre, qrot, krot, val_ref, lse_ref, att_ref, mid_ref = refs[:10]
    nmid_ref, gates_ref, zbuf, sbuf, wbuf, vacc = refs[10:16]
    zs, zr, ps, pr, ls, ms, mr, ts, tr, ds, dr, ks, fs = refs[16:]
    e, c = lax.axis_index("expert"), lax.axis_index("dp")
    z, r = e // per, e % per
    experts = OUTER * per
    bar = pltpu.get_barrier_semaphore()
    for d in range(1, experts):
        pl.semaphore_signal(bar, inc=1, device_id=((e + d) % experts, c), device_id_type=MESH)
    pl.semaphore_signal(bar, inc=1, device_id=(e, 1 - c), device_id_type=MESH)
    pl.semaphore_wait(bar, experts)
    span, width = x_ref.shape
    step = min(512, width)
    half = width // 2

    def share(d):
        to = (e + d) % experts
        return pltpu.make_async_remote_copy(
            src_ref=meta_ref.at[to], dst_ref=here_ref.at[e], send_sem=ms.at[d - 1],
            recv_sem=mr.at[d - 1], device_id=(to, c), device_id_type=MESH,
        )

    def table(d):
        to = (z + d) % OUTER
        return pltpu.make_async_remote_copy(
            src_ref=meta_ref.at[pl.ds(to * per, per)], dst_ref=pos_ref.at[z],
            send_sem=ts.at[d - 1], recv_sem=tr.at[z],
            device_id=(to * per + r, c), device_id_type=MESH,
        )

    def tabled(j):
        return pltpu.make_async_remote_copy(
            src_ref=meta_ref.at[pl.ds(0, per)], dst_ref=pos_ref.at[j], send_sem=ts.at[0],
            recv_sem=tr.at[j], device_id=(j * per + r, c), device_id_type=MESH,
        )

    def up(src, j):
        return pltpu.make_async_remote_copy(
            src_ref=src, dst_ref=zbuf.at[j], send_sem=zs.at[0, j], recv_sem=zr.at[j],
            device_id=((z + 1) * per + r, c), device_id_type=MESH,
        )

    def down(src, j):
        return pltpu.make_async_remote_copy(
            src_ref=src, dst_ref=zbuf.at[j], send_sem=zs.at[1, j], recv_sem=zr.at[j],
            device_id=((z - 1) * per + r, c), device_id_type=MESH,
        )

    def plane(i, j, n):
        return pltpu.make_async_remote_copy(
            src_ref=sbuf.at[i, n], dst_ref=out_ref.at[j, n], send_sem=ps.at[i, n],
            recv_sem=pr.at[i, n], device_id=(z * per + flip(r, n), c), device_id_type=MESH,
        )

    def local(i, j):
        return pltpu.make_async_copy(sbuf.at[i, 0], out_ref.at[j, 0], ls.at[i])

    def lines(owner):
        return pl.ds(pl.multiple_of(owner * half, half), half)

    def give(k):
        return pltpu.make_async_remote_copy(
            src_ref=parts[k], dst_ref=fulls[k].at[lines(c)] if k < 4 else fulls[k], send_sem=ds.at[k],
            recv_sem=dr.at[k], device_id=(e, 1 - c), device_id_type=MESH,
        )

    def hold(t):
        return pltpu.make_async_copy(wbuf.at[t % 2], fulls[jobs[t][0]].at[lines(c)], ks.at[t % 2])

    jobs = [(0, 0), (1, 0), (2, 0), (0, 1), (1, 1), (2, 1), (3, 0), (3, 1)]

    def fetch(t):
        k, far = jobs[t]
        src = fulls[k].at[lines(1 - c)] if far else parts[k]
        return pltpu.make_async_copy(src, wbuf.at[t % 2], fs.at[t % 2])

    def project(t):
        k, far = jobs[t]
        left = att_ref if k == 3 else nin_ref
        into = (qpre, kpre, vacc, mid_ref)[k]
        if t == 3:
            for q in range(2):
                give(q).wait_recv()
                fetch(t + q).start()
        fetch(t).wait()
        if not far:
            hold(t).start()
        mine = lines(1 - c if far else c)

        @pl.loop(0, width // step)
        def _(q):
            columns = pl.ds(pl.multiple_of(q * step, step), step)
            got = jnp.dot(left[:, mine], wbuf[t % 2, :, columns], preferred_element_type=F32)
            if k == 3 and not far:
                into[:, columns] = tok_ref[:, columns].astype(F32) + got
            elif far:
                into[:, columns] += got
            else:
                into[:, columns] = got

        if not far:
            hold(t).wait()
        if t in (0, 4):
            fetch(t + 2).start()
        elif t in (3, 5):
            give(jobs[t + 2][0]).wait_recv()
            fetch(t + 2).start()

    order = [z] + [pick(t, z) for t in NEAR]

    edge = jnp.logical_or(z == 0, z == OUTER - 1)

    def relay(places):
        @pl.when(jnp.logical_not(edge))
        def _():
            for i in places:
                j = order[i]
                up(x_ref, j).wait_recv()

                @pl.when(j < z)
                def _():
                    up(zbuf.at[j], j).start()

                @pl.when(j > z)
                def _():
                    down(zbuf.at[j], j).start()

    def choose(i, j):
        block = x_ref if i == 0 else zbuf.at[j]
        if i > 0:

            @pl.when(edge)
            def _():
                up(x_ref, j).wait_recv()

            tabled(j).wait_recv()

        marks = one_hot(pos_ref, r, j, per, cap)

        @pl.loop(0, width // step)
        def _(k):
            columns = pl.ds(pl.multiple_of(k * step, step), step)
            got = jnp.dot(marks, block[:, columns], preferred_element_type=F32).astype(BF16)
            for n in range(per):
                sbuf[i, n, :, columns] = got[n * cap : (n + 1) * cap]

        for n in range(1, per):
            plane(i, j, n).start()
        local(i, j).start()

    for d in range(1, OUTER):
        table(d).start()

    @pl.when(z < OUTER - 1)
    def _():
        up(x_ref, z).start()

    @pl.when(z > 0)
    def _():
        down(x_ref, z).start()

    fetch(0).start()
    fetch(1).start()
    pos_ref[z] = meta_ref[pl.ds(z * per, per)]
    here_ref[e] = meta_ref[e]
    choose(0, z)
    for k in range(6):
        give(k).start()
    for d in range(1, experts):
        share(d).start()

    inputs = tok_ref[...].astype(F32)
    nin_ref[...] = norm_apply(inputs, gains_ref[0:1]).astype(BF16)
    for t in range(3):
        project(t)
    relay((1, 2))
    choose(1, order[1])
    for t in range(3, 6):
        project(t)
    val_ref[...] = vacc[...].astype(BF16)
    query_scale = rms_scale(qpre[...])
    key_scale = rms_scale(kpre[...])
    turned_ref[0] = nin_ref[...].T
    score_scale = HD ** (-0.5)
    column = lax.broadcasted_iota(jnp.int32, (span, span), 1).astype(F32)

    def heads(first, last):
        @pl.loop(first, last)
        def _(h):
            columns = pl.ds(pl.multiple_of(h * HD, HD), HD)

            def turn(pre, scale, row):
                normed = pre[:, columns] * scale * gains_ref[row : row + 1, columns]
                return (
                    normed * cos_ref[...] + pltpu.roll(normed, HD // 2, 1) * sin_ref[...]
                ).astype(BF16)

            query = turn(qpre, query_scale, 1)
            key = turn(kpre, key_scale, 2)
            qrot[:, columns] = query
            krot[:, columns] = key
            scores = lax.dot_general(
                query, key, (((1,), (1,)), ((), ())), preferred_element_type=F32
            )
            scores = jnp.where(column <= limit_ref[...], scores * score_scale, -1e30)
            peak = jnp.max(scores, axis=-1, keepdims=True)
            total = peak + jnp.log(jnp.sum(jnp.exp(scores - peak), axis=-1, keepdims=True))
            lse_ref[h] = total
            weights = jnp.exp(scores - total).astype(BF16)
            att_ref[:, columns] = jnp.dot(
                weights, val_ref[:, columns], preferred_element_type=F32
            ).astype(BF16)

    heads(0, NH // 2)
    choose(2, order[2])
    relay((3,))
    heads(NH // 2, NH)
    project(6)
    choose(3, order[3])
    project(7)
    turned_ref[1] = att_ref[...].T
    middle = mid_ref[...]
    nmid_ref[...] = norm_apply(middle, gains_ref[3:4]).astype(BF16)
    logits = jnp.dot(nmid_ref[...], router_ref[...], preferred_element_type=F32)
    raised = jnp.exp(logits - jnp.max(logits, axis=-1, keepdims=True))
    gates_ref[...] = raised / jnp.sum(raised, axis=-1, keepdims=True)

    for i, j in enumerate(order):
        local(i, j).wait()
        for n in range(1, per):
            plane(i, j, n).wait()

    @pl.when(z < OUTER - 1)
    def _():
        up(x_ref, z).wait_send()

    @pl.when(z > 0)
    def _():
        down(x_ref, z).wait_send()

    for j in order[1:]:

        @pl.when(jnp.logical_and(j < z, z < OUTER - 1))
        def _():
            up(zbuf.at[j], j).wait_send()

        @pl.when(jnp.logical_and(j > z, z > 0))
        def _():
            down(zbuf.at[j], j).wait_send()

    for d in range(1, experts):
        share(d).wait()
    for d in range(1, OUTER):
        table(d).wait_send()
    for k in range(6):
        give(k).wait_send()
    for k in range(4, 6):
        give(k).wait_recv()


def attend(tokens, cotangent, meta, gains, tables, limit, router, parts, cap, number):
    experts, _, span = meta.shape
    per = experts // OUTER
    width = tokens.shape[1]
    half = parts[0].shape[0]
    vmem = pl.BlockSpec(memory_space=pltpu.VMEM)
    hbm = pl.BlockSpec(memory_space=pltpu.HBM)
    dma = pltpu.SemaphoreType.DMA
    low = jax.ShapeDtypeStruct((span, width), BF16)
    high = jax.ShapeDtypeStruct((span, width), F32)
    return pl.pallas_call(
        functools.partial(attend_body, per, cap),
        out_shape=(
            jax.ShapeDtypeStruct((OUTER, per, cap, width), BF16),
            jax.ShapeDtypeStruct((experts, 1, span), F32),
            jax.ShapeDtypeStruct((OUTER, per, 1, span), F32),
        )
        + (jax.ShapeDtypeStruct((2 * half, width), BF16),) * 4
        + tuple(jax.ShapeDtypeStruct(part.shape, BF16) for part in parts[4:])
        + (jax.ShapeDtypeStruct((2, width, span), BF16), low, high, high, low, low, low)
        + (jax.ShapeDtypeStruct((NH, span, 1), F32), low, high, low)
        + (jax.ShapeDtypeStruct((span, experts), F32),),
        in_specs=[vmem] * 8 + [hbm] * 6,
        out_specs=(hbm, vmem, vmem) + (hbm,) * 6 + (vmem,) * 12,
        scratch_shapes=[
            pltpu.VMEM((OUTER, span, width), BF16),
            pltpu.VMEM((OUTER, per, cap, width), BF16),
            pltpu.VMEM((2, half, width), BF16),
            pltpu.VMEM((span, width), F32),
            dma((2, OUTER)),
            dma((OUTER,)),
            dma((OUTER, per)),
            dma((OUTER, per)),
            dma((OUTER,)),
            dma((experts,)),
            dma((experts,)),
            dma((OUTER,)),
            dma((OUTER,)),
            dma((6,)),
            dma((6,)),
            dma((2,)),
            dma((2,)),
        ],
        compiler_params=pltpu.CompilerParams(
            collective_id=number, has_side_effects=True, vmem_limit_bytes=60 << 20
        ),
        name="attend",
    )(tokens, cotangent, meta, gains, *tables, limit, router, *parts)


def experts_body(per, cap, *refs):
    x_ref, gates_ref, pos_ref, posh_ref, cot_ref, gu_mine, dn_mine, gu_other, dn_other = refs[:9]
    refs = refs[1:]
    back_ref, pg_ref, out_ref, gl_ref, ul_ref, hg_ref, eo_ref = refs[8:15]
    zbuf, sbuf, wg, wu, wd, slb, ctb, glb, ulb, hlb, hgb, eob, ybuf, ubuf, rbuf = refs[15:30]
    here, ggv, sgv, tgv = refs[30:34]
    zs, zr, ps, pr, ls, ms, mr, ws, cs, os, es, bs, br, us, ur, gs, gr = refs[34:]
    e, c = lax.axis_index("expert"), lax.axis_index("dp")
    z, r = e // per, e % per
    experts = OUTER * per
    bar = pltpu.get_barrier_semaphore()
    for d in range(1, experts):
        pl.semaphore_signal(bar, inc=1, device_id=((e + d) % experts, c), device_id_type=MESH)
    pl.semaphore_wait(bar, experts - 1)
    span, width = x_ref.shape
    hidden = wg.shape[1]
    step = min(512, width)
    thin = min(256, hidden)
    halves = 2
    half = width // halves

    def share(d):
        to = (e + d) % experts
        return pltpu.make_async_remote_copy(
            src_ref=gates_ref.at[to], dst_ref=here.at[e], send_sem=ms.at[d - 1],
            recv_sem=mr.at[d - 1], device_id=(to, c), device_id_type=MESH,
        )

    def up(src, j):
        return pltpu.make_async_remote_copy(
            src_ref=src, dst_ref=zbuf.at[j], send_sem=zs.at[0, j], recv_sem=zr.at[j],
            device_id=((z + 1) * per + r, c), device_id_type=MESH,
        )

    def down(src, j):
        return pltpu.make_async_remote_copy(
            src_ref=src, dst_ref=zbuf.at[j], send_sem=zs.at[1, j], recv_sem=zr.at[j],
            device_id=((z - 1) * per + r, c), device_id_type=MESH,
        )

    def plane(i, j, n):
        return pltpu.make_async_remote_copy(
            src_ref=sbuf.at[i, n], dst_ref=out_ref.at[j, n], send_sem=ps.at[i, n],
            recv_sem=pr.at[i, n], device_id=(z * per + flip(r, n), c), device_id_type=MESH,
        )

    def local(i, j):
        return pltpu.make_async_copy(sbuf.at[i, 0], out_ref.at[j, 0], ls.at[i])

    def returned(i, n):
        return pltpu.make_async_remote_copy(
            src_ref=sbuf.at[i, n], dst_ref=ybuf.at[i, n - 1], send_sem=bs.at[i, n],
            recv_sem=br.at[i, n], device_id=(z * per + flip(r, n), c), device_id_type=MESH,
        )

    def part(h):
        return pl.ds(h * half, half)

    def rise(i, j, h, slot):
        return pltpu.make_async_remote_copy(
            src_ref=ubuf.at[i, h], dst_ref=rbuf.at[slot, h], send_sem=us.at[i, h],
            recv_sem=ur.at[slot, h], device_id=((z + 1) * per + r, c), device_id_type=MESH,
        )

    def fall(i, j, h, slot):
        return pltpu.make_async_remote_copy(
            src_ref=ubuf.at[i, h], dst_ref=rbuf.at[slot, h], send_sem=us.at[i, h],
            recv_sem=ur.at[slot, h], device_id=((z - 1) * per + r, c), device_id_type=MESH,
        )

    def graded(i, n, seq):
        return pltpu.make_async_remote_copy(
            src_ref=tgv.at[i, n], dst_ref=pg_ref.at[e], send_sem=gs.at[i, n],
            recv_sem=gr.at[e], device_id=(seq, c), device_id_type=MESH,
        )

    def grade(s):
        return pltpu.make_async_remote_copy(
            src_ref=tgv.at[0, 0], dst_ref=pg_ref.at[s], send_sem=gs.at[0, 0],
            recv_sem=gr.at[s], device_id=(s, c), device_id_type=MESH,
        )

    def columns_of(owner):
        return pl.ds(pl.multiple_of(owner * (hidden // 2), hidden // 2), hidden // 2)

    weights = [
        pltpu.make_async_copy(src, dst.at[:, columns_of(owner)], ws.at[k, f])
        for f, (owner, both, down_part) in enumerate(
            ((c, gu_mine, dn_mine), (1 - c, gu_other, dn_other))
        )
        for k, (src, dst) in enumerate(
            ((both.at[0, 0], wg), (both.at[0, 1], wu), (down_part.at[0], wd))
        )
    ]

    def pull(j):
        return pltpu.make_async_copy(cot_ref.at[j], ctb, cs)

    for d in range(1, experts):
        share(d).start()

    @pl.when(z < OUTER - 1)
    def _():
        up(x_ref, z).start()

    @pl.when(z > 0)
    def _():
        down(x_ref, z).start()

    here[e] = gates_ref[e]
    order = [z] + [pick(t, z) for t in NEAR]

    edge = jnp.logical_or(z == 0, z == OUTER - 1)

    def relay(places):
        @pl.when(jnp.logical_not(edge))
        def _():
            for i in places:
                j = order[i]
                up(x_ref, j).wait_recv()

                @pl.when(j < z)
                def _():
                    up(zbuf.at[j], j).start()

                @pl.when(j > z)
                def _():
                    down(zbuf.at[j], j).start()

    def choose(i, j):
        block = x_ref if i == 0 else zbuf.at[j]
        if i > 0:

            @pl.when(edge)
            def _():
                up(x_ref, j).wait_recv()

        marks = one_hot(pos_ref, r, j, per, cap)

        @pl.loop(0, width // step)
        def _(k):
            columns = pl.ds(pl.multiple_of(k * step, step), step)
            got = jnp.dot(marks, block[:, columns], preferred_element_type=F32).astype(BF16)
            for n in range(per):
                sbuf[i, n, :, columns] = got[n * cap : (n + 1) * cap]

        for n in range(1, per):
            plane(i, j, n).start()
        local(i, j).start()

    def outs(j):
        return [
            pltpu.make_async_copy(src, dst.at[j], os.at[k])
            for k, (src, dst) in enumerate(((glb, gl_ref), (ulb, ul_ref), (hgb, hg_ref)))
        ]

    def away(j):
        return pltpu.make_async_copy(eob, eo_ref.at[j], es)

    def marked(j, n):
        slot = lax.broadcasted_iota(jnp.int32, (cap, span), 0).astype(F32)
        return posh_ref[j * per + flip(r, n)] == slot

    def expert(i, j):
        for n in range(1, per):
            plane(i, j, n).wait()
        local(i, j).wait()
        if i == OUTER - 1:
            send_back(1)
        fetch = pltpu.make_async_copy(out_ref.at[j], slb, ls.at[OUTER])
        fetch.start()
        slot_gate = jnp.concatenate(
            [
                jnp.sum(
                    jnp.where(marked(j, n), here[j * per + flip(r, n)], 0.0), axis=1, keepdims=True
                )
                for n in range(per)
            ],
            axis=0,
        )
        sgv[i % 2] = slot_gate
        ggv[i % 2] = jnp.zeros(ggv.shape[1:], F32)
        pull(j).wait()
        fetch.wait()
        if i > 0:
            for copy in outs(order[i - 1]):
                copy.wait()

        @pl.loop(0, hidden // thin)
        def _(k):
            columns = pl.ds(pl.multiple_of(k * thin, thin), thin)
            rows = slb[...].reshape(per * cap, width)
            gate_pre = jnp.dot(rows, wg[:, columns], preferred_element_type=F32)
            up_pre = jnp.dot(rows, wu[:, columns], preferred_element_type=F32)
            pulled = jnp.dot(
                ctb[...].reshape(per * cap, width), wd[:, columns], preferred_element_type=F32
            )
            sigmoid_gate = jax.nn.sigmoid(gate_pre)
            silu_gate = gate_pre * sigmoid_gate
            low = (silu_gate * up_pre).astype(BF16)
            wide = low.astype(F32)
            ggv[i % 2] += jnp.sum(wide * pulled, axis=1, keepdims=True)
            hidden_grad = pulled * slot_gate
            glb[:, columns] = (
                hidden_grad * up_pre * sigmoid_gate * (1.0 + gate_pre * (1.0 - sigmoid_gate))
            ).astype(BF16)
            ulb[:, columns] = (hidden_grad * silu_gate).astype(BF16)
            hlb[i % 2, :, columns] = low
            hgb[:, columns] = (wide * slot_gate).astype(BF16)

        if i < OUTER - 1:
            pull(order[i + 1]).start()
        for copy in outs(j):
            copy.start()

        @pl.loop(0, width // step)
        def _(k):
            columns = pl.ds(pl.multiple_of(k * step, step), step)
            got = lax.dot_general(
                glb[...], wg[columns, :], (((1,), (1,)), ((), ())), preferred_element_type=F32
            ) + lax.dot_general(
                ulb[...], wu[columns, :], (((1,), (1,)), ((), ())), preferred_element_type=F32
            )
            got = got.astype(BF16)
            for n in range(per):
                sbuf[i, n, :, columns] = got[n * cap : (n + 1) * cap]

    def send_back(i):
        for n in range(1, per):
            returned(i, n).start()

    def finish(i, j):
        for n in range(per):
            seq = j * per + flip(r, n)
            row = jnp.sum(
                jnp.where(marked(j, n), ggv[i % 2, n * cap : (n + 1) * cap], 0.0),
                axis=0,
                keepdims=True,
            )
            tgv[i, n] = row
            if i == 0 and n == 0:
                pg_ref[e] = row
            else:
                graded(i, n, seq).start()
        if i > 0:
            away(order[i - 1]).wait()

        @pl.loop(0, width // step)
        def _(k):
            columns = pl.ds(pl.multiple_of(k * step, step), step)
            got = lax.dot_general(
                hlb[i % 2], wd[columns, :], (((1,), (1,)), ((), ())), preferred_element_type=F32
            )
            got = (got * sgv[i % 2]).astype(BF16)
            for n in range(per):
                eob[n, :, columns] = got[n * cap : (n + 1) * cap]

        away(j).start()

    choose(0, z)
    for copy in weights:
        copy.start()
    pull(z).start()
    relay((1, 2))
    choose(1, order[1])
    for copy in weights:
        copy.wait()
    for d in range(1, experts):
        share(d).wait()
    last = OUTER - 1
    for i in range(last):
        expert(i, order[i])
        if i + 2 <= last:
            choose(i + 2, order[i + 2])
            if i == 0:
                relay((3,))
            finish(i, order[i])
    expert(last, order[last])
    for i in (last, last - 1, 0):
        send_back(i)
    finish(last - 1, order[last - 1])

    def fold(i, j, h):
        marks = one_hot(pos_ref, r, j, per, cap)

        @pl.loop(0, half // step)
        def _(k):
            columns = pl.ds(pl.multiple_of(h * half + k * step, step), step)
            rows = jnp.concatenate(
                [ybuf[i, n - 1, :, columns] if n else sbuf[i, 0, :, columns] for n in range(per)],
                axis=0,
            )
            back_ref[:, columns] = lax.dot_general(
                marks, rows, (((0,), (0,)), ((), ())), preferred_element_type=F32
            )

    for p in range(last):
        i, j = pick(PLACE[p], z), pick(BLOCK[p], z)
        for n in range(1, per):
            returned(i, n).wait_recv()
        for h in range(halves):
            fold(i, j, h)

            @pl.when(jnp.logical_and(j > z, z > 0))
            def _():
                rise(0, j, h, j).wait_recv()
                back_ref[:, part(h)] += rbuf[j, h].astype(F32)

            @pl.when(jnp.logical_and(j < z, z < OUTER - 1))
            def _():
                fall(0, j, h, j).wait_recv()
                back_ref[:, part(h)] += rbuf[j, h].astype(F32)

            ubuf[p, h] = back_ref[:, part(h)].astype(BF16)

            @pl.when(j > z)
            def _():
                rise(p, j, h, j).start()

            @pl.when(jnp.logical_and(j < z, z - j > 1))
            def _():
                fall(p, j, h, j).start()

            @pl.when(z - j == 1)
            def _():
                fall(p, j, h, OUTER).start()

        if p == 0:
            finish(last, order[last])

    for n in range(1, per):
        returned(0, n).wait_recv()
    for h in range(halves):
        fold(0, z, h)

        @pl.when(z > 0)
        def _():
            rise(0, z, h, z).wait_recv()
            back_ref[:, part(h)] += rbuf[z, h].astype(F32)

        @pl.when(z < OUTER - 1)
        def _():
            fall(0, z, h, OUTER).wait_recv()
            back_ref[:, part(h)] += rbuf[OUTER, h].astype(F32)

    @pl.when(z < OUTER - 1)
    def _():
        up(x_ref, z).wait_send()

    @pl.when(z > 0)
    def _():
        down(x_ref, z).wait_send()

    for i, j in enumerate(order):
        for n in range(1, per):
            returned(i, n).wait_send()
        if i > 0:

            @pl.when(jnp.logical_and(j < z, z < OUTER - 1))
            def _():
                up(zbuf.at[j], j).wait_send()

            @pl.when(jnp.logical_and(j > z, z > 0))
            def _():
                down(zbuf.at[j], j).wait_send()

            for h in range(halves):
                rise(i - 1, j, h, j).wait_send()
        for n in range(per):
            if i or n:
                graded(i, n, j * per + flip(r, n)).wait_send()
    for d in range(1, experts):
        grade((e + d) % experts).wait_recv()
    for copy in outs(order[last]):
        copy.wait()
    away(order[last]).wait()


def run_experts(x, gates, pos, pos_here, cot_slots, weights, number):
    experts, _, span = gates.shape
    outer, per, cap, width = cot_slots.shape
    hidden = 2 * weights[0].shape[-1]
    block = per * cap
    vmem = pl.BlockSpec(memory_space=pltpu.VMEM)
    hbm = pl.BlockSpec(memory_space=pltpu.HBM)
    dma = pltpu.SemaphoreType.DMA
    rows = jax.ShapeDtypeStruct((OUTER, per, cap, width), BF16)
    thin = jax.ShapeDtypeStruct((OUTER, block, hidden), BF16)
    return pl.pallas_call(
        functools.partial(experts_body, per, cap),
        out_shape=(
            jax.ShapeDtypeStruct((span, width), F32),
            jax.ShapeDtypeStruct((experts, 1, span), F32),
            rows, thin, thin, thin, rows,
        ),
        in_specs=[vmem] * 4 + [hbm] * 5,
        out_specs=(vmem, vmem) + (hbm,) * 5,
        scratch_shapes=[
            pltpu.VMEM((OUTER, span, width), BF16),
            pltpu.VMEM((OUTER, per, cap, width), BF16),
            pltpu.VMEM((width, hidden), BF16),
            pltpu.VMEM((width, hidden), BF16),
            pltpu.VMEM((width, hidden), BF16),
            pltpu.VMEM((per, cap, width), BF16),
            pltpu.VMEM((per, cap, width), BF16),
            pltpu.VMEM((block, hidden), BF16),
            pltpu.VMEM((block, hidden), BF16),
            pltpu.VMEM((2, block, hidden), BF16),
            pltpu.VMEM((block, hidden), BF16),
            pltpu.VMEM((per, cap, width), BF16),
            pltpu.VMEM((OUTER, per - 1, cap, width), BF16),
            pltpu.VMEM((OUTER - 1, 2, span, width // 2), BF16),
            pltpu.VMEM((OUTER + 1, 2, span, width // 2), BF16),
            pltpu.VMEM((experts, 1, span), F32),
            pltpu.VMEM((2, block, 1), F32),
            pltpu.VMEM((2, block, 1), F32),
            pltpu.VMEM((OUTER, per, 1, span), F32),
            dma((2, OUTER)),
            dma((OUTER,)),
            dma((OUTER, per)),
            dma((OUTER, per)),
            dma((OUTER + 1,)),
            dma((experts,)),
            dma((experts,)),
            dma((3, 2)),
            dma,
            dma((3,)),
            dma,
            dma((OUTER, per)),
            dma((OUTER, per)),
            dma((OUTER - 1, 2)),
            dma((OUTER + 1, 2)),
            dma((OUTER, per)),
            dma((experts,)),
        ],
        compiler_params=pltpu.CompilerParams(
            collective_id=number, has_side_effects=True, vmem_limit_bytes=62 << 20
        ),
        name="experts",
    )(x, gates, pos, pos_here, cot_slots, *weights)


def combine_body(per, cap, *refs):
    y_ref, pos_ref, mid_ref, small_ref, slots_ref, cot_ref, gl_ref, ul_ref, hg_ref = refs[:9]
    res_ref, total_ref, gu_ref, dn_ref, out_ref, ybuf, ubuf, rbuf = refs[9:17]
    theirs, ours, lbuf, lturn, tbuf, rx, stage, lall, lsum, lz = refs[17:27]
    zs, zr, ps, pr, ls, rs, ws, ds, dr, gs, las, lar, tas, tar = refs[27:]
    e, c = lax.axis_index("expert"), lax.axis_index("dp")
    z, r = e // per, e % per
    bar = pltpu.get_barrier_semaphore()
    for d in range(1, OUTER):
        pl.semaphore_signal(
            bar, inc=1, device_id=((z + d) % OUTER * per + r, c), device_id_type=MESH
        )
    peers = [(n, f) for n in range(per) for f in range(2)]

    def device(n, f):
        return flip(r, n), (c + f) % 2

    for n, f in peers[1:]:
        q, k = device(n, f)
        pl.semaphore_signal(bar, inc=1, device_id=(z * per + q, k), device_id_type=MESH)
    pl.semaphore_wait(bar, OUTER - 1 + 2 * per - 1)
    span, width = out_ref.shape
    step = min(512, width)
    share = dn_ref.shape[1]
    thin = min(256, share)
    total = OUTER * per * cap

    def plane(i, j, n):
        return pltpu.make_async_remote_copy(
            src_ref=y_ref.at[j, n], dst_ref=ybuf.at[i, n], send_sem=ps.at[i, n],
            recv_sem=pr.at[i, n], device_id=(z * per + flip(r, n), c), device_id_type=MESH,
        )

    def local(i, j):
        return pltpu.make_async_copy(y_ref.at[j, 0], ybuf.at[i, 0], ls.at[i])

    halves = 2
    half = width // halves

    def part(h):
        return pl.ds(h * half, half)

    def rise(i, h, slot):
        return pltpu.make_async_remote_copy(
            src_ref=ubuf.at[i, h], dst_ref=rbuf.at[slot, h], send_sem=zs.at[i, h],
            recv_sem=zr.at[slot, h], device_id=((z + 1) * per + r, c), device_id_type=MESH,
        )

    def fall(i, h, slot):
        return pltpu.make_async_remote_copy(
            src_ref=ubuf.at[i, h], dst_ref=rbuf.at[slot, h], send_sem=zs.at[i, h],
            recv_sem=zr.at[slot, h], device_id=((z - 1) * per + r, c), device_id_type=MESH,
        )

    def rights(k, src, other):
        owner = 1 - c if other else c
        return pltpu.make_async_copy(
            src.at[:, :, pl.ds(pl.multiple_of(owner * share, share), share)],
            (theirs if other else ours).at[:, :, pl.ds(k * share, share)],
            rs.at[k, int(other)],
        )

    def across(k):
        return pltpu.make_async_remote_copy(
            src_ref=tbuf.at[k % 2], dst_ref=rx.at[k], send_sem=ds.at[k], recv_sem=dr.at[k],
            device_id=(e, 1 - c), device_id_type=MESH,
        )

    def stores(k):
        lines = pl.ds(k * step, step)
        return [
            pltpu.make_async_copy(
                stage.at[:, pl.ds(m * share, share)],
                dn_ref.at[lines] if m == 2 else gu_ref.at[m, lines],
                gs.at[m],
            )
            for m in range(3)
        ]

    def little(i):
        q, k = device(*peers[i])
        return pltpu.make_async_remote_copy(
            src_ref=small_ref.at[q * 2 + k], dst_ref=lall.at[i], send_sem=las.at[i],
            recv_sem=lar.at[i], device_id=(z * per + q, k), device_id_type=MESH,
        )

    def tall(d):
        to = (z + d) % OUTER
        return pltpu.make_async_remote_copy(
            src_ref=lsum.at[to], dst_ref=lz.at[d], send_sem=tas.at[d], recv_sem=tar.at[d],
            device_id=(to * per + r, c), device_id_type=MESH,
        )

    sources = (gl_ref, ul_ref, hg_ref)
    loads = [rights(k, src, other) for k, src in enumerate(sources) for other in (True, False)]

    def tile(k):
        if k == 0:
            for copy in loads:
                copy.wait()
        if k >= 2:
            across(k - 2).wait_send()
        if k >= 1:
            for copy in stores(k - 1):
                copy.wait()
        for src, first, count in ((slots_ref, 0, 2), (cot_ref, 2, 1)):
            fetch = pltpu.make_async_copy(
                src.at[:, :, :, pl.ds(k * step, step)], lbuf, ws
            )
            fetch.start()
            fetch.wait()
            lturn[...] = lbuf[...].reshape(total, step).T

            @pl.loop(0, count * share // thin)
            def _(q):
                at = pl.ds(pl.multiple_of(first * share + q * thin, thin), thin)
                tbuf[k % 2, :, at] = jnp.dot(
                    lturn[...], theirs[:, :, at].reshape(total, thin), preferred_element_type=F32
                ).astype(BF16)
                stage[:, at] = jnp.dot(
                    lturn[...], ours[:, :, at].reshape(total, thin), preferred_element_type=F32
                )

        across(k).start()
        across(k).wait_recv()
        stage[...] += rx[k].astype(F32)
        for copy in stores(k):
            copy.start()

    order = [pick(t, z) for t in FAR] + [z]
    for i, j in enumerate(order):
        for n in range(1, per):
            plane(i, j, n).start()
        local(i, j).start()
    for copy in loads:
        copy.start()
    for i in range(1, 2 * per):
        little(i).start()
    lall[0] = small_ref[r * 2 + c]
    tiles = width // step
    done = 0
    for i, j in enumerate(order):
        while done < tiles * (1, 2, 3, 4)[i] // 4:
            tile(done)
            done += 1
        if i == OUTER - 1:
            for k in range(1, 2 * per):
                little(k).wait_recv()
            lsum[...] = sum(lall[k] for k in range(2 * per))
            for d in range(1, OUTER):
                tall(d).start()
        marks = one_hot(pos_ref, r, j, per, cap)
        local(i, j).wait()
        for n in range(1, per):
            plane(i, j, n).wait_recv()
        for h in range(halves):

            @pl.loop(0, half // step)
            def _(k):
                columns = pl.ds(pl.multiple_of(h * half + k * step, step), step)
                rows = jnp.concatenate([ybuf[i, n, :, columns] for n in range(per)], axis=0)
                out_ref[:, columns] = lax.dot_general(
                    marks, rows, (((0,), (0,)), ((), ())), preferred_element_type=F32
                )

            if i < OUTER - 1:

                @pl.when(jnp.logical_and(j > z, z > 0))
                def _():
                    rise(0, h, j).wait_recv()
                    out_ref[:, part(h)] += rbuf[j, h].astype(F32)

                @pl.when(jnp.logical_and(j < z, z < OUTER - 1))
                def _():
                    fall(0, h, j).wait_recv()
                    out_ref[:, part(h)] += rbuf[j, h].astype(F32)

                ubuf[i, h] = out_ref[:, part(h)].astype(BF16)

                @pl.when(j > z)
                def _():
                    rise(i, h, j).start()

                @pl.when(jnp.logical_and(j < z, z - j > 1))
                def _():
                    fall(i, h, j).start()

                @pl.when(z - j == 1)
                def _():
                    fall(i, h, OUTER).start()
            else:

                @pl.when(z > 0)
                def _():
                    rise(0, h, z).wait_recv()
                    out_ref[:, part(h)] += rbuf[z, h].astype(F32)

                @pl.when(z < OUTER - 1)
                def _():
                    fall(0, h, OUTER).wait_recv()
                    out_ref[:, part(h)] += rbuf[OUTER, h].astype(F32)

                res_ref[:, part(h)] = (mid_ref[:, part(h)] + out_ref[:, part(h)]).astype(BF16)

    for i, j in enumerate(order):
        for n in range(1, per):
            plane(i, j, n).wait_send()
        if i < OUTER - 1:
            for h in range(halves):
                rise(i, h, j).wait_send()
    for d in range(1, OUTER):
        tall(d).wait()
    total_ref[...] = lsum[z] + sum(lz[d] for d in range(1, OUTER))
    for i in range(1, 2 * per):
        little(i).wait_send()
    for k in range(max(0, tiles - 2), tiles):
        across(k).wait_send()
    for copy in stores(tiles - 1):
        copy.wait()


def combine(y, pos_all, middle, small, slots, cot_slots, gate_low, up_low, hidden_gated, number):
    outer, per, cap, width = y.shape
    span = pos_all.shape[-1]
    block, hidden = gate_low.shape[1:]
    share = hidden // 2
    step = min(512, width)
    tiles = width // step
    vmem = pl.BlockSpec(memory_space=pltpu.VMEM)
    hbm = pl.BlockSpec(memory_space=pltpu.HBM)
    dma = pltpu.SemaphoreType.DMA
    return pl.pallas_call(
        functools.partial(combine_body, per, cap),
        out_shape=(
            jax.ShapeDtypeStruct((span, width), BF16),
            jax.ShapeDtypeStruct((1, small.shape[-1]), F32),
            jax.ShapeDtypeStruct((2, width, share), F32),
            jax.ShapeDtypeStruct((width, share), F32),
        ),
        in_specs=[hbm, vmem, vmem, vmem] + [hbm] * 5,
        out_specs=(vmem, vmem, hbm, hbm),
        scratch_shapes=[
            pltpu.VMEM((span, width), F32),
            pltpu.VMEM((OUTER, per, cap, width), BF16),
            pltpu.VMEM((OUTER - 1, 2, span, width // 2), BF16),
            pltpu.VMEM((OUTER + 1, 2, span, width // 2), BF16),
            pltpu.VMEM((OUTER, block, 3 * share), BF16),
            pltpu.VMEM((OUTER, block, 3 * share), BF16),
            pltpu.VMEM((OUTER, per, cap, step), BF16),
            pltpu.VMEM((step, OUTER * block), BF16),
            pltpu.VMEM((2, step, 3 * share), BF16),
            pltpu.VMEM((tiles, step, 3 * share), BF16),
            pltpu.VMEM((step, 3 * share), F32),
            pltpu.VMEM(small.shape, F32),
            pltpu.VMEM(small.shape[1:], F32),
            pltpu.VMEM(small.shape[1:], F32),
            dma((OUTER - 1, 2)),
            dma((OUTER + 1, 2)),
            dma((OUTER, per)),
            dma((OUTER, per)),
            dma((OUTER,)),
            dma((3, 2)),
            dma,
            dma((tiles,)),
            dma((tiles,)),
            dma((3,)),
            dma((2 * per,)),
            dma((2 * per,)),
            dma((OUTER,)),
            dma((OUTER,)),
        ],
        compiler_params=pltpu.CompilerParams(
            collective_id=number, has_side_effects=True, vmem_limit_bytes=62 << 20
        ),
        name="combine",
    )(y, pos_all, middle, small, slots, cot_slots, gate_low, up_low, hidden_gated)


def weights_body(rows, *refs):
    mats, per = len(SOURCE), 4
    x_refs, y_refs, refs = refs[:4], refs[4 : 4 + mats], refs[4 + mats :]
    w_refs, tok_ref, gain_ref, mg_ref, refs = refs[:3], refs[3], refs[4], refs[5], refs[6:]
    out_ref, tg_ref, gg_ref, refs = refs[0], refs[1], refs[2], refs[3:]
    xbuf, ybuf, keep, sbuf, srecv, ubuf, rbuf, hbuf, obuf, wbuf = refs[:10]
    xs, ys, yr, ss, sr, zs, zr, fs, fr, ws = refs[10:]
    e, c = lax.axis_index("expert"), lax.axis_index("dp")
    z, r = e // per, e % per
    x, y = r % 2, r // 2
    width = y_refs[0].shape[1]
    part = width // 4
    lines = width // OUTER
    peers = [(n, f) for n in range(per) for f in range(2)]
    trade = (y + c * (1 - 2 * y)) * 2 + x + (1 - c) * (1 - 2 * x)
    other = (y + (1 - c) * (1 - 2 * y)) * 2 + x + c * (1 - 2 * x)
    a_bit = (1 - c) * x + c * y
    b_bit = (1 - c) * y + c * x
    quarter = 2 * c + a_bit

    def device(n, f):
        return flip(r, n), (c + f) % 2

    bar = pltpu.get_barrier_semaphore()
    for d in range(1, OUTER):
        pl.semaphore_signal(
            bar, inc=1, device_id=((z + d) % OUTER * per + r, c), device_id_type=MESH
        )
    for n, f in peers[1:]:
        q, k = device(n, f)
        pl.semaphore_signal(bar, inc=1, device_id=(z * per + q, k), device_id_type=MESH)
    pl.semaphore_wait(bar, OUTER - 1 + 2 * per - 1)

    def block(q):
        return pl.ds(pl.multiple_of(q * part, part), part)

    targets = (
        (r, 1 - c, 2 * (1 - c) + (1 - c) * y + c * x),
        (trade, c, 2 * c + 1 - a_bit),
        (other, 1 - c, 2 * (1 - c) + 1 - b_bit),
    )

    def spread(m, i):
        q, k, at = targets[i]
        return pltpu.make_async_remote_copy(
            src_ref=y_refs[m].at[:, block(at)], dst_ref=ybuf.at[m, i + 1],
            send_sem=ys.at[m, i], recv_sem=yr.at[m, i],
            device_id=(z * per + q, k), device_id_type=MESH,
        )

    def swap(m, i):
        return pltpu.make_async_remote_copy(
            src_ref=sbuf.at[m, i], dst_ref=srecv.at[m, i], send_sem=ss.at[m, i],
            recv_sem=sr.at[m, i], device_id=(z * per + other, c), device_id_type=MESH,
        )

    def hop(m, i, j, way):
        return pltpu.make_async_remote_copy(
            src_ref=ubuf.at[m, i], dst_ref=rbuf.at[m, way, j],
            send_sem=zs.at[m, i], recv_sem=zr.at[m, way, j],
            device_id=((z + 1 - 2 * way) * per + r, c), device_id_type=MESH,
        )

    def final(m, t, f):
        there = a_bit + t * (1 - 2 * a_bit)
        core = (c + f) % 2
        q = ((1 - c) * y + c * there) * 2 + (1 - c) * there + c * x
        return pltpu.make_async_remote_copy(
            src_ref=hbuf.at[m, pl.ds(pl.multiple_of((there * 2 + core) * rows, rows), rows)],
            dst_ref=obuf.at[m, quarter], send_sem=fs.at[m, 2 * t + f],
            recv_sem=fr.at[m, quarter], device_id=(z * per + q, core), device_id_type=MESH,
        )

    def landed(m, q):
        return pltpu.make_async_remote_copy(
            src_ref=hbuf.at[m, pl.ds(0, rows)], dst_ref=obuf.at[m, q], send_sem=fs.at[m, 0],
            recv_sem=fr.at[m, q], device_id=(z * per + r, 1 - c), device_id_type=MESH,
        )

    strip = wbuf.shape[1]
    strips = width // strip
    jobs = [(k, q) for k in range(3) for q in range(strips)]

    def fetch(t):
        k, q = jobs[t]
        return pltpu.make_async_copy(
            w_refs[k].at[pl.ds(q * strip, strip)], wbuf.at[t % 2], ws.at[t % 2]
        )

    def pull_back(t):
        k, q = jobs[t]
        if t == 0:
            fetch(0).start()
        if t + 1 < len(jobs):
            fetch(t + 1).start()
        fetch(t).wait()
        got = lax.dot_general(
            y_refs[3 - k][...], wbuf[t % 2], (((1,), (1,)), ((), ())), preferred_element_type=F32
        )
        if k == 0:
            tg_ref[:, q * strip : (q + 1) * strip] = got
        else:
            tg_ref[:, q * strip : (q + 1) * strip] += got

    def norm_back():
        grad = tg_ref[...]
        values = tok_ref[...].astype(F32)
        scale = rms_scale(values)
        normed = values * scale
        gg_ref[...] = jnp.sum(grad * normed, axis=0, keepdims=True)
        grad = grad * gain_ref[...]
        centre = jnp.mean(grad * normed, axis=-1, keepdims=True)
        tg_ref[...] = mg_ref[...] + scale * (grad - normed * centre)

    loads = [pltpu.make_async_copy(x_refs[i], xbuf.at[i], xs.at[i]) for i in range(4)]
    def begin(m):
        for i in range(3):
            spread(m, i).start()

    begin(0)
    begin(1)
    for copy in loads:
        copy.start()
    for m in range(mats):
        ybuf[m, 0] = y_refs[m][:, block(quarter)]
    for copy in loads:
        copy.wait()
    order = [pick(t, z) for t in FAR]

    def pieces(j, bit):
        for t in range(2):
            at = j * lines + (1 - c) * (bit * 2 + t) * 2 * rows + c * (t * 2 + bit) * 2 * rows
            yield pl.ds(pl.multiple_of(at, 2 * rows), 2 * rows)

    def product(m, j, bit):
        total = None
        for i in range(4):
            left = jnp.concatenate([xbuf[i, SOURCE[m], at, :] for at in pieces(j, bit)], axis=0)
            term = jnp.dot(left, ybuf[m, i], preferred_element_type=F32)
            total = term if total is None else total + term
        return total

    edge = jnp.logical_or(z == 0, z == OUTER - 1)

    def outer(m):
        for i, j in enumerate(order):
            swap(m, i).wait_recv()
            ubuf[m, i] = (keep[m, i] + srecv[m, i].astype(F32)).astype(BF16)

            @pl.when(z == 0)
            def _():
                hop(m, i, j, 0).start()

            @pl.when(z > 0)
            def _():
                hop(m, i, j, 1).start()

    def inner(m):
        for i, j in enumerate(order):
            swap(m, i).wait_recv()

            @pl.when(j > z)
            def _():
                hop(m, 0, j, 0).wait_recv()
                ubuf[m, i] = (
                    keep[m, i] + srecv[m, i].astype(F32) + rbuf[m, 0, j].astype(F32)
                ).astype(BF16)
                hop(m, i, j, 0).start()

            @pl.when(j < z)
            def _():
                hop(m, 0, j, 1).wait_recv()
                ubuf[m, i] = (
                    keep[m, i] + srecv[m, i].astype(F32) + rbuf[m, 1, j].astype(F32)
                ).astype(BF16)
                hop(m, i, j, 1).start()

    for m in range(mats + 2):
        if m < mats:
            for i in range(3):
                spread(m, i).wait_recv()
            for i, j in enumerate(order + [z]):
                sbuf[m, i] = product(m, j, 1 - b_bit).astype(BF16)
                swap(m, i).start()
            if m + 2 < mats:
                begin(m + 2)
            for i, j in enumerate(order + [z]):
                keep[m, i] = product(m, j, b_bit)
        if 1 <= m <= mats:
            pl.when(edge)(functools.partial(outer, m - 1))
        if m >= 2:
            pl.when(jnp.logical_not(edge))(functools.partial(inner, m - 2))
        if m < 3:
            for t in range(m * strips, (m + 1) * strips):
                pull_back(t)
        elif m == 3:
            norm_back()

    last = OUTER - 1
    for m in range(mats):
        swap(m, last).wait_recv()
        keep[m, last] += srecv[m, last].astype(F32)

        @pl.when(z > 0)
        def _():
            hop(m, 0, z, 0).wait_recv()
            keep[m, last] += rbuf[m, 0, z].astype(F32)

        @pl.when(z < OUTER - 1)
        def _():
            hop(m, 0, z, 1).wait_recv()
            keep[m, last] += rbuf[m, 1, z].astype(F32)

        hbuf[m] = keep[m, last].astype(BF16)
        for t, f in ((1, 0), (1, 1), (0, 1)):
            final(m, t, f).start()

    for m in range(mats):
        mine = pl.ds(pl.multiple_of((a_bit * 2 + c) * rows, rows), rows)
        out_ref[m, :, block(quarter)] = keep[m, last, mine, :]
        for d in range(1, 4):
            q = (quarter + d) % 4
            landed(m, q).wait_recv()
            out_ref[m, :, block(q)] = obuf[m, q].astype(F32)
    for m in range(mats):
        for i in range(3):
            spread(m, i).wait_send()
        for i in range(OUTER):
            swap(m, i).wait_send()
        for t, f in ((1, 0), (1, 1), (0, 1)):
            final(m, t, f).wait_send()
        for i, j in enumerate(order):
            hop(m, i, j, 0).wait_send()


SOURCE = (1, 0, 0, 0)


def weight_grads(lefts, rights, weights, tokens, gain, middle_grad, experts, number):
    span, width = rights[0].shape
    rows = width // (2 * experts)
    part = width // 4
    half = width // OUTER // 2
    mats = len(rights)
    vmem = pl.BlockSpec(memory_space=pltpu.VMEM)
    hbm = pl.BlockSpec(memory_space=pltpu.HBM)
    dma = pltpu.SemaphoreType.DMA
    return pl.pallas_call(
        functools.partial(weights_body, rows),
        out_shape=(
            jax.ShapeDtypeStruct((mats, rows, width), F32),
            jax.ShapeDtypeStruct((span, width), F32),
            jax.ShapeDtypeStruct((1, width), F32),
        ),
        in_specs=[hbm] * 4 + [vmem] * mats + [hbm] * 3 + [vmem] * 3,
        out_specs=(vmem,) * 3,
        scratch_shapes=[
            pltpu.VMEM((4, 2, width, span), BF16),
            pltpu.VMEM((mats, 4, span, part), BF16),
            pltpu.VMEM((mats, OUTER, half, part), F32),
            pltpu.VMEM((mats, OUTER, half, part), BF16),
            pltpu.VMEM((mats, OUTER, half, part), BF16),
            pltpu.VMEM((mats, OUTER - 1, half, part), BF16),
            pltpu.VMEM((mats, 2, OUTER, half, part), BF16),
            pltpu.VMEM((mats, half, part), BF16),
            pltpu.VMEM((mats, 4, rows, part), BF16),
            pltpu.VMEM((2, width // OUTER // 2, width), BF16),
            dma((4,)),
            dma((mats, 3)),
            dma((mats, 3)),
            dma((mats, OUTER)),
            dma((mats, OUTER)),
            dma((mats, OUTER - 1)),
            dma((mats, 2, OUTER)),
            dma((mats, 4)),
            dma((mats, 4)),
            dma((2,)),
        ],
        compiler_params=pltpu.CompilerParams(
            collective_id=number, has_side_effects=True, vmem_limit_bytes=62 << 20
        ),
        name="weight_grads",
    )(*lefts, *rights, *weights, tokens, gain, middle_grad)


def body(
    tokens,
    cotangent,
    lengths,
    routes,
    attention_gain,
    query_gain,
    key_gain,
    feedforward_gain,
    query_weight,
    key_weight,
    value_weight,
    output_weight,
    router_weight,
    expert_gate_up,
    expert_down,
):
    span, width = tokens.shape
    core = lax.axis_index("dp")
    both = ("expert", "dp")
    devices = lax.axis_size("expert") * 2
    gains = jnp.concatenate([attention_gain, query_gain, key_gain, feedforward_gain])
    packed = jnp.concatenate([router_weight, gains.reshape(4, -1).T], axis=1)
    other = lax.ppermute(packed, both, [(d, d ^ 1) for d in range(devices)])
    packed = jnp.where(
        core == 0,
        jnp.concatenate([packed, other], axis=0),
        jnp.concatenate([other, packed], axis=0),
    )
    router_full, gains = packed[:, :-4], packed[:, -4:].T.astype(F32)
    gain_in, gain_query, gain_key, gain_mid = gains[0], gains[1], gains[2], gains[3]
    experts = router_full.shape[1]
    cap = span * TOP // experts
    per = experts // OUTER

    seq_length = lengths[0]
    index_rows = jnp.arange(span, dtype=jnp.int32)
    expert_ids = jnp.arange(experts, dtype=jnp.int32)
    hits = jnp.any(routes[None, :, :] == expert_ids[:, None, None], axis=-1)
    hits = hits & (index_rows < seq_length)[None, :]
    earlier = (index_rows[:, None] < index_rows[None, :]).astype(BF16)
    before = jnp.dot(hits.astype(BF16), earlier, preferred_element_type=F32)
    kept = hits & (before < cap)
    pos = jnp.where(kept, before, -1.0)
    inputs = tokens.astype(F32)
    cosine_table, sine_table = rotary_tables(index_rows.astype(F32))
    signs = jnp.where(jnp.arange(HD) < HD // 2, -1.0, 1.0)
    key_limit = jnp.minimum(index_rows, seq_length - 1)
    (
        cot_slots, pos_here, pos_all, query_full, key_full, value_full, output_full,
        other_gate_up, other_down, turned,
        normed_in, query_pre, key_pre, query_rot, key_rot, value_all, log_total, attended,
        middle, normed_mid, gates,
    ) = attend(
        tokens, cotangent, pos[:, None, :], gains, (cosine_table, sine_table * signs),
        key_limit.astype(F32)[:, None], router_full,
        (query_weight, key_weight, value_weight, output_weight, expert_gate_up, expert_down),
        cap, 1,
    )
    norm_mid_back = jax.vjp(norm_apply, middle, gain_mid)[1]
    query_back, key_back = [
        jax.vjp(
            lambda projected, gain: rotary_norm(projected, gain, cosine_table, sine_table),
            pre, gain,
        )[1]
        for pre, gain in ((query_pre, gain_query), (key_pre, gain_key))
    ]
    query_rot, key_rot, value_heads = [
        value.reshape(span, NH, HD) for value in (query_rot, key_rot, value_all)
    ]
    allowed = index_rows[None, :] <= key_limit[:, None]
    score_scale = HD ** (-0.5)

    def scores_of():
        raw = jnp.einsum("thd,shd->hts", query_rot, key_rot, preferred_element_type=F32)
        return jnp.where(allowed[None], raw * score_scale, -1e30)

    def mul(left, right, spec):
        return jnp.einsum(spec, left, right, preferred_element_type=F32)

    back_rows, prob_grad, slots, gate_grad_low, up_grad_low, hidden_gated, expert_out = run_experts(
        normed_mid, gates.T[:, None, :], pos_all, pos_here, cot_slots,
        (expert_gate_up, expert_down, other_gate_up, other_down), 2,
    )
    prob_grad = prob_grad[:, 0].T
    back_rows, turned = lax.optimization_barrier((back_rows, turned))
    wide = per == 4 and width % 512 == 0
    if wide:

        def moved(d, cross):
            to = d % 2 ^ cross
            return (d // 2 ^ 1 + to) * 2 + to

        lefts = [turned, lax.ppermute(turned, both, [(d, d ^ 1) for d in range(devices)])] + [
            lax.ppermute(turned, both, [(d, moved(d, cross)) for d in range(devices)])
            for cross in range(2)
        ]

    upstream = cotangent.astype(F32)
    logit_grad = (
        gates * (prob_grad - jnp.sum(gates * prob_grad, axis=-1, keepdims=True))
    ).astype(BF16)
    grad_router = mul(normed_mid, logit_grad, "td,te->de")
    mid_normed_grad = mul(logit_grad, router_full, "te,de->td") + back_rows
    mid_input_grad, grad_mid_gain = norm_mid_back(mid_normed_grad)
    middle_grad = upstream + mid_input_grad
    branch_grad = middle_grad.astype(BF16)
    attended_grad = mul(branch_grad, output_full, "to,io->ti").astype(BF16)
    attended_grad = attended_grad.reshape(span, NH, HD)
    weights_full = jnp.exp(scores_of() - log_total)
    weights_grad = mul(attended_grad, value_heads, "thd,shd->hts")
    value_grad = mul(weights_full.astype(BF16), attended_grad, "hts,thd->shd")
    value_grad = value_grad.reshape(span, width).astype(BF16)
    centre = jnp.sum(weights_full * weights_grad, axis=-1, keepdims=True)
    score_grad = (weights_full * (weights_grad - centre)).astype(BF16)
    query_rot_grad = mul(score_grad, key_rot, "hts,shd->thd").reshape(span, width) * score_scale
    key_rot_grad = mul(score_grad, query_rot, "hts,thd->shd").reshape(span, width) * score_scale
    query_pre_grad, grad_query_gain = query_back(query_rot_grad)
    key_pre_grad, grad_key_gain = key_back(key_rot_grad)
    query_low = query_pre_grad.astype(BF16)
    key_low = key_pre_grad.astype(BF16)
    rights = (branch_grad, value_grad, key_low, query_low)
    if wide:
        expert_out, lefts, rights = lax.optimization_barrier((expert_out, lefts, rights))
        grads, grad_tokens, grad_in_gain = weight_grads(
            lefts, rights, (query_full, key_full, value_full), tokens, gain_in[None],
            middle_grad, experts, 5,
        )
        grad_in_gain = grad_in_gain[0]
    else:
        grads = []
        for source, right in zip(SOURCE, rights):
            grad = jnp.dot(turned[source], right, preferred_element_type=F32).astype(BF16)
            grid = grad.reshape(experts, 2, width // experts // 2, width).swapaxes(0, 1)
            half = lax.psum_scatter(grid, "dp", scatter_dimension=0, tiled=False)
            half = lax.psum_scatter(half, "expert", scatter_dimension=0, tiled=False)
            grads.append(half.astype(F32))
        normed_in_grad = mul(query_low, query_full, "to,io->ti")
        normed_in_grad = normed_in_grad + mul(key_low, key_full, "to,io->ti")
        normed_in_grad = normed_in_grad + mul(value_grad, value_full, "to,io->ti")
        input_grad, grad_in_gain = jax.vjp(norm_apply, inputs, gain_in)[1](normed_in_grad)
        grad_tokens = middle_grad + input_grad

    small = jnp.concatenate(
        [
            jnp.stack([grad_in_gain, grad_query_gain, grad_key_gain, grad_mid_gain]).T,
            grad_router,
        ],
        axis=1,
    )
    kinds = small.shape[1]
    small = small.reshape(OUTER, 2 * per, -1, kinds).transpose(1, 0, 3, 2)
    output, small, grad_gate_up, grad_down = combine(
        expert_out, pos_all, middle, small.reshape(2 * per, OUTER, 1, -1), slots, cot_slots,
        gate_grad_low, up_grad_low, hidden_gated, 4,
    )
    small = small.reshape(kinds, -1).T
    return (
        output,
        grad_tokens,
        small[:, 0],
        small[:, 1],
        small[:, 2],
        small[:, 3],
        grads[3],
        grads[2],
        grads[1],
        grads[0],
        small[:, 4:],
        grad_gate_up[None],
        grad_down[None],
    )


def solution(mesh):
    both = P(("expert", "dp"))
    rows = P(("expert", "dp"), None)
    in_specs = (rows, rows, both, rows) + (P("dp"),) * 4 + (P("dp", None),) * 5 + (
        P("expert", None, None, "dp"),
        P("expert", None, "dp"),
    )
    out_specs = (rows, rows) + (both,) * 4 + (rows,) * 5 + (
        P("expert", None, None, "dp"),
        P("expert", None, "dp"),
    )
    return jax.shard_map(body, mesh=mesh, in_specs=in_specs, out_specs=out_specs, check_vma=False)
```

```python
import functools
import math

import jax
import jax.numpy as jnp
from jax import lax
from jax.experimental import pallas as pl
from jax.experimental.pallas import tpu as pltpu
from jax.sharding import PartitionSpec as P

NH = 16
HD = 128
TOP = 8
OUTER = 4

EPSILON = 1e-05
ROPE_BASE = 10000.0
MESH = pl.DeviceIdType.MESH
F32 = jnp.float32
BF16 = jnp.bfloat16


def rms_scale(values):
    return lax.rsqrt(jnp.mean(values * values, axis=-1, keepdims=True) + EPSILON)


def norm_apply(values, gain_vector):
    return values * rms_scale(values) * gain_vector


def rotary_tables(positions):
    frequencies = 1.0 / ROPE_BASE ** (jnp.arange(0, HD, 2).astype(F32) / HD)
    angles = positions[:, None] * frequencies[None, :]
    angles = jnp.concatenate([angles, angles], axis=-1)
    return (jnp.cos(angles), jnp.sin(angles))


def flip(r, n):
    out, bit = r, 1
    while bit <= n:
        if n & bit:
            out = out + bit - 2 * bit * ((r // bit) % 2)
        bit *= 2
    return out


def pick(table, z):
    code = sum(v * 4**k for k, v in enumerate(table))
    return (code // ((1 + 3 * (z % 2)) * (1 + 15 * (z // 2)))) % 4


NEAR = ((1, 0, 1, 2), (2, 2, 3, 1), (3, 3, 0, 0))
PLACE = ((1, 3, 3, 1), (3, 1, 2, 3), (2, 2, 1, 2))
BLOCK = ((1, 3, 0, 2), (3, 0, 3, 0), (2, 2, 1, 1))
FAR = ((3, 3, 0, 0), (2, 0, 3, 1), (1, 2, 1, 2))


def one_hot(pos_ref, r, j, per, cap):
    span = pos_ref.shape[-1]
    rows = []
    slot = lax.broadcasted_iota(jnp.int32, (cap, span), 0).astype(F32)
    for n in range(per):
        line = pos_ref[j, flip(r, n)]
        rows.append(jnp.where(line == slot, 1.0, 0.0).astype(BF16))
    return jnp.concatenate(rows, axis=0)


def attend_body(per, cap, *refs):
    tok_ref, x_ref, meta_ref, gains_ref, cos_ref, sin_ref, limit_ref, router_ref = refs[:8]
    parts, refs = refs[8:14], refs[14:]
    out_ref, here_ref, pos_ref = refs[:3]
    fulls, refs = refs[3:9], refs[9:]
    turned_ref, nin_ref, qpre, kpre, qrot, krot, val_ref, lse_ref, att_ref, mid_ref = refs[:10]
    nmid_ref, gates_ref, zbuf, sbuf, wbuf, vacc = refs[10:16]
    zs, zr, ps, pr, ls, ms, mr, ts, tr, ds, dr, ks, fs = refs[16:]
    e, c = lax.axis_index("expert"), lax.axis_index("dp")
    z, r = e // per, e % per
    experts = OUTER * per
    bar = pltpu.get_barrier_semaphore()
    for d in range(1, experts):
        pl.semaphore_signal(bar, inc=1, device_id=((e + d) % experts, c), device_id_type=MESH)
    pl.semaphore_signal(bar, inc=1, device_id=(e, 1 - c), device_id_type=MESH)
    pl.semaphore_wait(bar, experts)
    span, width = x_ref.shape
    step = min(512, width)
    half = width // 2

    def share(d):
        to = (e + d) % experts
        return pltpu.make_async_remote_copy(
            src_ref=meta_ref.at[to], dst_ref=here_ref.at[e], send_sem=ms.at[d - 1],
            recv_sem=mr.at[d - 1], device_id=(to, c), device_id_type=MESH,
        )

    def table(d):
        to = (z + d) % OUTER
        return pltpu.make_async_remote_copy(
            src_ref=meta_ref.at[pl.ds(to * per, per)], dst_ref=pos_ref.at[z],
            send_sem=ts.at[d - 1], recv_sem=tr.at[z],
            device_id=(to * per + r, c), device_id_type=MESH,
        )

    def tabled(j):
        return pltpu.make_async_remote_copy(
            src_ref=meta_ref.at[pl.ds(0, per)], dst_ref=pos_ref.at[j], send_sem=ts.at[0],
            recv_sem=tr.at[j], device_id=(j * per + r, c), device_id_type=MESH,
        )

    def up(src, j):
        return pltpu.make_async_remote_copy(
            src_ref=src, dst_ref=zbuf.at[j], send_sem=zs.at[0, j], recv_sem=zr.at[j],
            device_id=((z + 1) * per + r, c), device_id_type=MESH,
        )

    def down(src, j):
        return pltpu.make_async_remote_copy(
            src_ref=src, dst_ref=zbuf.at[j], send_sem=zs.at[1, j], recv_sem=zr.at[j],
            device_id=((z - 1) * per + r, c), device_id_type=MESH,
        )

    def plane(i, j, n):
        return pltpu.make_async_remote_copy(
            src_ref=sbuf.at[i, n], dst_ref=out_ref.at[j, n], send_sem=ps.at[i, n],
            recv_sem=pr.at[i, n], device_id=(z * per + flip(r, n), c), device_id_type=MESH,
        )

    def local(i, j):
        return pltpu.make_async_copy(sbuf.at[i, 0], out_ref.at[j, 0], ls.at[i])

    def lines(owner):
        return pl.ds(pl.multiple_of(owner * half, half), half)

    def give(k):
        return pltpu.make_async_remote_copy(
            src_ref=parts[k], dst_ref=fulls[k].at[lines(c)] if k < 4 else fulls[k], send_sem=ds.at[k],
            recv_sem=dr.at[k], device_id=(e, 1 - c), device_id_type=MESH,
        )

    def hold(t):
        return pltpu.make_async_copy(wbuf.at[t % 2], fulls[jobs[t][0]].at[lines(c)], ks.at[t % 2])

    jobs = [(0, 0), (1, 0), (2, 0), (0, 1), (1, 1), (2, 1), (3, 0), (3, 1)]

    def fetch(t):
        k, far = jobs[t]
        src = fulls[k].at[lines(1 - c)] if far else parts[k]
        return pltpu.make_async_copy(src, wbuf.at[t % 2], fs.at[t % 2])

    def project(t):
        k, far = jobs[t]
        left = att_ref if k == 3 else nin_ref
        into = (qpre, kpre, vacc, mid_ref)[k]
        if t == 3:
            for q in range(2):
                give(q).wait_recv()
                fetch(t + q).start()
        fetch(t).wait()
        if not far:
            hold(t).start()
        mine = lines(1 - c if far else c)

        @pl.loop(0, width // step)
        def _(q):
            columns = pl.ds(pl.multiple_of(q * step, step), step)
            got = jnp.dot(left[:, mine], wbuf[t % 2, :, columns], preferred_element_type=F32)
            if k == 3 and not far:
                into[:, columns] = tok_ref[:, columns].astype(F32) + got
            elif far:
                into[:, columns] += got
            else:
                into[:, columns] = got

        if not far:
            hold(t).wait()
        if t in (0, 4):
            fetch(t + 2).start()
        elif t in (3, 5):
            give(jobs[t + 2][0]).wait_recv()
            fetch(t + 2).start()

    order = [z] + [pick(t, z) for t in NEAR]

    edge = jnp.logical_or(z == 0, z == OUTER - 1)

    def relay(places):
        @pl.when(jnp.logical_not(edge))
        def _():
            for i in places:
                j = order[i]
                up(x_ref, j).wait_recv()

                @pl.when(j < z)
                def _():
                    up(zbuf.at[j], j).start()

                @pl.when(j > z)
                def _():
                    down(zbuf.at[j], j).start()

    def choose(i, j):
        block = x_ref if i == 0 else zbuf.at[j]
        if i > 0:

            @pl.when(edge)
            def _():
                up(x_ref, j).wait_recv()

            tabled(j).wait_recv()

        marks = one_hot(pos_ref, r, j, per, cap)

        @pl.loop(0, width // step)
        def _(k):
            columns = pl.ds(pl.multiple_of(k * step, step), step)
            got = jnp.dot(marks, block[:, columns], preferred_element_type=F32).astype(BF16)
            for n in range(per):
                sbuf[i, n, :, columns] = got[n * cap : (n + 1) * cap]

        for n in range(1, per):
            plane(i, j, n).start()
        local(i, j).start()

    for d in range(1, OUTER):
        table(d).start()

    @pl.when(z < OUTER - 1)
    def _():
        up(x_ref, z).start()

    @pl.when(z > 0)
    def _():
        down(x_ref, z).start()

    fetch(0).start()
    fetch(1).start()
    pos_ref[z] = meta_ref[pl.ds(z * per, per)]
    here_ref[e] = meta_ref[e]
    choose(0, z)
    for k in range(6):
        give(k).start()
    for d in range(1, experts):
        share(d).start()

    inputs = tok_ref[...].astype(F32)
    nin_ref[...] = norm_apply(inputs, gains_ref[0:1]).astype(BF16)
    for t in range(3):
        project(t)
    relay((1, 2))
    choose(1, order[1])
    for t in range(3, 6):
        project(t)
    val_ref[...] = vacc[...].astype(BF16)
    query_scale = rms_scale(qpre[...])
    key_scale = rms_scale(kpre[...])
    turned_ref[0] = nin_ref[...].T
    score_scale = HD ** (-0.5)
    column = lax.broadcasted_iota(jnp.int32, (span, span), 1).astype(F32)

    def heads(first, last):
        @pl.loop(first, last)
        def _(h):
            columns = pl.ds(pl.multiple_of(h * HD, HD), HD)

            def turn(pre, scale, row):
                normed = pre[:, columns] * scale * gains_ref[row : row + 1, columns]
                return (
                    normed * cos_ref[...] + pltpu.roll(normed, HD // 2, 1) * sin_ref[...]
                ).astype(BF16)

            query = turn(qpre, query_scale, 1)
            key = turn(kpre, key_scale, 2)
            qrot[:, columns] = query
            krot[:, columns] = key
            scores = lax.dot_general(
                query, key, (((1,), (1,)), ((), ())), preferred_element_type=F32
            )
            scores = jnp.where(column <= limit_ref[...], scores * score_scale, -1e30)
            peak = jnp.max(scores, axis=-1, keepdims=True)
            total = peak + jnp.log(jnp.sum(jnp.exp(scores - peak), axis=-1, keepdims=True))
            lse_ref[h] = total
            weights = jnp.exp(scores - total).astype(BF16)
            att_ref[:, columns] = jnp.dot(
                weights, val_ref[:, columns], preferred_element_type=F32
            ).astype(BF16)

    heads(0, NH // 2)
    choose(2, order[2])
    relay((3,))
    heads(NH // 2, NH)
    project(6)
    choose(3, order[3])
    project(7)
    turned_ref[1] = att_ref[...].T
    middle = mid_ref[...]
    nmid_ref[...] = norm_apply(middle, gains_ref[3:4]).astype(BF16)
    logits = jnp.dot(nmid_ref[...], router_ref[...], preferred_element_type=F32)
    raised = jnp.exp(logits - jnp.max(logits, axis=-1, keepdims=True))
    gates_ref[...] = raised / jnp.sum(raised, axis=-1, keepdims=True)

    for i, j in enumerate(order):
        local(i, j).wait()
        for n in range(1, per):
            plane(i, j, n).wait()

    @pl.when(z < OUTER - 1)
    def _():
        up(x_ref, z).wait_send()

    @pl.when(z > 0)
    def _():
        down(x_ref, z).wait_send()

    for j in order[1:]:

        @pl.when(jnp.logical_and(j < z, z < OUTER - 1))
        def _():
            up(zbuf.at[j], j).wait_send()

        @pl.when(jnp.logical_and(j > z, z > 0))
        def _():
            down(zbuf.at[j], j).wait_send()

    for d in range(1, experts):
        share(d).wait()
    for d in range(1, OUTER):
        table(d).wait_send()
    for k in range(6):
        give(k).wait_send()
    for k in range(4, 6):
        give(k).wait_recv()


def attend(tokens, cotangent, meta, gains, tables, limit, router, parts, cap, number):
    experts, _, span = meta.shape
    per = experts // OUTER
    width = tokens.shape[1]
    half = parts[0].shape[0]
    vmem = pl.BlockSpec(memory_space=pltpu.VMEM)
    hbm = pl.BlockSpec(memory_space=pltpu.HBM)
    dma = pltpu.SemaphoreType.DMA
    low = jax.ShapeDtypeStruct((span, width), BF16)
    high = jax.ShapeDtypeStruct((span, width), F32)
    return pl.pallas_call(
        functools.partial(attend_body, per, cap),
        out_shape=(
            jax.ShapeDtypeStruct((OUTER, per, cap, width), BF16),
            jax.ShapeDtypeStruct((experts, 1, span), F32),
            jax.ShapeDtypeStruct((OUTER, per, 1, span), F32),
        )
        + (jax.ShapeDtypeStruct((2 * half, width), BF16),) * 4
        + tuple(jax.ShapeDtypeStruct(part.shape, BF16) for part in parts[4:])
        + (jax.ShapeDtypeStruct((2, width, span), BF16), low, high, high, low, low, low)
        + (jax.ShapeDtypeStruct((NH, span, 1), F32), low, high, low)
        + (jax.ShapeDtypeStruct((span, experts), F32),),
        in_specs=[vmem] * 8 + [hbm] * 6,
        out_specs=(hbm, vmem, vmem) + (hbm,) * 6 + (vmem,) * 12,
        scratch_shapes=[
            pltpu.VMEM((OUTER, span, width), BF16),
            pltpu.VMEM((OUTER, per, cap, width), BF16),
            pltpu.VMEM((2, half, width), BF16),
            pltpu.VMEM((span, width), F32),
            dma((2, OUTER)),
            dma((OUTER,)),
            dma((OUTER, per)),
            dma((OUTER, per)),
            dma((OUTER,)),
            dma((experts,)),
            dma((experts,)),
            dma((OUTER,)),
            dma((OUTER,)),
            dma((6,)),
            dma((6,)),
            dma((2,)),
            dma((2,)),
        ],
        compiler_params=pltpu.CompilerParams(
            collective_id=number, has_side_effects=True, vmem_limit_bytes=60 << 20
        ),
        name="attend",
    )(tokens, cotangent, meta, gains, *tables, limit, router, *parts)


def experts_body(per, cap, *refs):
    x_ref, gates_ref, pos_ref, posh_ref, cot_ref, gu_mine, dn_mine, gu_other, dn_other = refs[:9]
    refs = refs[1:]
    back_ref, pg_ref, out_ref, gl_ref, ul_ref, hg_ref, eo_ref = refs[8:15]
    zbuf, sbuf, wg, wu, wd, slb, ctb, glb, ulb, hlb, hgb, eob, ybuf, ubuf, rbuf = refs[15:30]
    here, ggv, sgv, tgv = refs[30:34]
    zs, zr, ps, pr, ls, ms, mr, ws, cs, os, es, bs, br, us, ur, gs, gr = refs[34:]
    e, c = lax.axis_index("expert"), lax.axis_index("dp")
    z, r = e // per, e % per
    experts = OUTER * per
    bar = pltpu.get_barrier_semaphore()
    for d in range(1, experts):
        pl.semaphore_signal(bar, inc=1, device_id=((e + d) % experts, c), device_id_type=MESH)
    pl.semaphore_wait(bar, experts - 1)
    span, width = x_ref.shape
    hidden = wg.shape[1]
    step = min(512, width)
    thin = min(256, hidden)
    halves = 2
    half = width // halves

    def share(d):
        to = (e + d) % experts
        return pltpu.make_async_remote_copy(
            src_ref=gates_ref.at[to], dst_ref=here.at[e], send_sem=ms.at[d - 1],
            recv_sem=mr.at[d - 1], device_id=(to, c), device_id_type=MESH,
        )

    def up(src, j):
        return pltpu.make_async_remote_copy(
            src_ref=src, dst_ref=zbuf.at[j], send_sem=zs.at[0, j], recv_sem=zr.at[j],
            device_id=((z + 1) * per + r, c), device_id_type=MESH,
        )

    def down(src, j):
        return pltpu.make_async_remote_copy(
            src_ref=src, dst_ref=zbuf.at[j], send_sem=zs.at[1, j], recv_sem=zr.at[j],
            device_id=((z - 1) * per + r, c), device_id_type=MESH,
        )

    def plane(i, j, n):
        return pltpu.make_async_remote_copy(
            src_ref=sbuf.at[i, n], dst_ref=out_ref.at[j, n], send_sem=ps.at[i, n],
            recv_sem=pr.at[i, n], device_id=(z * per + flip(r, n), c), device_id_type=MESH,
        )

    def local(i, j):
        return pltpu.make_async_copy(sbuf.at[i, 0], out_ref.at[j, 0], ls.at[i])

    def returned(i, n):
        return pltpu.make_async_remote_copy(
            src_ref=sbuf.at[i, n], dst_ref=ybuf.at[i, n - 1], send_sem=bs.at[i, n],
            recv_sem=br.at[i, n], device_id=(z * per + flip(r, n), c), device_id_type=MESH,
        )

    def part(h):
        return pl.ds(h * half, half)

    def rise(i, j, h, slot):
        return pltpu.make_async_remote_copy(
            src_ref=ubuf.at[i, h], dst_ref=rbuf.at[slot, h], send_sem=us.at[i, h],
            recv_sem=ur.at[slot, h], device_id=((z + 1) * per + r, c), device_id_type=MESH,
        )

    def fall(i, j, h, slot):
        return pltpu.make_async_remote_copy(
            src_ref=ubuf.at[i, h], dst_ref=rbuf.at[slot, h], send_sem=us.at[i, h],
            recv_sem=ur.at[slot, h], device_id=((z - 1) * per + r, c), device_id_type=MESH,
        )

    def graded(i, n, seq):
        return pltpu.make_async_remote_copy(
            src_ref=tgv.at[i, n], dst_ref=pg_ref.at[e], send_sem=gs.at[i, n],
            recv_sem=gr.at[e], device_id=(seq, c), device_id_type=MESH,
        )

    def grade(s):
        return pltpu.make_async_remote_copy(
            src_ref=tgv.at[0, 0], dst_ref=pg_ref.at[s], send_sem=gs.at[0, 0],
            recv_sem=gr.at[s], device_id=(s, c), device_id_type=MESH,
        )

    def columns_of(owner):
        return pl.ds(pl.multiple_of(owner * (hidden // 2), hidden // 2), hidden // 2)

    weights = [
        pltpu.make_async_copy(src, dst.at[:, columns_of(owner)], ws.at[k, f])
        for f, (owner, both, down_part) in enumerate(
            ((c, gu_mine, dn_mine), (1 - c, gu_other, dn_other))
        )
        for k, (src, dst) in enumerate(
            ((both.at[0, 0], wg), (both.at[0, 1], wu), (down_part.at[0], wd))
        )
    ]

    def pull(j):
        return pltpu.make_async_copy(cot_ref.at[j], ctb, cs)

    for d in range(1, experts):
        share(d).start()

    @pl.when(z < OUTER - 1)
    def _():
        up(x_ref, z).start()

    @pl.when(z > 0)
    def _():
        down(x_ref, z).start()

    here[e] = gates_ref[e]
    order = [z] + [pick(t, z) for t in NEAR]

    edge = jnp.logical_or(z == 0, z == OUTER - 1)

    def relay(places):
        @pl.when(jnp.logical_not(edge))
        def _():
            for i in places:
                j = order[i]
                up(x_ref, j).wait_recv()

                @pl.when(j < z)
                def _():
                    up(zbuf.at[j], j).start()

                @pl.when(j > z)
                def _():
                    down(zbuf.at[j], j).start()

    def choose(i, j):
        block = x_ref if i == 0 else zbuf.at[j]
        if i > 0:

            @pl.when(edge)
            def _():
                up(x_ref, j).wait_recv()

        marks = one_hot(pos_ref, r, j, per, cap)

        @pl.loop(0, width // step)
        def _(k):
            columns = pl.ds(pl.multiple_of(k * step, step), step)
            got = jnp.dot(marks, block[:, columns], preferred_element_type=F32).astype(BF16)
            for n in range(per):
                sbuf[i, n, :, columns] = got[n * cap : (n + 1) * cap]

        for n in range(1, per):
            plane(i, j, n).start()
        local(i, j).start()

    def outs(j):
        return [
            pltpu.make_async_copy(src, dst.at[j], os.at[k])
            for k, (src, dst) in enumerate(((glb, gl_ref), (ulb, ul_ref), (hgb, hg_ref)))
        ]

    def away(j):
        return pltpu.make_async_copy(eob, eo_ref.at[j], es)

    def marked(j, n):
        slot = lax.broadcasted_iota(jnp.int32, (cap, span), 0).astype(F32)
        return posh_ref[j * per + flip(r, n)] == slot

    def expert(i, j):
        for n in range(1, per):
            plane(i, j, n).wait()
        local(i, j).wait()
        if i == OUTER - 1:
            send_back(1)
        fetch = pltpu.make_async_copy(out_ref.at[j], slb, ls.at[OUTER])
        fetch.start()
        slot_gate = jnp.concatenate(
            [
                jnp.sum(
                    jnp.where(marked(j, n), here[j * per + flip(r, n)], 0.0), axis=1, keepdims=True
                )
                for n in range(per)
            ],
            axis=0,
        )
        sgv[i % 2] = slot_gate
        ggv[i % 2] = jnp.zeros(ggv.shape[1:], F32)
        pull(j).wait()
        fetch.wait()
        if i > 0:
            for copy in outs(order[i - 1]):
                copy.wait()

        @pl.loop(0, hidden // thin)
        def _(k):
            columns = pl.ds(pl.multiple_of(k * thin, thin), thin)
            rows = slb[...].reshape(per * cap, width)
            gate_pre = jnp.dot(rows, wg[:, columns], preferred_element_type=F32)
            up_pre = jnp.dot(rows, wu[:, columns], preferred_element_type=F32)
            pulled = jnp.dot(
                ctb[...].reshape(per * cap, width), wd[:, columns], preferred_element_type=F32
            )
            sigmoid_gate = jax.nn.sigmoid(gate_pre)
            silu_gate = gate_pre * sigmoid_gate
            low = (silu_gate * up_pre).astype(BF16)
            wide = low.astype(F32)
            ggv[i % 2] += jnp.sum(wide * pulled, axis=1, keepdims=True)
            hidden_grad = pulled * slot_gate
            glb[:, columns] = (
                hidden_grad * up_pre * sigmoid_gate * (1.0 + gate_pre * (1.0 - sigmoid_gate))
            ).astype(BF16)
            ulb[:, columns] = (hidden_grad * silu_gate).astype(BF16)
            hlb[i % 2, :, columns] = low
            hgb[:, columns] = (wide * slot_gate).astype(BF16)

        if i < OUTER - 1:
            pull(order[i + 1]).start()
        for copy in outs(j):
            copy.start()

        @pl.loop(0, width // step)
        def _(k):
            columns = pl.ds(pl.multiple_of(k * step, step), step)
            got = lax.dot_general(
                glb[...], wg[columns, :], (((1,), (1,)), ((), ())), preferred_element_type=F32
            ) + lax.dot_general(
                ulb[...], wu[columns, :], (((1,), (1,)), ((), ())), preferred_element_type=F32
            )
            got = got.astype(BF16)
            for n in range(per):
                sbuf[i, n, :, columns] = got[n * cap : (n + 1) * cap]

    def send_back(i):
        for n in range(1, per):
            returned(i, n).start()

    def finish(i, j):
        for n in range(per):
            seq = j * per + flip(r, n)
            row = jnp.sum(
                jnp.where(marked(j, n), ggv[i % 2, n * cap : (n + 1) * cap], 0.0),
                axis=0,
                keepdims=True,
            )
            tgv[i, n] = row
            if i == 0 and n == 0:
                pg_ref[e] = row
            else:
                graded(i, n, seq).start()
        if i > 0:
            away(order[i - 1]).wait()

        @pl.loop(0, width // step)
        def _(k):
            columns = pl.ds(pl.multiple_of(k * step, step), step)
            got = lax.dot_general(
                hlb[i % 2], wd[columns, :], (((1,), (1,)), ((), ())), preferred_element_type=F32
            )
            got = (got * sgv[i % 2]).astype(BF16)
            for n in range(per):
                eob[n, :, columns] = got[n * cap : (n + 1) * cap]

        away(j).start()

    choose(0, z)
    for copy in weights:
        copy.start()
    pull(z).start()
    relay((1, 2))
    choose(1, order[1])
    for copy in weights:
        copy.wait()
    for d in range(1, experts):
        share(d).wait()
    last = OUTER - 1
    for i in range(last):
        expert(i, order[i])
        if i + 2 <= last:
            choose(i + 2, order[i + 2])
            if i == 0:
                relay((3,))
            finish(i, order[i])
    expert(last, order[last])
    for i in (last, last - 1, 0):
        send_back(i)
    finish(last - 1, order[last - 1])

    def fold(i, j, h):
        marks = one_hot(pos_ref, r, j, per, cap)

        @pl.loop(0, half // step)
        def _(k):
            columns = pl.ds(pl.multiple_of(h * half + k * step, step), step)
            rows = jnp.concatenate(
                [ybuf[i, n - 1, :, columns] if n else sbuf[i, 0, :, columns] for n in range(per)],
                axis=0,
            )
            back_ref[:, columns] = lax.dot_general(
                marks, rows, (((0,), (0,)), ((), ())), preferred_element_type=F32
            )

    for p in range(last):
        i, j = pick(PLACE[p], z), pick(BLOCK[p], z)
        for n in range(1, per):
            returned(i, n).wait_recv()
        for h in range(halves):
            fold(i, j, h)

            @pl.when(jnp.logical_and(j > z, z > 0))
            def _():
                rise(0, j, h, j).wait_recv()
                back_ref[:, part(h)] += rbuf[j, h].astype(F32)

            @pl.when(jnp.logical_and(j < z, z < OUTER - 1))
            def _():
                fall(0, j, h, j).wait_recv()
                back_ref[:, part(h)] += rbuf[j, h].astype(F32)

            ubuf[p, h] = back_ref[:, part(h)].astype(BF16)

            @pl.when(j > z)
            def _():
                rise(p, j, h, j).start()

            @pl.when(jnp.logical_and(j < z, z - j > 1))
            def _():
                fall(p, j, h, j).start()

            @pl.when(z - j == 1)
            def _():
                fall(p, j, h, OUTER).start()

        if p == 0:
            finish(last, order[last])

    for n in range(1, per):
        returned(0, n).wait_recv()
    for h in range(halves):
        fold(0, z, h)

        @pl.when(z > 0)
        def _():
            rise(0, z, h, z).wait_recv()
            back_ref[:, part(h)] += rbuf[z, h].astype(F32)

        @pl.when(z < OUTER - 1)
        def _():
            fall(0, z, h, OUTER).wait_recv()
            back_ref[:, part(h)] += rbuf[OUTER, h].astype(F32)

    @pl.when(z < OUTER - 1)
    def _():
        up(x_ref, z).wait_send()

    @pl.when(z > 0)
    def _():
        down(x_ref, z).wait_send()

    for i, j in enumerate(order):
        for n in range(1, per):
            returned(i, n).wait_send()
        if i > 0:

            @pl.when(jnp.logical_and(j < z, z < OUTER - 1))
            def _():
                up(zbuf.at[j], j).wait_send()

            @pl.when(jnp.logical_and(j > z, z > 0))
            def _():
                down(zbuf.at[j], j).wait_send()

            for h in range(halves):
                rise(i - 1, j, h, j).wait_send()
        for n in range(per):
            if i or n:
                graded(i, n, j * per + flip(r, n)).wait_send()
    for d in range(1, experts):
        grade((e + d) % experts).wait_recv()
    for copy in outs(order[last]):
        copy.wait()
    away(order[last]).wait()


def run_experts(x, gates, pos, pos_here, cot_slots, weights, number):
    experts, _, span = gates.shape
    outer, per, cap, width = cot_slots.shape
    hidden = 2 * weights[0].shape[-1]
    block = per * cap
    vmem = pl.BlockSpec(memory_space=pltpu.VMEM)
    hbm = pl.BlockSpec(memory_space=pltpu.HBM)
    dma = pltpu.SemaphoreType.DMA
    rows = jax.ShapeDtypeStruct((OUTER, per, cap, width), BF16)
    thin = jax.ShapeDtypeStruct((OUTER, block, hidden), BF16)
    return pl.pallas_call(
        functools.partial(experts_body, per, cap),
        out_shape=(
            jax.ShapeDtypeStruct((span, width), F32),
            jax.ShapeDtypeStruct((experts, 1, span), F32),
            rows, thin, thin, thin, rows,
        ),
        in_specs=[vmem] * 4 + [hbm] * 5,
        out_specs=(vmem, vmem) + (hbm,) * 5,
        scratch_shapes=[
            pltpu.VMEM((OUTER, span, width), BF16),
            pltpu.VMEM((OUTER, per, cap, width), BF16),
            pltpu.VMEM((width, hidden), BF16),
            pltpu.VMEM((width, hidden), BF16),
            pltpu.VMEM((width, hidden), BF16),
            pltpu.VMEM((per, cap, width), BF16),
            pltpu.VMEM((per, cap, width), BF16),
            pltpu.VMEM((block, hidden), BF16),
            pltpu.VMEM((block, hidden), BF16),
            pltpu.VMEM((2, block, hidden), BF16),
            pltpu.VMEM((block, hidden), BF16),
            pltpu.VMEM((per, cap, width), BF16),
            pltpu.VMEM((OUTER, per - 1, cap, width), BF16),
            pltpu.VMEM((OUTER - 1, 2, span, width // 2), BF16),
            pltpu.VMEM((OUTER + 1, 2, span, width // 2), BF16),
            pltpu.VMEM((experts, 1, span), F32),
            pltpu.VMEM((2, block, 1), F32),
            pltpu.VMEM((2, block, 1), F32),
            pltpu.VMEM((OUTER, per, 1, span), F32),
            dma((2, OUTER)),
            dma((OUTER,)),
            dma((OUTER, per)),
            dma((OUTER, per)),
            dma((OUTER + 1,)),
            dma((experts,)),
            dma((experts,)),
            dma((3, 2)),
            dma,
            dma((3,)),
            dma,
            dma((OUTER, per)),
            dma((OUTER, per)),
            dma((OUTER - 1, 2)),
            dma((OUTER + 1, 2)),
            dma((OUTER, per)),
            dma((experts,)),
        ],
        compiler_params=pltpu.CompilerParams(
            collective_id=number, has_side_effects=True, vmem_limit_bytes=62 << 20
        ),
        name="experts",
    )(x, gates, pos, pos_here, cot_slots, *weights)


def combine_body(per, cap, *refs):
    y_ref, pos_ref, mid_ref, small_ref, slots_ref, cot_ref, gl_ref, ul_ref, hg_ref = refs[:9]
    res_ref, total_ref, gu_ref, dn_ref, out_ref, ybuf, ubuf, rbuf = refs[9:17]
    theirs, ours, lbuf, lturn, tbuf, rx, stage, lall, lsum, lz = refs[17:27]
    zs, zr, ps, pr, ls, rs, ws, ds, dr, gs, las, lar, tas, tar = refs[27:]
    e, c = lax.axis_index("expert"), lax.axis_index("dp")
    z, r = e // per, e % per
    bar = pltpu.get_barrier_semaphore()
    for d in range(1, OUTER):
        pl.semaphore_signal(
            bar, inc=1, device_id=((z + d) % OUTER * per + r, c), device_id_type=MESH
        )
    peers = [(n, f) for n in range(per) for f in range(2)]

    def device(n, f):
        return flip(r, n), (c + f) % 2

    for n, f in peers[1:]:
        q, k = device(n, f)
        pl.semaphore_signal(bar, inc=1, device_id=(z * per + q, k), device_id_type=MESH)
    pl.semaphore_wait(bar, OUTER - 1 + 2 * per - 1)
    span, width = out_ref.shape
    step = min(512, width)
    share = dn_ref.shape[1]
    thin = min(256, share)
    total = OUTER * per * cap

    def plane(i, j, n):
        return pltpu.make_async_remote_copy(
            src_ref=y_ref.at[j, n], dst_ref=ybuf.at[i, n], send_sem=ps.at[i, n],
            recv_sem=pr.at[i, n], device_id=(z * per + flip(r, n), c), device_id_type=MESH,
        )

    def local(i, j):
        return pltpu.make_async_copy(y_ref.at[j, 0], ybuf.at[i, 0], ls.at[i])

    halves = 2
    half = width // halves

    def part(h):
        return pl.ds(h * half, half)

    def rise(i, h, slot):
        return pltpu.make_async_remote_copy(
            src_ref=ubuf.at[i, h], dst_ref=rbuf.at[slot, h], send_sem=zs.at[i, h],
            recv_sem=zr.at[slot, h], device_id=((z + 1) * per + r, c), device_id_type=MESH,
        )

    def fall(i, h, slot):
        return pltpu.make_async_remote_copy(
            src_ref=ubuf.at[i, h], dst_ref=rbuf.at[slot, h], send_sem=zs.at[i, h],
            recv_sem=zr.at[slot, h], device_id=((z - 1) * per + r, c), device_id_type=MESH,
        )

    def rights(k, src, other):
        owner = 1 - c if other else c
        return pltpu.make_async_copy(
            src.at[:, :, pl.ds(pl.multiple_of(owner * share, share), share)],
            (theirs if other else ours).at[:, :, pl.ds(k * share, share)],
            rs.at[k, int(other)],
        )

    def across(k):
        return pltpu.make_async_remote_copy(
            src_ref=tbuf.at[k % 2], dst_ref=rx.at[k], send_sem=ds.at[k], recv_sem=dr.at[k],
            device_id=(e, 1 - c), device_id_type=MESH,
        )

    def stores(k):
        lines = pl.ds(k * step, step)
        return [
            pltpu.make_async_copy(
                stage.at[:, pl.ds(m * share, share)],
                dn_ref.at[lines] if m == 2 else gu_ref.at[m, lines],
                gs.at[m],
            )
            for m in range(3)
        ]

    def little(i):
        q, k = device(*peers[i])
        return pltpu.make_async_remote_copy(
            src_ref=small_ref.at[q * 2 + k], dst_ref=lall.at[i], send_sem=las.at[i],
            recv_sem=lar.at[i], device_id=(z * per + q, k), device_id_type=MESH,
        )

    def tall(d):
        to = (z + d) % OUTER
        return pltpu.make_async_remote_copy(
            src_ref=lsum.at[to], dst_ref=lz.at[d], send_sem=tas.at[d], recv_sem=tar.at[d],
            device_id=(to * per + r, c), device_id_type=MESH,
        )

    sources = (gl_ref, ul_ref, hg_ref)
    loads = [rights(k, src, other) for k, src in enumerate(sources) for other in (True, False)]

    def tile(k):
        if k == 0:
            for copy in loads:
                copy.wait()
        if k >= 2:
            across(k - 2).wait_send()
        if k >= 1:
            for copy in stores(k - 1):
                copy.wait()
        for src, first, count in ((slots_ref, 0, 2), (cot_ref, 2, 1)):
            fetch = pltpu.make_async_copy(
                src.at[:, :, :, pl.ds(k * step, step)], lbuf, ws
            )
            fetch.start()
            fetch.wait()
            lturn[...] = lbuf[...].reshape(total, step).T

            @pl.loop(0, count * share // thin)
            def _(q):
                at = pl.ds(pl.multiple_of(first * share + q * thin, thin), thin)
                tbuf[k % 2, :, at] = jnp.dot(
                    lturn[...], theirs[:, :, at].reshape(total, thin), preferred_element_type=F32
                ).astype(BF16)
                stage[:, at] = jnp.dot(
                    lturn[...], ours[:, :, at].reshape(total, thin), preferred_element_type=F32
                )

        across(k).start()
        across(k).wait_recv()
        stage[...] += rx[k].astype(F32)
        for copy in stores(k):
            copy.start()

    order = [pick(t, z) for t in FAR] + [z]
    for i, j in enumerate(order):
        for n in range(1, per):
            plane(i, j, n).start()
        local(i, j).start()
    for copy in loads:
        copy.start()
    for i in range(1, 2 * per):
        little(i).start()
    lall[0] = small_ref[r * 2 + c]
    tiles = width // step
    done = 0
    for i, j in enumerate(order):
        while done < tiles * (1, 2, 3, 4)[i] // 4:
            tile(done)
            done += 1
        if i == OUTER - 1:
            for k in range(1, 2 * per):
                little(k).wait_recv()
            lsum[...] = sum(lall[k] for k in range(2 * per))
            for d in range(1, OUTER):
                tall(d).start()
        marks = one_hot(pos_ref, r, j, per, cap)
        local(i, j).wait()
        for n in range(1, per):
            plane(i, j, n).wait_recv()
        for h in range(halves):

            @pl.loop(0, half // step)
            def _(k):
                columns = pl.ds(pl.multiple_of(h * half + k * step, step), step)
                rows = jnp.concatenate([ybuf[i, n, :, columns] for n in range(per)], axis=0)
                out_ref[:, columns] = lax.dot_general(
                    marks, rows, (((0,), (0,)), ((), ())), preferred_element_type=F32
                )

            if i < OUTER - 1:

                @pl.when(jnp.logical_and(j > z, z > 0))
                def _():
                    rise(0, h, j).wait_recv()
                    out_ref[:, part(h)] += rbuf[j, h].astype(F32)

                @pl.when(jnp.logical_and(j < z, z < OUTER - 1))
                def _():
                    fall(0, h, j).wait_recv()
                    out_ref[:, part(h)] += rbuf[j, h].astype(F32)

                ubuf[i, h] = out_ref[:, part(h)].astype(BF16)

                @pl.when(j > z)
                def _():
                    rise(i, h, j).start()

                @pl.when(jnp.logical_and(j < z, z - j > 1))
                def _():
                    fall(i, h, j).start()

                @pl.when(z - j == 1)
                def _():
                    fall(i, h, OUTER).start()
            else:

                @pl.when(z > 0)
                def _():
                    rise(0, h, z).wait_recv()
                    out_ref[:, part(h)] += rbuf[z, h].astype(F32)

                @pl.when(z < OUTER - 1)
                def _():
                    fall(0, h, OUTER).wait_recv()
                    out_ref[:, part(h)] += rbuf[OUTER, h].astype(F32)

                res_ref[:, part(h)] = (mid_ref[:, part(h)] + out_ref[:, part(h)]).astype(BF16)

    for i, j in enumerate(order):
        for n in range(1, per):
            plane(i, j, n).wait_send()
        if i < OUTER - 1:
            for h in range(halves):
                rise(i, h, j).wait_send()
    for d in range(1, OUTER):
        tall(d).wait()
    total_ref[...] = lsum[z] + sum(lz[d] for d in range(1, OUTER))
    for i in range(1, 2 * per):
        little(i).wait_send()
    for k in range(max(0, tiles - 2), tiles):
        across(k).wait_send()
    for copy in stores(tiles - 1):
        copy.wait()


def combine(y, pos_all, middle, small, slots, cot_slots, gate_low, up_low, hidden_gated, number):
    outer, per, cap, width = y.shape
    span = pos_all.shape[-1]
    block, hidden = gate_low.shape[1:]
    share = hidden // 2
    step = min(512, width)
    tiles = width // step
    vmem = pl.BlockSpec(memory_space=pltpu.VMEM)
    hbm = pl.BlockSpec(memory_space=pltpu.HBM)
    dma = pltpu.SemaphoreType.DMA
    return pl.pallas_call(
        functools.partial(combine_body, per, cap),
        out_shape=(
            jax.ShapeDtypeStruct((span, width), BF16),
            jax.ShapeDtypeStruct((1, small.shape[-1]), F32),
            jax.ShapeDtypeStruct((2, width, share), F32),
            jax.ShapeDtypeStruct((width, share), F32),
        ),
        in_specs=[hbm, vmem, vmem, vmem] + [hbm] * 5,
        out_specs=(vmem, vmem, hbm, hbm),
        scratch_shapes=[
            pltpu.VMEM((span, width), F32),
            pltpu.VMEM((OUTER, per, cap, width), BF16),
            pltpu.VMEM((OUTER - 1, 2, span, width // 2), BF16),
            pltpu.VMEM((OUTER + 1, 2, span, width // 2), BF16),
            pltpu.VMEM((OUTER, block, 3 * share), BF16),
            pltpu.VMEM((OUTER, block, 3 * share), BF16),
            pltpu.VMEM((OUTER, per, cap, step), BF16),
            pltpu.VMEM((step, OUTER * block), BF16),
            pltpu.VMEM((2, step, 3 * share), BF16),
            pltpu.VMEM((tiles, step, 3 * share), BF16),
            pltpu.VMEM((step, 3 * share), F32),
            pltpu.VMEM(small.shape, F32),
            pltpu.VMEM(small.shape[1:], F32),
            pltpu.VMEM(small.shape[1:], F32),
            dma((OUTER - 1, 2)),
            dma((OUTER + 1, 2)),
            dma((OUTER, per)),
            dma((OUTER, per)),
            dma((OUTER,)),
            dma((3, 2)),
            dma,
            dma((tiles,)),
            dma((tiles,)),
            dma((3,)),
            dma((2 * per,)),
            dma((2 * per,)),
            dma((OUTER,)),
            dma((OUTER,)),
        ],
        compiler_params=pltpu.CompilerParams(
            collective_id=number, has_side_effects=True, vmem_limit_bytes=62 << 20
        ),
        name="combine",
    )(y, pos_all, middle, small, slots, cot_slots, gate_low, up_low, hidden_gated)


def weights_body(rows, *refs):
    mats, per = len(SOURCE), 4
    x_refs, y_refs, refs = refs[:4], refs[4 : 4 + mats], refs[4 + mats :]
    w_refs, tok_ref, gain_ref, mg_ref, refs = refs[:3], refs[3], refs[4], refs[5], refs[6:]
    out_ref, tg_ref, gg_ref, refs = refs[0], refs[1], refs[2], refs[3:]
    xbuf, ybuf, keep, sbuf, srecv, ubuf, rbuf, hbuf, obuf, wbuf = refs[:10]
    xs, ys, yr, ss, sr, zs, zr, fs, fr, ws = refs[10:]
    e, c = lax.axis_index("expert"), lax.axis_index("dp")
    z, r = e // per, e % per
    x, y = r % 2, r // 2
    width = y_refs[0].shape[1]
    part = width // 4
    lines = width // OUTER
    peers = [(n, f) for n in range(per) for f in range(2)]
    trade = (y + c * (1 - 2 * y)) * 2 + x + (1 - c) * (1 - 2 * x)
    other = (y + (1 - c) * (1 - 2 * y)) * 2 + x + c * (1 - 2 * x)
    a_bit = (1 - c) * x + c * y
    b_bit = (1 - c) * y + c * x
    quarter = 2 * c + a_bit

    def device(n, f):
        return flip(r, n), (c + f) % 2

    bar = pltpu.get_barrier_semaphore()
    for d in range(1, OUTER):
        pl.semaphore_signal(
            bar, inc=1, device_id=((z + d) % OUTER * per + r, c), device_id_type=MESH
        )
    for n, f in peers[1:]:
        q, k = device(n, f)
        pl.semaphore_signal(bar, inc=1, device_id=(z * per + q, k), device_id_type=MESH)
    pl.semaphore_wait(bar, OUTER - 1 + 2 * per - 1)

    def block(q):
        return pl.ds(pl.multiple_of(q * part, part), part)

    targets = (
        (r, 1 - c, 2 * (1 - c) + (1 - c) * y + c * x),
        (trade, c, 2 * c + 1 - a_bit),
        (other, 1 - c, 2 * (1 - c) + 1 - b_bit),
    )

    def spread(m, i):
        q, k, at = targets[i]
        return pltpu.make_async_remote_copy(
            src_ref=y_refs[m].at[:, block(at)], dst_ref=ybuf.at[m, i + 1],
            send_sem=ys.at[m, i], recv_sem=yr.at[m, i],
            device_id=(z * per + q, k), device_id_type=MESH,
        )

    def swap(m, i):
        return pltpu.make_async_remote_copy(
            src_ref=sbuf.at[m, i], dst_ref=srecv.at[m, i], send_sem=ss.at[m, i],
            recv_sem=sr.at[m, i], device_id=(z * per + other, c), device_id_type=MESH,
        )

    def hop(m, i, j, way):
        return pltpu.make_async_remote_copy(
            src_ref=ubuf.at[m, i], dst_ref=rbuf.at[m, way, j],
            send_sem=zs.at[m, i], recv_sem=zr.at[m, way, j],
            device_id=((z + 1 - 2 * way) * per + r, c), device_id_type=MESH,
        )

    def final(m, t, f):
        there = a_bit + t * (1 - 2 * a_bit)
        core = (c + f) % 2
        q = ((1 - c) * y + c * there) * 2 + (1 - c) * there + c * x
        return pltpu.make_async_remote_copy(
            src_ref=hbuf.at[m, pl.ds(pl.multiple_of((there * 2 + core) * rows, rows), rows)],
            dst_ref=obuf.at[m, quarter], send_sem=fs.at[m, 2 * t + f],
            recv_sem=fr.at[m, quarter], device_id=(z * per + q, core), device_id_type=MESH,
        )

    def landed(m, q):
        return pltpu.make_async_remote_copy(
            src_ref=hbuf.at[m, pl.ds(0, rows)], dst_ref=obuf.at[m, q], send_sem=fs.at[m, 0],
            recv_sem=fr.at[m, q], device_id=(z * per + r, 1 - c), device_id_type=MESH,
        )

    strip = wbuf.shape[1]
    strips = width // strip
    jobs = [(k, q) for k in range(3) for q in range(strips)]

    def fetch(t):
        k, q = jobs[t]
        return pltpu.make_async_copy(
            w_refs[k].at[pl.ds(q * strip, strip)], wbuf.at[t % 2], ws.at[t % 2]
        )

    def pull_back(t):
        k, q = jobs[t]
        if t == 0:
            fetch(0).start()
        if t + 1 < len(jobs):
            fetch(t + 1).start()
        fetch(t).wait()
        got = lax.dot_general(
            y_refs[3 - k][...], wbuf[t % 2], (((1,), (1,)), ((), ())), preferred_element_type=F32
        )
        if k == 0:
            tg_ref[:, q * strip : (q + 1) * strip] = got
        else:
            tg_ref[:, q * strip : (q + 1) * strip] += got

    def norm_back():
        grad = tg_ref[...]
        values = tok_ref[...].astype(F32)
        scale = rms_scale(values)
        normed = values * scale
        gg_ref[...] = jnp.sum(grad * normed, axis=0, keepdims=True)
        grad = grad * gain_ref[...]
        centre = jnp.mean(grad * normed, axis=-1, keepdims=True)
        tg_ref[...] = mg_ref[...] + scale * (grad - normed * centre)

    loads = [pltpu.make_async_copy(x_refs[i], xbuf.at[i], xs.at[i]) for i in range(4)]
    def begin(m):
        for i in range(3):
            spread(m, i).start()

    begin(0)
    begin(1)
    for copy in loads:
        copy.start()
    for m in range(mats):
        ybuf[m, 0] = y_refs[m][:, block(quarter)]
    for copy in loads:
        copy.wait()
    order = [pick(t, z) for t in FAR]

    def pieces(j, bit):
        for t in range(2):
            at = j * lines + (1 - c) * (bit * 2 + t) * 2 * rows + c * (t * 2 + bit) * 2 * rows
            yield pl.ds(pl.multiple_of(at, 2 * rows), 2 * rows)

    def product(m, j, bit):
        total = None
        for i in range(4):
            left = jnp.concatenate([xbuf[i, SOURCE[m], at, :] for at in pieces(j, bit)], axis=0)
            term = jnp.dot(left, ybuf[m, i], preferred_element_type=F32)
            total = term if total is None else total + term
        return total

    edge = jnp.logical_or(z == 0, z == OUTER - 1)

    def outer(m):
        for i, j in enumerate(order):
            swap(m, i).wait_recv()
            ubuf[m, i] = (keep[m, i] + srecv[m, i].astype(F32)).astype(BF16)

            @pl.when(z == 0)
            def _():
                hop(m, i, j, 0).start()

            @pl.when(z > 0)
            def _():
                hop(m, i, j, 1).start()

    def inner(m):
        for i, j in enumerate(order):
            swap(m, i).wait_recv()

            @pl.when(j > z)
            def _():
                hop(m, 0, j, 0).wait_recv()
                ubuf[m, i] = (
                    keep[m, i] + srecv[m, i].astype(F32) + rbuf[m, 0, j].astype(F32)
                ).astype(BF16)
                hop(m, i, j, 0).start()

            @pl.when(j < z)
            def _():
                hop(m, 0, j, 1).wait_recv()
                ubuf[m, i] = (
                    keep[m, i] + srecv[m, i].astype(F32) + rbuf[m, 1, j].astype(F32)
                ).astype(BF16)
                hop(m, i, j, 1).start()

    for m in range(mats + 2):
        if m < mats:
            for i in range(3):
                spread(m, i).wait_recv()
            for i, j in enumerate(order + [z]):
                sbuf[m, i] = product(m, j, 1 - b_bit).astype(BF16)
                swap(m, i).start()
            if m + 2 < mats:
                begin(m + 2)
            for i, j in enumerate(order + [z]):
                keep[m, i] = product(m, j, b_bit)
        if 1 <= m <= mats:
            pl.when(edge)(functools.partial(outer, m - 1))
        if m >= 2:
            pl.when(jnp.logical_not(edge))(functools.partial(inner, m - 2))
        if m < 3:
            for t in range(m * strips, (m + 1) * strips):
                pull_back(t)
        elif m == 3:
            norm_back()

    last = OUTER - 1
    for m in range(mats):
        swap(m, last).wait_recv()
        keep[m, last] += srecv[m, last].astype(F32)

        @pl.when(z > 0)
        def _():
            hop(m, 0, z, 0).wait_recv()
            keep[m, last] += rbuf[m, 0, z].astype(F32)

        @pl.when(z < OUTER - 1)
        def _():
            hop(m, 0, z, 1).wait_recv()
            keep[m, last] += rbuf[m, 1, z].astype(F32)

        hbuf[m] = keep[m, last].astype(BF16)
        for t, f in ((1, 0), (1, 1), (0, 1)):
            final(m, t, f).start()

    for m in range(mats):
        mine = pl.ds(pl.multiple_of((a_bit * 2 + c) * rows, rows), rows)
        out_ref[m, :, block(quarter)] = keep[m, last, mine, :]
        for d in range(1, 4):
            q = (quarter + d) % 4
            landed(m, q).wait_recv()
            out_ref[m, :, block(q)] = obuf[m, q].astype(F32)
    for m in range(mats):
        for i in range(3):
            spread(m, i).wait_send()
        for i in range(OUTER):
            swap(m, i).wait_send()
        for t, f in ((1, 0), (1, 1), (0, 1)):
            final(m, t, f).wait_send()
        for i, j in enumerate(order):
            hop(m, i, j, 0).wait_send()


SOURCE = (1, 0, 0, 0)


def weight_grads(lefts, rights, weights, tokens, gain, middle_grad, experts, number):
    span, width = rights[0].shape
    rows = width // (2 * experts)
    part = width // 4
    half = width // OUTER // 2
    mats = len(rights)
    vmem = pl.BlockSpec(memory_space=pltpu.VMEM)
    hbm = pl.BlockSpec(memory_space=pltpu.HBM)
    dma = pltpu.SemaphoreType.DMA
    return pl.pallas_call(
        functools.partial(weights_body, rows),
        out_shape=(
            jax.ShapeDtypeStruct((mats, rows, width), F32),
            jax.ShapeDtypeStruct((span, width), F32),
            jax.ShapeDtypeStruct((1, width), F32),
        ),
        in_specs=[hbm] * 4 + [vmem] * mats + [hbm] * 3 + [vmem] * 3,
        out_specs=(vmem,) * 3,
        scratch_shapes=[
            pltpu.VMEM((4, 2, width, span), BF16),
            pltpu.VMEM((mats, 4, span, part), BF16),
            pltpu.VMEM((mats, OUTER, half, part), F32),
            pltpu.VMEM((mats, OUTER, half, part), BF16),
            pltpu.VMEM((mats, OUTER, half, part), BF16),
            pltpu.VMEM((mats, OUTER - 1, half, part), BF16),
            pltpu.VMEM((mats, 2, OUTER, half, part), BF16),
            pltpu.VMEM((mats, half, part), BF16),
            pltpu.VMEM((mats, 4, rows, part), BF16),
            pltpu.VMEM((2, width // OUTER // 2, width), BF16),
            dma((4,)),
            dma((mats, 3)),
            dma((mats, 3)),
            dma((mats, OUTER)),
            dma((mats, OUTER)),
            dma((mats, OUTER - 1)),
            dma((mats, 2, OUTER)),
            dma((mats, 4)),
            dma((mats, 4)),
            dma((2,)),
        ],
        compiler_params=pltpu.CompilerParams(
            collective_id=number, has_side_effects=True, vmem_limit_bytes=62 << 20
        ),
        name="weight_grads",
    )(*lefts, *rights, *weights, tokens, gain, middle_grad)


def heads_back_body(*refs):
    q_ref, k_ref, v_ref, da_ref, lse_ref, limit_ref, cos_ref, sin_ref = refs[:8]
    qpre, kpre, gains_ref, vg_ref, ql_ref, kl_ref, gq_ref, gk_ref, dq, dk = refs[8:]
    span = q_ref.shape[0]
    score_scale = HD ** (-0.5)
    column = lax.broadcasted_iota(jnp.int32, (span, span), 1).astype(F32)
    across = (((1,), (1,)), ((), ()))
    down = (((0,), (0,)), ((), ()))

    @pl.loop(0, NH)
    def _(h):
        columns = pl.ds(pl.multiple_of(h * HD, HD), HD)
        query, key, grad = q_ref[:, columns], k_ref[:, columns], da_ref[:, columns]
        scores = lax.dot_general(query, key, across, preferred_element_type=F32)
        scores = jnp.where(column <= limit_ref[...], scores * score_scale, -1e30)
        weights = jnp.exp(scores - lse_ref[h])
        weights_grad = lax.dot_general(
            grad, v_ref[:, columns], across, preferred_element_type=F32
        )
        vg_ref[:, columns] = lax.dot_general(
            weights.astype(BF16), grad, down, preferred_element_type=F32
        ).astype(BF16)
        centre = jnp.sum(weights * weights_grad, axis=-1, keepdims=True)
        score_grad = (weights * (weights_grad - centre)).astype(BF16)

        def turn_back(rot_grad):
            return rot_grad * cos_ref[...] + pltpu.roll(rot_grad * sin_ref[...], HD // 2, 1)

        query_grad = jnp.dot(score_grad, key, preferred_element_type=F32) * score_scale
        key_grad = lax.dot_general(score_grad, query, down, preferred_element_type=F32)
        dq[:, columns] = turn_back(query_grad)
        dk[:, columns] = turn_back(key_grad * score_scale)

    for row, pre, grad_ref, low_ref, gain_ref in (
        (1, qpre, dq, ql_ref, gq_ref),
        (2, kpre, dk, kl_ref, gk_ref),
    ):
        grad = grad_ref[...]
        values = pre[...]
        scale = rms_scale(values)
        normed = values * scale
        gain_ref[...] = jnp.sum(grad * normed, axis=0, keepdims=True)
        grad = grad * gains_ref[row : row + 1]
        centre = jnp.mean(grad * normed, axis=-1, keepdims=True)
        low_ref[...] = (scale * (grad - normed * centre)).astype(BF16)


def heads_back(query, key, value, grad, log_total, limit, tables, query_pre, key_pre, gains):
    span, width = query.shape
    vmem = pl.BlockSpec(memory_space=pltpu.VMEM)
    low = jax.ShapeDtypeStruct((span, width), BF16)
    line = jax.ShapeDtypeStruct((1, width), F32)
    return pl.pallas_call(
        heads_back_body,
        out_shape=(low, low, low, line, line),
        in_specs=[vmem] * 11,
        out_specs=(vmem,) * 5,
        scratch_shapes=[pltpu.VMEM((span, width), F32), pltpu.VMEM((span, width), F32)],
        cost_estimate=pl.CostEstimate(
            flops=14 * span * span * width,
            bytes_accessed=40 * span * width,
            transcendentals=NH * span * span,
        ),
        compiler_params=pltpu.CompilerParams(vmem_limit_bytes=40 << 20),
        name="heads_back",
    )(query, key, value, grad, log_total, limit, *tables, query_pre, key_pre, gains)


def body(
    tokens,
    cotangent,
    lengths,
    routes,
    attention_gain,
    query_gain,
    key_gain,
    feedforward_gain,
    query_weight,
    key_weight,
    value_weight,
    output_weight,
    router_weight,
    expert_gate_up,
    expert_down,
):
    span, width = tokens.shape
    core = lax.axis_index("dp")
    both = ("expert", "dp")
    devices = lax.axis_size("expert") * 2
    gains = jnp.concatenate([attention_gain, query_gain, key_gain, feedforward_gain])
    packed = jnp.concatenate([router_weight, gains.reshape(4, -1).T], axis=1)
    other = lax.ppermute(packed, both, [(d, d ^ 1) for d in range(devices)])
    packed = jnp.where(
        core == 0,
        jnp.concatenate([packed, other], axis=0),
        jnp.concatenate([other, packed], axis=0),
    )
    router_full, gains = packed[:, :-4], packed[:, -4:].T.astype(F32)
    gain_in, gain_query, gain_key, gain_mid = gains[0], gains[1], gains[2], gains[3]
    experts = router_full.shape[1]
    cap = span * TOP // experts
    per = experts // OUTER

    seq_length = lengths[0]
    index_rows = jnp.arange(span, dtype=jnp.int32)
    expert_ids = jnp.arange(experts, dtype=jnp.int32)
    hits = jnp.any(routes[None, :, :] == expert_ids[:, None, None], axis=-1)
    hits = hits & (index_rows < seq_length)[None, :]
    earlier = (index_rows[:, None] < index_rows[None, :]).astype(BF16)
    before = jnp.dot(hits.astype(BF16), earlier, preferred_element_type=F32)
    kept = hits & (before < cap)
    pos = jnp.where(kept, before, -1.0)
    inputs = tokens.astype(F32)
    cosine_table, sine_table = rotary_tables(index_rows.astype(F32))
    signs = jnp.where(jnp.arange(HD) < HD // 2, -1.0, 1.0)
    limit = jnp.minimum(index_rows, seq_length - 1).astype(F32)[:, None]
    tables = (cosine_table, sine_table * signs)
    (
        cot_slots, pos_here, pos_all, query_full, key_full, value_full, output_full,
        other_gate_up, other_down, turned,
        normed_in, query_pre, key_pre, query_rot, key_rot, value_all, log_total, attended,
        middle, normed_mid, gates,
    ) = attend(
        tokens, cotangent, pos[:, None, :], gains, tables, limit, router_full,
        (query_weight, key_weight, value_weight, output_weight, expert_gate_up, expert_down),
        cap, 1,
    )
    norm_mid_back = jax.vjp(norm_apply, middle, gain_mid)[1]
    def mul(left, right, spec):
        return jnp.einsum(spec, left, right, preferred_element_type=F32)

    back_rows, prob_grad, slots, gate_grad_low, up_grad_low, hidden_gated, expert_out = run_experts(
        normed_mid, gates.T[:, None, :], pos_all, pos_here, cot_slots,
        (expert_gate_up, expert_down, other_gate_up, other_down), 2,
    )
    prob_grad = prob_grad[:, 0].T
    back_rows, turned = lax.optimization_barrier((back_rows, turned))
    wide = per == 4 and width % 512 == 0
    if wide:

        def moved(d, cross):
            to = d % 2 ^ cross
            return (d // 2 ^ 1 + to) * 2 + to

        lefts = [turned, lax.ppermute(turned, both, [(d, d ^ 1) for d in range(devices)])] + [
            lax.ppermute(turned, both, [(d, moved(d, cross)) for d in range(devices)])
            for cross in range(2)
        ]

    upstream = cotangent.astype(F32)
    logit_grad = (
        gates * (prob_grad - jnp.sum(gates * prob_grad, axis=-1, keepdims=True))
    ).astype(BF16)
    grad_router = mul(normed_mid, logit_grad, "td,te->de")
    mid_normed_grad = mul(logit_grad, router_full, "te,de->td") + back_rows
    mid_input_grad, grad_mid_gain = norm_mid_back(mid_normed_grad)
    middle_grad = upstream + mid_input_grad
    branch_grad = middle_grad.astype(BF16)
    attended_grad = mul(branch_grad, output_full, "to,io->ti").astype(BF16)
    value_grad, query_low, key_low, grad_query_gain, grad_key_gain = heads_back(
        query_rot, key_rot, value_all, attended_grad, log_total, limit, tables,
        query_pre, key_pre, gains,
    )
    grad_query_gain, grad_key_gain = grad_query_gain[0], grad_key_gain[0]
    rights = (branch_grad, value_grad, key_low, query_low)
    if wide:
        expert_out, lefts, rights = lax.optimization_barrier((expert_out, lefts, rights))
        grads, grad_tokens, grad_in_gain = weight_grads(
            lefts, rights, (query_full, key_full, value_full), tokens, gain_in[None],
            middle_grad, experts, 5,
        )
        grad_in_gain = grad_in_gain[0]
    else:
        grads = []
        for source, right in zip(SOURCE, rights):
            grad = jnp.dot(turned[source], right, preferred_element_type=F32).astype(BF16)
            grid = grad.reshape(experts, 2, width // experts // 2, width).swapaxes(0, 1)
            half = lax.psum_scatter(grid, "dp", scatter_dimension=0, tiled=False)
            half = lax.psum_scatter(half, "expert", scatter_dimension=0, tiled=False)
            grads.append(half.astype(F32))
        normed_in_grad = mul(query_low, query_full, "to,io->ti")
        normed_in_grad = normed_in_grad + mul(key_low, key_full, "to,io->ti")
        normed_in_grad = normed_in_grad + mul(value_grad, value_full, "to,io->ti")
        input_grad, grad_in_gain = jax.vjp(norm_apply, inputs, gain_in)[1](normed_in_grad)
        grad_tokens = middle_grad + input_grad

    small = jnp.concatenate(
        [
            jnp.stack([grad_in_gain, grad_query_gain, grad_key_gain, grad_mid_gain]).T,
            grad_router,
        ],
        axis=1,
    )
    kinds = small.shape[1]
    small = small.reshape(OUTER, 2 * per, -1, kinds).transpose(1, 0, 3, 2)
    output, small, grad_gate_up, grad_down = combine(
        expert_out, pos_all, middle, small.reshape(2 * per, OUTER, 1, -1), slots, cot_slots,
        gate_grad_low, up_grad_low, hidden_gated, 4,
    )
    small = small.reshape(kinds, -1).T
    return (
        output,
        grad_tokens,
        small[:, 0],
        small[:, 1],
        small[:, 2],
        small[:, 3],
        grads[3],
        grads[2],
        grads[1],
        grads[0],
        small[:, 4:],
        grad_gate_up[None],
        grad_down[None],
    )


def solution(mesh):
    both = P(("expert", "dp"))
    rows = P(("expert", "dp"), None)
    in_specs = (rows, rows, both, rows) + (P("dp"),) * 4 + (P("dp", None),) * 5 + (
        P("expert", None, None, "dp"),
        P("expert", None, "dp"),
    )
    out_specs = (rows, rows) + (both,) * 4 + (rows,) * 5 + (
        P("expert", None, None, "dp"),
        P("expert", None, "dp"),
    )
    return jax.shard_map(body, mesh=mesh, in_specs=in_specs, out_specs=out_specs, check_vma=False)
```

```python
import functools
import math

import jax
import jax.numpy as jnp
from jax import lax
from jax.experimental import pallas as pl
from jax.experimental.pallas import tpu as pltpu
from jax.sharding import PartitionSpec as P

NH = 16
HD = 128
TOP = 8
OUTER = 4

EPSILON = 1e-05
ROPE_BASE = 10000.0
MESH = pl.DeviceIdType.MESH
F32 = jnp.float32
BF16 = jnp.bfloat16


def rms_scale(values):
    return lax.rsqrt(jnp.mean(values * values, axis=-1, keepdims=True) + EPSILON)


def norm_apply(values, gain_vector):
    return values * rms_scale(values) * gain_vector


def rotary_tables(positions):
    frequencies = 1.0 / ROPE_BASE ** (jnp.arange(0, HD, 2).astype(F32) / HD)
    angles = positions[:, None] * frequencies[None, :]
    angles = jnp.concatenate([angles, angles], axis=-1)
    return (jnp.cos(angles), jnp.sin(angles))


def flip(r, n):
    out, bit = r, 1
    while bit <= n:
        if n & bit:
            out = out + bit - 2 * bit * ((r // bit) % 2)
        bit *= 2
    return out


def pick(table, z):
    code = sum(v * 4**k for k, v in enumerate(table))
    return (code // ((1 + 3 * (z % 2)) * (1 + 15 * (z // 2)))) % 4


NEAR = ((1, 0, 3, 2), (2, 2, 1, 1), (3, 3, 0, 0))
PLACE = (2, 3, 1)
BLOCK = ((2, 2, 1, 1), (3, 3, 0, 0), (1, 0, 3, 2))
FAR = ((3, 3, 0, 0), (2, 0, 3, 1), (1, 2, 1, 2))


def one_hot(pos_ref, r, j, per, cap):
    span = pos_ref.shape[-1]
    rows = []
    slot = lax.broadcasted_iota(jnp.int32, (cap, span), 0).astype(F32)
    for n in range(per):
        line = pos_ref[j, flip(r, n)]
        rows.append(jnp.where(line == slot, 1.0, 0.0).astype(BF16))
    return jnp.concatenate(rows, axis=0)


def attend_body(per, cap, *refs):
    tok_ref, x_ref, meta_ref, gains_ref, cos_ref, sin_ref, limit_ref, router_ref = refs[:8]
    parts, refs = refs[8:14], refs[14:]
    out_ref, here_ref, pos_ref = refs[:3]
    fulls, refs = refs[3:9], refs[9:]
    turned_ref, nin_ref, qpre, kpre, qrot, krot, val_ref, lse_ref, att_ref, mid_ref = refs[:10]
    nmid_ref, gates_ref, zbuf, sbuf, wbuf, vacc = refs[10:16]
    zs, zr, ps, pr, ls, ms, mr, ts, tr, ds, dr, ks, fs = refs[16:]
    e, c = lax.axis_index("expert"), lax.axis_index("dp")
    z, r = e // per, e % per
    experts = OUTER * per
    bar = pltpu.get_barrier_semaphore()
    for d in range(1, experts):
        pl.semaphore_signal(bar, inc=1, device_id=((e + d) % experts, c), device_id_type=MESH)
    pl.semaphore_signal(bar, inc=1, device_id=(e, 1 - c), device_id_type=MESH)
    pl.semaphore_wait(bar, experts)
    span, width = x_ref.shape
    step = min(512, width)
    half = width // 2

    def share(d):
        to = (e + d) % experts
        return pltpu.make_async_remote_copy(
            src_ref=meta_ref.at[to], dst_ref=here_ref.at[e], send_sem=ms.at[d - 1],
            recv_sem=mr.at[d - 1], device_id=(to, c), device_id_type=MESH,
        )

    def table(d):
        to = (z + d) % OUTER
        return pltpu.make_async_remote_copy(
            src_ref=meta_ref.at[pl.ds(to * per, per)], dst_ref=pos_ref.at[z],
            send_sem=ts.at[d - 1], recv_sem=tr.at[z],
            device_id=(to * per + r, c), device_id_type=MESH,
        )

    def tabled(j):
        return pltpu.make_async_remote_copy(
            src_ref=meta_ref.at[pl.ds(0, per)], dst_ref=pos_ref.at[j], send_sem=ts.at[0],
            recv_sem=tr.at[j], device_id=(j * per + r, c), device_id_type=MESH,
        )

    def up(src, j):
        return pltpu.make_async_remote_copy(
            src_ref=src, dst_ref=zbuf.at[j], send_sem=zs.at[0, j], recv_sem=zr.at[j],
            device_id=((z + 1) * per + r, c), device_id_type=MESH,
        )

    def down(src, j):
        return pltpu.make_async_remote_copy(
            src_ref=src, dst_ref=zbuf.at[j], send_sem=zs.at[1, j], recv_sem=zr.at[j],
            device_id=((z - 1) * per + r, c), device_id_type=MESH,
        )

    def plane(i, j, n):
        return pltpu.make_async_remote_copy(
            src_ref=sbuf.at[i, n], dst_ref=out_ref.at[j, n], send_sem=ps.at[i, n],
            recv_sem=pr.at[i, n], device_id=(z * per + flip(r, n), c), device_id_type=MESH,
        )

    def local(i, j):
        return pltpu.make_async_copy(sbuf.at[i, 0], out_ref.at[j, 0], ls.at[i])

    def lines(owner):
        return pl.ds(pl.multiple_of(owner * half, half), half)

    def give(k):
        return pltpu.make_async_remote_copy(
            src_ref=parts[k], dst_ref=fulls[k].at[lines(c)] if k < 4 else fulls[k], send_sem=ds.at[k],
            recv_sem=dr.at[k], device_id=(e, 1 - c), device_id_type=MESH,
        )

    def hold(t):
        return pltpu.make_async_copy(wbuf.at[t % 2], fulls[jobs[t][0]].at[lines(c)], ks.at[t % 2])

    jobs = [(0, 0), (1, 0), (2, 0), (0, 1), (1, 1), (2, 1), (3, 0), (3, 1)]

    def fetch(t):
        k, far = jobs[t]
        src = fulls[k].at[lines(1 - c)] if far else parts[k]
        return pltpu.make_async_copy(src, wbuf.at[t % 2], fs.at[t % 2])

    def project(t):
        k, far = jobs[t]
        left = att_ref if k == 3 else nin_ref
        into = (qpre, kpre, vacc, mid_ref)[k]
        if t == 3:
            for q in range(2):
                give(q).wait_recv()
                fetch(t + q).start()
        fetch(t).wait()
        if not far:
            hold(t).start()
        mine = lines(1 - c if far else c)

        @pl.loop(0, width // step)
        def _(q):
            columns = pl.ds(pl.multiple_of(q * step, step), step)
            got = jnp.dot(left[:, mine], wbuf[t % 2, :, columns], preferred_element_type=F32)
            if k == 3 and not far:
                into[:, columns] = tok_ref[:, columns].astype(F32) + got
            elif far:
                into[:, columns] += got
            else:
                into[:, columns] = got

        if not far:
            hold(t).wait()
        if t in (0, 4):
            fetch(t + 2).start()
        elif t in (3, 5):
            give(jobs[t + 2][0]).wait_recv()
            fetch(t + 2).start()

    order = [z] + [pick(t, z) for t in NEAR]

    edge = jnp.logical_or(z == 0, z == OUTER - 1)

    def relay(places):
        @pl.when(jnp.logical_not(edge))
        def _():
            for i in places:
                j = order[i]
                up(x_ref, j).wait_recv()

                @pl.when(j < z)
                def _():
                    up(zbuf.at[j], j).start()

                @pl.when(j > z)
                def _():
                    down(zbuf.at[j], j).start()

    def choose(i, j):
        block = x_ref if i == 0 else zbuf.at[j]
        if i > 0:

            @pl.when(edge)
            def _():
                up(x_ref, j).wait_recv()

            tabled(j).wait_recv()

        marks = one_hot(pos_ref, r, j, per, cap)

        @pl.loop(0, width // step)
        def _(k):
            columns = pl.ds(pl.multiple_of(k * step, step), step)
            got = jnp.dot(marks, block[:, columns], preferred_element_type=F32).astype(BF16)
            for n in range(per):
                sbuf[i, n, :, columns] = got[n * cap : (n + 1) * cap]

        for n in range(1, per):
            plane(i, j, n).start()
        local(i, j).start()

    for d in range(1, OUTER):
        table(d).start()

    @pl.when(z < OUTER - 1)
    def _():
        up(x_ref, z).start()

    @pl.when(z > 0)
    def _():
        down(x_ref, z).start()

    fetch(0).start()
    fetch(1).start()
    pos_ref[z] = meta_ref[pl.ds(z * per, per)]
    here_ref[e] = meta_ref[e]
    choose(0, z)
    for k in range(6):
        give(k).start()
    for d in range(1, experts):
        share(d).start()

    inputs = tok_ref[...].astype(F32)
    nin_ref[...] = norm_apply(inputs, gains_ref[0:1]).astype(BF16)
    for t in range(3):
        project(t)
    relay((1, 2))
    choose(1, order[1])
    for t in range(3, 6):
        project(t)
    val_ref[...] = vacc[...].astype(BF16)
    query_scale = rms_scale(qpre[...])
    key_scale = rms_scale(kpre[...])
    turned_ref[0] = nin_ref[...].T
    score_scale = HD ** (-0.5)
    column = lax.broadcasted_iota(jnp.int32, (span, span), 1).astype(F32)

    def heads(first, last):
        @pl.loop(first, last)
        def _(h):
            columns = pl.ds(pl.multiple_of(h * HD, HD), HD)

            def turn(pre, scale, row):
                normed = pre[:, columns] * scale * gains_ref[row : row + 1, columns]
                return (
                    normed * cos_ref[...] + pltpu.roll(normed, HD // 2, 1) * sin_ref[...]
                ).astype(BF16)

            query = turn(qpre, query_scale, 1)
            key = turn(kpre, key_scale, 2)
            qrot[:, columns] = query
            krot[:, columns] = key
            scores = lax.dot_general(
                query, key, (((1,), (1,)), ((), ())), preferred_element_type=F32
            )
            scores = jnp.where(column <= limit_ref[...], scores * score_scale, -1e30)
            peak = jnp.max(scores, axis=-1, keepdims=True)
            total = peak + jnp.log(jnp.sum(jnp.exp(scores - peak), axis=-1, keepdims=True))
            lse_ref[h] = total
            weights = jnp.exp(scores - total).astype(BF16)
            att_ref[:, columns] = jnp.dot(
                weights, val_ref[:, columns], preferred_element_type=F32
            ).astype(BF16)

    heads(0, NH // 2)
    choose(2, order[2])
    relay((3,))
    heads(NH // 2, NH)
    project(6)
    choose(3, order[3])
    project(7)
    turned_ref[1] = att_ref[...].T
    middle = mid_ref[...]
    nmid_ref[...] = norm_apply(middle, gains_ref[3:4]).astype(BF16)
    logits = jnp.dot(nmid_ref[...], router_ref[...], preferred_element_type=F32)
    raised = jnp.exp(logits - jnp.max(logits, axis=-1, keepdims=True))
    gates_ref[...] = raised / jnp.sum(raised, axis=-1, keepdims=True)

    for i, j in enumerate(order):
        local(i, j).wait()
        for n in range(1, per):
            plane(i, j, n).wait()

    @pl.when(z < OUTER - 1)
    def _():
        up(x_ref, z).wait_send()

    @pl.when(z > 0)
    def _():
        down(x_ref, z).wait_send()

    for j in order[1:]:

        @pl.when(jnp.logical_and(j < z, z < OUTER - 1))
        def _():
            up(zbuf.at[j], j).wait_send()

        @pl.when(jnp.logical_and(j > z, z > 0))
        def _():
            down(zbuf.at[j], j).wait_send()

    for d in range(1, experts):
        share(d).wait()
    for d in range(1, OUTER):
        table(d).wait_send()
    for k in range(6):
        give(k).wait_send()
    for k in range(4, 6):
        give(k).wait_recv()


def attend(tokens, cotangent, meta, gains, tables, limit, router, parts, cap, number):
    experts, _, span = meta.shape
    per = experts // OUTER
    width = tokens.shape[1]
    half = parts[0].shape[0]
    vmem = pl.BlockSpec(memory_space=pltpu.VMEM)
    hbm = pl.BlockSpec(memory_space=pltpu.HBM)
    dma = pltpu.SemaphoreType.DMA
    low = jax.ShapeDtypeStruct((span, width), BF16)
    high = jax.ShapeDtypeStruct((span, width), F32)
    return pl.pallas_call(
        functools.partial(attend_body, per, cap),
        out_shape=(
            jax.ShapeDtypeStruct((OUTER, per, cap, width), BF16),
            jax.ShapeDtypeStruct((experts, 1, span), F32),
            jax.ShapeDtypeStruct((OUTER, per, 1, span), F32),
        )
        + (jax.ShapeDtypeStruct((2 * half, width), BF16),) * 4
        + tuple(jax.ShapeDtypeStruct(part.shape, BF16) for part in parts[4:])
        + (jax.ShapeDtypeStruct((2, width, span), BF16), low, high, high, low, low, low)
        + (jax.ShapeDtypeStruct((NH, span, 1), F32), low, high, low)
        + (jax.ShapeDtypeStruct((span, experts), F32),),
        in_specs=[vmem] * 8 + [hbm] * 6,
        out_specs=(hbm, vmem, vmem) + (hbm,) * 6 + (vmem,) * 12,
        scratch_shapes=[
            pltpu.VMEM((OUTER, span, width), BF16),
            pltpu.VMEM((OUTER, per, cap, width), BF16),
            pltpu.VMEM((2, half, width), BF16),
            pltpu.VMEM((span, width), F32),
            dma((2, OUTER)),
            dma((OUTER,)),
            dma((OUTER, per)),
            dma((OUTER, per)),
            dma((OUTER,)),
            dma((experts,)),
            dma((experts,)),
            dma((OUTER,)),
            dma((OUTER,)),
            dma((6,)),
            dma((6,)),
            dma((2,)),
            dma((2,)),
        ],
        compiler_params=pltpu.CompilerParams(
            collective_id=number, has_side_effects=True, vmem_limit_bytes=60 << 20
        ),
        name="attend",
    )(tokens, cotangent, meta, gains, *tables, limit, router, *parts)


def experts_body(per, cap, *refs):
    x_ref, gates_ref, pos_ref, posh_ref, cot_ref, gu_mine, dn_mine, gu_other, dn_other = refs[:9]
    refs = refs[1:]
    back_ref, pg_ref, out_ref, gl_ref, ul_ref, hg_ref, eo_ref = refs[8:15]
    zbuf, sbuf, wg, wu, wd, slb, ctb, glb, ulb, hlb, hgb, eob, ybuf, ubuf, rbuf = refs[15:30]
    here, ggv, sgv, tgv = refs[30:34]
    zs, zr, ps, pr, ls, ms, mr, ws, cs, os, es, bs, br, us, ur, gs, gr = refs[34:]
    e, c = lax.axis_index("expert"), lax.axis_index("dp")
    z, r = e // per, e % per
    experts = OUTER * per
    bar = pltpu.get_barrier_semaphore()
    for d in range(1, experts):
        pl.semaphore_signal(bar, inc=1, device_id=((e + d) % experts, c), device_id_type=MESH)
    pl.semaphore_wait(bar, experts - 1)
    span, width = x_ref.shape
    hidden = wg.shape[1]
    step = min(512, width)
    thin = min(256, hidden)
    halves = 2
    half = width // halves

    def share(d):
        to = (e + d) % experts
        return pltpu.make_async_remote_copy(
            src_ref=gates_ref.at[to], dst_ref=here.at[e], send_sem=ms.at[d - 1],
            recv_sem=mr.at[d - 1], device_id=(to, c), device_id_type=MESH,
        )

    def up(src, j):
        return pltpu.make_async_remote_copy(
            src_ref=src, dst_ref=zbuf.at[j], send_sem=zs.at[0, j], recv_sem=zr.at[j],
            device_id=((z + 1) * per + r, c), device_id_type=MESH,
        )

    def down(src, j):
        return pltpu.make_async_remote_copy(
            src_ref=src, dst_ref=zbuf.at[j], send_sem=zs.at[1, j], recv_sem=zr.at[j],
            device_id=((z - 1) * per + r, c), device_id_type=MESH,
        )

    def plane(i, j, n):
        return pltpu.make_async_remote_copy(
            src_ref=sbuf.at[i, n], dst_ref=out_ref.at[j, n], send_sem=ps.at[i, n],
            recv_sem=pr.at[i, n], device_id=(z * per + flip(r, n), c), device_id_type=MESH,
        )

    def local(i, j):
        return pltpu.make_async_copy(sbuf.at[i, 0], out_ref.at[j, 0], ls.at[i])

    def returned(i, n):
        return pltpu.make_async_remote_copy(
            src_ref=sbuf.at[i, n], dst_ref=ybuf.at[i, n - 1], send_sem=bs.at[i, n],
            recv_sem=br.at[i, n], device_id=(z * per + flip(r, n), c), device_id_type=MESH,
        )

    def part(h):
        return pl.ds(h * half, half)

    def rise(i, j, h, slot):
        return pltpu.make_async_remote_copy(
            src_ref=ubuf.at[i, h], dst_ref=rbuf.at[slot, h], send_sem=us.at[i, h],
            recv_sem=ur.at[slot, h], device_id=((z + 1) * per + r, c), device_id_type=MESH,
        )

    def fall(i, j, h, slot):
        return pltpu.make_async_remote_copy(
            src_ref=ubuf.at[i, h], dst_ref=rbuf.at[slot, h], send_sem=us.at[i, h],
            recv_sem=ur.at[slot, h], device_id=((z - 1) * per + r, c), device_id_type=MESH,
        )

    def graded(i, n, seq):
        return pltpu.make_async_remote_copy(
            src_ref=tgv.at[i, n], dst_ref=pg_ref.at[e], send_sem=gs.at[i, n],
            recv_sem=gr.at[e], device_id=(seq, c), device_id_type=MESH,
        )

    def grade(s):
        return pltpu.make_async_remote_copy(
            src_ref=tgv.at[0, 0], dst_ref=pg_ref.at[s], send_sem=gs.at[0, 0],
            recv_sem=gr.at[s], device_id=(s, c), device_id_type=MESH,
        )

    def columns_of(owner):
        return pl.ds(pl.multiple_of(owner * (hidden // 2), hidden // 2), hidden // 2)

    weights = [
        pltpu.make_async_copy(src, dst.at[:, columns_of(owner)], ws.at[k, f])
        for f, (owner, both, down_part) in enumerate(
            ((c, gu_mine, dn_mine), (1 - c, gu_other, dn_other))
        )
        for k, (src, dst) in enumerate(
            ((both.at[0, 0], wg), (both.at[0, 1], wu), (down_part.at[0], wd))
        )
    ]

    def pull(j):
        return pltpu.make_async_copy(cot_ref.at[j], ctb, cs)

    for d in range(1, experts):
        share(d).start()

    @pl.when(z < OUTER - 1)
    def _():
        up(x_ref, z).start()

    @pl.when(z > 0)
    def _():
        down(x_ref, z).start()

    here[e] = gates_ref[e]
    order = [z] + [pick(t, z) for t in NEAR]

    edge = jnp.logical_or(z == 0, z == OUTER - 1)

    def relay(places):
        @pl.when(jnp.logical_not(edge))
        def _():
            for i in places:
                j = order[i]
                up(x_ref, j).wait_recv()

                @pl.when(j < z)
                def _():
                    up(zbuf.at[j], j).start()

                @pl.when(j > z)
                def _():
                    down(zbuf.at[j], j).start()

    def choose(i, j):
        block = x_ref if i == 0 else zbuf.at[j]
        if i > 0:

            @pl.when(edge)
            def _():
                up(x_ref, j).wait_recv()

        marks = one_hot(pos_ref, r, j, per, cap)

        @pl.loop(0, width // step)
        def _(k):
            columns = pl.ds(pl.multiple_of(k * step, step), step)
            got = jnp.dot(marks, block[:, columns], preferred_element_type=F32).astype(BF16)
            for n in range(per):
                sbuf[i, n, :, columns] = got[n * cap : (n + 1) * cap]

        for n in range(1, per):
            plane(i, j, n).start()
        local(i, j).start()

    def outs(j):
        return [
            pltpu.make_async_copy(src, dst.at[j], os.at[k])
            for k, (src, dst) in enumerate(((glb, gl_ref), (ulb, ul_ref), (hgb, hg_ref)))
        ]

    def away(j):
        return pltpu.make_async_copy(eob, eo_ref.at[j], es)

    def marked(j, n):
        slot = lax.broadcasted_iota(jnp.int32, (cap, span), 0).astype(F32)
        return posh_ref[j * per + flip(r, n)] == slot

    def expert(i, j):
        for n in range(1, per):
            plane(i, j, n).wait()
        local(i, j).wait()
        if i == OUTER - 1:
            send_back(PLACE[0])
        fetch = pltpu.make_async_copy(out_ref.at[j], slb, ls.at[OUTER])
        fetch.start()
        slot_gate = jnp.concatenate(
            [
                jnp.sum(
                    jnp.where(marked(j, n), here[j * per + flip(r, n)], 0.0), axis=1, keepdims=True
                )
                for n in range(per)
            ],
            axis=0,
        )
        sgv[i % 2] = slot_gate
        ggv[i % 2] = jnp.zeros(ggv.shape[1:], F32)
        pull(j).wait()
        fetch.wait()
        if i > 0:
            for copy in outs(order[i - 1]):
                copy.wait()

        @pl.loop(0, hidden // thin)
        def _(k):
            columns = pl.ds(pl.multiple_of(k * thin, thin), thin)
            rows = slb[...].reshape(per * cap, width)
            gate_pre = jnp.dot(rows, wg[:, columns], preferred_element_type=F32)
            up_pre = jnp.dot(rows, wu[:, columns], preferred_element_type=F32)
            pulled = jnp.dot(
                ctb[...].reshape(per * cap, width), wd[:, columns], preferred_element_type=F32
            )
            sigmoid_gate = jax.nn.sigmoid(gate_pre)
            silu_gate = gate_pre * sigmoid_gate
            low = (silu_gate * up_pre).astype(BF16)
            wide = low.astype(F32)
            ggv[i % 2] += jnp.sum(wide * pulled, axis=1, keepdims=True)
            hidden_grad = pulled * slot_gate
            glb[:, columns] = (
                hidden_grad * up_pre * sigmoid_gate * (1.0 + gate_pre * (1.0 - sigmoid_gate))
            ).astype(BF16)
            ulb[:, columns] = (hidden_grad * silu_gate).astype(BF16)
            hlb[i % 2, :, columns] = low
            hgb[:, columns] = (wide * slot_gate).astype(BF16)

        if i < OUTER - 1:
            pull(order[i + 1]).start()
        for copy in outs(j):
            copy.start()

        @pl.loop(0, width // step)
        def _(k):
            columns = pl.ds(pl.multiple_of(k * step, step), step)
            got = lax.dot_general(
                glb[...], wg[columns, :], (((1,), (1,)), ((), ())), preferred_element_type=F32
            ) + lax.dot_general(
                ulb[...], wu[columns, :], (((1,), (1,)), ((), ())), preferred_element_type=F32
            )
            got = got.astype(BF16)
            for n in range(per):
                sbuf[i, n, :, columns] = got[n * cap : (n + 1) * cap]

    def send_back(i):
        for n in range(1, per):
            returned(i, n).start()

    def finish(i, j):
        for n in range(per):
            seq = j * per + flip(r, n)
            row = jnp.sum(
                jnp.where(marked(j, n), ggv[i % 2, n * cap : (n + 1) * cap], 0.0),
                axis=0,
                keepdims=True,
            )
            tgv[i, n] = row
            if i == 0 and n == 0:
                pg_ref[e] = row
            else:
                graded(i, n, seq).start()
        if i > 0:
            away(order[i - 1]).wait()

        @pl.loop(0, width // step)
        def _(k):
            columns = pl.ds(pl.multiple_of(k * step, step), step)
            got = lax.dot_general(
                hlb[i % 2], wd[columns, :], (((1,), (1,)), ((), ())), preferred_element_type=F32
            )
            got = (got * sgv[i % 2]).astype(BF16)
            for n in range(per):
                eob[n, :, columns] = got[n * cap : (n + 1) * cap]

        away(j).start()

    choose(0, z)
    for copy in weights:
        copy.start()
    pull(z).start()
    relay((1, 2))
    choose(1, order[1])
    for copy in weights:
        copy.wait()
    for d in range(1, experts):
        share(d).wait()
    last = OUTER - 1
    for i in range(last):
        expert(i, order[i])
        if i + 2 <= last:
            choose(i + 2, order[i + 2])
            if i == 0:
                relay((3,))
            finish(i, order[i])
    expert(last, order[last])
    for i in (*PLACE[1:], 0):
        send_back(i)
    finish(last - 1, order[last - 1])

    def fold(i, j, h):
        marks = one_hot(pos_ref, r, j, per, cap)

        @pl.loop(0, half // step)
        def _(k):
            columns = pl.ds(pl.multiple_of(h * half + k * step, step), step)
            rows = jnp.concatenate(
                [ybuf[i, n - 1, :, columns] if n else sbuf[i, 0, :, columns] for n in range(per)],
                axis=0,
            )
            back_ref[:, columns] = lax.dot_general(
                marks, rows, (((0,), (0,)), ((), ())), preferred_element_type=F32
            )

    for p in range(last):
        i, j = PLACE[p], pick(BLOCK[p], z)
        for n in range(1, per):
            returned(i, n).wait_recv()
        for h in range(halves):
            fold(i, j, h)

            @pl.when(jnp.logical_and(j > z, z > 0))
            def _():
                rise(0, j, h, j).wait_recv()
                back_ref[:, part(h)] += rbuf[j, h].astype(F32)

            @pl.when(jnp.logical_and(j < z, z < OUTER - 1))
            def _():
                fall(0, j, h, j).wait_recv()
                back_ref[:, part(h)] += rbuf[j, h].astype(F32)

            ubuf[p, h] = back_ref[:, part(h)].astype(BF16)

            @pl.when(j > z)
            def _():
                rise(p, j, h, j).start()

            @pl.when(jnp.logical_and(j < z, z - j > 1))
            def _():
                fall(p, j, h, j).start()

            @pl.when(z - j == 1)
            def _():
                fall(p, j, h, OUTER).start()

        if p == 0:
            finish(last, order[last])

    for n in range(1, per):
        returned(0, n).wait_recv()
    for h in range(halves):
        fold(0, z, h)

        @pl.when(z > 0)
        def _():
            rise(0, z, h, z).wait_recv()
            back_ref[:, part(h)] += rbuf[z, h].astype(F32)

        @pl.when(z < OUTER - 1)
        def _():
            fall(0, z, h, OUTER).wait_recv()
            back_ref[:, part(h)] += rbuf[OUTER, h].astype(F32)

    @pl.when(z < OUTER - 1)
    def _():
        up(x_ref, z).wait_send()

    @pl.when(z > 0)
    def _():
        down(x_ref, z).wait_send()

    for i, j in enumerate(order):
        for n in range(1, per):
            returned(i, n).wait_send()
        if i > 0:

            @pl.when(jnp.logical_and(j < z, z < OUTER - 1))
            def _():
                up(zbuf.at[j], j).wait_send()

            @pl.when(jnp.logical_and(j > z, z > 0))
            def _():
                down(zbuf.at[j], j).wait_send()

            for h in range(halves):
                rise(i - 1, j, h, j).wait_send()
        for n in range(per):
            if i or n:
                graded(i, n, j * per + flip(r, n)).wait_send()
    for d in range(1, experts):
        grade((e + d) % experts).wait_recv()
    for copy in outs(order[last]):
        copy.wait()
    away(order[last]).wait()


def run_experts(x, gates, pos, pos_here, cot_slots, weights, number):
    experts, _, span = gates.shape
    outer, per, cap, width = cot_slots.shape
    hidden = 2 * weights[0].shape[-1]
    block = per * cap
    vmem = pl.BlockSpec(memory_space=pltpu.VMEM)
    hbm = pl.BlockSpec(memory_space=pltpu.HBM)
    dma = pltpu.SemaphoreType.DMA
    rows = jax.ShapeDtypeStruct((OUTER, per, cap, width), BF16)
    thin = jax.ShapeDtypeStruct((OUTER, block, hidden), BF16)
    return pl.pallas_call(
        functools.partial(experts_body, per, cap),
        out_shape=(
            jax.ShapeDtypeStruct((span, width), F32),
            jax.ShapeDtypeStruct((experts, 1, span), F32),
            rows, thin, thin, thin, rows,
        ),
        in_specs=[vmem] * 4 + [hbm] * 5,
        out_specs=(vmem, vmem) + (hbm,) * 5,
        scratch_shapes=[
            pltpu.VMEM((OUTER, span, width), BF16),
            pltpu.VMEM((OUTER, per, cap, width), BF16),
            pltpu.VMEM((width, hidden), BF16),
            pltpu.VMEM((width, hidden), BF16),
            pltpu.VMEM((width, hidden), BF16),
            pltpu.VMEM((per, cap, width), BF16),
            pltpu.VMEM((per, cap, width), BF16),
            pltpu.VMEM((block, hidden), BF16),
            pltpu.VMEM((block, hidden), BF16),
            pltpu.VMEM((2, block, hidden), BF16),
            pltpu.VMEM((block, hidden), BF16),
            pltpu.VMEM((per, cap, width), BF16),
            pltpu.VMEM((OUTER, per - 1, cap, width), BF16),
            pltpu.VMEM((OUTER - 1, 2, span, width // 2), BF16),
            pltpu.VMEM((OUTER + 1, 2, span, width // 2), BF16),
            pltpu.VMEM((experts, 1, span), F32),
            pltpu.VMEM((2, block, 1), F32),
            pltpu.VMEM((2, block, 1), F32),
            pltpu.VMEM((OUTER, per, 1, span), F32),
            dma((2, OUTER)),
            dma((OUTER,)),
            dma((OUTER, per)),
            dma((OUTER, per)),
            dma((OUTER + 1,)),
            dma((experts,)),
            dma((experts,)),
            dma((3, 2)),
            dma,
            dma((3,)),
            dma,
            dma((OUTER, per)),
            dma((OUTER, per)),
            dma((OUTER - 1, 2)),
            dma((OUTER + 1, 2)),
            dma((OUTER, per)),
            dma((experts,)),
        ],
        compiler_params=pltpu.CompilerParams(
            collective_id=number, has_side_effects=True, vmem_limit_bytes=62 << 20
        ),
        name="experts",
    )(x, gates, pos, pos_here, cot_slots, *weights)


def combine_body(per, cap, *refs):
    y_ref, pos_ref, mid_ref, small_ref, slots_ref, cot_ref, gl_ref, ul_ref, hg_ref = refs[:9]
    res_ref, total_ref, gu_ref, dn_ref, out_ref, ybuf, ubuf, rbuf = refs[9:17]
    theirs, ours, lbuf, lturn, tbuf, rx, stage, lall, lsum, lz = refs[17:27]
    zs, zr, ps, pr, ls, rs, ws, ds, dr, gs, las, lar, tas, tar = refs[27:]
    e, c = lax.axis_index("expert"), lax.axis_index("dp")
    z, r = e // per, e % per
    bar = pltpu.get_barrier_semaphore()
    for d in range(1, OUTER):
        pl.semaphore_signal(
            bar, inc=1, device_id=((z + d) % OUTER * per + r, c), device_id_type=MESH
        )
    peers = [(n, f) for n in range(per) for f in range(2)]

    def device(n, f):
        return flip(r, n), (c + f) % 2

    for n, f in peers[1:]:
        q, k = device(n, f)
        pl.semaphore_signal(bar, inc=1, device_id=(z * per + q, k), device_id_type=MESH)
    pl.semaphore_wait(bar, OUTER - 1 + 2 * per - 1)
    span, width = out_ref.shape
    step = min(512, width)
    share = dn_ref.shape[1]
    thin = min(256, share)
    total = OUTER * per * cap

    def plane(i, j, n):
        return pltpu.make_async_remote_copy(
            src_ref=y_ref.at[j, n], dst_ref=ybuf.at[i, n], send_sem=ps.at[i, n],
            recv_sem=pr.at[i, n], device_id=(z * per + flip(r, n), c), device_id_type=MESH,
        )

    def local(i, j):
        return pltpu.make_async_copy(y_ref.at[j, 0], ybuf.at[i, 0], ls.at[i])

    halves = 2
    half = width // halves

    def part(h):
        return pl.ds(h * half, half)

    def rise(i, h, slot):
        return pltpu.make_async_remote_copy(
            src_ref=ubuf.at[i, h], dst_ref=rbuf.at[slot, h], send_sem=zs.at[i, h],
            recv_sem=zr.at[slot, h], device_id=((z + 1) * per + r, c), device_id_type=MESH,
        )

    def fall(i, h, slot):
        return pltpu.make_async_remote_copy(
            src_ref=ubuf.at[i, h], dst_ref=rbuf.at[slot, h], send_sem=zs.at[i, h],
            recv_sem=zr.at[slot, h], device_id=((z - 1) * per + r, c), device_id_type=MESH,
        )

    def rights(k, src, other):
        owner = 1 - c if other else c
        return pltpu.make_async_copy(
            src.at[:, :, pl.ds(pl.multiple_of(owner * share, share), share)],
            (theirs if other else ours).at[:, :, pl.ds(k * share, share)],
            rs.at[k, int(other)],
        )

    def across(k):
        return pltpu.make_async_remote_copy(
            src_ref=tbuf.at[k % 2], dst_ref=rx.at[k], send_sem=ds.at[k], recv_sem=dr.at[k],
            device_id=(e, 1 - c), device_id_type=MESH,
        )

    def stores(k):
        lines = pl.ds(k * step, step)
        return [
            pltpu.make_async_copy(
                stage.at[:, pl.ds(m * share, share)],
                dn_ref.at[lines] if m == 2 else gu_ref.at[m, lines],
                gs.at[m],
            )
            for m in range(3)
        ]

    def little(i):
        q, k = device(*peers[i])
        return pltpu.make_async_remote_copy(
            src_ref=small_ref.at[q * 2 + k], dst_ref=lall.at[i], send_sem=las.at[i],
            recv_sem=lar.at[i], device_id=(z * per + q, k), device_id_type=MESH,
        )

    def tall(d):
        to = (z + d) % OUTER
        return pltpu.make_async_remote_copy(
            src_ref=lsum.at[to], dst_ref=lz.at[d], send_sem=tas.at[d], recv_sem=tar.at[d],
            device_id=(to * per + r, c), device_id_type=MESH,
        )

    sources = (gl_ref, ul_ref, hg_ref)
    loads = [rights(k, src, other) for k, src in enumerate(sources) for other in (True, False)]

    def tile(k):
        if k == 0:
            for copy in loads:
                copy.wait()
        if k >= 2:
            across(k - 2).wait_send()
        if k >= 1:
            for copy in stores(k - 1):
                copy.wait()
        for src, first, count in ((slots_ref, 0, 2), (cot_ref, 2, 1)):
            fetch = pltpu.make_async_copy(
                src.at[:, :, :, pl.ds(k * step, step)], lbuf, ws
            )
            fetch.start()
            fetch.wait()
            lturn[...] = lbuf[...].reshape(total, step).T

            @pl.loop(0, count * share // thin)
            def _(q):
                at = pl.ds(pl.multiple_of(first * share + q * thin, thin), thin)
                tbuf[k % 2, :, at] = jnp.dot(
                    lturn[...], theirs[:, :, at].reshape(total, thin), preferred_element_type=F32
                ).astype(BF16)
                stage[:, at] = jnp.dot(
                    lturn[...], ours[:, :, at].reshape(total, thin), preferred_element_type=F32
                )

        across(k).start()
        across(k).wait_recv()
        stage[...] += rx[k].astype(F32)
        for copy in stores(k):
            copy.start()

    order = [pick(t, z) for t in FAR] + [z]
    for i, j in enumerate(order):
        for n in range(1, per):
            plane(i, j, n).start()
        local(i, j).start()
    for copy in loads:
        copy.start()
    for i in range(1, 2 * per):
        little(i).start()
    lall[0] = small_ref[r * 2 + c]
    tiles = width // step
    done = 0
    for i, j in enumerate(order):
        while done < tiles * (1, 2, 3, 4)[i] // 4:
            tile(done)
            done += 1
        if i == OUTER - 1:
            for k in range(1, 2 * per):
                little(k).wait_recv()
            lsum[...] = sum(lall[k] for k in range(2 * per))
            for d in range(1, OUTER):
                tall(d).start()
        marks = one_hot(pos_ref, r, j, per, cap)
        local(i, j).wait()
        for n in range(1, per):
            plane(i, j, n).wait_recv()
        for h in range(halves):

            @pl.loop(0, half // step)
            def _(k):
                columns = pl.ds(pl.multiple_of(h * half + k * step, step), step)
                rows = jnp.concatenate([ybuf[i, n, :, columns] for n in range(per)], axis=0)
                out_ref[:, columns] = lax.dot_general(
                    marks, rows, (((0,), (0,)), ((), ())), preferred_element_type=F32
                )

            if i < OUTER - 1:

                @pl.when(jnp.logical_and(j > z, z > 0))
                def _():
                    rise(0, h, j).wait_recv()
                    out_ref[:, part(h)] += rbuf[j, h].astype(F32)

                @pl.when(jnp.logical_and(j < z, z < OUTER - 1))
                def _():
                    fall(0, h, j).wait_recv()
                    out_ref[:, part(h)] += rbuf[j, h].astype(F32)

                ubuf[i, h] = out_ref[:, part(h)].astype(BF16)

                @pl.when(j > z)
                def _():
                    rise(i, h, j).start()

                @pl.when(jnp.logical_and(j < z, z - j > 1))
                def _():
                    fall(i, h, j).start()

                @pl.when(z - j == 1)
                def _():
                    fall(i, h, OUTER).start()
            else:

                @pl.when(z > 0)
                def _():
                    rise(0, h, z).wait_recv()
                    out_ref[:, part(h)] += rbuf[z, h].astype(F32)

                @pl.when(z < OUTER - 1)
                def _():
                    fall(0, h, OUTER).wait_recv()
                    out_ref[:, part(h)] += rbuf[OUTER, h].astype(F32)

                res_ref[:, part(h)] = (mid_ref[:, part(h)] + out_ref[:, part(h)]).astype(BF16)

    for i, j in enumerate(order):
        for n in range(1, per):
            plane(i, j, n).wait_send()
        if i < OUTER - 1:
            for h in range(halves):
                rise(i, h, j).wait_send()
    for d in range(1, OUTER):
        tall(d).wait()
    total_ref[...] = lsum[z] + sum(lz[d] for d in range(1, OUTER))
    for i in range(1, 2 * per):
        little(i).wait_send()
    for k in range(max(0, tiles - 2), tiles):
        across(k).wait_send()
    for copy in stores(tiles - 1):
        copy.wait()


def combine(y, pos_all, middle, small, slots, cot_slots, gate_low, up_low, hidden_gated, number):
    outer, per, cap, width = y.shape
    span = pos_all.shape[-1]
    block, hidden = gate_low.shape[1:]
    share = hidden // 2
    step = min(512, width)
    tiles = width // step
    vmem = pl.BlockSpec(memory_space=pltpu.VMEM)
    hbm = pl.BlockSpec(memory_space=pltpu.HBM)
    dma = pltpu.SemaphoreType.DMA
    return pl.pallas_call(
        functools.partial(combine_body, per, cap),
        out_shape=(
            jax.ShapeDtypeStruct((span, width), BF16),
            jax.ShapeDtypeStruct((1, small.shape[-1]), F32),
            jax.ShapeDtypeStruct((2, width, share), F32),
            jax.ShapeDtypeStruct((width, share), F32),
        ),
        in_specs=[hbm, vmem, vmem, vmem] + [hbm] * 5,
        out_specs=(vmem, vmem, hbm, hbm),
        scratch_shapes=[
            pltpu.VMEM((span, width), F32),
            pltpu.VMEM((OUTER, per, cap, width), BF16),
            pltpu.VMEM((OUTER - 1, 2, span, width // 2), BF16),
            pltpu.VMEM((OUTER + 1, 2, span, width // 2), BF16),
            pltpu.VMEM((OUTER, block, 3 * share), BF16),
            pltpu.VMEM((OUTER, block, 3 * share), BF16),
            pltpu.VMEM((OUTER, per, cap, step), BF16),
            pltpu.VMEM((step, OUTER * block), BF16),
            pltpu.VMEM((2, step, 3 * share), BF16),
            pltpu.VMEM((tiles, step, 3 * share), BF16),
            pltpu.VMEM((step, 3 * share), F32),
            pltpu.VMEM(small.shape, F32),
            pltpu.VMEM(small.shape[1:], F32),
            pltpu.VMEM(small.shape[1:], F32),
            dma((OUTER - 1, 2)),
            dma((OUTER + 1, 2)),
            dma((OUTER, per)),
            dma((OUTER, per)),
            dma((OUTER,)),
            dma((3, 2)),
            dma,
            dma((tiles,)),
            dma((tiles,)),
            dma((3,)),
            dma((2 * per,)),
            dma((2 * per,)),
            dma((OUTER,)),
            dma((OUTER,)),
        ],
        compiler_params=pltpu.CompilerParams(
            collective_id=number, has_side_effects=True, vmem_limit_bytes=62 << 20
        ),
        name="combine",
    )(y, pos_all, middle, small, slots, cot_slots, gate_low, up_low, hidden_gated)


def weights_body(rows, *refs):
    mats, per = len(SOURCE), 4
    x_refs, y_refs, refs = refs[:4], refs[4 : 4 + mats], refs[4 + mats :]
    w_refs, tok_ref, gain_ref, mg_ref, refs = refs[:3], refs[3], refs[4], refs[5], refs[6:]
    out_ref, tg_ref, gg_ref, refs = refs[0], refs[1], refs[2], refs[3:]
    xbuf, ybuf, keep, sbuf, srecv, ubuf, rbuf, hbuf, obuf, wbuf = refs[:10]
    xs, ys, yr, ss, sr, zs, zr, fs, fr, ws = refs[10:]
    e, c = lax.axis_index("expert"), lax.axis_index("dp")
    z, r = e // per, e % per
    x, y = r % 2, r // 2
    width = y_refs[0].shape[1]
    part = width // 4
    lines = width // OUTER
    peers = [(n, f) for n in range(per) for f in range(2)]
    trade = (y + c * (1 - 2 * y)) * 2 + x + (1 - c) * (1 - 2 * x)
    other = (y + (1 - c) * (1 - 2 * y)) * 2 + x + c * (1 - 2 * x)
    a_bit = (1 - c) * x + c * y
    b_bit = (1 - c) * y + c * x
    quarter = 2 * c + a_bit

    def device(n, f):
        return flip(r, n), (c + f) % 2

    bar = pltpu.get_barrier_semaphore()
    for d in range(1, OUTER):
        pl.semaphore_signal(
            bar, inc=1, device_id=((z + d) % OUTER * per + r, c), device_id_type=MESH
        )
    for n, f in peers[1:]:
        q, k = device(n, f)
        pl.semaphore_signal(bar, inc=1, device_id=(z * per + q, k), device_id_type=MESH)
    pl.semaphore_wait(bar, OUTER - 1 + 2 * per - 1)

    def block(q):
        return pl.ds(pl.multiple_of(q * part, part), part)

    targets = (
        (r, 1 - c, 2 * (1 - c) + (1 - c) * y + c * x),
        (trade, c, 2 * c + 1 - a_bit),
        (other, 1 - c, 2 * (1 - c) + 1 - b_bit),
    )

    def spread(m, i):
        q, k, at = targets[i]
        return pltpu.make_async_remote_copy(
            src_ref=y_refs[m].at[:, block(at)], dst_ref=ybuf.at[m, i + 1],
            send_sem=ys.at[m, i], recv_sem=yr.at[m, i],
            device_id=(z * per + q, k), device_id_type=MESH,
        )

    def swap(m, i):
        return pltpu.make_async_remote_copy(
            src_ref=sbuf.at[m, i], dst_ref=srecv.at[m, i], send_sem=ss.at[m, i],
            recv_sem=sr.at[m, i], device_id=(z * per + other, c), device_id_type=MESH,
        )

    def hop(m, i, j, way):
        return pltpu.make_async_remote_copy(
            src_ref=ubuf.at[m, i], dst_ref=rbuf.at[m, way, j],
            send_sem=zs.at[m, i], recv_sem=zr.at[m, way, j],
            device_id=((z + 1 - 2 * way) * per + r, c), device_id_type=MESH,
        )

    def final(m, t, f):
        there = a_bit + t * (1 - 2 * a_bit)
        core = (c + f) % 2
        q = ((1 - c) * y + c * there) * 2 + (1 - c) * there + c * x
        return pltpu.make_async_remote_copy(
            src_ref=hbuf.at[m, pl.ds(pl.multiple_of((there * 2 + core) * rows, rows), rows)],
            dst_ref=obuf.at[m, quarter], send_sem=fs.at[m, 2 * t + f],
            recv_sem=fr.at[m, quarter], device_id=(z * per + q, core), device_id_type=MESH,
        )

    def landed(m, q):
        return pltpu.make_async_remote_copy(
            src_ref=hbuf.at[m, pl.ds(0, rows)], dst_ref=obuf.at[m, q], send_sem=fs.at[m, 0],
            recv_sem=fr.at[m, q], device_id=(z * per + r, 1 - c), device_id_type=MESH,
        )

    strip = wbuf.shape[1]
    strips = width // strip
    jobs = [(k, q) for k in range(3) for q in range(strips)]

    def fetch(t):
        k, q = jobs[t]
        return pltpu.make_async_copy(
            w_refs[k].at[pl.ds(q * strip, strip)], wbuf.at[t % 2], ws.at[t % 2]
        )

    def pull_back(t):
        k, q = jobs[t]
        if t == 0:
            fetch(0).start()
        if t + 1 < len(jobs):
            fetch(t + 1).start()
        fetch(t).wait()
        got = lax.dot_general(
            y_refs[3 - k][...], wbuf[t % 2], (((1,), (1,)), ((), ())), preferred_element_type=F32
        )
        if k == 0:
            tg_ref[:, q * strip : (q + 1) * strip] = got
        else:
            tg_ref[:, q * strip : (q + 1) * strip] += got

    def norm_back():
        grad = tg_ref[...]
        values = tok_ref[...].astype(F32)
        scale = rms_scale(values)
        normed = values * scale
        gg_ref[...] = jnp.sum(grad * normed, axis=0, keepdims=True)
        grad = grad * gain_ref[...]
        centre = jnp.mean(grad * normed, axis=-1, keepdims=True)
        tg_ref[...] = mg_ref[...] + scale * (grad - normed * centre)

    loads = [pltpu.make_async_copy(x_refs[i], xbuf.at[i], xs.at[i]) for i in range(4)]
    def begin(m):
        for i in range(3):
            spread(m, i).start()

    begin(0)
    begin(1)
    for copy in loads:
        copy.start()
    for m in range(mats):
        ybuf[m, 0] = y_refs[m][:, block(quarter)]
    for copy in loads:
        copy.wait()
    order = [pick(t, z) for t in FAR]

    def pieces(j, bit):
        for t in range(2):
            at = j * lines + (1 - c) * (bit * 2 + t) * 2 * rows + c * (t * 2 + bit) * 2 * rows
            yield pl.ds(pl.multiple_of(at, 2 * rows), 2 * rows)

    def product(m, j, bit):
        total = None
        for i in range(4):
            left = jnp.concatenate([xbuf[i, SOURCE[m], at, :] for at in pieces(j, bit)], axis=0)
            term = jnp.dot(left, ybuf[m, i], preferred_element_type=F32)
            total = term if total is None else total + term
        return total

    edge = jnp.logical_or(z == 0, z == OUTER - 1)

    def outer(m):
        for i, j in enumerate(order):
            swap(m, i).wait_recv()
            ubuf[m, i] = (keep[m, i] + srecv[m, i].astype(F32)).astype(BF16)

            @pl.when(z == 0)
            def _():
                hop(m, i, j, 0).start()

            @pl.when(z > 0)
            def _():
                hop(m, i, j, 1).start()

    def inner(m):
        for i, j in enumerate(order):
            swap(m, i).wait_recv()

            @pl.when(j > z)
            def _():
                hop(m, 0, j, 0).wait_recv()
                ubuf[m, i] = (
                    keep[m, i] + srecv[m, i].astype(F32) + rbuf[m, 0, j].astype(F32)
                ).astype(BF16)
                hop(m, i, j, 0).start()

            @pl.when(j < z)
            def _():
                hop(m, 0, j, 1).wait_recv()
                ubuf[m, i] = (
                    keep[m, i] + srecv[m, i].astype(F32) + rbuf[m, 1, j].astype(F32)
                ).astype(BF16)
                hop(m, i, j, 1).start()

    for m in range(mats + 2):
        if m < mats:
            for i in range(3):
                spread(m, i).wait_recv()
            for i, j in enumerate(order + [z]):
                sbuf[m, i] = product(m, j, 1 - b_bit).astype(BF16)
                swap(m, i).start()
            if m + 2 < mats:
                begin(m + 2)
            for i, j in enumerate(order + [z]):
                keep[m, i] = product(m, j, b_bit)
        if 1 <= m <= mats:
            pl.when(edge)(functools.partial(outer, m - 1))
        if m >= 2:
            pl.when(jnp.logical_not(edge))(functools.partial(inner, m - 2))
        if m < 3:
            for t in range(m * strips, (m + 1) * strips):
                pull_back(t)
        elif m == 3:
            norm_back()

    last = OUTER - 1
    for m in range(mats):
        swap(m, last).wait_recv()
        keep[m, last] += srecv[m, last].astype(F32)

        @pl.when(z > 0)
        def _():
            hop(m, 0, z, 0).wait_recv()
            keep[m, last] += rbuf[m, 0, z].astype(F32)

        @pl.when(z < OUTER - 1)
        def _():
            hop(m, 0, z, 1).wait_recv()
            keep[m, last] += rbuf[m, 1, z].astype(F32)

        hbuf[m] = keep[m, last].astype(BF16)
        for t, f in ((1, 0), (1, 1), (0, 1)):
            final(m, t, f).start()

    for m in range(mats):
        mine = pl.ds(pl.multiple_of((a_bit * 2 + c) * rows, rows), rows)
        out_ref[m, :, block(quarter)] = keep[m, last, mine, :]
        for d in range(1, 4):
            q = (quarter + d) % 4
            landed(m, q).wait_recv()
            out_ref[m, :, block(q)] = obuf[m, q].astype(F32)
    for m in range(mats):
        for i in range(3):
            spread(m, i).wait_send()
        for i in range(OUTER):
            swap(m, i).wait_send()
        for t, f in ((1, 0), (1, 1), (0, 1)):
            final(m, t, f).wait_send()
        for i, j in enumerate(order):
            hop(m, i, j, 0).wait_send()


SOURCE = (1, 0, 0, 0)


def weight_grads(lefts, rights, weights, tokens, gain, middle_grad, experts, number):
    span, width = rights[0].shape
    rows = width // (2 * experts)
    part = width // 4
    half = width // OUTER // 2
    mats = len(rights)
    vmem = pl.BlockSpec(memory_space=pltpu.VMEM)
    hbm = pl.BlockSpec(memory_space=pltpu.HBM)
    dma = pltpu.SemaphoreType.DMA
    return pl.pallas_call(
        functools.partial(weights_body, rows),
        out_shape=(
            jax.ShapeDtypeStruct((mats, rows, width), F32),
            jax.ShapeDtypeStruct((span, width), F32),
            jax.ShapeDtypeStruct((1, width), F32),
        ),
        in_specs=[hbm] * 4 + [vmem] * mats + [hbm] * 3 + [vmem] * 3,
        out_specs=(vmem,) * 3,
        scratch_shapes=[
            pltpu.VMEM((4, 2, width, span), BF16),
            pltpu.VMEM((mats, 4, span, part), BF16),
            pltpu.VMEM((mats, OUTER, half, part), F32),
            pltpu.VMEM((mats, OUTER, half, part), BF16),
            pltpu.VMEM((mats, OUTER, half, part), BF16),
            pltpu.VMEM((mats, OUTER - 1, half, part), BF16),
            pltpu.VMEM((mats, 2, OUTER, half, part), BF16),
            pltpu.VMEM((mats, half, part), BF16),
            pltpu.VMEM((mats, 4, rows, part), BF16),
            pltpu.VMEM((2, width // OUTER // 2, width), BF16),
            dma((4,)),
            dma((mats, 3)),
            dma((mats, 3)),
            dma((mats, OUTER)),
            dma((mats, OUTER)),
            dma((mats, OUTER - 1)),
            dma((mats, 2, OUTER)),
            dma((mats, 4)),
            dma((mats, 4)),
            dma((2,)),
        ],
        compiler_params=pltpu.CompilerParams(
            collective_id=number, has_side_effects=True, vmem_limit_bytes=62 << 20
        ),
        name="weight_grads",
    )(*lefts, *rights, *weights, tokens, gain, middle_grad)


def heads_back_body(*refs):
    q_ref, k_ref, v_ref, da_ref, lse_ref, limit_ref, cos_ref, sin_ref = refs[:8]
    qpre, kpre, gains_ref, vg_ref, ql_ref, kl_ref, gq_ref, gk_ref, dq, dk = refs[8:]
    span = q_ref.shape[0]
    score_scale = HD ** (-0.5)
    column = lax.broadcasted_iota(jnp.int32, (span, span), 1).astype(F32)
    across = (((1,), (1,)), ((), ()))
    down = (((0,), (0,)), ((), ()))

    @pl.loop(0, NH)
    def _(h):
        columns = pl.ds(pl.multiple_of(h * HD, HD), HD)
        query, key, grad = q_ref[:, columns], k_ref[:, columns], da_ref[:, columns]
        scores = lax.dot_general(query, key, across, preferred_element_type=F32)
        scores = jnp.where(column <= limit_ref[...], scores * score_scale, -1e30)
        weights = jnp.exp(scores - lse_ref[h])
        weights_grad = lax.dot_general(
            grad, v_ref[:, columns], across, preferred_element_type=F32
        )
        vg_ref[:, columns] = lax.dot_general(
            weights.astype(BF16), grad, down, preferred_element_type=F32
        ).astype(BF16)
        centre = jnp.sum(weights * weights_grad, axis=-1, keepdims=True)
        score_grad = (weights * (weights_grad - centre)).astype(BF16)

        def turn_back(rot_grad):
            return rot_grad * cos_ref[...] + pltpu.roll(rot_grad * sin_ref[...], HD // 2, 1)

        query_grad = jnp.dot(score_grad, key, preferred_element_type=F32) * score_scale
        key_grad = lax.dot_general(score_grad, query, down, preferred_element_type=F32)
        dq[:, columns] = turn_back(query_grad)
        dk[:, columns] = turn_back(key_grad * score_scale)

    for row, pre, grad_ref, low_ref, gain_ref in (
        (1, qpre, dq, ql_ref, gq_ref),
        (2, kpre, dk, kl_ref, gk_ref),
    ):
        grad = grad_ref[...]
        values = pre[...]
        scale = rms_scale(values)
        normed = values * scale
        gain_ref[...] = jnp.sum(grad * normed, axis=0, keepdims=True)
        grad = grad * gains_ref[row : row + 1]
        centre = jnp.mean(grad * normed, axis=-1, keepdims=True)
        low_ref[...] = (scale * (grad - normed * centre)).astype(BF16)


def heads_back(query, key, value, grad, log_total, limit, tables, query_pre, key_pre, gains):
    span, width = query.shape
    vmem = pl.BlockSpec(memory_space=pltpu.VMEM)
    low = jax.ShapeDtypeStruct((span, width), BF16)
    line = jax.ShapeDtypeStruct((1, width), F32)
    return pl.pallas_call(
        heads_back_body,
        out_shape=(low, low, low, line, line),
        in_specs=[vmem] * 11,
        out_specs=(vmem,) * 5,
        scratch_shapes=[pltpu.VMEM((span, width), F32), pltpu.VMEM((span, width), F32)],
        cost_estimate=pl.CostEstimate(
            flops=14 * span * span * width,
            bytes_accessed=40 * span * width,
            transcendentals=NH * span * span,
        ),
        compiler_params=pltpu.CompilerParams(vmem_limit_bytes=40 << 20),
        name="heads_back",
    )(query, key, value, grad, log_total, limit, *tables, query_pre, key_pre, gains)


def body(
    tokens,
    cotangent,
    lengths,
    routes,
    attention_gain,
    query_gain,
    key_gain,
    feedforward_gain,
    query_weight,
    key_weight,
    value_weight,
    output_weight,
    router_weight,
    expert_gate_up,
    expert_down,
):
    span, width = tokens.shape
    core = lax.axis_index("dp")
    both = ("expert", "dp")
    devices = lax.axis_size("expert") * 2
    gains = jnp.concatenate([attention_gain, query_gain, key_gain, feedforward_gain])
    packed = jnp.concatenate([router_weight, gains.reshape(4, -1).T], axis=1)
    other = lax.ppermute(packed, both, [(d, d ^ 1) for d in range(devices)])
    packed = jnp.where(
        core == 0,
        jnp.concatenate([packed, other], axis=0),
        jnp.concatenate([other, packed], axis=0),
    )
    router_full, gains = packed[:, :-4], packed[:, -4:].T.astype(F32)
    gain_in, gain_query, gain_key, gain_mid = gains[0], gains[1], gains[2], gains[3]
    experts = router_full.shape[1]
    cap = span * TOP // experts
    per = experts // OUTER

    seq_length = lengths[0]
    index_rows = jnp.arange(span, dtype=jnp.int32)
    expert_ids = jnp.arange(experts, dtype=jnp.int32)
    hits = jnp.any(routes[None, :, :] == expert_ids[:, None, None], axis=-1)
    hits = hits & (index_rows < seq_length)[None, :]
    earlier = (index_rows[:, None] < index_rows[None, :]).astype(BF16)
    before = jnp.dot(hits.astype(BF16), earlier, preferred_element_type=F32)
    kept = hits & (before < cap)
    pos = jnp.where(kept, before, -1.0)
    inputs = tokens.astype(F32)
    cosine_table, sine_table = rotary_tables(index_rows.astype(F32))
    signs = jnp.where(jnp.arange(HD) < HD // 2, -1.0, 1.0)
    limit = jnp.minimum(index_rows, seq_length - 1).astype(F32)[:, None]
    tables = (cosine_table, sine_table * signs)
    (
        cot_slots, pos_here, pos_all, query_full, key_full, value_full, output_full,
        other_gate_up, other_down, turned,
        normed_in, query_pre, key_pre, query_rot, key_rot, value_all, log_total, attended,
        middle, normed_mid, gates,
    ) = attend(
        tokens, cotangent, pos[:, None, :], gains, tables, limit, router_full,
        (query_weight, key_weight, value_weight, output_weight, expert_gate_up, expert_down),
        cap, 1,
    )
    norm_mid_back = jax.vjp(norm_apply, middle, gain_mid)[1]
    def mul(left, right, spec):
        return jnp.einsum(spec, left, right, preferred_element_type=F32)

    back_rows, prob_grad, slots, gate_grad_low, up_grad_low, hidden_gated, expert_out = run_experts(
        normed_mid, gates.T[:, None, :], pos_all, pos_here, cot_slots,
        (expert_gate_up, expert_down, other_gate_up, other_down), 2,
    )
    prob_grad = prob_grad[:, 0].T
    back_rows, turned = lax.optimization_barrier((back_rows, turned))
    wide = per == 4 and width % 512 == 0
    if wide:

        def moved(d, cross):
            to = d % 2 ^ cross
            return (d // 2 ^ 1 + to) * 2 + to

        lefts = [turned, lax.ppermute(turned, both, [(d, d ^ 1) for d in range(devices)])] + [
            lax.ppermute(turned, both, [(d, moved(d, cross)) for d in range(devices)])
            for cross in range(2)
        ]

    upstream = cotangent.astype(F32)
    logit_grad = (
        gates * (prob_grad - jnp.sum(gates * prob_grad, axis=-1, keepdims=True))
    ).astype(BF16)
    grad_router = mul(normed_mid, logit_grad, "td,te->de")
    mid_normed_grad = mul(logit_grad, router_full, "te,de->td") + back_rows
    mid_input_grad, grad_mid_gain = norm_mid_back(mid_normed_grad)
    middle_grad = upstream + mid_input_grad
    branch_grad = middle_grad.astype(BF16)
    attended_grad = mul(branch_grad, output_full, "to,io->ti").astype(BF16)
    value_grad, query_low, key_low, grad_query_gain, grad_key_gain = heads_back(
        query_rot, key_rot, value_all, attended_grad, log_total, limit, tables,
        query_pre, key_pre, gains,
    )
    grad_query_gain, grad_key_gain = grad_query_gain[0], grad_key_gain[0]
    rights = (branch_grad, value_grad, key_low, query_low)
    if wide:
        expert_out, lefts, rights = lax.optimization_barrier((expert_out, lefts, rights))
        grads, grad_tokens, grad_in_gain = weight_grads(
            lefts, rights, (query_full, key_full, value_full), tokens, gain_in[None],
            middle_grad, experts, 5,
        )
        grad_in_gain = grad_in_gain[0]
    else:
        grads = []
        for source, right in zip(SOURCE, rights):
            grad = jnp.dot(turned[source], right, preferred_element_type=F32).astype(BF16)
            grid = grad.reshape(experts, 2, width // experts // 2, width).swapaxes(0, 1)
            half = lax.psum_scatter(grid, "dp", scatter_dimension=0, tiled=False)
            half = lax.psum_scatter(half, "expert", scatter_dimension=0, tiled=False)
            grads.append(half.astype(F32))
        normed_in_grad = mul(query_low, query_full, "to,io->ti")
        normed_in_grad = normed_in_grad + mul(key_low, key_full, "to,io->ti")
        normed_in_grad = normed_in_grad + mul(value_grad, value_full, "to,io->ti")
        input_grad, grad_in_gain = jax.vjp(norm_apply, inputs, gain_in)[1](normed_in_grad)
        grad_tokens = middle_grad + input_grad

    small = jnp.concatenate(
        [
            jnp.stack([grad_in_gain, grad_query_gain, grad_key_gain, grad_mid_gain]).T,
            grad_router,
        ],
        axis=1,
    )
    kinds = small.shape[1]
    small = small.reshape(OUTER, 2 * per, -1, kinds).transpose(1, 0, 3, 2)
    output, small, grad_gate_up, grad_down = combine(
        expert_out, pos_all, middle, small.reshape(2 * per, OUTER, 1, -1), slots, cot_slots,
        gate_grad_low, up_grad_low, hidden_gated, 4,
    )
    small = small.reshape(kinds, -1).T
    return (
        output,
        grad_tokens,
        small[:, 0],
        small[:, 1],
        small[:, 2],
        small[:, 3],
        grads[3],
        grads[2],
        grads[1],
        grads[0],
        small[:, 4:],
        grad_gate_up[None],
        grad_down[None],
    )


def solution(mesh):
    both = P(("expert", "dp"))
    rows = P(("expert", "dp"), None)
    in_specs = (rows, rows, both, rows) + (P("dp"),) * 4 + (P("dp", None),) * 5 + (
        P("expert", None, None, "dp"),
        P("expert", None, "dp"),
    )
    out_specs = (rows, rows) + (both,) * 4 + (rows,) * 5 + (
        P("expert", None, None, "dp"),
        P("expert", None, "dp"),
    )
    return jax.shard_map(body, mesh=mesh, in_specs=in_specs, out_specs=out_specs, check_vma=False)
```

```python
import functools
import math

import jax
import jax.numpy as jnp
from jax import lax
from jax.experimental import pallas as pl
from jax.experimental.pallas import tpu as pltpu
from jax.sharding import PartitionSpec as P

NH = 16
HD = 128
TOP = 8
OUTER = 4

EPSILON = 1e-05
ROPE_BASE = 10000.0
MESH = pl.DeviceIdType.MESH
F32 = jnp.float32
BF16 = jnp.bfloat16


def rms_scale(values):
    return lax.rsqrt(jnp.mean(values * values, axis=-1, keepdims=True) + EPSILON)


def norm_apply(values, gain_vector):
    return values * rms_scale(values) * gain_vector


def rotary_tables(positions):
    frequencies = 1.0 / ROPE_BASE ** (jnp.arange(0, HD, 2).astype(F32) / HD)
    angles = positions[:, None] * frequencies[None, :]
    angles = jnp.concatenate([angles, angles], axis=-1)
    return (jnp.cos(angles), jnp.sin(angles))


def flip(r, n):
    out, bit = r, 1
    while bit <= n:
        if n & bit:
            out = out + bit - 2 * bit * ((r // bit) % 2)
        bit *= 2
    return out


def pick(table, z):
    code = sum(v * 4**k for k, v in enumerate(table))
    return (code // ((1 + 3 * (z % 2)) * (1 + 15 * (z // 2)))) % 4


NEAR = ((1, 0, 3, 2), (2, 2, 1, 1), (3, 3, 0, 0))
PLACE = (2, 3, 1)
BLOCK = ((2, 2, 1, 1), (3, 3, 0, 0), (1, 0, 3, 2))
FAR = ((3, 3, 0, 0), (2, 0, 3, 1), (1, 2, 1, 2))


def one_hot(pos_ref, r, j, per, cap):
    span = pos_ref.shape[-1]
    rows = []
    slot = lax.broadcasted_iota(jnp.int32, (cap, span), 0).astype(F32)
    for n in range(per):
        line = pos_ref[j, flip(r, n)]
        rows.append(jnp.where(line == slot, 1.0, 0.0).astype(BF16))
    return jnp.concatenate(rows, axis=0)


def attend_body(per, cap, *refs):
    tok_ref, x_ref, meta_ref, gains_ref, cos_ref, sin_ref, limit_ref, router_ref = refs[:8]
    parts, refs = refs[8:14], refs[14:]
    out_ref, here_ref, pos_ref = refs[:3]
    fulls, refs = refs[3:9], refs[9:]
    turned_ref, nin_ref, qpre, kpre, qrot, krot, val_ref, lse_ref, att_ref, mid_ref = refs[:10]
    nmid_ref, gates_ref, zbuf, sbuf, wbuf, vacc = refs[10:16]
    zs, zr, ps, pr, ls, ms, mr, ts, tr, ds, dr, ks, fs = refs[16:]
    e, c = lax.axis_index("expert"), lax.axis_index("dp")
    z, r = e // per, e % per
    experts = OUTER * per
    bar = pltpu.get_barrier_semaphore()
    for d in range(1, experts):
        pl.semaphore_signal(bar, inc=1, device_id=((e + d) % experts, c), device_id_type=MESH)
    pl.semaphore_signal(bar, inc=1, device_id=(e, 1 - c), device_id_type=MESH)
    pl.semaphore_wait(bar, experts)
    span, width = x_ref.shape
    step = min(512, width)
    half = width // 2

    def share(d):
        to = (e + d) % experts
        return pltpu.make_async_remote_copy(
            src_ref=meta_ref.at[to], dst_ref=here_ref.at[e], send_sem=ms.at[d - 1],
            recv_sem=mr.at[d - 1], device_id=(to, c), device_id_type=MESH,
        )

    def table(d):
        to = (z + d) % OUTER
        return pltpu.make_async_remote_copy(
            src_ref=meta_ref.at[pl.ds(to * per, per)], dst_ref=pos_ref.at[z],
            send_sem=ts.at[d - 1], recv_sem=tr.at[z],
            device_id=(to * per + r, c), device_id_type=MESH,
        )

    def tabled(j):
        return pltpu.make_async_remote_copy(
            src_ref=meta_ref.at[pl.ds(0, per)], dst_ref=pos_ref.at[j], send_sem=ts.at[0],
            recv_sem=tr.at[j], device_id=(j * per + r, c), device_id_type=MESH,
        )

    def up(src, j):
        return pltpu.make_async_remote_copy(
            src_ref=src, dst_ref=zbuf.at[j], send_sem=zs.at[0, j], recv_sem=zr.at[j],
            device_id=((z + 1) * per + r, c), device_id_type=MESH,
        )

    def down(src, j):
        return pltpu.make_async_remote_copy(
            src_ref=src, dst_ref=zbuf.at[j], send_sem=zs.at[1, j], recv_sem=zr.at[j],
            device_id=((z - 1) * per + r, c), device_id_type=MESH,
        )

    def plane(i, j, n):
        return pltpu.make_async_remote_copy(
            src_ref=sbuf.at[i, n], dst_ref=out_ref.at[j, n], send_sem=ps.at[i, n],
            recv_sem=pr.at[i, n], device_id=(z * per + flip(r, n), c), device_id_type=MESH,
        )

    def local(i, j):
        return pltpu.make_async_copy(sbuf.at[i, 0], out_ref.at[j, 0], ls.at[i])

    def lines(owner):
        return pl.ds(pl.multiple_of(owner * half, half), half)

    def give(k):
        return pltpu.make_async_remote_copy(
            src_ref=parts[k], dst_ref=fulls[k].at[lines(c)] if k < 4 else fulls[k], send_sem=ds.at[k],
            recv_sem=dr.at[k], device_id=(e, 1 - c), device_id_type=MESH,
        )

    def hold(t):
        return pltpu.make_async_copy(wbuf.at[t % 2], fulls[jobs[t][0]].at[lines(c)], ks.at[t % 2])

    jobs = [(0, 0), (1, 0), (2, 0), (0, 1), (1, 1), (2, 1), (3, 0), (3, 1)]

    def fetch(t):
        k, far = jobs[t]
        src = fulls[k].at[lines(1 - c)] if far else parts[k]
        return pltpu.make_async_copy(src, wbuf.at[t % 2], fs.at[t % 2])

    def project(t):
        k, far = jobs[t]
        left = att_ref if k == 3 else nin_ref
        into = (qpre, kpre, vacc, mid_ref)[k]
        if t == 3:
            for q in range(2):
                give(q).wait_recv()
                fetch(t + q).start()
        fetch(t).wait()
        if not far:
            hold(t).start()
        mine = lines(1 - c if far else c)

        @pl.loop(0, width // step)
        def _(q):
            columns = pl.ds(pl.multiple_of(q * step, step), step)
            got = jnp.dot(left[:, mine], wbuf[t % 2, :, columns], preferred_element_type=F32)
            if k == 3 and not far:
                into[:, columns] = tok_ref[:, columns].astype(F32) + got
            elif far:
                into[:, columns] += got
            else:
                into[:, columns] = got

        if not far:
            hold(t).wait()
        if t in (0, 4):
            fetch(t + 2).start()
        elif t in (3, 5):
            give(jobs[t + 2][0]).wait_recv()
            fetch(t + 2).start()

    order = [z] + [pick(t, z) for t in NEAR]

    edge = jnp.logical_or(z == 0, z == OUTER - 1)

    def relay(places):
        @pl.when(jnp.logical_not(edge))
        def _():
            for i in places:
                j = order[i]
                up(x_ref, j).wait_recv()

                @pl.when(j < z)
                def _():
                    up(zbuf.at[j], j).start()

                @pl.when(j > z)
                def _():
                    down(zbuf.at[j], j).start()

    def choose(i, j):
        block = x_ref if i == 0 else zbuf.at[j]
        if i > 0:

            @pl.when(edge)
            def _():
                up(x_ref, j).wait_recv()

            tabled(j).wait_recv()

        marks = one_hot(pos_ref, r, j, per, cap)

        @pl.loop(0, width // step)
        def _(k):
            columns = pl.ds(pl.multiple_of(k * step, step), step)
            got = jnp.dot(marks, block[:, columns], preferred_element_type=F32).astype(BF16)
            for n in range(per):
                sbuf[i, n, :, columns] = got[n * cap : (n + 1) * cap]

        for n in range(1, per):
            plane(i, j, n).start()
        local(i, j).start()

    for d in range(1, OUTER):
        table(d).start()

    @pl.when(z < OUTER - 1)
    def _():
        up(x_ref, z).start()

    @pl.when(z > 0)
    def _():
        down(x_ref, z).start()

    fetch(0).start()
    fetch(1).start()
    pos_ref[z] = meta_ref[pl.ds(z * per, per)]
    here_ref[e] = meta_ref[e]
    choose(0, z)
    for k in range(6):
        give(k).start()
    for d in range(1, experts):
        share(d).start()

    inputs = tok_ref[...].astype(F32)
    nin_ref[...] = norm_apply(inputs, gains_ref[0:1]).astype(BF16)
    for t in range(3):
        project(t)
    relay((1, 2))
    choose(1, order[1])
    for t in range(3, 6):
        project(t)
    val_ref[...] = vacc[...].astype(BF16)
    query_scale = rms_scale(qpre[...])
    key_scale = rms_scale(kpre[...])
    turned_ref[0] = nin_ref[...].T
    score_scale = HD ** (-0.5)
    column = lax.broadcasted_iota(jnp.int32, (span, span), 1).astype(F32)

    def heads(first, last):
        @pl.loop(first, last)
        def _(h):
            columns = pl.ds(pl.multiple_of(h * HD, HD), HD)

            def turn(pre, scale, row):
                normed = pre[:, columns] * scale * gains_ref[row : row + 1, columns]
                return (
                    normed * cos_ref[...] + pltpu.roll(normed, HD // 2, 1) * sin_ref[...]
                ).astype(BF16)

            query = turn(qpre, query_scale, 1)
            key = turn(kpre, key_scale, 2)
            qrot[:, columns] = query
            krot[:, columns] = key
            scores = lax.dot_general(
                query, key, (((1,), (1,)), ((), ())), preferred_element_type=F32
            )
            scores = jnp.where(column <= limit_ref[...], scores * score_scale, -1e30)
            peak = jnp.max(scores, axis=-1, keepdims=True)
            total = peak + jnp.log(jnp.sum(jnp.exp(scores - peak), axis=-1, keepdims=True))
            lse_ref[h] = total
            weights = jnp.exp(scores - total).astype(BF16)
            att_ref[:, columns] = jnp.dot(
                weights, val_ref[:, columns], preferred_element_type=F32
            ).astype(BF16)

    heads(0, NH // 2)
    choose(2, order[2])
    relay((3,))
    heads(NH // 2, NH)
    project(6)
    choose(3, order[3])
    project(7)
    turned_ref[1] = att_ref[...].T
    middle = mid_ref[...]
    nmid_ref[...] = norm_apply(middle, gains_ref[3:4]).astype(BF16)
    logits = jnp.dot(nmid_ref[...], router_ref[...], preferred_element_type=F32)
    raised = jnp.exp(logits - jnp.max(logits, axis=-1, keepdims=True))
    gates_ref[...] = raised / jnp.sum(raised, axis=-1, keepdims=True)

    for i, j in enumerate(order):
        local(i, j).wait()
        for n in range(1, per):
            plane(i, j, n).wait()

    @pl.when(z < OUTER - 1)
    def _():
        up(x_ref, z).wait_send()

    @pl.when(z > 0)
    def _():
        down(x_ref, z).wait_send()

    for j in order[1:]:

        @pl.when(jnp.logical_and(j < z, z < OUTER - 1))
        def _():
            up(zbuf.at[j], j).wait_send()

        @pl.when(jnp.logical_and(j > z, z > 0))
        def _():
            down(zbuf.at[j], j).wait_send()

    for d in range(1, experts):
        share(d).wait()
    for d in range(1, OUTER):
        table(d).wait_send()
    for k in range(6):
        give(k).wait_send()
    for k in range(4, 6):
        give(k).wait_recv()


def attend(tokens, cotangent, meta, gains, tables, limit, router, parts, cap, number):
    experts, _, span = meta.shape
    per = experts // OUTER
    width = tokens.shape[1]
    half = parts[0].shape[0]
    vmem = pl.BlockSpec(memory_space=pltpu.VMEM)
    hbm = pl.BlockSpec(memory_space=pltpu.HBM)
    dma = pltpu.SemaphoreType.DMA
    low = jax.ShapeDtypeStruct((span, width), BF16)
    high = jax.ShapeDtypeStruct((span, width), F32)
    return pl.pallas_call(
        functools.partial(attend_body, per, cap),
        out_shape=(
            jax.ShapeDtypeStruct((OUTER, per, cap, width), BF16),
            jax.ShapeDtypeStruct((experts, 1, span), F32),
            jax.ShapeDtypeStruct((OUTER, per, 1, span), F32),
        )
        + (jax.ShapeDtypeStruct((2 * half, width), BF16),) * 4
        + tuple(jax.ShapeDtypeStruct(part.shape, BF16) for part in parts[4:])
        + (jax.ShapeDtypeStruct((2, width, span), BF16), low, high, high, low, low, low)
        + (jax.ShapeDtypeStruct((NH, span, 1), F32), low, high, low)
        + (jax.ShapeDtypeStruct((span, experts), F32),),
        in_specs=[vmem] * 8 + [hbm] * 6,
        out_specs=(hbm, vmem, vmem) + (hbm,) * 6 + (vmem,) * 12,
        scratch_shapes=[
            pltpu.VMEM((OUTER, span, width), BF16),
            pltpu.VMEM((OUTER, per, cap, width), BF16),
            pltpu.VMEM((2, half, width), BF16),
            pltpu.VMEM((span, width), F32),
            dma((2, OUTER)),
            dma((OUTER,)),
            dma((OUTER, per)),
            dma((OUTER, per)),
            dma((OUTER,)),
            dma((experts,)),
            dma((experts,)),
            dma((OUTER,)),
            dma((OUTER,)),
            dma((6,)),
            dma((6,)),
            dma((2,)),
            dma((2,)),
        ],
        compiler_params=pltpu.CompilerParams(
            collective_id=number, has_side_effects=True, vmem_limit_bytes=60 << 20
        ),
        name="attend",
    )(tokens, cotangent, meta, gains, *tables, limit, router, *parts)


def experts_body(per, cap, *refs):
    x_ref, gates_ref, pos_ref, posh_ref, cot_ref, gu_mine, dn_mine, gu_other, dn_other = refs[:9]
    refs = refs[1:]
    back_ref, pg_ref, out_ref, gl_ref, ul_ref, hg_ref, eo_ref = refs[8:15]
    zbuf, sbuf, wg, wu, wd, slb, ctb, glb, ulb, hlb, hgb, eob, ybuf, ubuf, rbuf = refs[15:30]
    here, ggv, sgv, tgv = refs[30:34]
    zs, zr, ps, pr, ls, ms, mr, ws, cs, os, es, bs, br, us, ur, gs, gr = refs[34:]
    e, c = lax.axis_index("expert"), lax.axis_index("dp")
    z, r = e // per, e % per
    experts = OUTER * per
    bar = pltpu.get_barrier_semaphore()
    for d in range(1, experts):
        pl.semaphore_signal(bar, inc=1, device_id=((e + d) % experts, c), device_id_type=MESH)
    pl.semaphore_wait(bar, experts - 1)
    span, width = x_ref.shape
    hidden = wg.shape[1]
    step = min(512, width)
    thin = min(256, hidden)
    halves = 2
    half = width // halves

    def share(d):
        to = (e + d) % experts
        return pltpu.make_async_remote_copy(
            src_ref=gates_ref.at[to], dst_ref=here.at[e], send_sem=ms.at[d - 1],
            recv_sem=mr.at[d - 1], device_id=(to, c), device_id_type=MESH,
        )

    def up(src, j):
        return pltpu.make_async_remote_copy(
            src_ref=src, dst_ref=zbuf.at[j], send_sem=zs.at[0, j], recv_sem=zr.at[j],
            device_id=((z + 1) * per + r, c), device_id_type=MESH,
        )

    def down(src, j):
        return pltpu.make_async_remote_copy(
            src_ref=src, dst_ref=zbuf.at[j], send_sem=zs.at[1, j], recv_sem=zr.at[j],
            device_id=((z - 1) * per + r, c), device_id_type=MESH,
        )

    def plane(i, j, n):
        return pltpu.make_async_remote_copy(
            src_ref=sbuf.at[i, n], dst_ref=out_ref.at[j, n], send_sem=ps.at[i, n],
            recv_sem=pr.at[i, n], device_id=(z * per + flip(r, n), c), device_id_type=MESH,
        )

    def local(i, j):
        return pltpu.make_async_copy(sbuf.at[i, 0], out_ref.at[j, 0], ls.at[i])

    def returned(i, n):
        return pltpu.make_async_remote_copy(
            src_ref=sbuf.at[i, n], dst_ref=ybuf.at[i, n - 1], send_sem=bs.at[i, n],
            recv_sem=br.at[i, n], device_id=(z * per + flip(r, n), c), device_id_type=MESH,
        )

    def part(h):
        return pl.ds(h * half, half)

    def rise(i, j, h, slot):
        return pltpu.make_async_remote_copy(
            src_ref=ubuf.at[i, h], dst_ref=rbuf.at[slot, h], send_sem=us.at[i, h],
            recv_sem=ur.at[slot, h], device_id=((z + 1) * per + r, c), device_id_type=MESH,
        )

    def fall(i, j, h, slot):
        return pltpu.make_async_remote_copy(
            src_ref=ubuf.at[i, h], dst_ref=rbuf.at[slot, h], send_sem=us.at[i, h],
            recv_sem=ur.at[slot, h], device_id=((z - 1) * per + r, c), device_id_type=MESH,
        )

    def graded(i, n, seq):
        return pltpu.make_async_remote_copy(
            src_ref=tgv.at[i, n], dst_ref=pg_ref.at[e], send_sem=gs.at[i, n],
            recv_sem=gr.at[e], device_id=(seq, c), device_id_type=MESH,
        )

    def grade(s):
        return pltpu.make_async_remote_copy(
            src_ref=tgv.at[0, 0], dst_ref=pg_ref.at[s], send_sem=gs.at[0, 0],
            recv_sem=gr.at[s], device_id=(s, c), device_id_type=MESH,
        )

    def columns_of(owner):
        return pl.ds(pl.multiple_of(owner * (hidden // 2), hidden // 2), hidden // 2)

    weights = [
        pltpu.make_async_copy(src, dst.at[:, columns_of(owner)], ws.at[k, f])
        for f, (owner, both, down_part) in enumerate(
            ((c, gu_mine, dn_mine), (1 - c, gu_other, dn_other))
        )
        for k, (src, dst) in enumerate(
            ((both.at[0, 0], wg), (both.at[0, 1], wu), (down_part.at[0], wd))
        )
    ]

    def pull(j):
        return pltpu.make_async_copy(cot_ref.at[j], ctb, cs)

    for d in range(1, experts):
        share(d).start()

    @pl.when(z < OUTER - 1)
    def _():
        up(x_ref, z).start()

    @pl.when(z > 0)
    def _():
        down(x_ref, z).start()

    here[e] = gates_ref[e]
    order = [z] + [pick(t, z) for t in NEAR]

    edge = jnp.logical_or(z == 0, z == OUTER - 1)

    def relay(places):
        @pl.when(jnp.logical_not(edge))
        def _():
            for i in places:
                j = order[i]
                up(x_ref, j).wait_recv()

                @pl.when(j < z)
                def _():
                    up(zbuf.at[j], j).start()

                @pl.when(j > z)
                def _():
                    down(zbuf.at[j], j).start()

    def choose(i, j):
        block = x_ref if i == 0 else zbuf.at[j]
        if i > 0:

            @pl.when(edge)
            def _():
                up(x_ref, j).wait_recv()

        marks = one_hot(pos_ref, r, j, per, cap)

        @pl.loop(0, width // step)
        def _(k):
            columns = pl.ds(pl.multiple_of(k * step, step), step)
            got = jnp.dot(marks, block[:, columns], preferred_element_type=F32).astype(BF16)
            for n in range(per):
                sbuf[i, n, :, columns] = got[n * cap : (n + 1) * cap]

        for n in range(1, per):
            plane(i, j, n).start()
        local(i, j).start()

    def outs(j):
        return [
            pltpu.make_async_copy(src, dst.at[j], os.at[k])
            for k, (src, dst) in enumerate(((glb, gl_ref), (ulb, ul_ref), (hgb, hg_ref)))
        ]

    def away(j):
        return pltpu.make_async_copy(eob, eo_ref.at[j], es)

    def marked(j, n):
        slot = lax.broadcasted_iota(jnp.int32, (cap, span), 0).astype(F32)
        return posh_ref[j * per + flip(r, n)] == slot

    def expert(i, j):
        for n in range(1, per):
            plane(i, j, n).wait()
        local(i, j).wait()
        if i == OUTER - 1:
            send_back(PLACE[0])
        fetch = pltpu.make_async_copy(out_ref.at[j], slb, ls.at[OUTER])
        fetch.start()
        slot_gate = jnp.concatenate(
            [
                jnp.sum(
                    jnp.where(marked(j, n), here[j * per + flip(r, n)], 0.0), axis=1, keepdims=True
                )
                for n in range(per)
            ],
            axis=0,
        )
        sgv[i % 2] = slot_gate
        ggv[i % 2] = jnp.zeros(ggv.shape[1:], F32)
        pull(j).wait()
        fetch.wait()
        if i > 0:
            for copy in outs(order[i - 1]):
                copy.wait()

        @pl.loop(0, hidden // thin)
        def _(k):
            columns = pl.ds(pl.multiple_of(k * thin, thin), thin)
            rows = slb[...].reshape(per * cap, width)
            gate_pre = jnp.dot(rows, wg[:, columns], preferred_element_type=F32)
            up_pre = jnp.dot(rows, wu[:, columns], preferred_element_type=F32)
            pulled = jnp.dot(
                ctb[...].reshape(per * cap, width), wd[:, columns], preferred_element_type=F32
            )
            sigmoid_gate = jax.nn.sigmoid(gate_pre)
            silu_gate = gate_pre * sigmoid_gate
            low = (silu_gate * up_pre).astype(BF16)
            wide = low.astype(F32)
            ggv[i % 2] += jnp.sum(wide * pulled, axis=1, keepdims=True)
            hidden_grad = pulled * slot_gate
            glb[:, columns] = (
                hidden_grad * up_pre * sigmoid_gate * (1.0 + gate_pre * (1.0 - sigmoid_gate))
            ).astype(BF16)
            ulb[:, columns] = (hidden_grad * silu_gate).astype(BF16)
            hlb[i % 2, :, columns] = low
            hgb[:, columns] = (wide * slot_gate).astype(BF16)

        if i < OUTER - 1:
            pull(order[i + 1]).start()
        for copy in outs(j):
            copy.start()

        @pl.loop(0, width // step)
        def _(k):
            columns = pl.ds(pl.multiple_of(k * step, step), step)
            got = lax.dot_general(
                glb[...], wg[columns, :], (((1,), (1,)), ((), ())), preferred_element_type=F32
            ) + lax.dot_general(
                ulb[...], wu[columns, :], (((1,), (1,)), ((), ())), preferred_element_type=F32
            )
            got = got.astype(BF16)
            for n in range(per):
                sbuf[i, n, :, columns] = got[n * cap : (n + 1) * cap]

    def send_back(i):
        for n in range(1, per):
            returned(i, n).start()

    def finish(i, j):
        for n in range(per):
            seq = j * per + flip(r, n)
            row = jnp.sum(
                jnp.where(marked(j, n), ggv[i % 2, n * cap : (n + 1) * cap], 0.0),
                axis=0,
                keepdims=True,
            )
            tgv[i, n] = row
            if i == 0 and n == 0:
                pg_ref[e] = row
            else:
                graded(i, n, seq).start()
        if i > 0:
            away(order[i - 1]).wait()

        @pl.loop(0, width // step)
        def _(k):
            columns = pl.ds(pl.multiple_of(k * step, step), step)
            got = lax.dot_general(
                hlb[i % 2], wd[columns, :], (((1,), (1,)), ((), ())), preferred_element_type=F32
            )
            got = (got * sgv[i % 2]).astype(BF16)
            for n in range(per):
                eob[n, :, columns] = got[n * cap : (n + 1) * cap]

        away(j).start()

    choose(0, z)
    for copy in weights:
        copy.start()
    pull(z).start()
    relay((1, 2))
    choose(1, order[1])
    for copy in weights:
        copy.wait()
    for d in range(1, experts):
        share(d).wait()
    last = OUTER - 1
    for i in range(last):
        expert(i, order[i])
        if i + 2 <= last:
            choose(i + 2, order[i + 2])
            if i == 0:
                relay((3,))
            finish(i, order[i])
    expert(last, order[last])
    for i in (*PLACE[1:], 0):
        send_back(i)
    finish(last - 1, order[last - 1])

    def fold(i, j, h):
        marks = one_hot(pos_ref, r, j, per, cap)

        @pl.loop(0, half // step)
        def _(k):
            columns = pl.ds(pl.multiple_of(h * half + k * step, step), step)
            rows = jnp.concatenate(
                [ybuf[i, n - 1, :, columns] if n else sbuf[i, 0, :, columns] for n in range(per)],
                axis=0,
            )
            back_ref[:, columns] = lax.dot_general(
                marks, rows, (((0,), (0,)), ((), ())), preferred_element_type=F32
            )

    for p in range(last):
        i, j = PLACE[p], pick(BLOCK[p], z)
        for n in range(1, per):
            returned(i, n).wait_recv()
        for h in range(halves):
            fold(i, j, h)

            @pl.when(jnp.logical_and(j > z, z > 0))
            def _():
                rise(0, j, h, j).wait_recv()
                back_ref[:, part(h)] += rbuf[j, h].astype(F32)

            @pl.when(jnp.logical_and(j < z, z < OUTER - 1))
            def _():
                fall(0, j, h, j).wait_recv()
                back_ref[:, part(h)] += rbuf[j, h].astype(F32)

            ubuf[p, h] = back_ref[:, part(h)].astype(BF16)

            @pl.when(j > z)
            def _():
                rise(p, j, h, j).start()

            @pl.when(jnp.logical_and(j < z, z - j > 1))
            def _():
                fall(p, j, h, j).start()

            @pl.when(z - j == 1)
            def _():
                fall(p, j, h, OUTER).start()

        if p == 0:
            finish(last, order[last])

    for n in range(1, per):
        returned(0, n).wait_recv()
    for h in range(halves):
        fold(0, z, h)

        @pl.when(z > 0)
        def _():
            rise(0, z, h, z).wait_recv()
            back_ref[:, part(h)] += rbuf[z, h].astype(F32)

        @pl.when(z < OUTER - 1)
        def _():
            fall(0, z, h, OUTER).wait_recv()
            back_ref[:, part(h)] += rbuf[OUTER, h].astype(F32)

    @pl.when(z < OUTER - 1)
    def _():
        up(x_ref, z).wait_send()

    @pl.when(z > 0)
    def _():
        down(x_ref, z).wait_send()

    for i, j in enumerate(order):
        for n in range(1, per):
            returned(i, n).wait_send()
        if i > 0:

            @pl.when(jnp.logical_and(j < z, z < OUTER - 1))
            def _():
                up(zbuf.at[j], j).wait_send()

            @pl.when(jnp.logical_and(j > z, z > 0))
            def _():
                down(zbuf.at[j], j).wait_send()

            for h in range(halves):
                rise(i - 1, j, h, j).wait_send()
        for n in range(per):
            if i or n:
                graded(i, n, j * per + flip(r, n)).wait_send()
    for d in range(1, experts):
        grade((e + d) % experts).wait_recv()
    for copy in outs(order[last]):
        copy.wait()
    away(order[last]).wait()


def run_experts(x, gates, pos, pos_here, cot_slots, weights, number):
    experts, _, span = gates.shape
    outer, per, cap, width = cot_slots.shape
    hidden = 2 * weights[0].shape[-1]
    block = per * cap
    vmem = pl.BlockSpec(memory_space=pltpu.VMEM)
    hbm = pl.BlockSpec(memory_space=pltpu.HBM)
    dma = pltpu.SemaphoreType.DMA
    rows = jax.ShapeDtypeStruct((OUTER, per, cap, width), BF16)
    thin = jax.ShapeDtypeStruct((OUTER, block, hidden), BF16)
    return pl.pallas_call(
        functools.partial(experts_body, per, cap),
        out_shape=(
            jax.ShapeDtypeStruct((span, width), F32),
            jax.ShapeDtypeStruct((experts, 1, span), F32),
            rows, thin, thin, thin, rows,
        ),
        in_specs=[vmem] * 4 + [hbm] * 5,
        out_specs=(vmem, vmem) + (hbm,) * 5,
        scratch_shapes=[
            pltpu.VMEM((OUTER, span, width), BF16),
            pltpu.VMEM((OUTER, per, cap, width), BF16),
            pltpu.VMEM((width, hidden), BF16),
            pltpu.VMEM((width, hidden), BF16),
            pltpu.VMEM((width, hidden), BF16),
            pltpu.VMEM((per, cap, width), BF16),
            pltpu.VMEM((per, cap, width), BF16),
            pltpu.VMEM((block, hidden), BF16),
            pltpu.VMEM((block, hidden), BF16),
            pltpu.VMEM((2, block, hidden), BF16),
            pltpu.VMEM((block, hidden), BF16),
            pltpu.VMEM((per, cap, width), BF16),
            pltpu.VMEM((OUTER, per - 1, cap, width), BF16),
            pltpu.VMEM((OUTER - 1, 2, span, width // 2), BF16),
            pltpu.VMEM((OUTER + 1, 2, span, width // 2), BF16),
            pltpu.VMEM((experts, 1, span), F32),
            pltpu.VMEM((2, block, 1), F32),
            pltpu.VMEM((2, block, 1), F32),
            pltpu.VMEM((OUTER, per, 1, span), F32),
            dma((2, OUTER)),
            dma((OUTER,)),
            dma((OUTER, per)),
            dma((OUTER, per)),
            dma((OUTER + 1,)),
            dma((experts,)),
            dma((experts,)),
            dma((3, 2)),
            dma,
            dma((3,)),
            dma,
            dma((OUTER, per)),
            dma((OUTER, per)),
            dma((OUTER - 1, 2)),
            dma((OUTER + 1, 2)),
            dma((OUTER, per)),
            dma((experts,)),
        ],
        compiler_params=pltpu.CompilerParams(
            collective_id=number, has_side_effects=True, vmem_limit_bytes=62 << 20
        ),
        name="experts",
    )(x, gates, pos, pos_here, cot_slots, *weights)


def combine_body(per, cap, *refs):
    y_ref, pos_ref, mid_ref, small_ref, slots_ref, cot_ref, gl_ref, ul_ref, hg_ref = refs[:9]
    res_ref, total_ref, gu_ref, dn_ref, out_ref, ybuf, ubuf, rbuf = refs[9:17]
    theirs, ours, lbuf, lturn, tbuf, rx, stage, lall, lsum, lz = refs[17:27]
    zs, zr, ps, pr, ls, rs, ws, ds, dr, gs, las, lar, tas, tar = refs[27:]
    e, c = lax.axis_index("expert"), lax.axis_index("dp")
    z, r = e // per, e % per
    bar = pltpu.get_barrier_semaphore()
    for d in range(1, OUTER):
        pl.semaphore_signal(
            bar, inc=1, device_id=((z + d) % OUTER * per + r, c), device_id_type=MESH
        )
    peers = [(n, f) for n in range(per) for f in range(2)]

    def device(n, f):
        return flip(r, n), (c + f) % 2

    for n, f in peers[1:]:
        q, k = device(n, f)
        pl.semaphore_signal(bar, inc=1, device_id=(z * per + q, k), device_id_type=MESH)
    pl.semaphore_wait(bar, OUTER - 1 + 2 * per - 1)
    span, width = out_ref.shape
    step = min(512, width)
    share = dn_ref.shape[1]
    thin = min(256, share)
    total = OUTER * per * cap

    def plane(i, j, n):
        return pltpu.make_async_remote_copy(
            src_ref=y_ref.at[j, n], dst_ref=ybuf.at[i, n], send_sem=ps.at[i, n],
            recv_sem=pr.at[i, n], device_id=(z * per + flip(r, n), c), device_id_type=MESH,
        )

    def local(i, j):
        return pltpu.make_async_copy(y_ref.at[j, 0], ybuf.at[i, 0], ls.at[i])

    halves = 2
    half = width // halves

    def part(h):
        return pl.ds(h * half, half)

    def rise(i, h, slot):
        return pltpu.make_async_remote_copy(
            src_ref=ubuf.at[i, h], dst_ref=rbuf.at[slot, h], send_sem=zs.at[i, h],
            recv_sem=zr.at[slot, h], device_id=((z + 1) * per + r, c), device_id_type=MESH,
        )

    def fall(i, h, slot):
        return pltpu.make_async_remote_copy(
            src_ref=ubuf.at[i, h], dst_ref=rbuf.at[slot, h], send_sem=zs.at[i, h],
            recv_sem=zr.at[slot, h], device_id=((z - 1) * per + r, c), device_id_type=MESH,
        )

    def rights(k, src, other):
        owner = 1 - c if other else c
        return pltpu.make_async_copy(
            src.at[:, :, pl.ds(pl.multiple_of(owner * share, share), share)],
            (theirs if other else ours).at[:, :, pl.ds(k * share, share)],
            rs.at[k, int(other)],
        )

    def across(k):
        return pltpu.make_async_remote_copy(
            src_ref=tbuf.at[k % 2], dst_ref=rx.at[k], send_sem=ds.at[k], recv_sem=dr.at[k],
            device_id=(e, 1 - c), device_id_type=MESH,
        )

    def stores(k):
        lines = pl.ds(k * step, step)
        return [
            pltpu.make_async_copy(
                stage.at[:, pl.ds(m * share, share)],
                dn_ref.at[lines] if m == 2 else gu_ref.at[m, lines],
                gs.at[m],
            )
            for m in range(3)
        ]

    def little(i):
        q, k = device(*peers[i])
        return pltpu.make_async_remote_copy(
            src_ref=small_ref.at[q * 2 + k], dst_ref=lall.at[i], send_sem=las.at[i],
            recv_sem=lar.at[i], device_id=(z * per + q, k), device_id_type=MESH,
        )

    def tall(d):
        to = (z + d) % OUTER
        return pltpu.make_async_remote_copy(
            src_ref=lsum.at[to], dst_ref=lz.at[d], send_sem=tas.at[d], recv_sem=tar.at[d],
            device_id=(to * per + r, c), device_id_type=MESH,
        )

    sources = (gl_ref, ul_ref, hg_ref)
    loads = [rights(k, src, other) for k, src in enumerate(sources) for other in (True, False)]

    def tile(k):
        if k == 0:
            for copy in loads:
                copy.wait()
        if k >= 2:
            across(k - 2).wait_send()
        if k >= 1:
            for copy in stores(k - 1):
                copy.wait()
        for src, first, count in ((slots_ref, 0, 2), (cot_ref, 2, 1)):
            fetch = pltpu.make_async_copy(
                src.at[:, :, :, pl.ds(k * step, step)], lbuf, ws
            )
            fetch.start()
            fetch.wait()
            lturn[...] = lbuf[...].reshape(total, step).T

            @pl.loop(0, count * share // thin)
            def _(q):
                at = pl.ds(pl.multiple_of(first * share + q * thin, thin), thin)
                tbuf[k % 2, :, at] = jnp.dot(
                    lturn[...], theirs[:, :, at].reshape(total, thin), preferred_element_type=F32
                ).astype(BF16)
                stage[:, at] = jnp.dot(
                    lturn[...], ours[:, :, at].reshape(total, thin), preferred_element_type=F32
                )

        across(k).start()
        across(k).wait_recv()
        stage[...] += rx[k].astype(F32)
        for copy in stores(k):
            copy.start()

    order = [pick(t, z) for t in FAR] + [z]
    for i, j in enumerate(order):
        for n in range(1, per):
            plane(i, j, n).start()
        local(i, j).start()
    for copy in loads:
        copy.start()
    for i in range(1, 2 * per):
        little(i).start()
    lall[0] = small_ref[r * 2 + c]
    tiles = width // step
    done = 0
    for i, j in enumerate(order):
        while done < tiles * (1, 2, 3, 4)[i] // 4:
            tile(done)
            done += 1
        if i == OUTER - 1:
            for k in range(1, 2 * per):
                little(k).wait_recv()
            lsum[...] = sum(lall[k] for k in range(2 * per))
            for d in range(1, OUTER):
                tall(d).start()
        marks = one_hot(pos_ref, r, j, per, cap)
        local(i, j).wait()
        for n in range(1, per):
            plane(i, j, n).wait_recv()
        for h in range(halves):

            @pl.loop(0, half // step)
            def _(k):
                columns = pl.ds(pl.multiple_of(h * half + k * step, step), step)
                rows = jnp.concatenate([ybuf[i, n, :, columns] for n in range(per)], axis=0)
                out_ref[:, columns] = lax.dot_general(
                    marks, rows, (((0,), (0,)), ((), ())), preferred_element_type=F32
                )

            if i < OUTER - 1:

                @pl.when(jnp.logical_and(j > z, z > 0))
                def _():
                    rise(0, h, j).wait_recv()
                    out_ref[:, part(h)] += rbuf[j, h].astype(F32)

                @pl.when(jnp.logical_and(j < z, z < OUTER - 1))
                def _():
                    fall(0, h, j).wait_recv()
                    out_ref[:, part(h)] += rbuf[j, h].astype(F32)

                ubuf[i, h] = out_ref[:, part(h)].astype(BF16)

                @pl.when(j > z)
                def _():
                    rise(i, h, j).start()

                @pl.when(jnp.logical_and(j < z, z - j > 1))
                def _():
                    fall(i, h, j).start()

                @pl.when(z - j == 1)
                def _():
                    fall(i, h, OUTER).start()
            else:

                @pl.when(z > 0)
                def _():
                    rise(0, h, z).wait_recv()
                    out_ref[:, part(h)] += rbuf[z, h].astype(F32)

                @pl.when(z < OUTER - 1)
                def _():
                    fall(0, h, OUTER).wait_recv()
                    out_ref[:, part(h)] += rbuf[OUTER, h].astype(F32)

                res_ref[:, part(h)] = (mid_ref[:, part(h)] + out_ref[:, part(h)]).astype(BF16)

    for i, j in enumerate(order):
        for n in range(1, per):
            plane(i, j, n).wait_send()
        if i < OUTER - 1:
            for h in range(halves):
                rise(i, h, j).wait_send()
    for d in range(1, OUTER):
        tall(d).wait()
    total_ref[...] = lsum[z] + sum(lz[d] for d in range(1, OUTER))
    for i in range(1, 2 * per):
        little(i).wait_send()
    for k in range(max(0, tiles - 2), tiles):
        across(k).wait_send()
    for copy in stores(tiles - 1):
        copy.wait()


def combine(y, pos_all, middle, small, slots, cot_slots, gate_low, up_low, hidden_gated, number):
    outer, per, cap, width = y.shape
    span = pos_all.shape[-1]
    block, hidden = gate_low.shape[1:]
    share = hidden // 2
    step = min(512, width)
    tiles = width // step
    vmem = pl.BlockSpec(memory_space=pltpu.VMEM)
    hbm = pl.BlockSpec(memory_space=pltpu.HBM)
    dma = pltpu.SemaphoreType.DMA
    return pl.pallas_call(
        functools.partial(combine_body, per, cap),
        out_shape=(
            jax.ShapeDtypeStruct((span, width), BF16),
            jax.ShapeDtypeStruct((1, small.shape[-1]), F32),
            jax.ShapeDtypeStruct((2, width, share), F32),
            jax.ShapeDtypeStruct((width, share), F32),
        ),
        in_specs=[hbm, vmem, vmem, vmem] + [hbm] * 5,
        out_specs=(vmem, vmem, hbm, hbm),
        scratch_shapes=[
            pltpu.VMEM((span, width), F32),
            pltpu.VMEM((OUTER, per, cap, width), BF16),
            pltpu.VMEM((OUTER - 1, 2, span, width // 2), BF16),
            pltpu.VMEM((OUTER + 1, 2, span, width // 2), BF16),
            pltpu.VMEM((OUTER, block, 3 * share), BF16),
            pltpu.VMEM((OUTER, block, 3 * share), BF16),
            pltpu.VMEM((OUTER, per, cap, step), BF16),
            pltpu.VMEM((step, OUTER * block), BF16),
            pltpu.VMEM((2, step, 3 * share), BF16),
            pltpu.VMEM((tiles, step, 3 * share), BF16),
            pltpu.VMEM((step, 3 * share), F32),
            pltpu.VMEM(small.shape, F32),
            pltpu.VMEM(small.shape[1:], F32),
            pltpu.VMEM(small.shape[1:], F32),
            dma((OUTER - 1, 2)),
            dma((OUTER + 1, 2)),
            dma((OUTER, per)),
            dma((OUTER, per)),
            dma((OUTER,)),
            dma((3, 2)),
            dma,
            dma((tiles,)),
            dma((tiles,)),
            dma((3,)),
            dma((2 * per,)),
            dma((2 * per,)),
            dma((OUTER,)),
            dma((OUTER,)),
        ],
        compiler_params=pltpu.CompilerParams(
            collective_id=number, has_side_effects=True, vmem_limit_bytes=62 << 20
        ),
        name="combine",
    )(y, pos_all, middle, small, slots, cot_slots, gate_low, up_low, hidden_gated)


def weights_body(rows, *refs):
    mats, per = len(SOURCE), 4
    x_refs, y_refs, refs = refs[:4], refs[4 : 4 + mats], refs[4 + mats :]
    w_refs, tok_ref, gain_ref, mg_ref, refs = refs[:3], refs[3], refs[4], refs[5], refs[6:]
    out_ref, tg_ref, gg_ref, refs = refs[0], refs[1], refs[2], refs[3:]
    xbuf, ybuf, keep, sbuf, srecv, ubuf, rbuf, hbuf, obuf, wbuf = refs[:10]
    xs, ys, yr, ss, sr, zs, zr, fs, fr, ws, ns, nr = refs[10:]
    e, c = lax.axis_index("expert"), lax.axis_index("dp")
    z, r = e // per, e % per
    x, y = r % 2, r // 2
    width = y_refs[0].shape[1]
    part = width // 4
    lines = width // OUTER
    peers = [(n, f) for n in range(per) for f in range(2)]
    trade = (y + c * (1 - 2 * y)) * 2 + x + (1 - c) * (1 - 2 * x)
    other = (y + (1 - c) * (1 - 2 * y)) * 2 + x + c * (1 - 2 * x)
    a_bit = (1 - c) * x + c * y
    b_bit = (1 - c) * y + c * x
    quarter = 2 * c + a_bit

    def device(n, f):
        return flip(r, n), (c + f) % 2

    bar = pltpu.get_barrier_semaphore()
    for d in range(1, OUTER):
        pl.semaphore_signal(
            bar, inc=1, device_id=((z + d) % OUTER * per + r, c), device_id_type=MESH
        )
    for n, f in peers[1:]:
        q, k = device(n, f)
        pl.semaphore_signal(bar, inc=1, device_id=(z * per + q, k), device_id_type=MESH)
    pl.semaphore_wait(bar, OUTER - 1 + 2 * per - 1)

    def block(q):
        return pl.ds(pl.multiple_of(q * part, part), part)

    targets = (
        (r, 1 - c, 2 * (1 - c) + (1 - c) * y + c * x),
        (trade, c, 2 * c + 1 - a_bit),
        (other, 1 - c, 2 * (1 - c) + 1 - b_bit),
    )

    def spread(m, i):
        q, k, at = targets[i]
        return pltpu.make_async_remote_copy(
            src_ref=y_refs[m].at[:, block(at)], dst_ref=ybuf.at[m, i + 1],
            send_sem=ys.at[m, i], recv_sem=yr.at[m, i],
            device_id=(z * per + q, k), device_id_type=MESH,
        )

    def swap(m, i):
        return pltpu.make_async_remote_copy(
            src_ref=sbuf.at[m, i], dst_ref=srecv.at[m, i], send_sem=ss.at[m, i],
            recv_sem=sr.at[m, i], device_id=(z * per + other, c), device_id_type=MESH,
        )

    def hop(m, i, j, way):
        return pltpu.make_async_remote_copy(
            src_ref=ubuf.at[m, i], dst_ref=rbuf.at[m, way, j],
            send_sem=zs.at[m, i], recv_sem=zr.at[m, way, j],
            device_id=((z + 1 - 2 * way) * per + r, c), device_id_type=MESH,
        )

    def final(m, t, f):
        there = a_bit + t * (1 - 2 * a_bit)
        core = (c + f) % 2
        q = ((1 - c) * y + c * there) * 2 + (1 - c) * there + c * x
        return pltpu.make_async_remote_copy(
            src_ref=hbuf.at[m, pl.ds(pl.multiple_of((there * 2 + core) * rows, rows), rows)],
            dst_ref=obuf.at[m, quarter], send_sem=fs.at[m, 2 * t + f],
            recv_sem=fr.at[m, quarter], device_id=(z * per + q, core), device_id_type=MESH,
        )

    def landed(m, q):
        return pltpu.make_async_remote_copy(
            src_ref=hbuf.at[m, pl.ds(0, rows)], dst_ref=obuf.at[m, q], send_sem=fs.at[m, 0],
            recv_sem=fr.at[m, q], device_id=(z * per + r, 1 - c), device_id_type=MESH,
        )

    strip = wbuf.shape[1]
    strips = width // strip
    jobs = [(k, q) for k in range(3) for q in range(strips)]

    def fetch(t):
        k, q = jobs[t]
        return pltpu.make_async_copy(
            w_refs[k].at[pl.ds(q * strip, strip)], wbuf.at[t % 2], ws.at[t % 2]
        )

    def pull_back(t):
        k, q = jobs[t]
        if t == 0:
            fetch(0).start()
        if t + 1 < len(jobs):
            fetch(t + 1).start()
        fetch(t).wait()
        got = lax.dot_general(
            y_refs[3 - k][...], wbuf[t % 2], (((1,), (1,)), ((), ())), preferred_element_type=F32
        )
        if k == 0:
            tg_ref[:, q * strip : (q + 1) * strip] = got
        else:
            tg_ref[:, q * strip : (q + 1) * strip] += got

    def norm_back():
        grad = tg_ref[...]
        values = tok_ref[...].astype(F32)
        scale = rms_scale(values)
        normed = values * scale
        gg_ref[...] = jnp.sum(grad * normed, axis=0, keepdims=True)
        grad = grad * gain_ref[...]
        centre = jnp.mean(grad * normed, axis=-1, keepdims=True)
        tg_ref[...] = mg_ref[...] + scale * (grad - normed * centre)

    loads = [
        pltpu.make_async_copy(x_refs[i], xbuf.at[i] if i < 3 else xbuf.at[3, 1], xs.at[i])
        for i in range(4)
    ]
    late = pltpu.make_async_remote_copy(
        src_ref=x_refs[0].at[0], dst_ref=xbuf.at[3, 0], send_sem=ns, recv_sem=nr,
        device_id=(z * per + targets[2][0], targets[2][1]), device_id_type=MESH,
    )
    def begin(m):
        for i in range(3):
            spread(m, i).start()

    begin(0)
    begin(1)
    late.start()
    for copy in loads:
        copy.start()
    for m in range(mats):
        ybuf[m, 0] = y_refs[m][:, block(quarter)]
    for copy in loads:
        copy.wait()
    order = [pick(t, z) for t in FAR]

    def pieces(j, bit):
        for t in range(2):
            at = j * lines + (1 - c) * (bit * 2 + t) * 2 * rows + c * (t * 2 + bit) * 2 * rows
            yield pl.ds(pl.multiple_of(at, 2 * rows), 2 * rows)

    def product(m, j, bit):
        total = None
        for i in range(4):
            left = jnp.concatenate([xbuf[i, SOURCE[m], at, :] for at in pieces(j, bit)], axis=0)
            term = jnp.dot(left, ybuf[m, i], preferred_element_type=F32)
            total = term if total is None else total + term
        return total

    edge = jnp.logical_or(z == 0, z == OUTER - 1)

    def outer(m):
        for i, j in enumerate(order):
            swap(m, i).wait_recv()
            ubuf[m, i] = (keep[m, i] + srecv[m, i].astype(F32)).astype(BF16)

            @pl.when(z == 0)
            def _():
                hop(m, i, j, 0).start()

            @pl.when(z > 0)
            def _():
                hop(m, i, j, 1).start()

    def inner(m):
        for i, j in enumerate(order):
            swap(m, i).wait_recv()

            @pl.when(j > z)
            def _():
                hop(m, 0, j, 0).wait_recv()
                ubuf[m, i] = (
                    keep[m, i] + srecv[m, i].astype(F32) + rbuf[m, 0, j].astype(F32)
                ).astype(BF16)
                hop(m, i, j, 0).start()

            @pl.when(j < z)
            def _():
                hop(m, 0, j, 1).wait_recv()
                ubuf[m, i] = (
                    keep[m, i] + srecv[m, i].astype(F32) + rbuf[m, 1, j].astype(F32)
                ).astype(BF16)
                hop(m, i, j, 1).start()

    for m in range(mats + 2):
        if m < mats:
            for i in range(3):
                spread(m, i).wait_recv()
            if m == 1:
                late.wait_recv()
            for i, j in enumerate(order + [z]):
                sbuf[m, i] = product(m, j, 1 - b_bit).astype(BF16)
                swap(m, i).start()
            if m + 2 < mats:
                begin(m + 2)
            for i, j in enumerate(order + [z]):
                keep[m, i] = product(m, j, b_bit)
        if 1 <= m <= mats:
            pl.when(edge)(functools.partial(outer, m - 1))
        if m >= 2:
            pl.when(jnp.logical_not(edge))(functools.partial(inner, m - 2))
        if m < 3:
            for t in range(m * strips, (m + 1) * strips):
                pull_back(t)
        elif m == 3:
            norm_back()

    last = OUTER - 1
    for m in range(mats):
        swap(m, last).wait_recv()
        keep[m, last] += srecv[m, last].astype(F32)

        @pl.when(z > 0)
        def _():
            hop(m, 0, z, 0).wait_recv()
            keep[m, last] += rbuf[m, 0, z].astype(F32)

        @pl.when(z < OUTER - 1)
        def _():
            hop(m, 0, z, 1).wait_recv()
            keep[m, last] += rbuf[m, 1, z].astype(F32)

        hbuf[m] = keep[m, last].astype(BF16)
        for t, f in ((1, 0), (1, 1), (0, 1)):
            final(m, t, f).start()

    for m in range(mats):
        mine = pl.ds(pl.multiple_of((a_bit * 2 + c) * rows, rows), rows)
        out_ref[m, :, block(quarter)] = keep[m, last, mine, :]
        for d in range(1, 4):
            q = (quarter + d) % 4
            landed(m, q).wait_recv()
            out_ref[m, :, block(q)] = obuf[m, q].astype(F32)
    late.wait_send()
    for m in range(mats):
        for i in range(3):
            spread(m, i).wait_send()
        for i in range(OUTER):
            swap(m, i).wait_send()
        for t, f in ((1, 0), (1, 1), (0, 1)):
            final(m, t, f).wait_send()
        for i, j in enumerate(order):
            hop(m, i, j, 0).wait_send()


SOURCE = (1, 0, 0, 0)


def weight_grads(lefts, rights, weights, tokens, gain, middle_grad, experts, number):
    span, width = rights[0].shape
    rows = width // (2 * experts)
    part = width // 4
    half = width // OUTER // 2
    mats = len(rights)
    vmem = pl.BlockSpec(memory_space=pltpu.VMEM)
    hbm = pl.BlockSpec(memory_space=pltpu.HBM)
    dma = pltpu.SemaphoreType.DMA
    return pl.pallas_call(
        functools.partial(weights_body, rows),
        out_shape=(
            jax.ShapeDtypeStruct((mats, rows, width), F32),
            jax.ShapeDtypeStruct((span, width), F32),
            jax.ShapeDtypeStruct((1, width), F32),
        ),
        in_specs=[hbm] * 4 + [vmem] * mats + [hbm] * 3 + [vmem] * 3,
        out_specs=(vmem,) * 3,
        scratch_shapes=[
            pltpu.VMEM((4, 2, width, span), BF16),
            pltpu.VMEM((mats, 4, span, part), BF16),
            pltpu.VMEM((mats, OUTER, half, part), F32),
            pltpu.VMEM((mats, OUTER, half, part), BF16),
            pltpu.VMEM((mats, OUTER, half, part), BF16),
            pltpu.VMEM((mats, OUTER - 1, half, part), BF16),
            pltpu.VMEM((mats, 2, OUTER, half, part), BF16),
            pltpu.VMEM((mats, half, part), BF16),
            pltpu.VMEM((mats, 4, rows, part), BF16),
            pltpu.VMEM((2, width // OUTER // 2, width), BF16),
            dma((4,)),
            dma((mats, 3)),
            dma((mats, 3)),
            dma((mats, OUTER)),
            dma((mats, OUTER)),
            dma((mats, OUTER - 1)),
            dma((mats, 2, OUTER)),
            dma((mats, 4)),
            dma((mats, 4)),
            dma((2,)),
            dma,
            dma,
        ],
        compiler_params=pltpu.CompilerParams(
            collective_id=number, has_side_effects=True, vmem_limit_bytes=62 << 20
        ),
        name="weight_grads",
    )(*lefts, *rights, *weights, tokens, gain, middle_grad)


def heads_back_body(*refs):
    q_ref, k_ref, v_ref, da_ref, lse_ref, limit_ref, cos_ref, sin_ref = refs[:8]
    qpre, kpre, gains_ref, vg_ref, ql_ref, kl_ref, gq_ref, gk_ref, dq, dk = refs[8:]
    span = q_ref.shape[0]
    score_scale = HD ** (-0.5)
    column = lax.broadcasted_iota(jnp.int32, (span, span), 1).astype(F32)
    across = (((1,), (1,)), ((), ()))
    down = (((0,), (0,)), ((), ()))

    @pl.loop(0, NH)
    def _(h):
        columns = pl.ds(pl.multiple_of(h * HD, HD), HD)
        query, key, grad = q_ref[:, columns], k_ref[:, columns], da_ref[:, columns]
        scores = lax.dot_general(query, key, across, preferred_element_type=F32)
        scores = jnp.where(column <= limit_ref[...], scores * score_scale, -1e30)
        weights = jnp.exp(scores - lse_ref[h])
        weights_grad = lax.dot_general(
            grad, v_ref[:, columns], across, preferred_element_type=F32
        )
        vg_ref[:, columns] = lax.dot_general(
            weights.astype(BF16), grad, down, preferred_element_type=F32
        ).astype(BF16)
        centre = jnp.sum(weights * weights_grad, axis=-1, keepdims=True)
        score_grad = (weights * (weights_grad - centre)).astype(BF16)

        def turn_back(rot_grad):
            return rot_grad * cos_ref[...] + pltpu.roll(rot_grad * sin_ref[...], HD // 2, 1)

        query_grad = jnp.dot(score_grad, key, preferred_element_type=F32) * score_scale
        key_grad = lax.dot_general(score_grad, query, down, preferred_element_type=F32)
        dq[:, columns] = turn_back(query_grad)
        dk[:, columns] = turn_back(key_grad * score_scale)

    for row, pre, grad_ref, low_ref, gain_ref in (
        (1, qpre, dq, ql_ref, gq_ref),
        (2, kpre, dk, kl_ref, gk_ref),
    ):
        grad = grad_ref[...]
        values = pre[...]
        scale = rms_scale(values)
        normed = values * scale
        gain_ref[...] = jnp.sum(grad * normed, axis=0, keepdims=True)
        grad = grad * gains_ref[row : row + 1]
        centre = jnp.mean(grad * normed, axis=-1, keepdims=True)
        low_ref[...] = (scale * (grad - normed * centre)).astype(BF16)


def heads_back(query, key, value, grad, log_total, limit, tables, query_pre, key_pre, gains):
    span, width = query.shape
    vmem = pl.BlockSpec(memory_space=pltpu.VMEM)
    low = jax.ShapeDtypeStruct((span, width), BF16)
    line = jax.ShapeDtypeStruct((1, width), F32)
    return pl.pallas_call(
        heads_back_body,
        out_shape=(low, low, low, line, line),
        in_specs=[vmem] * 11,
        out_specs=(vmem,) * 5,
        scratch_shapes=[pltpu.VMEM((span, width), F32), pltpu.VMEM((span, width), F32)],
        cost_estimate=pl.CostEstimate(
            flops=14 * span * span * width,
            bytes_accessed=40 * span * width,
            transcendentals=NH * span * span,
        ),
        compiler_params=pltpu.CompilerParams(vmem_limit_bytes=40 << 20),
        name="heads_back",
    )(query, key, value, grad, log_total, limit, *tables, query_pre, key_pre, gains)


def body(
    tokens,
    cotangent,
    lengths,
    routes,
    attention_gain,
    query_gain,
    key_gain,
    feedforward_gain,
    query_weight,
    key_weight,
    value_weight,
    output_weight,
    router_weight,
    expert_gate_up,
    expert_down,
):
    span, width = tokens.shape
    core = lax.axis_index("dp")
    both = ("expert", "dp")
    devices = lax.axis_size("expert") * 2
    gains = jnp.concatenate([attention_gain, query_gain, key_gain, feedforward_gain])
    packed = jnp.concatenate([router_weight, gains.reshape(4, -1).T], axis=1)
    other = lax.ppermute(packed, both, [(d, d ^ 1) for d in range(devices)])
    packed = jnp.where(
        core == 0,
        jnp.concatenate([packed, other], axis=0),
        jnp.concatenate([other, packed], axis=0),
    )
    router_full, gains = packed[:, :-4], packed[:, -4:].T.astype(F32)
    gain_in, gain_query, gain_key, gain_mid = gains[0], gains[1], gains[2], gains[3]
    experts = router_full.shape[1]
    cap = span * TOP // experts
    per = experts // OUTER

    seq_length = lengths[0]
    index_rows = jnp.arange(span, dtype=jnp.int32)
    expert_ids = jnp.arange(experts, dtype=jnp.int32)
    hits = jnp.any(routes[None, :, :] == expert_ids[:, None, None], axis=-1)
    hits = hits & (index_rows < seq_length)[None, :]
    earlier = (index_rows[:, None] < index_rows[None, :]).astype(BF16)
    before = jnp.dot(hits.astype(BF16), earlier, preferred_element_type=F32)
    kept = hits & (before < cap)
    pos = jnp.where(kept, before, -1.0)
    inputs = tokens.astype(F32)
    cosine_table, sine_table = rotary_tables(index_rows.astype(F32))
    signs = jnp.where(jnp.arange(HD) < HD // 2, -1.0, 1.0)
    limit = jnp.minimum(index_rows, seq_length - 1).astype(F32)[:, None]
    tables = (cosine_table, sine_table * signs)
    (
        cot_slots, pos_here, pos_all, query_full, key_full, value_full, output_full,
        other_gate_up, other_down, turned,
        normed_in, query_pre, key_pre, query_rot, key_rot, value_all, log_total, attended,
        middle, normed_mid, gates,
    ) = attend(
        tokens, cotangent, pos[:, None, :], gains, tables, limit, router_full,
        (query_weight, key_weight, value_weight, output_weight, expert_gate_up, expert_down),
        cap, 1,
    )
    norm_mid_back = jax.vjp(norm_apply, middle, gain_mid)[1]
    def mul(left, right, spec):
        return jnp.einsum(spec, left, right, preferred_element_type=F32)

    back_rows, prob_grad, slots, gate_grad_low, up_grad_low, hidden_gated, expert_out = run_experts(
        normed_mid, gates.T[:, None, :], pos_all, pos_here, cot_slots,
        (expert_gate_up, expert_down, other_gate_up, other_down), 2,
    )
    prob_grad = prob_grad[:, 0].T
    back_rows, turned = lax.optimization_barrier((back_rows, turned))
    wide = per == 4 and width % 512 == 0
    if wide:

        def moved(d, cross):
            to = d % 2 ^ cross
            return (d // 2 ^ 1 + to) * 2 + to

        lefts = [turned, lax.ppermute(turned, both, [(d, d ^ 1) for d in range(devices)])] + [
            lax.ppermute(
                turned[1] if cross else turned, both, [(d, moved(d, cross)) for d in range(devices)]
            )
            for cross in range(2)
        ]

    upstream = cotangent.astype(F32)
    logit_grad = (
        gates * (prob_grad - jnp.sum(gates * prob_grad, axis=-1, keepdims=True))
    ).astype(BF16)
    grad_router = mul(normed_mid, logit_grad, "td,te->de")
    mid_normed_grad = mul(logit_grad, router_full, "te,de->td") + back_rows
    mid_input_grad, grad_mid_gain = norm_mid_back(mid_normed_grad)
    middle_grad = upstream + mid_input_grad
    branch_grad = middle_grad.astype(BF16)
    attended_grad = mul(branch_grad, output_full, "to,io->ti").astype(BF16)
    value_grad, query_low, key_low, grad_query_gain, grad_key_gain = heads_back(
        query_rot, key_rot, value_all, attended_grad, log_total, limit, tables,
        query_pre, key_pre, gains,
    )
    grad_query_gain, grad_key_gain = grad_query_gain[0], grad_key_gain[0]
    rights = (branch_grad, value_grad, key_low, query_low)
    if wide:
        expert_out, lefts, rights = lax.optimization_barrier((expert_out, lefts, rights))
        grads, grad_tokens, grad_in_gain = weight_grads(
            lefts, rights, (query_full, key_full, value_full), tokens, gain_in[None],
            middle_grad, experts, 5,
        )
        grad_in_gain = grad_in_gain[0]
    else:
        grads = []
        for source, right in zip(SOURCE, rights):
            grad = jnp.dot(turned[source], right, preferred_element_type=F32).astype(BF16)
            grid = grad.reshape(experts, 2, width // experts // 2, width).swapaxes(0, 1)
            half = lax.psum_scatter(grid, "dp", scatter_dimension=0, tiled=False)
            half = lax.psum_scatter(half, "expert", scatter_dimension=0, tiled=False)
            grads.append(half.astype(F32))
        normed_in_grad = mul(query_low, query_full, "to,io->ti")
        normed_in_grad = normed_in_grad + mul(key_low, key_full, "to,io->ti")
        normed_in_grad = normed_in_grad + mul(value_grad, value_full, "to,io->ti")
        input_grad, grad_in_gain = jax.vjp(norm_apply, inputs, gain_in)[1](normed_in_grad)
        grad_tokens = middle_grad + input_grad

    small = jnp.concatenate(
        [
            jnp.stack([grad_in_gain, grad_query_gain, grad_key_gain, grad_mid_gain]).T,
            grad_router,
        ],
        axis=1,
    )
    kinds = small.shape[1]
    small = small.reshape(OUTER, 2 * per, -1, kinds).transpose(1, 0, 3, 2)
    output, small, grad_gate_up, grad_down = combine(
        expert_out, pos_all, middle, small.reshape(2 * per, OUTER, 1, -1), slots, cot_slots,
        gate_grad_low, up_grad_low, hidden_gated, 4,
    )
    small = small.reshape(kinds, -1).T
    return (
        output,
        grad_tokens,
        small[:, 0],
        small[:, 1],
        small[:, 2],
        small[:, 3],
        grads[3],
        grads[2],
        grads[1],
        grads[0],
        small[:, 4:],
        grad_gate_up[None],
        grad_down[None],
    )


def solution(mesh):
    both = P(("expert", "dp"))
    rows = P(("expert", "dp"), None)
    in_specs = (rows, rows, both, rows) + (P("dp"),) * 4 + (P("dp", None),) * 5 + (
        P("expert", None, None, "dp"),
        P("expert", None, "dp"),
    )
    out_specs = (rows, rows) + (both,) * 4 + (rows,) * 5 + (
        P("expert", None, None, "dp"),
        P("expert", None, "dp"),
    )
    return jax.shard_map(body, mesh=mesh, in_specs=in_specs, out_specs=out_specs, check_vma=False)
```
